128 devices in a mesh: rep: 4 (over z_hi, core), ctx: 4 (over y), fsdp: 8 (over z_lo, x).
Axes of the slice: x: 4, y: 4, z: 4 (z_hi: 2, z_lo: 2; z = z_hi * 2 + z_lo), core: 2. Of those that a mesh axis runs over, the one named last changes fastest.
Arguments:
- tokens: bfloat16 [32, 1024, 1024], P(('rep', 'fsdp'), 'ctx'), may hold values from -6 to 6
- norm_gain: bfloat16 [1024], P(('ctx', 'fsdp')), may hold values from 0.5 to 1.5
- norm_shift: bfloat16 [1024], P(('ctx', 'fsdp')), may hold values from -2 to 2
- triple_weight: bfloat16 [1024, 3072], P(('ctx', 'fsdp')), may hold values from -0.25 to 0.25
- mixer_weight: bfloat16 [1024, 1024], P(('ctx', 'fsdp')), may hold values from -0.75 to 0.75
- inner_weight: bfloat16 [1024, 4096], P(('ctx', 'fsdp')), may hold values from -0.1875 to 0.1875
- inner_bias: bfloat16 [4096], P(('ctx', 'fsdp')), may hold values from -2 to 2
- outer_weight: bfloat16 [4096, 1024], P(('ctx', 'fsdp')), may hold values from -0.125 to 0.125
- outer_bias: bfloat16 [1024], P(('ctx', 'fsdp')), may hold values from -2 to 2
- prefix_length: int32 [32], P(('rep', 'fsdp')), may hold values from 102 to 512
- pad_mask: int32 [32], P(('rep', 'fsdp')), may hold values from 0 to 31, each once
- cotangent: bfloat16 [32, 1024, 1024], P(('rep', 'fsdp'), 'ctx'), may hold values from -6 to 6
Outputs:
- layer_output: bfloat16 [32, 1024, 1024], P(('rep', 'fsdp'), 'ctx')
- input_grad: bfloat16 [32, 1024, 1024], P(('rep', 'fsdp'), 'ctx')
- grad_norm_gain: float32 [1024], P(('ctx', 'fsdp'))
- grad_norm_shift: float32 [1024], P(('ctx', 'fsdp'))
- grad_triple_weight: float32 [1024, 3072], P(('ctx', 'fsdp'))
- grad_mixer_weight: float32 [1024, 1024], P(('ctx', 'fsdp'))
- grad_inner_weight: float32 [1024, 4096], P(('ctx', 'fsdp'))
- grad_inner_bias: float32 [4096], P(('ctx', 'fsdp'))
- grad_outer_weight: float32 [4096, 1024], P(('ctx', 'fsdp'))
- grad_outer_bias: float32 [1024], P(('ctx', 'fsdp'))
The draws below stay inside these ranges and needn't reach their ends.
Inputs may be any that keep to these rules, and one draw needn't show every extreme that they name: `pad_mask`: each number of 0 to 31 stands in exactly one slot; the slot holding 0 is the pad slot.
All inputs are finite; a program needn't handle non-finite values.
Results may differ from the reference program's by a relative error of at most 0.025.
Values may be sent and summed in bfloat16 or wider, within the bound.
No kernel may reach another device: no remote copies, remote signals or barrier semaphores. Data moves between devices by JAX's collectives and lax.ppermute only.
A program may use at most 192 MiB of HBM per device.

```python
import jax
import jax.numpy as jnp
from jax import lax

D = 1024
HEADS = 16
HEAD_DIM = 64
ROT = 32
FF = 4096
SEQ_LEN = 1024
SEQS = 32


def with_ends(drawn, key, smallest, largest):
    spot = [jax.random.randint(jax.random.fold_in(key, axis), (), 0, length) for axis, length in enumerate(drawn.shape)]
    longest = drawn.shape.index(max(drawn.shape))
    neighbour = spot[:longest] + [(spot[longest] + 1) % drawn.shape[longest]] + spot[longest + 1:]
    return drawn.at[tuple(spot)].set(smallest).at[tuple(neighbour)].set(largest)


def steps_of(key, dims, pieces, least, top_value):
    def one(axis_at, shards_of):
        steps = jax.random.uniform(jax.random.fold_in(jax.random.fold_in(key, 6), axis_at), (shards_of,), jnp.float32, least / len(pieces), top_value / len(pieces))
        return jnp.repeat(jnp.exp(steps), dims[axis_at] // shards_of).reshape((-1,) + (1,) * (len(dims) - axis_at - 1))

    loudness = one(*pieces[0])
    for cut in pieces[1:]:
        loudness = loudness * one(*cut)
    return loudness


def normal_values(key, extent, deviation, reach, cuts=(), kind=jnp.bfloat16):
    gain = steps_of(key, extent, cuts, -0.22, 0.18) if cuts else 1.0
    drawn = jax.random.normal(key, extent, jnp.float32) * deviation * gain
    return jnp.minimum(jnp.maximum(drawn, -reach), reach).astype(kind)


def setup_inputs(seed: int = 0) -> dict:
    key_list = jax.random.split(jax.random.key(seed), 13)
    return {
        "tokens": normal_values(key_list[0], (SEQS, SEQ_LEN, D), 1.0, 6.0, ((0, 32), (1, 4))),
        "norm_gain": jnp.clip(1.0 + 0.1 * jax.random.normal(key_list[1], (D,), jnp.float32), 0.5, 1.5).astype(jnp.bfloat16),
        "norm_shift": normal_values(key_list[2], (D,), 0.3, 2.0, ((0, 32),)),
        "triple_weight": normal_values(key_list[3], (D, 3 * D), (D // 2) ** -0.5, 0.25, ((0, 32),)),
        "mixer_weight": normal_values(key_list[4], (D, D), (D // 16) ** -0.5, 0.75, ((0, 32),)),
        "inner_weight": normal_values(key_list[5], (D, FF), D ** -0.5, 0.1875, ((0, 32),)),
        "inner_bias": normal_values(key_list[6], (FF,), 0.3, 2.0, ((0, 32),)),
        "outer_weight": normal_values(key_list[7], (FF, D), (FF // 2) ** -0.5, 0.125, ((0, 32),)),
        "outer_bias": normal_values(key_list[8], (D,), 0.3, 2.0, ((0, 32),)),
        "prefix_length": with_ends(jax.random.randint(key_list[9], (SEQS,), SEQ_LEN // 10, SEQ_LEN // 2 + 1), jax.random.fold_in(key_list[9], 1), SEQ_LEN // 10, (SEQ_LEN // 2 + 1) - 1).astype(jnp.int32),
        "pad_mask": jax.random.permutation(key_list[10], SEQS).astype(jnp.int32),
        "cotangent": normal_values(key_list[11], (SEQS, SEQ_LEN, D), 1.0, 6.0, ((0, 32), (1, 4))),
    }


eps = 1e-05
highest = lax.Precision.HIGHEST

@jax.custom_vjp
def low(v):
    return lax.optimization_barrier(v.astype(jnp.bfloat16)).astype(jnp.float32)

@jax.custom_vjp
def low_back(v):
    return v

def low_keep(v):
    return (low(v), None)

def low_pass(kept, grad):
    return (grad,)

def back_keep(v):
    return (v, None)

def back_low(kept, grad):
    return (low(grad),)
low.defvjp(low_keep, low_pass)
low_back.defvjp(back_keep, back_low)

def rounded(value):
    return low(low_back(value))

def angles(positions):
    frequency = 10000.0 ** (-(jnp.arange(ROT // 2, dtype=jnp.float32) * 2.0) / ROT)
    phases = positions.astype(jnp.float32)[:, None] * frequency[None, :]
    return (jnp.cos(phases), jnp.sin(phases))

def rotate(field, cos_table, sin_table):
    leading = field.shape[:-1]
    paired = field[..., :ROT].reshape(leading + (ROT // 2, 2))
    even_part = paired[..., 0]
    odd_part = paired[..., 1]
    cos_wide = cos_table[:, None, :]
    sin_wide = sin_table[:, None, :]
    turned = jnp.stack([even_part * cos_wide - odd_part * sin_wide, odd_part * cos_wide + even_part * sin_wide], -1)
    return jnp.concatenate([turned.reshape(leading + (ROT,)), field[..., ROT:]], -1)

def layer(input_rows, norm_gain, norm_shift, triple_weight, mixer_weight, inner_weight, inner_bias, outer_weight, outer_bias, prefix_span):
    length = input_rows.shape[0]
    center = input_rows - lax.optimization_barrier(jnp.mean(input_rows, -1, keepdims=True))
    spread = lax.optimization_barrier(jnp.mean(center * center, -1, keepdims=True))
    normalized_input = low(center * lax.rsqrt(spread + eps) * norm_gain + norm_shift)
    query_key_value = low_back(jnp.dot(normalized_input, triple_weight, precision=highest))
    heads_shape = (length, HEADS, HEAD_DIM)
    cos_table, sin_table = angles(jnp.arange(length))
    queries = low(rotate(query_key_value[:, :D].reshape(heads_shape), cos_table, sin_table) * HEAD_DIM ** (-0.5))
    key_rows = low(rotate(query_key_value[:, D:2 * D].reshape(heads_shape), cos_table, sin_table))
    value_rows = low(query_key_value[:, 2 * D:].reshape(heads_shape))
    scores = low_back(jnp.einsum('qhd,khd->hqk', queries, key_rows, precision=highest))
    places = jnp.arange(length)
    allowed = (places[None, :] <= places[:, None]) | (places[None, :] < prefix_span)
    scores = jnp.where(allowed[None], scores, -1e+30)
    probability = jax.nn.softmax(scores, -1)
    mixture = jnp.einsum('hqk,khd->qhd', low(probability), value_rows, precision=highest).reshape(length, D)
    attention = jnp.dot(rounded(mixture), mixer_weight, precision=highest)
    preact = low_back(jnp.dot(normalized_input, inner_weight, precision=highest) + inner_bias)
    gelu_result = low(jax.nn.gelu(preact, approximate=True))
    feedforward = jnp.dot(gelu_result, outer_weight, precision=highest) + outer_bias
    return input_rows + attention + feedforward

def reference(tokens, norm_gain, norm_shift, triple_weight, mixer_weight, inner_weight, inner_bias, outer_weight, outer_bias, prefix_length, pad_mask, cotangent):
    params = tuple((member.astype(jnp.float32) for member in (norm_gain, norm_shift, triple_weight, mixer_weight, inner_weight, inner_bias, outer_weight, outer_bias)))

    def one_sequence(totals, single_element):
        input_rows, prefix_span, slot_number, incoming_gradient = single_element

        def forward(source, *weights):
            return layer(source, *weights, prefix_span)
        output, reverse_function = jax.vjp(forward, input_rows.astype(jnp.float32), *params)
        visible = (slot_number != 0).astype(jnp.float32)
        weight_gradients = reverse_function(incoming_gradient.astype(jnp.float32) * visible)
        totals = tuple((running + newest for running, newest in zip(totals, weight_gradients[1:])))
        return (totals, (output.astype(jnp.bfloat16), weight_gradients[0].astype(jnp.bfloat16)))
    initial = tuple((jnp.zeros(member.shape, jnp.float32) for member in params))
    totals, (outputs, input_grad) = lax.scan(one_sequence, initial, (tokens, prefix_length, pad_mask, cotangent))
    return (outputs, input_grad, totals[0], totals[1], totals[2], totals[3], totals[4], totals[5], totals[6], totals[7])
```

```python
from functools import partial

import jax
import jax.numpy as jnp
from jax import lax
from jax.sharding import PartitionSpec as P

HEADS = 16
HEAD_DIM = 64
ROT = 32


eps = 1e-05


def angles(positions):
    frequency = 10000.0 ** (-(jnp.arange(ROT // 2, dtype=jnp.float32) * 2.0) / ROT)
    phases = positions.astype(jnp.float32)[:, None] * frequency[None, :]
    return (jnp.cos(phases), jnp.sin(phases))


def rotate(field, cos_table, sin_table):
    leading = field.shape[:-1]
    paired = field[..., :ROT].reshape(leading + (ROT // 2, 2))
    even_part = paired[..., 0]
    odd_part = paired[..., 1]
    cos_wide = cos_table[:, None, :]
    sin_wide = sin_table[:, None, :]
    turned = jnp.stack(
        [even_part * cos_wide - odd_part * sin_wide, odd_part * cos_wide + even_part * sin_wide], -1
    )
    return jnp.concatenate([turned.reshape(leading + (ROT,)), field[..., ROT:]], -1)


def ring_pairs(n, step):
    return [(i, (i + step) % n) for i in range(n)]


def ring_gather(block, axis):
    n = lax.axis_size(axis)
    half = block.shape[0] // 2
    from_left = lax.ppermute(block, axis, ring_pairs(n, 1))
    from_right = lax.ppermute(block, axis, ring_pairs(n, -1))
    far_first = lax.ppermute(from_left[:half], axis, ring_pairs(n, 1))
    far_second = lax.ppermute(from_right[half:], axis, ring_pairs(n, -1))
    far = jnp.concatenate([far_first, far_second], 0)
    return jnp.stack([block, from_right, far, from_left])


def ring_scatter(parts, axis):
    n = lax.axis_size(axis)
    half = parts.shape[1] // 2
    wire = jnp.bfloat16
    got_left = lax.ppermute(parts[2, :half].astype(wire), axis, ring_pairs(n, 1))
    got_right = lax.ppermute(parts[2, half:].astype(wire), axis, ring_pairs(n, -1))
    to_right = jnp.concatenate([parts[1, :half] + got_left.astype(jnp.float32), parts[1, half:]], 0)
    to_left = jnp.concatenate([parts[3, :half], parts[3, half:] + got_right.astype(jnp.float32)], 0)
    from_left = lax.ppermute(to_right.astype(wire), axis, ring_pairs(n, 1))
    from_right = lax.ppermute(to_left.astype(wire), axis, ring_pairs(n, -1))
    return parts[0] + from_left.astype(jnp.float32) + from_right.astype(jnp.float32)


def ring_all_to_all(payload, axis):
    n = lax.axis_size(axis)
    me = lax.axis_index(axis)
    pick = lambda d: lax.dynamic_index_in_dim(payload, d % n, 0, keepdims=False)
    got = [pick(me)] + [
        lax.ppermute(pick(me + s), axis, ring_pairs(n, s)) for s in range(1, n)
    ]
    mirrored = jnp.stack([got[(-k) % n] for k in range(n)])
    doubled = jnp.concatenate([mirrored, mirrored], 0)
    return lax.dynamic_slice_in_dim(doubled, n - me, n, 0)


def replica_sum(values, axis):
    n = lax.axis_size(axis)
    f32, wire = jnp.float32, jnp.bfloat16
    values = values.astype(wire)
    if n != 4:
        return lax.psum(values, axis).astype(f32)
    pair = values.astype(f32) + lax.ppermute(values, axis, [(i, i ^ 1) for i in range(n)]).astype(f32)
    pair = pair.astype(wire)
    return pair.astype(f32) + lax.ppermute(pair, axis, [(i, i ^ 2) for i in range(n)]).astype(f32)


def masked_scores(queries, key_rows, prefix_length, places):
    scores = jnp.einsum("qhd,khd->hqk", queries, key_rows, preferred_element_type=jnp.float32)
    allowed = (places[None, :] <= places[:, None]) | (places[None, :] < prefix_length)
    return jnp.where(allowed[None], scores, -1e30)


def local(
    tokens,
    norm_gain,
    norm_shift,
    triple_weight,
    mixer_weight,
    inner_weight,
    inner_bias,
    outer_weight,
    outer_bias,
    prefix_length,
    pad_mask,
    cotangent,
):
    nc = lax.axis_size("ctx")
    nf = lax.axis_size("fsdp")
    me = lax.axis_index("ctx")
    _, own_rows, width = tokens.shape
    length = own_rows * nc
    shard_rows = triple_weight.shape[0]
    heads_here = HEADS // nc
    head_cols = heads_here * HEAD_DIM
    ff_here = inner_weight.shape[1] // nc
    ff_rows = outer_weight.shape[0]
    f32, bf16 = jnp.float32, jnp.bfloat16

    triple_cols = (
        triple_weight.reshape(shard_rows, 3, nc, head_cols)
        .transpose(2, 0, 1, 3)
        .reshape(nc, shard_rows, 3 * head_cols)
    )
    inner_cols = inner_weight.reshape(shard_rows, nc, ff_here).transpose(1, 0, 2)
    small = jnp.stack([norm_gain, norm_shift, outer_bias], -1)
    small = jnp.pad(small, ((0, 0), (0, 128 - small.shape[-1])))
    small = jnp.broadcast_to(small[None], (nc,) + small.shape)
    column_payload = jnp.concatenate([triple_cols, inner_cols, small], -1)
    column_payload = ring_all_to_all(column_payload, "ctx")
    column_block = lax.all_gather(column_payload, "fsdp", axis=0, tiled=False)
    column_block = column_block.swapaxes(0, 1).reshape(nc * nf * shard_rows, -1)
    triple_here = column_block[:, : 3 * head_cols]
    inner_here = column_block[:, 3 * head_cols : 3 * head_cols + ff_here]
    gain = column_block[:, 3 * head_cols + ff_here].astype(f32)
    shift = column_block[:, 3 * head_cols + ff_here + 1].astype(f32)
    obias = column_block[:, 3 * head_cols + ff_here + 2].astype(f32)

    bias_rows = jnp.pad(inner_bias[None], ((0, 15), (0, width - inner_bias.shape[0])))
    row_payload = jnp.concatenate([mixer_weight, outer_weight, bias_rows], 0)
    row_block = lax.all_gather(row_payload, "fsdp", axis=0, tiled=False)
    mixer_here = row_block[:, :shard_rows].reshape(nf * shard_rows, width)
    outer_here = row_block[:, shard_rows : shard_rows + ff_rows].reshape(nf * ff_rows, width)
    ibias_here = row_block[:, shard_rows + ff_rows, : inner_bias.shape[0]].reshape(-1).astype(f32)

    all_tokens = ring_gather(tokens[0], "ctx").reshape(length, width)
    visible = (pad_mask[0] != 0).astype(f32)
    own_upstream = cotangent[0].astype(f32) * visible
    all_upstream = ring_gather(own_upstream.astype(bf16), "ctx").reshape(length, width)

    input_rows = all_tokens.astype(f32)
    center = input_rows - jnp.mean(input_rows, -1, keepdims=True)
    scaling = lax.rsqrt(jnp.mean(center * center, -1, keepdims=True) + eps)
    whitened = center * scaling
    normed = (whitened * gain + shift).astype(bf16)

    owners = (me + jnp.arange(nc)) % nc
    positions = (owners[:, None] * own_rows + jnp.arange(own_rows)[None, :]).reshape(length)
    cos_table, sin_table = angles(positions)
    query_key_value = jnp.dot(normed, triple_here, preferred_element_type=f32)
    heads_shape = (length, heads_here, HEAD_DIM)
    queries = (
        rotate(query_key_value[:, :head_cols].reshape(heads_shape), cos_table, sin_table)
        * HEAD_DIM ** (-0.5)
    ).astype(bf16)
    key_rows = rotate(
        query_key_value[:, head_cols : 2 * head_cols].reshape(heads_shape), cos_table, sin_table
    ).astype(bf16)
    value_rows = query_key_value[:, 2 * head_cols :].reshape(heads_shape).astype(bf16)
    span = prefix_length[0]
    scores = masked_scores(queries, key_rows, span, positions)
    row_peak = jnp.max(scores, -1, keepdims=True)
    exponents = jnp.exp(scores - row_peak)
    row_total = jnp.sum(exponents, -1, keepdims=True)
    log_total = row_peak + jnp.log(row_total)
    probability = exponents / row_total
    mixture = jnp.einsum(
        "hqk,khd->qhd", probability.astype(bf16), value_rows, preferred_element_type=f32
    )
    mixture = mixture.reshape(length, head_cols).astype(bf16)
    attention = jnp.dot(mixture, mixer_here, preferred_element_type=f32)
    preact = jnp.dot(normed, inner_here, preferred_element_type=f32) + ibias_here
    gelu_result = jax.nn.gelu(preact, approximate=True).astype(bf16)
    feedforward = jnp.dot(gelu_result, outer_here, preferred_element_type=f32)
    block_sum = ring_scatter((attention + feedforward).reshape(nc, own_rows, width), "ctx")
    layer_output = (tokens[0].astype(f32) + block_sum + obias).astype(bf16)

    ones_block = jnp.ones((length, 16), bf16)
    row_lhs = jnp.concatenate([mixture, gelu_result, ones_block], -1)
    row_product = jnp.dot(row_lhs.T, all_upstream, preferred_element_type=f32).astype(bf16)
    grad_activated = jnp.dot(all_upstream, outer_here.T, preferred_element_type=f32)
    unused_value, gelu_pull = jax.vjp(partial(jax.nn.gelu, approximate=True), preact)
    grad_before_gelu = gelu_pull(grad_activated)[0].astype(bf16)
    grad_inner_weight = jnp.dot(normed.T, grad_before_gelu, preferred_element_type=f32)
    grad_inner_bias = jnp.sum(grad_before_gelu.astype(f32), 0)
    grad_mixture = jnp.dot(all_upstream, mixer_here.T, preferred_element_type=f32)
    grad_mixture = grad_mixture.reshape(heads_shape).astype(bf16)
    again_scores = masked_scores(queries, key_rows, span, positions)
    again_probability = jnp.exp(again_scores - log_total)
    grad_probability = jnp.einsum(
        "qhd,khd->hqk", grad_mixture, value_rows, preferred_element_type=f32
    )
    inner_sum = jnp.sum(again_probability * grad_probability, -1, keepdims=True)
    grad_scores = (again_probability * (grad_probability - inner_sum)).astype(bf16)
    grad_queries = jnp.einsum("hqk,khd->qhd", grad_scores, key_rows, preferred_element_type=f32)
    grad_keys = jnp.einsum("hqk,qhd->khd", grad_scores, queries, preferred_element_type=f32)
    grad_values = jnp.einsum(
        "hqk,qhd->khd", again_probability.astype(bf16), grad_mixture, preferred_element_type=f32
    )
    flat_shape = (length, head_cols)
    grad_query_key_value = jnp.concatenate(
        [
            rotate(grad_queries * HEAD_DIM ** (-0.5), cos_table, -sin_table).reshape(flat_shape),
            rotate(grad_keys, cos_table, -sin_table).reshape(flat_shape),
            grad_values.reshape(flat_shape),
        ],
        -1,
    ).astype(bf16)
    grad_triple_weight = jnp.dot(normed.T, grad_query_key_value, preferred_element_type=f32)
    grad_normed = jnp.dot(grad_query_key_value, triple_here.T, preferred_element_type=f32)
    grad_normed = grad_normed + jnp.dot(grad_before_gelu, inner_here.T, preferred_element_type=f32)
    grad_normed = ring_scatter(grad_normed.reshape(nc, own_rows, width), "ctx")

    own_whitened = whitened[:own_rows]
    own_scaling = scaling[:own_rows]
    grad_norm_gain = jnp.sum(grad_normed * own_whitened, 0)
    grad_norm_shift = jnp.sum(grad_normed, 0)
    grad_white = grad_normed * gain
    grad_inputs = own_scaling * (
        grad_white
        - jnp.mean(grad_white, -1, keepdims=True)
        - own_whitened * jnp.mean(grad_white * own_whitened, -1, keepdims=True)
    )
    input_grad = (own_upstream + grad_inputs).astype(bf16)

    small_grads = jnp.stack([grad_norm_gain, grad_norm_shift], -1)
    small_grads = jnp.pad(small_grads, ((0, 0), (0, 128 - small_grads.shape[-1])))
    column_grads = jnp.concatenate(
        [grad_triple_weight, grad_inner_weight, small_grads], -1
    ).astype(bf16)
    column_grads = column_grads.reshape(nc, nf, shard_rows, -1).swapaxes(0, 1).reshape(width, -1)
    column_grads = lax.psum_scatter(column_grads, "fsdp", scatter_dimension=0, tiled=True)
    column_grads = replica_sum(column_grads, "rep").astype(bf16)
    column_grads = column_grads.reshape(nc, shard_rows, -1)
    column_grads = ring_all_to_all(column_grads, "ctx").astype(f32)
    grad_triple_out = (
        column_grads[:, :, : 3 * head_cols]
        .reshape(nc, shard_rows, 3, head_cols)
        .transpose(1, 2, 0, 3)
        .reshape(shard_rows, 3 * nc * head_cols)
    )
    grad_inner_out = (
        column_grads[:, :, 3 * head_cols : 3 * head_cols + ff_here]
        .transpose(1, 0, 2)
        .reshape(shard_rows, nc * ff_here)
    )
    grad_gain_out = jnp.sum(column_grads[:, :, 3 * head_cols + ff_here], 0)
    grad_shift_out = jnp.sum(column_grads[:, :, 3 * head_cols + ff_here + 1], 0)

    mixer_part = row_product[:head_cols].reshape(nf, shard_rows, width)
    outer_part = row_product[head_cols : head_cols + ff_here].reshape(nf, ff_rows, width)
    sums_part = jnp.broadcast_to(row_product[head_cols + ff_here :][None], (nf, 16, width))
    row_grads = jnp.concatenate([mixer_part, outer_part, sums_part], 1)
    row_grads = row_grads.at[:, ff_rows + shard_rows + 1, :ff_rows].set(
        grad_inner_bias.reshape(nf, ff_rows).astype(bf16)
    )
    row_grads = lax.psum_scatter(row_grads, "fsdp", scatter_dimension=0, tiled=True)
    row_grads = replica_sum(row_grads, "rep")[0]
    grad_mixer_out = row_grads[:shard_rows]
    grad_outer_out = row_grads[shard_rows : shard_rows + ff_rows]
    grad_ibias_out = row_grads[shard_rows + ff_rows + 1, :ff_rows]
    fsdp_me = lax.axis_index("fsdp")
    grad_obias_out = lax.dynamic_slice_in_dim(
        row_grads[shard_rows + ff_rows], (me * nf + fsdp_me) * shard_rows, shard_rows
    )

    return (
        layer_output[None],
        input_grad[None],
        grad_gain_out,
        grad_shift_out,
        grad_triple_out,
        grad_mixer_out,
        grad_inner_out,
        grad_ibias_out,
        grad_outer_out,
        grad_obias_out,
    )


def solution(mesh):
    placed = (
        P(("rep", "fsdp"), "ctx", None),
        P(("ctx", "fsdp")),
        P(("ctx", "fsdp")),
        P(("ctx", "fsdp"), None),
        P(("ctx", "fsdp"), None),
        P(("ctx", "fsdp"), None),
        P(("ctx", "fsdp")),
        P(("ctx", "fsdp"), None),
        P(("ctx", "fsdp")),
        P(("rep", "fsdp")),
        P(("rep", "fsdp")),
        P(("rep", "fsdp"), "ctx", None),
    )
    return jax.shard_map(
        local,
        mesh=mesh,
        in_specs=placed,
        out_specs=(
            P(("rep", "fsdp"), "ctx", None),
            P(("rep", "fsdp"), "ctx", None),
            P(("ctx", "fsdp")),
            P(("ctx", "fsdp")),
            P(("ctx", "fsdp"), None),
            P(("ctx", "fsdp"), None),
            P(("ctx", "fsdp"), None),
            P(("ctx", "fsdp")),
            P(("ctx", "fsdp"), None),
            P(("ctx", "fsdp")),
        ),
        check_vma=False,
    )
```

```python
from functools import partial

import jax
import jax.numpy as jnp
from jax import lax
from jax.experimental import pallas as pl
from jax.experimental.pallas import tpu as pltpu
from jax.sharding import PartitionSpec as P

HEADS = 16
HEAD_DIM = 64
ROT = 32


eps = 1e-05


def angles(positions):
    frequency = 10000.0 ** (-(jnp.arange(ROT // 2, dtype=jnp.float32) * 2.0) / ROT)
    phases = positions.astype(jnp.float32)[:, None] * frequency[None, :]
    return (jnp.cos(phases), jnp.sin(phases))


def rotate(field, cos_table, sin_table):
    leading = field.shape[:-1]
    paired = field[..., :ROT].reshape(leading + (ROT // 2, 2))
    even_part = paired[..., 0]
    odd_part = paired[..., 1]
    cos_wide = cos_table[:, None, :]
    sin_wide = sin_table[:, None, :]
    turned = jnp.stack(
        [even_part * cos_wide - odd_part * sin_wide, odd_part * cos_wide + even_part * sin_wide], -1
    )
    return jnp.concatenate([turned.reshape(leading + (ROT,)), field[..., ROT:]], -1)


def ring_pairs(n, step):
    return [(i, (i + step) % n) for i in range(n)]


def ring_gather(block, axis):
    n = lax.axis_size(axis)
    half = block.shape[0] // 2
    from_left = lax.ppermute(block, axis, ring_pairs(n, 1))
    from_right = lax.ppermute(block, axis, ring_pairs(n, -1))
    far_first = lax.ppermute(from_left[:half], axis, ring_pairs(n, 1))
    far_second = lax.ppermute(from_right[half:], axis, ring_pairs(n, -1))
    far = jnp.concatenate([far_first, far_second], 0)
    return jnp.stack([block, from_right, far, from_left])


def ring_scatter(parts, axis):
    n = lax.axis_size(axis)
    half = parts.shape[1] // 2
    wire = jnp.bfloat16
    got_left = lax.ppermute(parts[2, :half].astype(wire), axis, ring_pairs(n, 1))
    got_right = lax.ppermute(parts[2, half:].astype(wire), axis, ring_pairs(n, -1))
    to_right = jnp.concatenate([parts[1, :half] + got_left.astype(jnp.float32), parts[1, half:]], 0)
    to_left = jnp.concatenate([parts[3, :half], parts[3, half:] + got_right.astype(jnp.float32)], 0)
    from_left = lax.ppermute(to_right.astype(wire), axis, ring_pairs(n, 1))
    from_right = lax.ppermute(to_left.astype(wire), axis, ring_pairs(n, -1))
    return parts[0] + from_left.astype(jnp.float32) + from_right.astype(jnp.float32)


def ring_all_to_all(payload, axis):
    n = lax.axis_size(axis)
    me = lax.axis_index(axis)
    pick = lambda d: lax.dynamic_index_in_dim(payload, d % n, 0, keepdims=False)
    got = [pick(me)] + [
        lax.ppermute(pick(me + s), axis, ring_pairs(n, s)) for s in range(1, n)
    ]
    mirrored = jnp.stack([got[(-k) % n] for k in range(n)])
    doubled = jnp.concatenate([mirrored, mirrored], 0)
    return lax.dynamic_slice_in_dim(doubled, n - me, n, 0)


def replica_sum(values, axis):
    n = lax.axis_size(axis)
    f32, wire = jnp.float32, jnp.bfloat16
    values = values.astype(wire)
    if n != 4:
        return lax.psum(values, axis).astype(f32)
    pair = values.astype(f32) + lax.ppermute(values, axis, [(i, i ^ 1) for i in range(n)]).astype(f32)
    pair = pair.astype(wire)
    return pair.astype(f32) + lax.ppermute(pair, axis, [(i, i ^ 2) for i in range(n)]).astype(f32)


def attention_kernel(span_ref, q_ref, k_ref, v_ref, gm_ref, qpos_ref, kpos_ref,
                     mix_ref, gq_ref, gk_ref, gv_ref):
    f32, bf16 = jnp.float32, jnp.bfloat16
    block = pl.program_id(1)
    q = q_ref[...]
    k = k_ref[...]
    v = v_ref[...]
    gm = gm_ref[...]
    scores = lax.dot_general(q, k, (((1,), (1,)), ((), ())), preferred_element_type=f32)
    qpos = qpos_ref[...]
    kpos = kpos_ref[...]
    allowed = (kpos <= qpos) | (kpos < span_ref[0])
    scores = jnp.where(allowed, scores, -1e30)
    peak = jnp.max(scores, axis=1, keepdims=True)
    exps = jnp.exp(scores - peak)
    total = jnp.sum(exps, axis=1, keepdims=True)
    probs = exps * (1.0 / total)
    low_probs = probs.astype(bf16)
    mix_ref[...] = jnp.dot(low_probs, v, preferred_element_type=f32).astype(mix_ref.dtype)
    grad_probs = lax.dot_general(gm, v, (((1,), (1,)), ((), ())), preferred_element_type=f32)
    inner = jnp.sum(probs * grad_probs, axis=1, keepdims=True)
    grad_scores = (probs * (grad_probs - inner)).astype(bf16)
    gq_ref[...] = jnp.dot(grad_scores, k, preferred_element_type=f32)
    gk_part = lax.dot_general(grad_scores, q, (((0,), (0,)), ((), ())), preferred_element_type=f32)
    gv_part = lax.dot_general(low_probs, gm, (((0,), (0,)), ((), ())), preferred_element_type=f32)

    @pl.when(block == 0)
    def _():
        gk_ref[...] = gk_part
        gv_ref[...] = gv_part

    @pl.when(block != 0)
    def _():
        gk_ref[...] += gk_part
        gv_ref[...] += gv_part


def fused_attention(span, queries, keys, values, grad_mixture, positions, rows=256):
    heads, length, dim = queries.shape
    blocks = length // rows
    qpos = positions.reshape(length, 1).astype(jnp.int32)
    kpos = positions.reshape(1, length).astype(jnp.int32)
    row_block = pl.BlockSpec((None, rows, dim), lambda h, b, s: (h, b, 0))
    whole = pl.BlockSpec((None, length, dim), lambda h, b, s: (h, 0, 0))
    f32 = jnp.float32
    return pl.pallas_call(
        attention_kernel,
        out_shape=(
            jax.ShapeDtypeStruct((heads, length, dim), jnp.bfloat16),
            jax.ShapeDtypeStruct((heads, length, dim), f32),
            jax.ShapeDtypeStruct((heads, length, dim), f32),
            jax.ShapeDtypeStruct((heads, length, dim), f32),
        ),
        grid_spec=pltpu.PrefetchScalarGridSpec(
            num_scalar_prefetch=1,
            grid=(heads, blocks),
            in_specs=[
                row_block, whole, whole, row_block,
                pl.BlockSpec((rows, 1), lambda h, b, s: (b, 0)),
                pl.BlockSpec((1, length), lambda h, b, s: (0, 0)),
            ],
            out_specs=[row_block, row_block, whole, whole],
        ),
        compiler_params=pltpu.CompilerParams(dimension_semantics=("arbitrary", "arbitrary")),
        cost_estimate=pl.CostEstimate(
            flops=12 * heads * length * length * dim,
            transcendentals=heads * length * length,
            bytes_accessed=heads * length * dim * (4 * 2 + 3 * 4 + 2),
        ),
    )(span.reshape(1).astype(jnp.int32), queries, keys, values, grad_mixture, qpos, kpos)


def local(
    tokens,
    norm_gain,
    norm_shift,
    triple_weight,
    mixer_weight,
    inner_weight,
    inner_bias,
    outer_weight,
    outer_bias,
    prefix_length,
    pad_mask,
    cotangent,
):
    nc = lax.axis_size("ctx")
    nf = lax.axis_size("fsdp")
    me = lax.axis_index("ctx")
    _, own_rows, width = tokens.shape
    length = own_rows * nc
    shard_rows = triple_weight.shape[0]
    heads_here = HEADS // nc
    head_cols = heads_here * HEAD_DIM
    ff_here = inner_weight.shape[1] // nc
    ff_rows = outer_weight.shape[0]
    f32, bf16 = jnp.float32, jnp.bfloat16

    triple_cols = (
        triple_weight.reshape(shard_rows, 3, nc, head_cols)
        .transpose(2, 0, 1, 3)
        .reshape(nc, shard_rows, 3 * head_cols)
    )
    inner_cols = inner_weight.reshape(shard_rows, nc, ff_here).transpose(1, 0, 2)
    small = jnp.stack([norm_gain, norm_shift, outer_bias], -1)
    small = jnp.pad(small, ((0, 0), (0, 128 - small.shape[-1])))
    small = jnp.broadcast_to(small[None], (nc,) + small.shape)
    column_payload = jnp.concatenate([triple_cols, inner_cols, small], -1)
    column_payload = ring_all_to_all(column_payload, "ctx")
    column_block = lax.all_gather(column_payload, "fsdp", axis=0, tiled=False)
    column_block = column_block.swapaxes(0, 1).reshape(nc * nf * shard_rows, -1)
    triple_here = column_block[:, : 3 * head_cols]
    inner_here = column_block[:, 3 * head_cols : 3 * head_cols + ff_here]
    gain = column_block[:, 3 * head_cols + ff_here].astype(f32)
    shift = column_block[:, 3 * head_cols + ff_here + 1].astype(f32)
    obias = column_block[:, 3 * head_cols + ff_here + 2].astype(f32)

    bias_rows = jnp.pad(inner_bias[None], ((0, 15), (0, width - inner_bias.shape[0])))
    row_payload = jnp.concatenate([mixer_weight, outer_weight, bias_rows], 0)
    row_block = lax.all_gather(row_payload, "fsdp", axis=0, tiled=False)
    mixer_here = row_block[:, :shard_rows].reshape(nf * shard_rows, width)
    outer_here = row_block[:, shard_rows : shard_rows + ff_rows].reshape(nf * ff_rows, width)
    ibias_here = row_block[:, shard_rows + ff_rows, : inner_bias.shape[0]].reshape(-1).astype(f32)

    all_tokens = ring_gather(tokens[0], "ctx").reshape(length, width)
    visible = (pad_mask[0] != 0).astype(f32)
    own_upstream = cotangent[0].astype(f32) * visible
    all_upstream = ring_gather(own_upstream.astype(bf16), "ctx").reshape(length, width)

    input_rows = all_tokens.astype(f32)
    center = input_rows - jnp.mean(input_rows, -1, keepdims=True)
    scaling = lax.rsqrt(jnp.mean(center * center, -1, keepdims=True) + eps)
    whitened = center * scaling
    normed = (whitened * gain + shift).astype(bf16)

    owners = (me + jnp.arange(nc)) % nc
    positions = (owners[:, None] * own_rows + jnp.arange(own_rows)[None, :]).reshape(length)
    cos_table, sin_table = angles(positions)
    query_key_value = jnp.dot(normed, triple_here, preferred_element_type=f32)
    heads_shape = (length, heads_here, HEAD_DIM)
    queries = (
        rotate(query_key_value[:, :head_cols].reshape(heads_shape), cos_table, sin_table)
        * HEAD_DIM ** (-0.5)
    ).astype(bf16)
    key_rows = rotate(
        query_key_value[:, head_cols : 2 * head_cols].reshape(heads_shape), cos_table, sin_table
    ).astype(bf16)
    value_rows = query_key_value[:, 2 * head_cols :].reshape(heads_shape).astype(bf16)
    span = prefix_length[0]
    grad_mixture = jnp.dot(all_upstream, mixer_here.T, preferred_element_type=f32).astype(bf16)
    by_head = lambda values: values.reshape(heads_shape).swapaxes(0, 1)
    mixture, grad_queries, grad_keys, grad_values = fused_attention(
        span, by_head(queries), by_head(key_rows), by_head(value_rows), by_head(grad_mixture), positions
    )
    grad_queries, grad_keys, grad_values = (
        values.swapaxes(0, 1) for values in (grad_queries, grad_keys, grad_values)
    )
    mixture = mixture.swapaxes(0, 1).reshape(length, head_cols)
    attention = jnp.dot(mixture, mixer_here, preferred_element_type=f32)
    preact = jnp.dot(normed, inner_here, preferred_element_type=f32) + ibias_here
    gelu_result = jax.nn.gelu(preact, approximate=True).astype(bf16)
    feedforward = jnp.dot(gelu_result, outer_here, preferred_element_type=f32)
    block_sum = ring_scatter((attention + feedforward).reshape(nc, own_rows, width), "ctx")
    layer_output = (tokens[0].astype(f32) + block_sum + obias).astype(bf16)

    ones_block = jnp.ones((length, 16), bf16)
    row_lhs = jnp.concatenate([mixture, gelu_result, ones_block], -1)
    row_product = jnp.dot(row_lhs.T, all_upstream, preferred_element_type=f32).astype(bf16)
    grad_activated = jnp.dot(all_upstream, outer_here.T, preferred_element_type=f32)
    unused_value, gelu_pull = jax.vjp(partial(jax.nn.gelu, approximate=True), preact)
    grad_before_gelu = gelu_pull(grad_activated)[0].astype(bf16)
    grad_inner_weight = jnp.dot(normed.T, grad_before_gelu, preferred_element_type=f32)
    grad_inner_bias = jnp.sum(grad_before_gelu.astype(f32), 0)
    flat_shape = (length, head_cols)
    grad_query_key_value = jnp.concatenate(
        [
            rotate(grad_queries * HEAD_DIM ** (-0.5), cos_table, -sin_table).reshape(flat_shape),
            rotate(grad_keys, cos_table, -sin_table).reshape(flat_shape),
            grad_values.reshape(flat_shape),
        ],
        -1,
    ).astype(bf16)
    grad_triple_weight = jnp.dot(normed.T, grad_query_key_value, preferred_element_type=f32)
    grad_normed = jnp.dot(grad_query_key_value, triple_here.T, preferred_element_type=f32)
    grad_normed = grad_normed + jnp.dot(grad_before_gelu, inner_here.T, preferred_element_type=f32)
    grad_normed = ring_scatter(grad_normed.reshape(nc, own_rows, width), "ctx")

    own_whitened = whitened[:own_rows]
    own_scaling = scaling[:own_rows]
    grad_norm_gain = jnp.sum(grad_normed * own_whitened, 0)
    grad_norm_shift = jnp.sum(grad_normed, 0)
    grad_white = grad_normed * gain
    grad_inputs = own_scaling * (
        grad_white
        - jnp.mean(grad_white, -1, keepdims=True)
        - own_whitened * jnp.mean(grad_white * own_whitened, -1, keepdims=True)
    )
    input_grad = (own_upstream + grad_inputs).astype(bf16)

    small_grads = jnp.stack([grad_norm_gain, grad_norm_shift], -1)
    small_grads = jnp.pad(small_grads, ((0, 0), (0, 128 - small_grads.shape[-1])))
    column_grads = jnp.concatenate(
        [grad_triple_weight, grad_inner_weight, small_grads], -1
    ).astype(bf16)
    column_grads = column_grads.reshape(nc, nf, shard_rows, -1).swapaxes(0, 1).reshape(width, -1)
    column_grads = lax.psum_scatter(column_grads, "fsdp", scatter_dimension=0, tiled=True)
    column_grads = replica_sum(column_grads, "rep").astype(bf16)
    column_grads = column_grads.reshape(nc, shard_rows, -1)
    column_grads = ring_all_to_all(column_grads, "ctx").astype(f32)
    grad_triple_out = (
        column_grads[:, :, : 3 * head_cols]
        .reshape(nc, shard_rows, 3, head_cols)
        .transpose(1, 2, 0, 3)
        .reshape(shard_rows, 3 * nc * head_cols)
    )
    grad_inner_out = (
        column_grads[:, :, 3 * head_cols : 3 * head_cols + ff_here]
        .transpose(1, 0, 2)
        .reshape(shard_rows, nc * ff_here)
    )
    grad_gain_out = jnp.sum(column_grads[:, :, 3 * head_cols + ff_here], 0)
    grad_shift_out = jnp.sum(column_grads[:, :, 3 * head_cols + ff_here + 1], 0)

    mixer_part = row_product[:head_cols].reshape(nf, shard_rows, width)
    outer_part = row_product[head_cols : head_cols + ff_here].reshape(nf, ff_rows, width)
    sums_part = jnp.broadcast_to(row_product[head_cols + ff_here :][None], (nf, 16, width))
    row_grads = jnp.concatenate([mixer_part, outer_part, sums_part], 1)
    row_grads = row_grads.at[:, ff_rows + shard_rows + 1, :ff_rows].set(
        grad_inner_bias.reshape(nf, ff_rows).astype(bf16)
    )
    row_grads = lax.psum_scatter(row_grads, "fsdp", scatter_dimension=0, tiled=True)
    row_grads = replica_sum(row_grads, "rep")[0]
    grad_mixer_out = row_grads[:shard_rows]
    grad_outer_out = row_grads[shard_rows : shard_rows + ff_rows]
    grad_ibias_out = row_grads[shard_rows + ff_rows + 1, :ff_rows]
    fsdp_me = lax.axis_index("fsdp")
    grad_obias_out = lax.dynamic_slice_in_dim(
        row_grads[shard_rows + ff_rows], (me * nf + fsdp_me) * shard_rows, shard_rows
    )

    return (
        layer_output[None],
        input_grad[None],
        grad_gain_out,
        grad_shift_out,
        grad_triple_out,
        grad_mixer_out,
        grad_inner_out,
        grad_ibias_out,
        grad_outer_out,
        grad_obias_out,
    )


def solution(mesh):
    placed = (
        P(("rep", "fsdp"), "ctx", None),
        P(("ctx", "fsdp")),
        P(("ctx", "fsdp")),
        P(("ctx", "fsdp"), None),
        P(("ctx", "fsdp"), None),
        P(("ctx", "fsdp"), None),
        P(("ctx", "fsdp")),
        P(("ctx", "fsdp"), None),
        P(("ctx", "fsdp")),
        P(("rep", "fsdp")),
        P(("rep", "fsdp")),
        P(("rep", "fsdp"), "ctx", None),
    )
    return jax.shard_map(
        local,
        mesh=mesh,
        in_specs=placed,
        out_specs=(
            P(("rep", "fsdp"), "ctx", None),
            P(("rep", "fsdp"), "ctx", None),
            P(("ctx", "fsdp")),
            P(("ctx", "fsdp")),
            P(("ctx", "fsdp"), None),
            P(("ctx", "fsdp"), None),
            P(("ctx", "fsdp"), None),
            P(("ctx", "fsdp")),
            P(("ctx", "fsdp"), None),
            P(("ctx", "fsdp")),
        ),
        check_vma=False,
    )
```

```python
from functools import partial

import jax
import jax.numpy as jnp
from jax import lax
from jax.experimental import pallas as pl
from jax.experimental.pallas import tpu as pltpu
from jax.sharding import PartitionSpec as P

HEADS = 16
HEAD_DIM = 64
ROT = 32


eps = 1e-05


def angles(positions):
    frequency = 10000.0 ** (-(jnp.arange(ROT // 2, dtype=jnp.float32) * 2.0) / ROT)
    phases = positions.astype(jnp.float32)[:, None] * frequency[None, :]
    return (jnp.cos(phases), jnp.sin(phases))


def rotate(field, cos_table, sin_table):
    leading = field.shape[:-1]
    paired = field[..., :ROT].reshape(leading + (ROT // 2, 2))
    even_part = paired[..., 0]
    odd_part = paired[..., 1]
    cos_wide = cos_table[:, None, :]
    sin_wide = sin_table[:, None, :]
    turned = jnp.stack(
        [even_part * cos_wide - odd_part * sin_wide, odd_part * cos_wide + even_part * sin_wide], -1
    )
    return jnp.concatenate([turned.reshape(leading + (ROT,)), field[..., ROT:]], -1)


def ring_pairs(n, step):
    return [(i, (i + step) % n) for i in range(n)]


def ring_gather(block, axis):
    n = lax.axis_size(axis)
    half = block.shape[0] // 2
    from_left = lax.ppermute(block, axis, ring_pairs(n, 1))
    from_right = lax.ppermute(block, axis, ring_pairs(n, -1))
    far_first = lax.ppermute(from_left[:half], axis, ring_pairs(n, 1))
    far_second = lax.ppermute(from_right[half:], axis, ring_pairs(n, -1))
    far = jnp.concatenate([far_first, far_second], 0)
    return jnp.stack([block, from_right, far, from_left])


def ring_scatter(parts, axis):
    n = lax.axis_size(axis)
    half = parts.shape[1] // 2
    wire = jnp.bfloat16
    got_left = lax.ppermute(parts[2, :half].astype(wire), axis, ring_pairs(n, 1))
    got_right = lax.ppermute(parts[2, half:].astype(wire), axis, ring_pairs(n, -1))
    to_right = jnp.concatenate([parts[1, :half] + got_left.astype(jnp.float32), parts[1, half:]], 0)
    to_left = jnp.concatenate([parts[3, :half], parts[3, half:] + got_right.astype(jnp.float32)], 0)
    from_left = lax.ppermute(to_right.astype(wire), axis, ring_pairs(n, 1))
    from_right = lax.ppermute(to_left.astype(wire), axis, ring_pairs(n, -1))
    return parts[0] + from_left.astype(jnp.float32) + from_right.astype(jnp.float32)


def ring_all_to_all(payload, axis):
    n = lax.axis_size(axis)
    me = lax.axis_index(axis)
    pick = lambda d: lax.dynamic_index_in_dim(payload, d % n, 0, keepdims=False)
    got = [pick(me)] + [
        lax.ppermute(pick(me + s), axis, ring_pairs(n, s)) for s in range(1, n)
    ]
    mirrored = jnp.stack([got[(-k) % n] for k in range(n)])
    doubled = jnp.concatenate([mirrored, mirrored], 0)
    return lax.dynamic_slice_in_dim(doubled, n - me, n, 0)


def replica_sum(values, axis):
    n = lax.axis_size(axis)
    f32, wire = jnp.float32, jnp.bfloat16
    values = values.astype(wire)
    if n != 4:
        return lax.psum(values, axis).astype(f32)
    pair = values.astype(f32) + lax.ppermute(values, axis, [(i, i ^ 1) for i in range(n)]).astype(f32)
    pair = pair.astype(wire)
    return pair.astype(f32) + lax.ppermute(pair, axis, [(i, i ^ 2) for i in range(n)]).astype(f32)


def attention_kernel(span_ref, q_ref, k_ref, v_ref, gm_ref, qpos_ref, kpos_ref,
                     mix_ref, gq_ref, gk_ref, gv_ref):
    f32, bf16 = jnp.float32, jnp.bfloat16
    block = pl.program_id(1)
    q = q_ref[...]
    k = k_ref[...]
    v = v_ref[...]
    gm = gm_ref[...]
    scores = lax.dot_general(q, k, (((1,), (1,)), ((), ())), preferred_element_type=f32)
    qpos = qpos_ref[...]
    kpos = kpos_ref[...]
    allowed = (kpos <= qpos) | (kpos < span_ref[0])
    scores = jnp.where(allowed, scores, -1e30)
    peak = jnp.max(scores, axis=1, keepdims=True)
    exps = jnp.exp(scores - peak)
    total = jnp.sum(exps, axis=1, keepdims=True)
    probs = exps * (1.0 / total)
    low_probs = probs.astype(bf16)
    mix_ref[...] = jnp.dot(low_probs, v, preferred_element_type=f32).astype(mix_ref.dtype)
    grad_probs = lax.dot_general(gm, v, (((1,), (1,)), ((), ())), preferred_element_type=f32)
    inner = jnp.sum(probs * grad_probs, axis=1, keepdims=True)
    grad_scores = (probs * (grad_probs - inner)).astype(bf16)
    gq_ref[...] = jnp.dot(grad_scores, k, preferred_element_type=f32)
    gk_part = lax.dot_general(grad_scores, q, (((0,), (0,)), ((), ())), preferred_element_type=f32)
    gv_part = lax.dot_general(low_probs, gm, (((0,), (0,)), ((), ())), preferred_element_type=f32)

    @pl.when(block == 0)
    def _():
        gk_ref[...] = gk_part
        gv_ref[...] = gv_part

    @pl.when(block != 0)
    def _():
        gk_ref[...] += gk_part
        gv_ref[...] += gv_part


def fused_attention(span, queries, keys, values, grad_mixture, positions, rows=256):
    heads, length, dim = queries.shape
    blocks = length // rows
    qpos = positions.reshape(length, 1).astype(jnp.int32)
    kpos = positions.reshape(1, length).astype(jnp.int32)
    row_block = pl.BlockSpec((None, rows, dim), lambda h, b, s: (h, b, 0))
    whole = pl.BlockSpec((None, length, dim), lambda h, b, s: (h, 0, 0))
    f32 = jnp.float32
    return pl.pallas_call(
        attention_kernel,
        out_shape=(
            jax.ShapeDtypeStruct((heads, length, dim), jnp.bfloat16),
            jax.ShapeDtypeStruct((heads, length, dim), f32),
            jax.ShapeDtypeStruct((heads, length, dim), f32),
            jax.ShapeDtypeStruct((heads, length, dim), f32),
        ),
        grid_spec=pltpu.PrefetchScalarGridSpec(
            num_scalar_prefetch=1,
            grid=(heads, blocks),
            in_specs=[
                row_block, whole, whole, row_block,
                pl.BlockSpec((rows, 1), lambda h, b, s: (b, 0)),
                pl.BlockSpec((1, length), lambda h, b, s: (0, 0)),
            ],
            out_specs=[row_block, row_block, whole, whole],
        ),
        compiler_params=pltpu.CompilerParams(dimension_semantics=("arbitrary", "arbitrary")),
        cost_estimate=pl.CostEstimate(
            flops=12 * heads * length * length * dim,
            transcendentals=heads * length * length,
            bytes_accessed=heads * length * dim * (4 * 2 + 3 * 4 + 2),
        ),
    )(span.reshape(1).astype(jnp.int32), queries, keys, values, grad_mixture, qpos, kpos)


def local(
    tokens,
    norm_gain,
    norm_shift,
    triple_weight,
    mixer_weight,
    inner_weight,
    inner_bias,
    outer_weight,
    outer_bias,
    prefix_length,
    pad_mask,
    cotangent,
):
    nc = lax.axis_size("ctx")
    nf = lax.axis_size("fsdp")
    me = lax.axis_index("ctx")
    _, own_rows, width = tokens.shape
    length = own_rows * nc
    shard_rows = triple_weight.shape[0]
    heads_here = HEADS // nc
    head_cols = heads_here * HEAD_DIM
    ff_here = inner_weight.shape[1] // nc
    ff_rows = outer_weight.shape[0]
    f32, bf16 = jnp.float32, jnp.bfloat16

    triple_cols = (
        triple_weight.reshape(shard_rows, 3, nc, head_cols)
        .transpose(2, 0, 1, 3)
        .reshape(nc, shard_rows, 3 * head_cols)
    )
    inner_cols = inner_weight.reshape(shard_rows, nc, ff_here).transpose(1, 0, 2)
    small = jnp.stack([norm_gain, norm_shift, outer_bias], -1)
    small = jnp.pad(small, ((0, 0), (0, 128 - small.shape[-1])))
    small = jnp.broadcast_to(small[None], (nc,) + small.shape)
    column_payload = jnp.concatenate([triple_cols, inner_cols, small], -1)
    column_payload = ring_all_to_all(column_payload, "ctx")
    column_block = lax.all_gather(column_payload, "fsdp", axis=0, tiled=False)
    column_block = column_block.swapaxes(0, 1).reshape(nc * nf * shard_rows, -1)
    triple_here = column_block[:, : 3 * head_cols]
    inner_here = column_block[:, 3 * head_cols : 3 * head_cols + ff_here]
    gain = column_block[:, 3 * head_cols + ff_here].astype(f32)
    shift = column_block[:, 3 * head_cols + ff_here + 1].astype(f32)
    obias = column_block[:, 3 * head_cols + ff_here + 2].astype(f32)

    bias_rows = jnp.pad(inner_bias[None], ((0, 15), (0, width - inner_bias.shape[0])))
    row_payload = jnp.concatenate([mixer_weight, outer_weight, bias_rows], 0)
    row_payload, column_block = lax.optimization_barrier((row_payload, column_block))
    row_block = lax.all_gather(row_payload, "fsdp", axis=0, tiled=False)
    mixer_here = row_block[:, :shard_rows].reshape(nf * shard_rows, width)
    outer_here = row_block[:, shard_rows : shard_rows + ff_rows].reshape(nf * ff_rows, width)
    ibias_here = row_block[:, shard_rows + ff_rows, : inner_bias.shape[0]].reshape(-1).astype(f32)

    all_tokens = ring_gather(tokens[0], "ctx").reshape(length, width)
    visible = (pad_mask[0] != 0).astype(f32)
    own_upstream = cotangent[0].astype(f32) * visible
    all_upstream = ring_gather(own_upstream.astype(bf16), "ctx").reshape(length, width)

    input_rows = all_tokens.astype(f32)
    center = input_rows - jnp.mean(input_rows, -1, keepdims=True)
    scaling = lax.rsqrt(jnp.mean(center * center, -1, keepdims=True) + eps)
    whitened = center * scaling
    normed = (whitened * gain + shift).astype(bf16)

    owners = (me + jnp.arange(nc)) % nc
    positions = (owners[:, None] * own_rows + jnp.arange(own_rows)[None, :]).reshape(length)
    cos_table, sin_table = angles(positions)
    query_key_value = jnp.dot(normed, triple_here, preferred_element_type=f32)
    heads_shape = (length, heads_here, HEAD_DIM)
    queries = (
        rotate(query_key_value[:, :head_cols].reshape(heads_shape), cos_table, sin_table)
        * HEAD_DIM ** (-0.5)
    ).astype(bf16)
    key_rows = rotate(
        query_key_value[:, head_cols : 2 * head_cols].reshape(heads_shape), cos_table, sin_table
    ).astype(bf16)
    value_rows = query_key_value[:, 2 * head_cols :].reshape(heads_shape).astype(bf16)
    span = prefix_length[0]
    grad_mixture = jnp.dot(all_upstream, mixer_here.T, preferred_element_type=f32).astype(bf16)
    by_head = lambda values: values.reshape(heads_shape).swapaxes(0, 1)
    mixture, grad_queries, grad_keys, grad_values = fused_attention(
        span, by_head(queries), by_head(key_rows), by_head(value_rows), by_head(grad_mixture), positions
    )
    grad_queries, grad_keys, grad_values = (
        values.swapaxes(0, 1) for values in (grad_queries, grad_keys, grad_values)
    )
    mixture = mixture.swapaxes(0, 1).reshape(length, head_cols)
    attention = jnp.dot(mixture, mixer_here, preferred_element_type=f32)
    preact = jnp.dot(normed, inner_here, preferred_element_type=f32) + ibias_here
    gelu_result = jax.nn.gelu(preact, approximate=True).astype(bf16)
    feedforward = jnp.dot(gelu_result, outer_here, preferred_element_type=f32)
    block_sum = ring_scatter((attention + feedforward).reshape(nc, own_rows, width), "ctx")
    layer_output = (tokens[0].astype(f32) + block_sum + obias).astype(bf16)

    ones_block = jnp.ones((length, 16), bf16)
    row_lhs = jnp.concatenate([mixture, gelu_result, ones_block], -1)
    row_product = jnp.dot(row_lhs.T, all_upstream, preferred_element_type=f32).astype(bf16)
    grad_activated = jnp.dot(all_upstream, outer_here.T, preferred_element_type=f32)
    unused_value, gelu_pull = jax.vjp(partial(jax.nn.gelu, approximate=True), preact)
    grad_before_gelu = gelu_pull(grad_activated)[0].astype(bf16)
    grad_inner_weight = jnp.dot(normed.T, grad_before_gelu, preferred_element_type=f32)
    grad_inner_bias = jnp.sum(grad_before_gelu.astype(f32), 0)
    flat_shape = (length, head_cols)
    grad_query_key_value = jnp.concatenate(
        [
            rotate(grad_queries * HEAD_DIM ** (-0.5), cos_table, -sin_table).reshape(flat_shape),
            rotate(grad_keys, cos_table, -sin_table).reshape(flat_shape),
            grad_values.reshape(flat_shape),
        ],
        -1,
    ).astype(bf16)
    grad_triple_weight = jnp.dot(normed.T, grad_query_key_value, preferred_element_type=f32)
    grad_normed = jnp.dot(grad_query_key_value, triple_here.T, preferred_element_type=f32)
    grad_normed = grad_normed + jnp.dot(grad_before_gelu, inner_here.T, preferred_element_type=f32)
    grad_norm_gain = jnp.sum(grad_normed * whitened, 0)
    grad_norm_shift = jnp.sum(grad_normed, 0)
    grad_normed = ring_scatter(grad_normed.reshape(nc, own_rows, width), "ctx")

    own_whitened = whitened[:own_rows]
    own_scaling = scaling[:own_rows]
    grad_white = grad_normed * gain
    grad_inputs = own_scaling * (
        grad_white
        - jnp.mean(grad_white, -1, keepdims=True)
        - own_whitened * jnp.mean(grad_white * own_whitened, -1, keepdims=True)
    )
    input_grad = (own_upstream + grad_inputs).astype(bf16)

    def to_owners(grads):
        grads = grads.astype(bf16).reshape(nc, nf, shard_rows, -1).swapaxes(0, 1).reshape(width, -1)
        grads = lax.psum_scatter(grads, "fsdp", scatter_dimension=0, tiled=True)
        grads = replica_sum(grads, "rep").astype(bf16)
        return ring_all_to_all(grads.reshape(nc, shard_rows, -1), "ctx").astype(f32)

    inner_grads = to_owners(grad_inner_weight)
    grad_inner_out = inner_grads.transpose(1, 0, 2).reshape(shard_rows, nc * ff_here)
    small_grads = jnp.stack([grad_norm_gain, grad_norm_shift], -1)
    small_grads = jnp.pad(small_grads, ((0, 0), (0, 128 - small_grads.shape[-1])))
    column_grads = to_owners(jnp.concatenate([grad_triple_weight, small_grads], -1))
    grad_triple_out = (
        column_grads[:, :, : 3 * head_cols]
        .reshape(nc, shard_rows, 3, head_cols)
        .transpose(1, 2, 0, 3)
        .reshape(shard_rows, 3 * nc * head_cols)
    )
    grad_gain_out = jnp.sum(column_grads[:, :, 3 * head_cols], 0)
    grad_shift_out = jnp.sum(column_grads[:, :, 3 * head_cols + 1], 0)

    mixer_part = row_product[:head_cols].reshape(nf, shard_rows, width)
    outer_part = row_product[head_cols : head_cols + ff_here].reshape(nf, ff_rows, width)
    sums_part = jnp.broadcast_to(row_product[head_cols + ff_here :][None], (nf, 16, width))
    row_grads = jnp.concatenate([mixer_part, outer_part, sums_part], 1)
    row_grads = row_grads.at[:, ff_rows + shard_rows + 1, :ff_rows].set(
        grad_inner_bias.reshape(nf, ff_rows).astype(bf16)
    )
    row_grads = lax.psum_scatter(row_grads, "fsdp", scatter_dimension=0, tiled=True)
    row_grads = replica_sum(row_grads, "rep")[0]
    grad_mixer_out = row_grads[:shard_rows]
    grad_outer_out = row_grads[shard_rows : shard_rows + ff_rows]
    grad_ibias_out = row_grads[shard_rows + ff_rows + 1, :ff_rows]
    fsdp_me = lax.axis_index("fsdp")
    grad_obias_out = lax.dynamic_slice_in_dim(
        row_grads[shard_rows + ff_rows], (me * nf + fsdp_me) * shard_rows, shard_rows
    )

    return (
        layer_output[None],
        input_grad[None],
        grad_gain_out,
        grad_shift_out,
        grad_triple_out,
        grad_mixer_out,
        grad_inner_out,
        grad_ibias_out,
        grad_outer_out,
        grad_obias_out,
    )


def solution(mesh):
    placed = (
        P(("rep", "fsdp"), "ctx", None),
        P(("ctx", "fsdp")),
        P(("ctx", "fsdp")),
        P(("ctx", "fsdp"), None),
        P(("ctx", "fsdp"), None),
        P(("ctx", "fsdp"), None),
        P(("ctx", "fsdp")),
        P(("ctx", "fsdp"), None),
        P(("ctx", "fsdp")),
        P(("rep", "fsdp")),
        P(("rep", "fsdp")),
        P(("rep", "fsdp"), "ctx", None),
    )
    return jax.shard_map(
        local,
        mesh=mesh,
        in_specs=placed,
        out_specs=(
            P(("rep", "fsdp"), "ctx", None),
            P(("rep", "fsdp"), "ctx", None),
            P(("ctx", "fsdp")),
            P(("ctx", "fsdp")),
            P(("ctx", "fsdp"), None),
            P(("ctx", "fsdp"), None),
            P(("ctx", "fsdp"), None),
            P(("ctx", "fsdp")),
            P(("ctx", "fsdp"), None),
            P(("ctx", "fsdp")),
        ),
        check_vma=False,
    )
```

```python
from functools import partial

import jax
import jax.numpy as jnp
from jax import lax
from jax.experimental import pallas as pl
from jax.experimental.pallas import tpu as pltpu
from jax.sharding import PartitionSpec as P

HEADS = 16
HEAD_DIM = 64
ROT = 32


eps = 1e-05


def angles(positions):
    frequency = 10000.0 ** (-(jnp.arange(ROT // 2, dtype=jnp.float32) * 2.0) / ROT)
    phases = positions.astype(jnp.float32)[:, None] * frequency[None, :]
    return (jnp.cos(phases), jnp.sin(phases))


def rotate(field, cos_table, sin_table):
    leading = field.shape[:-1]
    paired = field[..., :ROT].reshape(leading + (ROT // 2, 2))
    even_part = paired[..., 0]
    odd_part = paired[..., 1]
    cos_wide = cos_table[:, None, :]
    sin_wide = sin_table[:, None, :]
    turned = jnp.stack(
        [even_part * cos_wide - odd_part * sin_wide, odd_part * cos_wide + even_part * sin_wide], -1
    )
    return jnp.concatenate([turned.reshape(leading + (ROT,)), field[..., ROT:]], -1)


def ring_pairs(n, step):
    return [(i, (i + step) % n) for i in range(n)]


def ring_gather(block, axis):
    n = lax.axis_size(axis)
    half = block.shape[0] // 2
    from_left = lax.ppermute(block, axis, ring_pairs(n, 1))
    from_right = lax.ppermute(block, axis, ring_pairs(n, -1))
    far_first = lax.ppermute(from_left[:half], axis, ring_pairs(n, 1))
    far_second = lax.ppermute(from_right[half:], axis, ring_pairs(n, -1))
    far = jnp.concatenate([far_first, far_second], 0)
    return jnp.stack([block, from_right, far, from_left])


def ring_scatter(parts, axis):
    n = lax.axis_size(axis)
    half = parts.shape[1] // 2
    wire = jnp.bfloat16
    got_left = lax.ppermute(parts[2, :half].astype(wire), axis, ring_pairs(n, 1))
    got_right = lax.ppermute(parts[2, half:].astype(wire), axis, ring_pairs(n, -1))
    to_right = jnp.concatenate([parts[1, :half] + got_left.astype(jnp.float32), parts[1, half:]], 0)
    to_left = jnp.concatenate([parts[3, :half], parts[3, half:] + got_right.astype(jnp.float32)], 0)
    from_left = lax.ppermute(to_right.astype(wire), axis, ring_pairs(n, 1))
    from_right = lax.ppermute(to_left.astype(wire), axis, ring_pairs(n, -1))
    return parts[0] + from_left.astype(jnp.float32) + from_right.astype(jnp.float32)


def ring_all_to_all(payload, axis):
    n = lax.axis_size(axis)
    me = lax.axis_index(axis)
    pick = lambda d: lax.dynamic_index_in_dim(payload, d % n, 0, keepdims=False)
    got = [pick(me)] + [
        lax.ppermute(pick(me + s), axis, ring_pairs(n, s)) for s in range(1, n)
    ]
    mirrored = jnp.stack([got[(-k) % n] for k in range(n)])
    doubled = jnp.concatenate([mirrored, mirrored], 0)
    return lax.dynamic_slice_in_dim(doubled, n - me, n, 0)


def replica_sum(values, axis):
    n = lax.axis_size(axis)
    f32, wire = jnp.float32, jnp.bfloat16
    values = values.astype(wire)
    if n != 4:
        return lax.psum(values, axis).astype(f32)
    pair = values.astype(f32) + lax.ppermute(values, axis, [(i, i ^ 1) for i in range(n)]).astype(f32)
    pair = pair.astype(wire)
    return pair.astype(f32) + lax.ppermute(pair, axis, [(i, i ^ 2) for i in range(n)]).astype(f32)


def attention_kernel(span_ref, q_ref, k_ref, v_ref, gm_ref, qpos_ref, kpos_ref,
                     mix_ref, gq_ref, gk_ref, gv_ref):
    f32, bf16 = jnp.float32, jnp.bfloat16
    block = pl.program_id(1)
    q = q_ref[...]
    k = k_ref[...]
    v = v_ref[...]
    gm = gm_ref[...]
    scores = lax.dot_general(q, k, (((1,), (1,)), ((), ())), preferred_element_type=f32)
    qpos = qpos_ref[...]
    kpos = kpos_ref[...]
    allowed = (kpos <= qpos) | (kpos < span_ref[0])
    scores = jnp.where(allowed, scores, -1e30)
    peak = jnp.max(scores, axis=1, keepdims=True)
    exps = jnp.exp(scores - peak)
    total = jnp.sum(exps, axis=1, keepdims=True)
    probs = exps * (1.0 / total)
    low_probs = probs.astype(bf16)
    mix_ref[...] = jnp.dot(low_probs, v, preferred_element_type=f32).astype(mix_ref.dtype)
    grad_probs = lax.dot_general(gm, v, (((1,), (1,)), ((), ())), preferred_element_type=f32)
    inner = jnp.sum(probs * grad_probs, axis=1, keepdims=True)
    grad_scores = (probs * (grad_probs - inner)).astype(bf16)
    gq_ref[...] = jnp.dot(grad_scores, k, preferred_element_type=f32)
    gk_part = lax.dot_general(grad_scores, q, (((0,), (0,)), ((), ())), preferred_element_type=f32)
    gv_part = lax.dot_general(low_probs, gm, (((0,), (0,)), ((), ())), preferred_element_type=f32)

    @pl.when(block == 0)
    def _():
        gk_ref[...] = gk_part
        gv_ref[...] = gv_part

    @pl.when(block != 0)
    def _():
        gk_ref[...] += gk_part
        gv_ref[...] += gv_part


def fused_attention(span, queries, keys, values, grad_mixture, positions, rows=256):
    heads, length, dim = queries.shape
    blocks = length // rows
    qpos = positions.reshape(length, 1).astype(jnp.int32)
    kpos = positions.reshape(1, length).astype(jnp.int32)
    row_block = pl.BlockSpec((None, rows, dim), lambda h, b, s: (h, b, 0))
    whole = pl.BlockSpec((None, length, dim), lambda h, b, s: (h, 0, 0))
    f32 = jnp.float32
    return pl.pallas_call(
        attention_kernel,
        out_shape=(
            jax.ShapeDtypeStruct((heads, length, dim), jnp.bfloat16),
            jax.ShapeDtypeStruct((heads, length, dim), f32),
            jax.ShapeDtypeStruct((heads, length, dim), f32),
            jax.ShapeDtypeStruct((heads, length, dim), f32),
        ),
        grid_spec=pltpu.PrefetchScalarGridSpec(
            num_scalar_prefetch=1,
            grid=(heads, blocks),
            in_specs=[
                row_block, whole, whole, row_block,
                pl.BlockSpec((rows, 1), lambda h, b, s: (b, 0)),
                pl.BlockSpec((1, length), lambda h, b, s: (0, 0)),
            ],
            out_specs=[row_block, row_block, whole, whole],
        ),
        compiler_params=pltpu.CompilerParams(dimension_semantics=("arbitrary", "arbitrary")),
        cost_estimate=pl.CostEstimate(
            flops=12 * heads * length * length * dim,
            transcendentals=heads * length * length,
            bytes_accessed=heads * length * dim * (4 * 2 + 3 * 4 + 2),
        ),
    )(span.reshape(1).astype(jnp.int32), queries, keys, values, grad_mixture, qpos, kpos)


def local(
    tokens,
    norm_gain,
    norm_shift,
    triple_weight,
    mixer_weight,
    inner_weight,
    inner_bias,
    outer_weight,
    outer_bias,
    prefix_length,
    pad_mask,
    cotangent,
):
    nc = lax.axis_size("ctx")
    nf = lax.axis_size("fsdp")
    me = lax.axis_index("ctx")
    _, own_rows, width = tokens.shape
    length = own_rows * nc
    shard_rows = triple_weight.shape[0]
    heads_here = HEADS // nc
    head_cols = heads_here * HEAD_DIM
    ff_here = inner_weight.shape[1] // nc
    ff_rows = outer_weight.shape[0]
    f32, bf16 = jnp.float32, jnp.bfloat16

    triple_cols = (
        triple_weight.reshape(shard_rows, 3, nc, head_cols)
        .transpose(2, 0, 1, 3)
        .reshape(nc, shard_rows, 3 * head_cols)
    )
    inner_cols = inner_weight.reshape(shard_rows, nc, ff_here).transpose(1, 0, 2)
    small = jnp.stack([norm_gain, norm_shift, outer_bias], -1)
    small = jnp.pad(small, ((0, 0), (0, 128 - small.shape[-1])))
    small = jnp.broadcast_to(small[None], (nc,) + small.shape)
    column_payload = jnp.concatenate([triple_cols, inner_cols, small], -1)
    column_payload = ring_all_to_all(column_payload, "ctx")
    column_block = lax.all_gather(column_payload, "fsdp", axis=0, tiled=False)
    column_block = column_block.swapaxes(0, 1).reshape(nc * nf * shard_rows, -1)
    triple_here = column_block[:, : 3 * head_cols]
    inner_here = column_block[:, 3 * head_cols : 3 * head_cols + ff_here]
    gain = column_block[:, 3 * head_cols + ff_here].astype(f32)
    shift = column_block[:, 3 * head_cols + ff_here + 1].astype(f32)
    obias = column_block[:, 3 * head_cols + ff_here + 2].astype(f32)

    bias_rows = jnp.pad(inner_bias[None], ((0, 15), (0, width - inner_bias.shape[0])))
    row_payload = jnp.concatenate([mixer_weight, outer_weight, bias_rows], 0)
    row_block = lax.all_gather(row_payload, "fsdp", axis=0, tiled=False)
    mixer_here = row_block[:, :shard_rows].reshape(nf * shard_rows, width)
    outer_here = row_block[:, shard_rows : shard_rows + ff_rows].reshape(nf * ff_rows, width)
    ibias_here = row_block[:, shard_rows + ff_rows, : inner_bias.shape[0]].reshape(-1).astype(f32)

    visible = (pad_mask[0] != 0).astype(f32)
    own_upstream = cotangent[0].astype(f32) * visible
    both = jnp.concatenate([tokens[0], own_upstream.astype(bf16)], -1)
    both = ring_gather(both, "ctx").reshape(length, 2 * width)
    all_tokens = both[:, :width]
    all_upstream = both[:, width:]

    input_rows = all_tokens.astype(f32)
    center = input_rows - jnp.mean(input_rows, -1, keepdims=True)
    scaling = lax.rsqrt(jnp.mean(center * center, -1, keepdims=True) + eps)
    whitened = center * scaling
    normed = (whitened * gain + shift).astype(bf16)

    owners = (me + jnp.arange(nc)) % nc
    positions = (owners[:, None] * own_rows + jnp.arange(own_rows)[None, :]).reshape(length)
    cos_table, sin_table = angles(positions)
    query_key_value = jnp.dot(normed, triple_here, preferred_element_type=f32)
    heads_shape = (length, heads_here, HEAD_DIM)
    queries = (
        rotate(query_key_value[:, :head_cols].reshape(heads_shape), cos_table, sin_table)
        * HEAD_DIM ** (-0.5)
    ).astype(bf16)
    key_rows = rotate(
        query_key_value[:, head_cols : 2 * head_cols].reshape(heads_shape), cos_table, sin_table
    ).astype(bf16)
    value_rows = query_key_value[:, 2 * head_cols :].reshape(heads_shape).astype(bf16)
    span = prefix_length[0]
    grad_mixture = jnp.dot(all_upstream, mixer_here.T, preferred_element_type=f32).astype(bf16)
    by_head = lambda values: values.reshape(heads_shape).swapaxes(0, 1)
    mixture, grad_queries, grad_keys, grad_values = fused_attention(
        span, by_head(queries), by_head(key_rows), by_head(value_rows), by_head(grad_mixture), positions
    )
    grad_queries, grad_keys, grad_values = (
        values.swapaxes(0, 1) for values in (grad_queries, grad_keys, grad_values)
    )
    mixture = mixture.swapaxes(0, 1).reshape(length, head_cols)
    attention = jnp.dot(mixture, mixer_here, preferred_element_type=f32)
    preact = jnp.dot(normed, inner_here, preferred_element_type=f32) + ibias_here
    gelu_result = jax.nn.gelu(preact, approximate=True).astype(bf16)
    feedforward = jnp.dot(gelu_result, outer_here, preferred_element_type=f32)
    block_sum = (attention + feedforward).astype(bf16).reshape(nc, own_rows, width)
    block_sum = lax.dynamic_slice_in_dim(jnp.concatenate([block_sum, block_sum], 0), nc - me, nc, 0)
    block_sum = lax.psum_scatter(block_sum, "ctx", scatter_dimension=0, tiled=True)[0].astype(f32)
    layer_output = (tokens[0].astype(f32) + block_sum + obias).astype(bf16)

    ones_block = jnp.ones((length, 16), bf16)
    row_lhs = jnp.concatenate([mixture, gelu_result, ones_block], -1)
    row_product = jnp.dot(row_lhs.T, all_upstream, preferred_element_type=f32).astype(bf16)
    grad_activated = jnp.dot(all_upstream, outer_here.T, preferred_element_type=f32)
    unused_value, gelu_pull = jax.vjp(partial(jax.nn.gelu, approximate=True), preact)
    grad_before_gelu = gelu_pull(grad_activated)[0].astype(bf16)
    grad_inner_weight = jnp.dot(normed.T, grad_before_gelu, preferred_element_type=f32)
    grad_inner_bias = jnp.sum(grad_before_gelu.astype(f32), 0)
    flat_shape = (length, head_cols)
    grad_query_key_value = jnp.concatenate(
        [
            rotate(grad_queries * HEAD_DIM ** (-0.5), cos_table, -sin_table).reshape(flat_shape),
            rotate(grad_keys, cos_table, -sin_table).reshape(flat_shape),
            grad_values.reshape(flat_shape),
        ],
        -1,
    ).astype(bf16)
    grad_triple_weight = jnp.dot(normed.T, grad_query_key_value, preferred_element_type=f32)
    grad_normed = jnp.dot(grad_query_key_value, triple_here.T, preferred_element_type=f32)
    grad_normed = grad_normed + jnp.dot(grad_before_gelu, inner_here.T, preferred_element_type=f32)
    grad_normed = ring_scatter(grad_normed.reshape(nc, own_rows, width), "ctx")

    own_whitened = whitened[:own_rows]
    own_scaling = scaling[:own_rows]
    grad_norm_gain = jnp.sum(grad_normed * own_whitened, 0)
    grad_norm_shift = jnp.sum(grad_normed, 0)
    grad_white = grad_normed * gain
    grad_inputs = own_scaling * (
        grad_white
        - jnp.mean(grad_white, -1, keepdims=True)
        - own_whitened * jnp.mean(grad_white * own_whitened, -1, keepdims=True)
    )
    input_grad = (own_upstream + grad_inputs).astype(bf16)

    small_grads = jnp.stack([grad_norm_gain, grad_norm_shift], -1)
    small_grads = jnp.pad(small_grads, ((0, 0), (0, 128 - small_grads.shape[-1])))
    column_grads = jnp.concatenate(
        [grad_triple_weight, grad_inner_weight, small_grads], -1
    ).astype(bf16)
    column_grads = column_grads.reshape(nc, nf, shard_rows, -1).swapaxes(0, 1).reshape(width, -1)
    column_grads = lax.psum_scatter(column_grads, "fsdp", scatter_dimension=0, tiled=True)
    column_grads = replica_sum(column_grads, "rep").astype(bf16)
    column_grads = column_grads.reshape(nc, shard_rows, -1)
    column_grads = ring_all_to_all(column_grads, "ctx").astype(f32)
    grad_triple_out = (
        column_grads[:, :, : 3 * head_cols]
        .reshape(nc, shard_rows, 3, head_cols)
        .transpose(1, 2, 0, 3)
        .reshape(shard_rows, 3 * nc * head_cols)
    )
    grad_inner_out = (
        column_grads[:, :, 3 * head_cols : 3 * head_cols + ff_here]
        .transpose(1, 0, 2)
        .reshape(shard_rows, nc * ff_here)
    )
    grad_gain_out = jnp.sum(column_grads[:, :, 3 * head_cols + ff_here], 0)
    grad_shift_out = jnp.sum(column_grads[:, :, 3 * head_cols + ff_here + 1], 0)

    mixer_part = row_product[:head_cols].reshape(nf, shard_rows, width)
    outer_part = row_product[head_cols : head_cols + ff_here].reshape(nf, ff_rows, width)
    sums_part = jnp.broadcast_to(row_product[head_cols + ff_here :][None], (nf, 16, width))
    row_grads = jnp.concatenate([mixer_part, outer_part, sums_part], 1)
    row_grads = row_grads.at[:, ff_rows + shard_rows + 1, :ff_rows].set(
        grad_inner_bias.reshape(nf, ff_rows).astype(bf16)
    )
    row_grads = lax.psum_scatter(row_grads, "fsdp", scatter_dimension=0, tiled=True)
    row_grads = replica_sum(row_grads, "rep")[0]
    grad_mixer_out = row_grads[:shard_rows]
    grad_outer_out = row_grads[shard_rows : shard_rows + ff_rows]
    grad_ibias_out = row_grads[shard_rows + ff_rows + 1, :ff_rows]
    fsdp_me = lax.axis_index("fsdp")
    grad_obias_out = lax.dynamic_slice_in_dim(
        row_grads[shard_rows + ff_rows], (me * nf + fsdp_me) * shard_rows, shard_rows
    )

    return (
        layer_output[None],
        input_grad[None],
        grad_gain_out,
        grad_shift_out,
        grad_triple_out,
        grad_mixer_out,
        grad_inner_out,
        grad_ibias_out,
        grad_outer_out,
        grad_obias_out,
    )


def solution(mesh):
    placed = (
        P(("rep", "fsdp"), "ctx", None),
        P(("ctx", "fsdp")),
        P(("ctx", "fsdp")),
        P(("ctx", "fsdp"), None),
        P(("ctx", "fsdp"), None),
        P(("ctx", "fsdp"), None),
        P(("ctx", "fsdp")),
        P(("ctx", "fsdp"), None),
        P(("ctx", "fsdp")),
        P(("rep", "fsdp")),
        P(("rep", "fsdp")),
        P(("rep", "fsdp"), "ctx", None),
    )
    return jax.shard_map(
        local,
        mesh=mesh,
        in_specs=placed,
        out_specs=(
            P(("rep", "fsdp"), "ctx", None),
            P(("rep", "fsdp"), "ctx", None),
            P(("ctx", "fsdp")),
            P(("ctx", "fsdp")),
            P(("ctx", "fsdp"), None),
            P(("ctx", "fsdp"), None),
            P(("ctx", "fsdp"), None),
            P(("ctx", "fsdp")),
            P(("ctx", "fsdp"), None),
            P(("ctx", "fsdp")),
        ),
        check_vma=False,
    )
```

```python
from functools import partial

import jax
import jax.numpy as jnp
from jax import lax
from jax.experimental import pallas as pl
from jax.experimental.pallas import tpu as pltpu
from jax.sharding import PartitionSpec as P

HEADS = 16
HEAD_DIM = 64
ROT = 32


eps = 1e-05


def angles(positions):
    frequency = 10000.0 ** (-(jnp.arange(ROT // 2, dtype=jnp.float32) * 2.0) / ROT)
    phases = positions.astype(jnp.float32)[:, None] * frequency[None, :]
    return (jnp.cos(phases), jnp.sin(phases))


def rotate(field, cos_table, sin_table):
    leading = field.shape[:-1]
    paired = field[..., :ROT].reshape(leading + (ROT // 2, 2))
    even_part = paired[..., 0]
    odd_part = paired[..., 1]
    cos_wide = cos_table[:, None, :]
    sin_wide = sin_table[:, None, :]
    turned = jnp.stack(
        [even_part * cos_wide - odd_part * sin_wide, odd_part * cos_wide + even_part * sin_wide], -1
    )
    return jnp.concatenate([turned.reshape(leading + (ROT,)), field[..., ROT:]], -1)


def ring_pairs(n, step):
    return [(i, (i + step) % n) for i in range(n)]


def ring_gather(block, axis):
    n = lax.axis_size(axis)
    half = block.shape[0] // 2
    from_left = lax.ppermute(block, axis, ring_pairs(n, 1))
    from_right = lax.ppermute(block, axis, ring_pairs(n, -1))
    far_first = lax.ppermute(from_left[:half], axis, ring_pairs(n, 1))
    far_second = lax.ppermute(from_right[half:], axis, ring_pairs(n, -1))
    far = jnp.concatenate([far_first, far_second], 0)
    return jnp.stack([block, from_right, far, from_left])


def ring_scatter(parts, axis):
    n = lax.axis_size(axis)
    half = parts.shape[1] // 2
    wire = jnp.bfloat16
    got_left = lax.ppermute(parts[2, :half].astype(wire), axis, ring_pairs(n, 1))
    got_right = lax.ppermute(parts[2, half:].astype(wire), axis, ring_pairs(n, -1))
    to_right = jnp.concatenate([parts[1, :half] + got_left.astype(jnp.float32), parts[1, half:]], 0)
    to_left = jnp.concatenate([parts[3, :half], parts[3, half:] + got_right.astype(jnp.float32)], 0)
    from_left = lax.ppermute(to_right.astype(wire), axis, ring_pairs(n, 1))
    from_right = lax.ppermute(to_left.astype(wire), axis, ring_pairs(n, -1))
    return parts[0] + from_left.astype(jnp.float32) + from_right.astype(jnp.float32)


def ring_all_to_all(payload, axis):
    n = lax.axis_size(axis)
    me = lax.axis_index(axis)
    pick = lambda d: lax.dynamic_index_in_dim(payload, d % n, 0, keepdims=False)
    got = [pick(me)] + [
        lax.ppermute(pick(me + s), axis, ring_pairs(n, s)) for s in range(1, n)
    ]
    mirrored = jnp.stack([got[(-k) % n] for k in range(n)])
    doubled = jnp.concatenate([mirrored, mirrored], 0)
    return lax.dynamic_slice_in_dim(doubled, n - me, n, 0)


def replica_sum(values, axis):
    n = lax.axis_size(axis)
    f32, wire = jnp.float32, jnp.bfloat16
    values = values.astype(wire)
    if n != 4:
        return lax.psum(values, axis).astype(f32)
    pair = values.astype(f32) + lax.ppermute(values, axis, [(i, i ^ 1) for i in range(n)]).astype(f32)
    pair = pair.astype(wire)
    return pair.astype(f32) + lax.ppermute(pair, axis, [(i, i ^ 2) for i in range(n)]).astype(f32)


def attention_kernel(span_ref, q_ref, k_ref, v_ref, gm_ref, qpos_ref, kpos_ref,
                     mix_ref, gq_ref, gk_ref, gv_ref):
    f32, bf16 = jnp.float32, jnp.bfloat16
    block = pl.program_id(1)
    q = q_ref[...]
    k = k_ref[...]
    v = v_ref[...]
    gm = gm_ref[...]
    scores = lax.dot_general(q, k, (((1,), (1,)), ((), ())), preferred_element_type=f32)
    qpos = qpos_ref[...]
    kpos = kpos_ref[...]
    allowed = (kpos <= qpos) | (kpos < span_ref[0])
    scores = jnp.where(allowed, scores, -1e30)
    peak = jnp.max(scores, axis=1, keepdims=True)
    exps = jnp.exp(scores - peak)
    total = jnp.sum(exps, axis=1, keepdims=True)
    probs = exps * (1.0 / total)
    low_probs = probs.astype(bf16)
    mix_ref[...] = jnp.dot(low_probs, v, preferred_element_type=f32).astype(mix_ref.dtype)
    grad_probs = lax.dot_general(gm, v, (((1,), (1,)), ((), ())), preferred_element_type=f32)
    inner = jnp.sum(probs * grad_probs, axis=1, keepdims=True)
    grad_scores = (probs * (grad_probs - inner)).astype(bf16)
    gq_ref[...] = jnp.dot(grad_scores, k, preferred_element_type=f32)
    gk_part = lax.dot_general(grad_scores, q, (((0,), (0,)), ((), ())), preferred_element_type=f32)
    gv_part = lax.dot_general(low_probs, gm, (((0,), (0,)), ((), ())), preferred_element_type=f32)

    @pl.when(block == 0)
    def _():
        gk_ref[...] = gk_part
        gv_ref[...] = gv_part

    @pl.when(block != 0)
    def _():
        gk_ref[...] += gk_part
        gv_ref[...] += gv_part


def fused_attention(span, queries, keys, values, grad_mixture, positions, rows=256):
    heads, length, dim = queries.shape
    blocks = length // rows
    qpos = positions.reshape(length, 1).astype(jnp.int32)
    kpos = positions.reshape(1, length).astype(jnp.int32)
    row_block = pl.BlockSpec((None, rows, dim), lambda h, b, s: (h, b, 0))
    whole = pl.BlockSpec((None, length, dim), lambda h, b, s: (h, 0, 0))
    f32 = jnp.float32
    return pl.pallas_call(
        attention_kernel,
        out_shape=(
            jax.ShapeDtypeStruct((heads, length, dim), jnp.bfloat16),
            jax.ShapeDtypeStruct((heads, length, dim), f32),
            jax.ShapeDtypeStruct((heads, length, dim), f32),
            jax.ShapeDtypeStruct((heads, length, dim), f32),
        ),
        grid_spec=pltpu.PrefetchScalarGridSpec(
            num_scalar_prefetch=1,
            grid=(heads, blocks),
            in_specs=[
                row_block, whole, whole, row_block,
                pl.BlockSpec((rows, 1), lambda h, b, s: (b, 0)),
                pl.BlockSpec((1, length), lambda h, b, s: (0, 0)),
            ],
            out_specs=[row_block, row_block, whole, whole],
        ),
        compiler_params=pltpu.CompilerParams(dimension_semantics=("arbitrary", "arbitrary")),
        cost_estimate=pl.CostEstimate(
            flops=12 * heads * length * length * dim,
            transcendentals=heads * length * length,
            bytes_accessed=heads * length * dim * (4 * 2 + 3 * 4 + 2),
        ),
    )(span.reshape(1).astype(jnp.int32), queries, keys, values, grad_mixture, qpos, kpos)


def local(
    tokens,
    norm_gain,
    norm_shift,
    triple_weight,
    mixer_weight,
    inner_weight,
    inner_bias,
    outer_weight,
    outer_bias,
    prefix_length,
    pad_mask,
    cotangent,
):
    nc = lax.axis_size("ctx")
    nf = lax.axis_size("fsdp")
    me = lax.axis_index("ctx")
    _, own_rows, width = tokens.shape
    length = own_rows * nc
    shard_rows = triple_weight.shape[0]
    heads_here = HEADS // nc
    head_cols = heads_here * HEAD_DIM
    ff_here = inner_weight.shape[1] // nc
    ff_rows = outer_weight.shape[0]
    f32, bf16 = jnp.float32, jnp.bfloat16

    triple_cols = (
        triple_weight.reshape(shard_rows, 3, nc, head_cols)
        .transpose(2, 0, 1, 3)
        .reshape(nc, shard_rows, 3 * head_cols)
    )
    inner_cols = inner_weight.reshape(shard_rows, nc, ff_here).transpose(1, 0, 2)
    small = jnp.stack([norm_gain, norm_shift, outer_bias], -1)
    small = jnp.pad(small, ((0, 0), (0, 128 - small.shape[-1])))
    small = jnp.broadcast_to(small[None], (nc,) + small.shape)
    column_payload = jnp.concatenate([triple_cols, inner_cols, small], -1)
    column_payload = ring_all_to_all(column_payload, "ctx")
    column_block = lax.all_gather(column_payload, "fsdp", axis=0, tiled=False)
    column_block = column_block.swapaxes(0, 1).reshape(nc * nf * shard_rows, -1)
    triple_here = column_block[:, : 3 * head_cols]
    inner_here = column_block[:, 3 * head_cols : 3 * head_cols + ff_here]
    gain = column_block[:, 3 * head_cols + ff_here].astype(f32)
    shift = column_block[:, 3 * head_cols + ff_here + 1].astype(f32)
    obias = column_block[:, 3 * head_cols + ff_here + 2].astype(f32)

    bias_rows = jnp.pad(inner_bias[None], ((0, 15), (0, width - inner_bias.shape[0])))
    row_payload = jnp.concatenate([mixer_weight, outer_weight, bias_rows], 0)
    row_block = lax.all_gather(row_payload, "fsdp", axis=0, tiled=False)
    mixer_here = row_block[:, :shard_rows].reshape(nf * shard_rows, width)
    outer_here = row_block[:, shard_rows : shard_rows + ff_rows].reshape(nf * ff_rows, width)
    ibias_here = row_block[:, shard_rows + ff_rows, : inner_bias.shape[0]].reshape(-1).astype(f32)

    visible = (pad_mask[0] != 0).astype(f32)
    own_upstream = cotangent[0].astype(f32) * visible
    both = jnp.concatenate([tokens[0], own_upstream.astype(bf16)], -1)
    both = ring_gather(both, "ctx").reshape(length, 2 * width)
    all_tokens = both[:, :width]
    all_upstream = both[:, width:]

    input_rows = all_tokens.astype(f32)
    center = input_rows - jnp.mean(input_rows, -1, keepdims=True)
    scaling = lax.rsqrt(jnp.mean(center * center, -1, keepdims=True) + eps)
    whitened = center * scaling
    normed = (whitened * gain + shift).astype(bf16)

    owners = (me + jnp.arange(nc)) % nc
    positions = (owners[:, None] * own_rows + jnp.arange(own_rows)[None, :]).reshape(length)
    cos_table, sin_table = angles(positions)
    query_key_value = jnp.dot(normed, triple_here, preferred_element_type=f32)
    heads_shape = (length, heads_here, HEAD_DIM)
    queries = (
        rotate(query_key_value[:, :head_cols].reshape(heads_shape), cos_table, sin_table)
        * HEAD_DIM ** (-0.5)
    ).astype(bf16)
    key_rows = rotate(
        query_key_value[:, head_cols : 2 * head_cols].reshape(heads_shape), cos_table, sin_table
    ).astype(bf16)
    value_rows = query_key_value[:, 2 * head_cols :].reshape(heads_shape).astype(bf16)
    span = prefix_length[0]
    grad_mixture = jnp.dot(all_upstream, mixer_here.T, preferred_element_type=f32).astype(bf16)
    by_head = lambda values: values.reshape(heads_shape).swapaxes(0, 1)
    mixture, grad_queries, grad_keys, grad_values = fused_attention(
        span, by_head(queries), by_head(key_rows), by_head(value_rows), by_head(grad_mixture), positions
    )
    grad_queries, grad_keys, grad_values = (
        values.swapaxes(0, 1) for values in (grad_queries, grad_keys, grad_values)
    )
    mixture = mixture.swapaxes(0, 1).reshape(length, head_cols)
    attention = jnp.dot(mixture, mixer_here, preferred_element_type=f32)
    preact = jnp.dot(normed, inner_here, preferred_element_type=f32) + ibias_here
    gelu_result = jax.nn.gelu(preact, approximate=True).astype(bf16)
    feedforward = jnp.dot(gelu_result, outer_here, preferred_element_type=f32)
    block_sum = ring_scatter((attention + feedforward).reshape(nc, own_rows, width), "ctx")
    layer_output = (tokens[0].astype(f32) + block_sum + obias).astype(bf16)

    ones_block = jnp.ones((length, 16), bf16)
    row_lhs = jnp.concatenate([mixture, gelu_result, ones_block], -1)
    row_product = jnp.dot(row_lhs.T, all_upstream, preferred_element_type=f32).astype(bf16)
    grad_activated = jnp.dot(all_upstream, outer_here.T, preferred_element_type=f32)
    unused_value, gelu_pull = jax.vjp(partial(jax.nn.gelu, approximate=True), preact)
    grad_before_gelu = gelu_pull(grad_activated)[0].astype(bf16)
    grad_inner_weight = jnp.dot(normed.T, grad_before_gelu, preferred_element_type=f32)
    grad_inner_bias = jnp.sum(grad_before_gelu.astype(f32), 0)
    flat_shape = (length, head_cols)
    grad_query_key_value = jnp.concatenate(
        [
            rotate(grad_queries * HEAD_DIM ** (-0.5), cos_table, -sin_table).reshape(flat_shape),
            rotate(grad_keys, cos_table, -sin_table).reshape(flat_shape),
            grad_values.reshape(flat_shape),
        ],
        -1,
    ).astype(bf16)
    grad_triple_weight = jnp.dot(normed.T, grad_query_key_value, preferred_element_type=f32)
    grad_normed = jnp.dot(grad_query_key_value, triple_here.T, preferred_element_type=f32)
    grad_normed = grad_normed + jnp.dot(grad_before_gelu, inner_here.T, preferred_element_type=f32)
    grad_norm_gain = jnp.sum(grad_normed * whitened, 0)
    grad_norm_shift = jnp.sum(grad_normed, 0)
    grad_normed = ring_scatter(grad_normed.reshape(nc, own_rows, width), "ctx")

    own_whitened = whitened[:own_rows]
    own_scaling = scaling[:own_rows]
    grad_white = grad_normed * gain
    grad_inputs = own_scaling * (
        grad_white
        - jnp.mean(grad_white, -1, keepdims=True)
        - own_whitened * jnp.mean(grad_white * own_whitened, -1, keepdims=True)
    )
    input_grad = (own_upstream + grad_inputs).astype(bf16)

    small_grads = jnp.stack([grad_norm_gain, grad_norm_shift], -1)
    small_grads = jnp.pad(small_grads, ((0, 0), (0, 128 - small_grads.shape[-1])))
    column_grads = jnp.concatenate(
        [grad_triple_weight, grad_inner_weight, small_grads], -1
    ).astype(bf16)
    column_grads = column_grads.reshape(nc, nf, shard_rows, -1).swapaxes(0, 1).reshape(width, -1)
    column_grads = lax.psum_scatter(column_grads, "fsdp", scatter_dimension=0, tiled=True)
    column_grads = replica_sum(column_grads, "rep").astype(bf16)
    column_grads = column_grads.reshape(nc, shard_rows, -1)
    column_grads = ring_all_to_all(column_grads, "ctx").astype(f32)
    grad_triple_out = (
        column_grads[:, :, : 3 * head_cols]
        .reshape(nc, shard_rows, 3, head_cols)
        .transpose(1, 2, 0, 3)
        .reshape(shard_rows, 3 * nc * head_cols)
    )
    grad_inner_out = (
        column_grads[:, :, 3 * head_cols : 3 * head_cols + ff_here]
        .transpose(1, 0, 2)
        .reshape(shard_rows, nc * ff_here)
    )
    grad_gain_out = jnp.sum(column_grads[:, :, 3 * head_cols + ff_here], 0)
    grad_shift_out = jnp.sum(column_grads[:, :, 3 * head_cols + ff_here + 1], 0)

    mixer_part = row_product[:head_cols].reshape(nf, shard_rows, width)
    outer_part = row_product[head_cols : head_cols + ff_here].reshape(nf, ff_rows, width)
    sums_part = jnp.broadcast_to(row_product[head_cols + ff_here :][None], (nf, 16, width))
    row_grads = jnp.concatenate([mixer_part, outer_part, sums_part], 1)
    row_grads = row_grads.at[:, ff_rows + shard_rows + 1, :ff_rows].set(
        grad_inner_bias.reshape(nf, ff_rows).astype(bf16)
    )
    row_grads = lax.psum_scatter(row_grads, "fsdp", scatter_dimension=0, tiled=True)
    row_grads = replica_sum(row_grads, "rep")[0]
    grad_mixer_out = row_grads[:shard_rows]
    grad_outer_out = row_grads[shard_rows : shard_rows + ff_rows]
    grad_ibias_out = row_grads[shard_rows + ff_rows + 1, :ff_rows]
    fsdp_me = lax.axis_index("fsdp")
    grad_obias_out = lax.dynamic_slice_in_dim(
        row_grads[shard_rows + ff_rows], (me * nf + fsdp_me) * shard_rows, shard_rows
    )

    return (
        layer_output[None],
        input_grad[None],
        grad_gain_out,
        grad_shift_out,
        grad_triple_out,
        grad_mixer_out,
        grad_inner_out,
        grad_ibias_out,
        grad_outer_out,
        grad_obias_out,
    )


def solution(mesh):
    placed = (
        P(("rep", "fsdp"), "ctx", None),
        P(("ctx", "fsdp")),
        P(("ctx", "fsdp")),
        P(("ctx", "fsdp"), None),
        P(("ctx", "fsdp"), None),
        P(("ctx", "fsdp"), None),
        P(("ctx", "fsdp")),
        P(("ctx", "fsdp"), None),
        P(("ctx", "fsdp")),
        P(("rep", "fsdp")),
        P(("rep", "fsdp")),
        P(("rep", "fsdp"), "ctx", None),
    )
    return jax.shard_map(
        local,
        mesh=mesh,
        in_specs=placed,
        out_specs=(
            P(("rep", "fsdp"), "ctx", None),
            P(("rep", "fsdp"), "ctx", None),
            P(("ctx", "fsdp")),
            P(("ctx", "fsdp")),
            P(("ctx", "fsdp"), None),
            P(("ctx", "fsdp"), None),
            P(("ctx", "fsdp"), None),
            P(("ctx", "fsdp")),
            P(("ctx", "fsdp"), None),
            P(("ctx", "fsdp")),
        ),
        check_vma=False,
    )
```

```python
from functools import partial

import jax
import jax.numpy as jnp
from jax import lax
from jax.experimental import pallas as pl
from jax.experimental.pallas import tpu as pltpu
from jax.sharding import PartitionSpec as P

HEADS = 16
HEAD_DIM = 64
ROT = 32


eps = 1e-05


def angles(positions):
    frequency = 10000.0 ** (-(jnp.arange(ROT // 2, dtype=jnp.float32) * 2.0) / ROT)
    phases = positions.astype(jnp.float32)[:, None] * frequency[None, :]
    return (jnp.cos(phases), jnp.sin(phases))


def rotate(field, cos_table, sin_table):
    leading = field.shape[:-1]
    paired = field[..., :ROT].reshape(leading + (ROT // 2, 2))
    even_part = paired[..., 0]
    odd_part = paired[..., 1]
    cos_wide = cos_table[:, None, :]
    sin_wide = sin_table[:, None, :]
    turned = jnp.stack(
        [even_part * cos_wide - odd_part * sin_wide, odd_part * cos_wide + even_part * sin_wide], -1
    )
    return jnp.concatenate([turned.reshape(leading + (ROT,)), field[..., ROT:]], -1)


def ring_pairs(n, step):
    return [(i, (i + step) % n) for i in range(n)]


def ring_gather(block, axis):
    n = lax.axis_size(axis)
    half = block.shape[0] // 2
    from_left = lax.ppermute(block, axis, ring_pairs(n, 1))
    from_right = lax.ppermute(block, axis, ring_pairs(n, -1))
    far_first = lax.ppermute(from_left[:half], axis, ring_pairs(n, 1))
    far_second = lax.ppermute(from_right[half:], axis, ring_pairs(n, -1))
    far = jnp.concatenate([far_first, far_second], 0)
    return jnp.stack([block, from_right, far, from_left])


def ring_scatter(parts, axis):
    n = lax.axis_size(axis)
    half = parts.shape[1] // 2
    wire = jnp.bfloat16
    got_left = lax.ppermute(parts[2, :half].astype(wire), axis, ring_pairs(n, 1))
    got_right = lax.ppermute(parts[2, half:].astype(wire), axis, ring_pairs(n, -1))
    to_right = jnp.concatenate([parts[1, :half] + got_left.astype(jnp.float32), parts[1, half:]], 0)
    to_left = jnp.concatenate([parts[3, :half], parts[3, half:] + got_right.astype(jnp.float32)], 0)
    from_left = lax.ppermute(to_right.astype(wire), axis, ring_pairs(n, 1))
    from_right = lax.ppermute(to_left.astype(wire), axis, ring_pairs(n, -1))
    return parts[0] + from_left.astype(jnp.float32) + from_right.astype(jnp.float32)


def ring_all_to_all(payload, axis):
    n = lax.axis_size(axis)
    me = lax.axis_index(axis)
    pick = lambda d: lax.dynamic_index_in_dim(payload, d % n, 0, keepdims=False)
    got = [pick(me)] + [
        lax.ppermute(pick(me + s), axis, ring_pairs(n, s)) for s in range(1, n)
    ]
    mirrored = jnp.stack([got[(-k) % n] for k in range(n)])
    doubled = jnp.concatenate([mirrored, mirrored], 0)
    return lax.dynamic_slice_in_dim(doubled, n - me, n, 0)


def shift_gather(block, axis):
    n = lax.axis_size(axis)
    me = lax.axis_index(axis)
    got = [block] + [lax.ppermute(block, axis, ring_pairs(n, s)) for s in range(1, n)]
    mirrored = jnp.stack([got[(-k) % n] for k in range(n)])
    doubled = jnp.concatenate([mirrored, mirrored], 0)
    return lax.dynamic_slice_in_dim(doubled, n - me, n, 0)


def replica_sum(values, axis):
    n = lax.axis_size(axis)
    f32, wire = jnp.float32, jnp.bfloat16
    values = values.astype(wire)
    if n != 4:
        return lax.psum(values, axis).astype(f32)
    pair = values.astype(f32) + lax.ppermute(values, axis, [(i, i ^ 1) for i in range(n)]).astype(f32)
    pair = pair.astype(wire)
    return pair.astype(f32) + lax.ppermute(pair, axis, [(i, i ^ 2) for i in range(n)]).astype(f32)


def attention_kernel(span_ref, q_ref, k_ref, v_ref, gm_ref, qpos_ref, kpos_ref,
                     mix_ref, gq_ref, gk_ref, gv_ref):
    f32, bf16 = jnp.float32, jnp.bfloat16
    block = pl.program_id(1)
    q = q_ref[...]
    k = k_ref[...]
    v = v_ref[...]
    gm = gm_ref[...]
    scores = lax.dot_general(q, k, (((1,), (1,)), ((), ())), preferred_element_type=f32)
    qpos = qpos_ref[...]
    kpos = kpos_ref[...]
    allowed = (kpos <= qpos) | (kpos < span_ref[0])
    scores = jnp.where(allowed, scores, -1e30)
    peak = jnp.max(scores, axis=1, keepdims=True)
    exps = jnp.exp(scores - peak)
    total = jnp.sum(exps, axis=1, keepdims=True)
    probs = exps * (1.0 / total)
    low_probs = probs.astype(bf16)
    mix_ref[...] = jnp.dot(low_probs, v, preferred_element_type=f32).astype(mix_ref.dtype)
    grad_probs = lax.dot_general(gm, v, (((1,), (1,)), ((), ())), preferred_element_type=f32)
    inner = jnp.sum(probs * grad_probs, axis=1, keepdims=True)
    grad_scores = (probs * (grad_probs - inner)).astype(bf16)
    gq_ref[...] = jnp.dot(grad_scores, k, preferred_element_type=f32)
    gk_part = lax.dot_general(grad_scores, q, (((0,), (0,)), ((), ())), preferred_element_type=f32)
    gv_part = lax.dot_general(low_probs, gm, (((0,), (0,)), ((), ())), preferred_element_type=f32)

    @pl.when(block == 0)
    def _():
        gk_ref[...] = gk_part
        gv_ref[...] = gv_part

    @pl.when(block != 0)
    def _():
        gk_ref[...] += gk_part
        gv_ref[...] += gv_part


def fused_attention(span, queries, keys, values, grad_mixture, positions, rows=256):
    heads, length, dim = queries.shape
    blocks = length // rows
    qpos = positions.reshape(length, 1).astype(jnp.int32)
    kpos = positions.reshape(1, length).astype(jnp.int32)
    row_block = pl.BlockSpec((None, rows, dim), lambda h, b, s: (h, b, 0))
    whole = pl.BlockSpec((None, length, dim), lambda h, b, s: (h, 0, 0))
    f32 = jnp.float32
    return pl.pallas_call(
        attention_kernel,
        out_shape=(
            jax.ShapeDtypeStruct((heads, length, dim), jnp.bfloat16),
            jax.ShapeDtypeStruct((heads, length, dim), f32),
            jax.ShapeDtypeStruct((heads, length, dim), f32),
            jax.ShapeDtypeStruct((heads, length, dim), f32),
        ),
        grid_spec=pltpu.PrefetchScalarGridSpec(
            num_scalar_prefetch=1,
            grid=(heads, blocks),
            in_specs=[
                row_block, whole, whole, row_block,
                pl.BlockSpec((rows, 1), lambda h, b, s: (b, 0)),
                pl.BlockSpec((1, length), lambda h, b, s: (0, 0)),
            ],
            out_specs=[row_block, row_block, whole, whole],
        ),
        compiler_params=pltpu.CompilerParams(dimension_semantics=("arbitrary", "arbitrary")),
        cost_estimate=pl.CostEstimate(
            flops=12 * heads * length * length * dim,
            transcendentals=heads * length * length,
            bytes_accessed=heads * length * dim * (4 * 2 + 3 * 4 + 2),
        ),
    )(span.reshape(1).astype(jnp.int32), queries, keys, values, grad_mixture, qpos, kpos)


def local(
    tokens,
    norm_gain,
    norm_shift,
    triple_weight,
    mixer_weight,
    inner_weight,
    inner_bias,
    outer_weight,
    outer_bias,
    prefix_length,
    pad_mask,
    cotangent,
):
    nc = lax.axis_size("ctx")
    nf = lax.axis_size("fsdp")
    me = lax.axis_index("ctx")
    _, own_rows, width = tokens.shape
    length = own_rows * nc
    shard_rows = triple_weight.shape[0]
    heads_here = HEADS // nc
    head_cols = heads_here * HEAD_DIM
    ff_here = inner_weight.shape[1] // nc
    ff_rows = outer_weight.shape[0]
    f32, bf16 = jnp.float32, jnp.bfloat16

    triple_cols = (
        triple_weight.reshape(shard_rows, 3, nc, head_cols)
        .transpose(2, 0, 1, 3)
        .reshape(nc, shard_rows, 3 * head_cols)
    )
    inner_cols = inner_weight.reshape(shard_rows, nc, ff_here).transpose(1, 0, 2)
    small = jnp.stack([norm_gain, norm_shift, outer_bias], -1)
    small = jnp.pad(small, ((0, 0), (0, 128 - small.shape[-1])))
    small = jnp.broadcast_to(small[None], (nc,) + small.shape)
    column_payload = jnp.concatenate([triple_cols, inner_cols, small], -1)
    column_payload = ring_all_to_all(column_payload, "ctx")
    column_block = lax.all_gather(column_payload, "fsdp", axis=0, tiled=False)
    column_block = column_block.swapaxes(0, 1).reshape(nc * nf * shard_rows, -1)
    triple_here = column_block[:, : 3 * head_cols]
    inner_here = column_block[:, 3 * head_cols : 3 * head_cols + ff_here]
    gain = column_block[:, 3 * head_cols + ff_here].astype(f32)
    shift = column_block[:, 3 * head_cols + ff_here + 1].astype(f32)
    obias = column_block[:, 3 * head_cols + ff_here + 2].astype(f32)

    bias_rows = jnp.pad(inner_bias[None], ((0, 15), (0, width - inner_bias.shape[0])))
    row_payload = jnp.concatenate([mixer_weight, outer_weight, bias_rows], 0)
    row_block = shift_gather(row_payload, "fsdp")
    mixer_here = row_block[:, :shard_rows].reshape(nf * shard_rows, width)
    outer_here = row_block[:, shard_rows : shard_rows + ff_rows].reshape(nf * ff_rows, width)
    ibias_here = row_block[:, shard_rows + ff_rows, : inner_bias.shape[0]].reshape(-1).astype(f32)

    visible = (pad_mask[0] != 0).astype(f32)
    own_upstream = cotangent[0].astype(f32) * visible
    both = jnp.concatenate([tokens[0], own_upstream.astype(bf16)], -1)
    both = ring_gather(both, "ctx").reshape(length, 2 * width)
    all_tokens = both[:, :width]
    all_upstream = both[:, width:]

    input_rows = all_tokens.astype(f32)
    center = input_rows - jnp.mean(input_rows, -1, keepdims=True)
    scaling = lax.rsqrt(jnp.mean(center * center, -1, keepdims=True) + eps)
    whitened = center * scaling
    normed = (whitened * gain + shift).astype(bf16)

    owners = (me + jnp.arange(nc)) % nc
    positions = (owners[:, None] * own_rows + jnp.arange(own_rows)[None, :]).reshape(length)
    cos_table, sin_table = angles(positions)
    query_key_value = jnp.dot(normed, triple_here, preferred_element_type=f32)
    heads_shape = (length, heads_here, HEAD_DIM)
    queries = (
        rotate(query_key_value[:, :head_cols].reshape(heads_shape), cos_table, sin_table)
        * HEAD_DIM ** (-0.5)
    ).astype(bf16)
    key_rows = rotate(
        query_key_value[:, head_cols : 2 * head_cols].reshape(heads_shape), cos_table, sin_table
    ).astype(bf16)
    value_rows = query_key_value[:, 2 * head_cols :].reshape(heads_shape).astype(bf16)
    span = prefix_length[0]
    grad_mixture = jnp.dot(all_upstream, mixer_here.T, preferred_element_type=f32).astype(bf16)
    by_head = lambda values: values.reshape(heads_shape).swapaxes(0, 1)
    mixture, grad_queries, grad_keys, grad_values = fused_attention(
        span, by_head(queries), by_head(key_rows), by_head(value_rows), by_head(grad_mixture), positions
    )
    grad_queries, grad_keys, grad_values = (
        values.swapaxes(0, 1) for values in (grad_queries, grad_keys, grad_values)
    )
    mixture = mixture.swapaxes(0, 1).reshape(length, head_cols)
    attention = jnp.dot(mixture, mixer_here, preferred_element_type=f32)
    preact = jnp.dot(normed, inner_here, preferred_element_type=f32) + ibias_here
    gelu_result = jax.nn.gelu(preact, approximate=True).astype(bf16)
    feedforward = jnp.dot(gelu_result, outer_here, preferred_element_type=f32)
    block_sum = ring_scatter((attention + feedforward).reshape(nc, own_rows, width), "ctx")
    layer_output = (tokens[0].astype(f32) + block_sum + obias).astype(bf16)

    ones_block = jnp.ones((length, 16), bf16)
    row_lhs = jnp.concatenate([mixture, gelu_result, ones_block], -1)
    row_product = jnp.dot(row_lhs.T, all_upstream, preferred_element_type=f32).astype(bf16)
    grad_activated = jnp.dot(all_upstream, outer_here.T, preferred_element_type=f32)
    unused_value, gelu_pull = jax.vjp(partial(jax.nn.gelu, approximate=True), preact)
    grad_before_gelu = gelu_pull(grad_activated)[0].astype(bf16)
    grad_inner_weight = jnp.dot(normed.T, grad_before_gelu, preferred_element_type=f32)
    grad_inner_bias = jnp.sum(grad_before_gelu.astype(f32), 0)
    flat_shape = (length, head_cols)
    grad_query_key_value = jnp.concatenate(
        [
            rotate(grad_queries * HEAD_DIM ** (-0.5), cos_table, -sin_table).reshape(flat_shape),
            rotate(grad_keys, cos_table, -sin_table).reshape(flat_shape),
            grad_values.reshape(flat_shape),
        ],
        -1,
    ).astype(bf16)
    grad_triple_weight = jnp.dot(normed.T, grad_query_key_value, preferred_element_type=f32)
    grad_normed = jnp.dot(grad_query_key_value, triple_here.T, preferred_element_type=f32)
    grad_normed = grad_normed + jnp.dot(grad_before_gelu, inner_here.T, preferred_element_type=f32)
    grad_norm_gain = jnp.sum(grad_normed * whitened, 0)
    grad_norm_shift = jnp.sum(grad_normed, 0)
    grad_normed = ring_scatter(grad_normed.reshape(nc, own_rows, width), "ctx")

    own_whitened = whitened[:own_rows]
    own_scaling = scaling[:own_rows]
    grad_white = grad_normed * gain
    grad_inputs = own_scaling * (
        grad_white
        - jnp.mean(grad_white, -1, keepdims=True)
        - own_whitened * jnp.mean(grad_white * own_whitened, -1, keepdims=True)
    )
    input_grad = (own_upstream + grad_inputs).astype(bf16)

    small_grads = jnp.stack([grad_norm_gain, grad_norm_shift], -1)
    small_grads = jnp.pad(small_grads, ((0, 0), (0, 128 - small_grads.shape[-1])))
    column_grads = jnp.concatenate(
        [grad_triple_weight, grad_inner_weight, small_grads], -1
    ).astype(bf16)
    column_grads = column_grads.reshape(nc, nf, shard_rows, -1).swapaxes(0, 1).reshape(width, -1)
    column_grads = lax.psum_scatter(column_grads, "fsdp", scatter_dimension=0, tiled=True)
    column_grads = replica_sum(column_grads, "rep").astype(bf16)
    column_grads = column_grads.reshape(nc, shard_rows, -1)
    column_grads = ring_all_to_all(column_grads, "ctx").astype(f32)
    grad_triple_out = (
        column_grads[:, :, : 3 * head_cols]
        .reshape(nc, shard_rows, 3, head_cols)
        .transpose(1, 2, 0, 3)
        .reshape(shard_rows, 3 * nc * head_cols)
    )
    grad_inner_out = (
        column_grads[:, :, 3 * head_cols : 3 * head_cols + ff_here]
        .transpose(1, 0, 2)
        .reshape(shard_rows, nc * ff_here)
    )
    grad_gain_out = jnp.sum(column_grads[:, :, 3 * head_cols + ff_here], 0)
    grad_shift_out = jnp.sum(column_grads[:, :, 3 * head_cols + ff_here + 1], 0)

    mixer_part = row_product[:head_cols].reshape(nf, shard_rows, width)
    outer_part = row_product[head_cols : head_cols + ff_here].reshape(nf, ff_rows, width)
    sums_part = jnp.broadcast_to(row_product[head_cols + ff_here :][None], (nf, 16, width))
    row_grads = jnp.concatenate([mixer_part, outer_part, sums_part], 1)
    row_grads = row_grads.at[:, ff_rows + shard_rows + 1, :ff_rows].set(
        grad_inner_bias.reshape(nf, ff_rows).astype(bf16)
    )
    row_grads = lax.psum_scatter(row_grads, "fsdp", scatter_dimension=0, tiled=True)
    row_grads = replica_sum(row_grads, "rep")[0]
    grad_mixer_out = row_grads[:shard_rows]
    grad_outer_out = row_grads[shard_rows : shard_rows + ff_rows]
    grad_ibias_out = row_grads[shard_rows + ff_rows + 1, :ff_rows]
    fsdp_me = lax.axis_index("fsdp")
    grad_obias_out = lax.dynamic_slice_in_dim(
        row_grads[shard_rows + ff_rows], (me * nf + fsdp_me) * shard_rows, shard_rows
    )

    return (
        layer_output[None],
        input_grad[None],
        grad_gain_out,
        grad_shift_out,
        grad_triple_out,
        grad_mixer_out,
        grad_inner_out,
        grad_ibias_out,
        grad_outer_out,
        grad_obias_out,
    )


def solution(mesh):
    placed = (
        P(("rep", "fsdp"), "ctx", None),
        P(("ctx", "fsdp")),
        P(("ctx", "fsdp")),
        P(("ctx", "fsdp"), None),
        P(("ctx", "fsdp"), None),
        P(("ctx", "fsdp"), None),
        P(("ctx", "fsdp")),
        P(("ctx", "fsdp"), None),
        P(("ctx", "fsdp")),
        P(("rep", "fsdp")),
        P(("rep", "fsdp")),
        P(("rep", "fsdp"), "ctx", None),
    )
    return jax.shard_map(
        local,
        mesh=mesh,
        in_specs=placed,
        out_specs=(
            P(("rep", "fsdp"), "ctx", None),
            P(("rep", "fsdp"), "ctx", None),
            P(("ctx", "fsdp")),
            P(("ctx", "fsdp")),
            P(("ctx", "fsdp"), None),
            P(("ctx", "fsdp"), None),
            P(("ctx", "fsdp"), None),
            P(("ctx", "fsdp")),
            P(("ctx", "fsdp"), None),
            P(("ctx", "fsdp")),
        ),
        check_vma=False,
    )
```

```python
from functools import partial

import jax
import jax.numpy as jnp
from jax import lax
from jax.experimental import pallas as pl
from jax.experimental.pallas import tpu as pltpu
from jax.sharding import PartitionSpec as P

HEADS = 16
HEAD_DIM = 64
ROT = 32


eps = 1e-05


def angles(positions):
    frequency = 10000.0 ** (-(jnp.arange(ROT // 2, dtype=jnp.float32) * 2.0) / ROT)
    phases = positions.astype(jnp.float32)[:, None] * frequency[None, :]
    return (jnp.cos(phases), jnp.sin(phases))


def rotate(field, cos_table, sin_table):
    leading = field.shape[:-1]
    paired = field[..., :ROT].reshape(leading + (ROT // 2, 2))
    even_part = paired[..., 0]
    odd_part = paired[..., 1]
    cos_wide = cos_table[:, None, :]
    sin_wide = sin_table[:, None, :]
    turned = jnp.stack(
        [even_part * cos_wide - odd_part * sin_wide, odd_part * cos_wide + even_part * sin_wide], -1
    )
    return jnp.concatenate([turned.reshape(leading + (ROT,)), field[..., ROT:]], -1)


def pair_tables(positions, width):
    f32 = jnp.float32
    highest = lax.Precision.HIGHEST
    cos_table, sin_table = angles(positions)
    feature = jnp.arange(width) % HEAD_DIM
    pick = (feature[None, :] // 2 == jnp.arange(ROT // 2)[:, None]) & (feature[None, :] < ROT)
    pick = pick.astype(f32)
    sign = jnp.where(feature % 2 == 0, -1.0, 1.0).astype(f32)
    cos_full = jnp.dot(cos_table, pick, precision=highest) + (feature >= ROT).astype(f32)
    sin_full = jnp.dot(sin_table, pick, precision=highest) * sign
    return cos_full, sin_full


def swap_pairs(values):
    width = values.shape[-1]
    index = jnp.arange(width)
    swap = (index[:, None] == (index[None, :] ^ 1)).astype(jnp.float32)
    return jnp.dot(values, swap, precision=lax.Precision.HIGHEST)


def ring_pairs(n, step):
    return [(i, (i + step) % n) for i in range(n)]


def ring_gather(block, axis):
    n = lax.axis_size(axis)
    half = block.shape[0] // 2
    from_left = lax.ppermute(block, axis, ring_pairs(n, 1))
    from_right = lax.ppermute(block, axis, ring_pairs(n, -1))
    far_first = lax.ppermute(from_left[:half], axis, ring_pairs(n, 1))
    far_second = lax.ppermute(from_right[half:], axis, ring_pairs(n, -1))
    far = jnp.concatenate([far_first, far_second], 0)
    return jnp.stack([block, from_right, far, from_left])


def ring_scatter(parts, axis):
    n = lax.axis_size(axis)
    half = parts.shape[1] // 2
    wire = jnp.bfloat16
    got_left = lax.ppermute(parts[2, :half].astype(wire), axis, ring_pairs(n, 1))
    got_right = lax.ppermute(parts[2, half:].astype(wire), axis, ring_pairs(n, -1))
    to_right = jnp.concatenate([parts[1, :half] + got_left.astype(jnp.float32), parts[1, half:]], 0)
    to_left = jnp.concatenate([parts[3, :half], parts[3, half:] + got_right.astype(jnp.float32)], 0)
    from_left = lax.ppermute(to_right.astype(wire), axis, ring_pairs(n, 1))
    from_right = lax.ppermute(to_left.astype(wire), axis, ring_pairs(n, -1))
    return parts[0] + from_left.astype(jnp.float32) + from_right.astype(jnp.float32)


def ring_all_to_all(payload, axis):
    n = lax.axis_size(axis)
    me = lax.axis_index(axis)
    pick = lambda d: lax.dynamic_index_in_dim(payload, d % n, 0, keepdims=False)
    got = [pick(me)] + [
        lax.ppermute(pick(me + s), axis, ring_pairs(n, s)) for s in range(1, n)
    ]
    mirrored = jnp.stack([got[(-k) % n] for k in range(n)])
    doubled = jnp.concatenate([mirrored, mirrored], 0)
    return lax.dynamic_slice_in_dim(doubled, n - me, n, 0)


def replica_sum(values, axis):
    n = lax.axis_size(axis)
    f32, wire = jnp.float32, jnp.bfloat16
    values = values.astype(wire)
    if n != 4:
        return lax.psum(values, axis).astype(f32)
    pair = values.astype(f32) + lax.ppermute(values, axis, [(i, i ^ 1) for i in range(n)]).astype(f32)
    pair = pair.astype(wire)
    return pair.astype(f32) + lax.ppermute(pair, axis, [(i, i ^ 2) for i in range(n)]).astype(f32)


def attention_kernel(span_ref, q_ref, k_ref, v_ref, gm_ref, qpos_ref, kpos_ref,
                     mix_ref, gq_ref, gk_ref, gv_ref):
    f32, bf16 = jnp.float32, jnp.bfloat16
    block = pl.program_id(1)
    q = q_ref[...]
    k = k_ref[...]
    v = v_ref[...]
    gm = gm_ref[...]
    scores = lax.dot_general(q, k, (((1,), (1,)), ((), ())), preferred_element_type=f32)
    qpos = qpos_ref[...]
    kpos = kpos_ref[...]
    allowed = (kpos <= qpos) | (kpos < span_ref[0])
    scores = jnp.where(allowed, scores, -1e30)
    peak = jnp.max(scores, axis=1, keepdims=True)
    exps = jnp.exp(scores - peak)
    total = jnp.sum(exps, axis=1, keepdims=True)
    probs = exps * (1.0 / total)
    low_probs = probs.astype(bf16)
    mix_ref[...] = jnp.dot(low_probs, v, preferred_element_type=f32).astype(mix_ref.dtype)
    grad_probs = lax.dot_general(gm, v, (((1,), (1,)), ((), ())), preferred_element_type=f32)
    inner = jnp.sum(probs * grad_probs, axis=1, keepdims=True)
    grad_scores = (probs * (grad_probs - inner)).astype(bf16)
    gq_ref[...] = jnp.dot(grad_scores, k, preferred_element_type=f32)
    gk_part = lax.dot_general(grad_scores, q, (((0,), (0,)), ((), ())), preferred_element_type=f32)
    gv_part = lax.dot_general(low_probs, gm, (((0,), (0,)), ((), ())), preferred_element_type=f32)

    @pl.when(block == 0)
    def _():
        gk_ref[...] = gk_part
        gv_ref[...] = gv_part

    @pl.when(block != 0)
    def _():
        gk_ref[...] += gk_part
        gv_ref[...] += gv_part


def fused_attention(span, queries, keys, values, grad_mixture, positions, rows=256):
    heads, length, dim = queries.shape
    blocks = length // rows
    qpos = positions.reshape(length, 1).astype(jnp.int32)
    kpos = positions.reshape(1, length).astype(jnp.int32)
    row_block = pl.BlockSpec((None, rows, dim), lambda h, b, s: (h, b, 0))
    whole = pl.BlockSpec((None, length, dim), lambda h, b, s: (h, 0, 0))
    f32 = jnp.float32
    return pl.pallas_call(
        attention_kernel,
        out_shape=(
            jax.ShapeDtypeStruct((heads, length, dim), jnp.bfloat16),
            jax.ShapeDtypeStruct((heads, length, dim), f32),
            jax.ShapeDtypeStruct((heads, length, dim), f32),
            jax.ShapeDtypeStruct((heads, length, dim), f32),
        ),
        grid_spec=pltpu.PrefetchScalarGridSpec(
            num_scalar_prefetch=1,
            grid=(heads, blocks),
            in_specs=[
                row_block, whole, whole, row_block,
                pl.BlockSpec((rows, 1), lambda h, b, s: (b, 0)),
                pl.BlockSpec((1, length), lambda h, b, s: (0, 0)),
            ],
            out_specs=[row_block, row_block, whole, whole],
        ),
        compiler_params=pltpu.CompilerParams(dimension_semantics=("arbitrary", "arbitrary")),
        cost_estimate=pl.CostEstimate(
            flops=12 * heads * length * length * dim,
            transcendentals=heads * length * length,
            bytes_accessed=heads * length * dim * (4 * 2 + 3 * 4 + 2),
        ),
    )(span.reshape(1).astype(jnp.int32), queries, keys, values, grad_mixture, qpos, kpos)


def local(
    tokens,
    norm_gain,
    norm_shift,
    triple_weight,
    mixer_weight,
    inner_weight,
    inner_bias,
    outer_weight,
    outer_bias,
    prefix_length,
    pad_mask,
    cotangent,
):
    nc = lax.axis_size("ctx")
    nf = lax.axis_size("fsdp")
    me = lax.axis_index("ctx")
    _, own_rows, width = tokens.shape
    length = own_rows * nc
    shard_rows = triple_weight.shape[0]
    heads_here = HEADS // nc
    head_cols = heads_here * HEAD_DIM
    ff_here = inner_weight.shape[1] // nc
    ff_rows = outer_weight.shape[0]
    f32, bf16 = jnp.float32, jnp.bfloat16

    triple_cols = (
        triple_weight.reshape(shard_rows, 3, nc, head_cols)
        .transpose(2, 0, 1, 3)
        .reshape(nc, shard_rows, 3 * head_cols)
    )
    inner_cols = inner_weight.reshape(shard_rows, nc, ff_here).transpose(1, 0, 2)
    small = jnp.stack([norm_gain, norm_shift, outer_bias], -1)
    small = jnp.pad(small, ((0, 0), (0, 128 - small.shape[-1])))
    small = jnp.broadcast_to(small[None], (nc,) + small.shape)
    column_payload = jnp.concatenate([triple_cols, inner_cols, small], -1)
    column_payload = ring_all_to_all(column_payload, "ctx")
    column_block = lax.all_gather(column_payload, "fsdp", axis=0, tiled=False)
    column_block = column_block.swapaxes(0, 1).reshape(nc * nf * shard_rows, -1)
    triple_here = column_block[:, : 3 * head_cols]
    inner_here = column_block[:, 3 * head_cols : 3 * head_cols + ff_here]
    gain = column_block[:, 3 * head_cols + ff_here].astype(f32)
    shift = column_block[:, 3 * head_cols + ff_here + 1].astype(f32)
    obias = column_block[:, 3 * head_cols + ff_here + 2].astype(f32)

    bias_rows = jnp.pad(inner_bias[None], ((0, 15), (0, width - inner_bias.shape[0])))
    row_payload = jnp.concatenate([mixer_weight, outer_weight, bias_rows], 0)
    row_block = lax.all_gather(row_payload, "fsdp", axis=0, tiled=False)
    mixer_here = row_block[:, :shard_rows].reshape(nf * shard_rows, width)
    outer_here = row_block[:, shard_rows : shard_rows + ff_rows].reshape(nf * ff_rows, width)
    ibias_here = row_block[:, shard_rows + ff_rows, : inner_bias.shape[0]].reshape(-1).astype(f32)

    visible = (pad_mask[0] != 0).astype(f32)
    own_upstream = cotangent[0].astype(f32) * visible
    both = jnp.concatenate([tokens[0], own_upstream.astype(bf16)], -1)
    both = ring_gather(both, "ctx").reshape(length, 2 * width)
    all_tokens = both[:, :width]
    all_upstream = both[:, width:]

    input_rows = all_tokens.astype(f32)
    center = input_rows - jnp.mean(input_rows, -1, keepdims=True)
    scaling = lax.rsqrt(jnp.mean(center * center, -1, keepdims=True) + eps)
    whitened = center * scaling
    normed = (whitened * gain + shift).astype(bf16)

    owners = (me + jnp.arange(nc)) % nc
    positions = (owners[:, None] * own_rows + jnp.arange(own_rows)[None, :]).reshape(length)
    cos_full, sin_full = pair_tables(positions, 2 * head_cols)
    query_key_value = jnp.dot(normed, triple_here, preferred_element_type=f32)
    heads_shape = (length, heads_here, HEAD_DIM)
    turned = query_key_value[:, : 2 * head_cols]
    turned = turned * cos_full + swap_pairs(turned) * sin_full
    queries = (turned[:, :head_cols] * HEAD_DIM ** (-0.5)).astype(bf16).reshape(heads_shape)
    key_rows = turned[:, head_cols:].astype(bf16).reshape(heads_shape)
    value_rows = query_key_value[:, 2 * head_cols :].reshape(heads_shape).astype(bf16)
    span = prefix_length[0]
    grad_mixture = jnp.dot(all_upstream, mixer_here.T, preferred_element_type=f32).astype(bf16)
    by_head = lambda values: values.reshape(heads_shape).swapaxes(0, 1)
    mixture, grad_queries, grad_keys, grad_values = fused_attention(
        span, by_head(queries), by_head(key_rows), by_head(value_rows), by_head(grad_mixture), positions
    )
    grad_queries, grad_keys, grad_values = (
        values.swapaxes(0, 1) for values in (grad_queries, grad_keys, grad_values)
    )
    mixture = mixture.swapaxes(0, 1).reshape(length, head_cols)
    attention = jnp.dot(mixture, mixer_here, preferred_element_type=f32)
    preact = jnp.dot(normed, inner_here, preferred_element_type=f32) + ibias_here
    gelu_result = jax.nn.gelu(preact, approximate=True).astype(bf16)
    feedforward = jnp.dot(gelu_result, outer_here, preferred_element_type=f32)
    block_sum = ring_scatter((attention + feedforward).reshape(nc, own_rows, width), "ctx")
    layer_output = (tokens[0].astype(f32) + block_sum + obias).astype(bf16)

    ones_block = jnp.ones((length, 16), bf16)
    row_lhs = jnp.concatenate([mixture, gelu_result, ones_block], -1)
    row_product = jnp.dot(row_lhs.T, all_upstream, preferred_element_type=f32).astype(bf16)
    grad_activated = jnp.dot(all_upstream, outer_here.T, preferred_element_type=f32)
    unused_value, gelu_pull = jax.vjp(partial(jax.nn.gelu, approximate=True), preact)
    grad_before_gelu = gelu_pull(grad_activated)[0].astype(bf16)
    grad_inner_weight = jnp.dot(normed.T, grad_before_gelu, preferred_element_type=f32)
    grad_inner_bias = jnp.sum(grad_before_gelu.astype(f32), 0)
    flat_shape = (length, head_cols)
    grad_turned = jnp.concatenate(
        [(grad_queries * HEAD_DIM ** (-0.5)).reshape(flat_shape), grad_keys.reshape(flat_shape)], -1
    )
    grad_turned = grad_turned * cos_full - swap_pairs(grad_turned) * sin_full
    grad_query_key_value = jnp.concatenate(
        [grad_turned, grad_values.reshape(flat_shape)], -1
    ).astype(bf16)
    grad_triple_weight = jnp.dot(normed.T, grad_query_key_value, preferred_element_type=f32)
    grad_normed = jnp.dot(grad_query_key_value, triple_here.T, preferred_element_type=f32)
    grad_normed = grad_normed + jnp.dot(grad_before_gelu, inner_here.T, preferred_element_type=f32)
    grad_norm_gain = jnp.sum(grad_normed * whitened, 0)
    grad_norm_shift = jnp.sum(grad_normed, 0)
    grad_normed = ring_scatter(grad_normed.reshape(nc, own_rows, width), "ctx")

    own_whitened = whitened[:own_rows]
    own_scaling = scaling[:own_rows]
    grad_white = grad_normed * gain
    grad_inputs = own_scaling * (
        grad_white
        - jnp.mean(grad_white, -1, keepdims=True)
        - own_whitened * jnp.mean(grad_white * own_whitened, -1, keepdims=True)
    )
    input_grad = (own_upstream + grad_inputs).astype(bf16)

    small_grads = jnp.stack([grad_norm_gain, grad_norm_shift], -1)
    small_grads = jnp.pad(small_grads, ((0, 0), (0, 128 - small_grads.shape[-1])))
    column_grads = jnp.concatenate(
        [grad_triple_weight, grad_inner_weight, small_grads], -1
    ).astype(bf16)
    column_grads = column_grads.reshape(nc, nf, shard_rows, -1).swapaxes(0, 1).reshape(width, -1)
    column_grads = lax.psum_scatter(column_grads, "fsdp", scatter_dimension=0, tiled=True)
    column_grads = replica_sum(column_grads, "rep").astype(bf16)
    column_grads = column_grads.reshape(nc, shard_rows, -1)
    column_grads = ring_all_to_all(column_grads, "ctx").astype(f32)
    grad_triple_out = (
        column_grads[:, :, : 3 * head_cols]
        .reshape(nc, shard_rows, 3, head_cols)
        .transpose(1, 2, 0, 3)
        .reshape(shard_rows, 3 * nc * head_cols)
    )
    grad_inner_out = (
        column_grads[:, :, 3 * head_cols : 3 * head_cols + ff_here]
        .transpose(1, 0, 2)
        .reshape(shard_rows, nc * ff_here)
    )
    grad_gain_out = jnp.sum(column_grads[:, :, 3 * head_cols + ff_here], 0)
    grad_shift_out = jnp.sum(column_grads[:, :, 3 * head_cols + ff_here + 1], 0)

    mixer_part = row_product[:head_cols].reshape(nf, shard_rows, width)
    outer_part = row_product[head_cols : head_cols + ff_here].reshape(nf, ff_rows, width)
    sums_part = jnp.broadcast_to(row_product[head_cols + ff_here :][None], (nf, 16, width))
    row_grads = jnp.concatenate([mixer_part, outer_part, sums_part], 1)
    row_grads = row_grads.at[:, ff_rows + shard_rows + 1, :ff_rows].set(
        grad_inner_bias.reshape(nf, ff_rows).astype(bf16)
    )
    row_grads = lax.psum_scatter(row_grads, "fsdp", scatter_dimension=0, tiled=True)
    row_grads = replica_sum(row_grads, "rep")[0]
    grad_mixer_out = row_grads[:shard_rows]
    grad_outer_out = row_grads[shard_rows : shard_rows + ff_rows]
    grad_ibias_out = row_grads[shard_rows + ff_rows + 1, :ff_rows]
    fsdp_me = lax.axis_index("fsdp")
    grad_obias_out = lax.dynamic_slice_in_dim(
        row_grads[shard_rows + ff_rows], (me * nf + fsdp_me) * shard_rows, shard_rows
    )

    return (
        layer_output[None],
        input_grad[None],
        grad_gain_out,
        grad_shift_out,
        grad_triple_out,
        grad_mixer_out,
        grad_inner_out,
        grad_ibias_out,
        grad_outer_out,
        grad_obias_out,
    )


def solution(mesh):
    placed = (
        P(("rep", "fsdp"), "ctx", None),
        P(("ctx", "fsdp")),
        P(("ctx", "fsdp")),
        P(("ctx", "fsdp"), None),
        P(("ctx", "fsdp"), None),
        P(("ctx", "fsdp"), None),
        P(("ctx", "fsdp")),
        P(("ctx", "fsdp"), None),
        P(("ctx", "fsdp")),
        P(("rep", "fsdp")),
        P(("rep", "fsdp")),
        P(("rep", "fsdp"), "ctx", None),
    )
    return jax.shard_map(
        local,
        mesh=mesh,
        in_specs=placed,
        out_specs=(
            P(("rep", "fsdp"), "ctx", None),
            P(("rep", "fsdp"), "ctx", None),
            P(("ctx", "fsdp")),
            P(("ctx", "fsdp")),
            P(("ctx", "fsdp"), None),
            P(("ctx", "fsdp"), None),
            P(("ctx", "fsdp"), None),
            P(("ctx", "fsdp")),
            P(("ctx", "fsdp"), None),
            P(("ctx", "fsdp")),
        ),
        check_vma=False,
    )
```

```python
from functools import partial

import jax
import jax.numpy as jnp
from jax import lax
from jax.experimental import pallas as pl
from jax.experimental.pallas import tpu as pltpu
from jax.sharding import PartitionSpec as P

HEADS = 16
HEAD_DIM = 64
ROT = 32


eps = 1e-05


def angles(positions):
    frequency = 10000.0 ** (-(jnp.arange(ROT // 2, dtype=jnp.float32) * 2.0) / ROT)
    phases = positions.astype(jnp.float32)[:, None] * frequency[None, :]
    return (jnp.cos(phases), jnp.sin(phases))


def rotate(field, cos_table, sin_table):
    leading = field.shape[:-1]
    paired = field[..., :ROT].reshape(leading + (ROT // 2, 2))
    even_part = paired[..., 0]
    odd_part = paired[..., 1]
    cos_wide = cos_table[:, None, :]
    sin_wide = sin_table[:, None, :]
    turned = jnp.stack(
        [even_part * cos_wide - odd_part * sin_wide, odd_part * cos_wide + even_part * sin_wide], -1
    )
    return jnp.concatenate([turned.reshape(leading + (ROT,)), field[..., ROT:]], -1)


def ring_pairs(n, step):
    return [(i, (i + step) % n) for i in range(n)]


def ring_gather(block, axis):
    n = lax.axis_size(axis)
    half = block.shape[0] // 2
    from_left = lax.ppermute(block, axis, ring_pairs(n, 1))
    from_right = lax.ppermute(block, axis, ring_pairs(n, -1))
    far_first = lax.ppermute(from_left[:half], axis, ring_pairs(n, 1))
    far_second = lax.ppermute(from_right[half:], axis, ring_pairs(n, -1))
    far = jnp.concatenate([far_first, far_second], 0)
    return jnp.stack([block, from_right, far, from_left])


def ring_scatter(parts, axis):
    n = lax.axis_size(axis)
    half = parts.shape[1] // 2
    wire = jnp.bfloat16
    got_left = lax.ppermute(parts[2, :half].astype(wire), axis, ring_pairs(n, 1))
    got_right = lax.ppermute(parts[2, half:].astype(wire), axis, ring_pairs(n, -1))
    to_right = jnp.concatenate([parts[1, :half] + got_left.astype(jnp.float32), parts[1, half:]], 0)
    to_left = jnp.concatenate([parts[3, :half], parts[3, half:] + got_right.astype(jnp.float32)], 0)
    from_left = lax.ppermute(to_right.astype(wire), axis, ring_pairs(n, 1))
    from_right = lax.ppermute(to_left.astype(wire), axis, ring_pairs(n, -1))
    return parts[0] + from_left.astype(jnp.float32) + from_right.astype(jnp.float32)


def ring_all_to_all(payload, axis):
    n = lax.axis_size(axis)
    me = lax.axis_index(axis)
    pick = lambda d: lax.dynamic_index_in_dim(payload, d % n, 0, keepdims=False)
    got = [pick(me)] + [
        lax.ppermute(pick(me + s), axis, ring_pairs(n, s)) for s in range(1, n)
    ]
    mirrored = jnp.stack([got[(-k) % n] for k in range(n)])
    doubled = jnp.concatenate([mirrored, mirrored], 0)
    return lax.dynamic_slice_in_dim(doubled, n - me, n, 0)


def replica_sum(values, axis):
    n = lax.axis_size(axis)
    f32, wire = jnp.float32, jnp.bfloat16
    values = values.astype(wire)
    if n != 4:
        return lax.psum(values, axis).astype(f32)
    pair = values.astype(f32) + lax.ppermute(values, axis, [(i, i ^ 1) for i in range(n)]).astype(f32)
    pair = pair.astype(wire)
    return pair.astype(f32) + lax.ppermute(pair, axis, [(i, i ^ 2) for i in range(n)]).astype(f32)


def attention_kernel(span_ref, q_ref, k_ref, v_ref, gm_ref, qpos_ref, kpos_ref,
                     mix_ref, gq_ref, gk_ref, gv_ref, bias_ref):
    f32, bf16 = jnp.float32, jnp.bfloat16
    block = pl.program_id(0)
    head = pl.program_id(1)

    @pl.when(head == 0)
    def _():
        allowed = (kpos_ref[...] <= qpos_ref[...]) | (kpos_ref[...] < span_ref[0])
        bias_ref[...] = jnp.where(allowed, 0.0, -1e30).astype(f32)

    q = q_ref[...]
    k = k_ref[...]
    v = v_ref[...]
    gm = gm_ref[...]
    scores = lax.dot_general(q, k, (((1,), (1,)), ((), ())), preferred_element_type=f32)
    scores = scores + bias_ref[...]
    peak = jnp.max(scores, axis=1, keepdims=True)
    exps = jnp.exp(scores - peak)
    total = jnp.sum(exps, axis=1, keepdims=True)
    probs = exps * (1.0 / total)
    low_probs = probs.astype(bf16)
    mix_ref[...] = jnp.dot(low_probs, v, preferred_element_type=f32).astype(mix_ref.dtype)
    grad_probs = lax.dot_general(gm, v, (((1,), (1,)), ((), ())), preferred_element_type=f32)
    inner = jnp.sum(probs * grad_probs, axis=1, keepdims=True)
    grad_scores = (probs * (grad_probs - inner)).astype(bf16)
    gq_ref[...] = jnp.dot(grad_scores, k, preferred_element_type=f32)
    gk_part = lax.dot_general(grad_scores, q, (((0,), (0,)), ((), ())), preferred_element_type=f32)
    gv_part = lax.dot_general(low_probs, gm, (((0,), (0,)), ((), ())), preferred_element_type=f32)

    @pl.when(block == 0)
    def _():
        gk_ref[head] = gk_part
        gv_ref[head] = gv_part

    @pl.when(block != 0)
    def _():
        gk_ref[head] += gk_part
        gv_ref[head] += gv_part


def fused_attention(span, queries, keys, values, grad_mixture, positions, rows=256):
    heads, length, dim = queries.shape
    blocks = length // rows
    qpos = positions.reshape(length, 1).astype(jnp.int32)
    kpos = positions.reshape(1, length).astype(jnp.int32)
    row_block = pl.BlockSpec((None, rows, dim), lambda b, h, s: (h, b, 0))
    whole_head = pl.BlockSpec((None, length, dim), lambda b, h, s: (h, 0, 0))
    resident = pl.BlockSpec((heads, length, dim), lambda b, h, s: (0, 0, 0))
    f32 = jnp.float32
    return pl.pallas_call(
        attention_kernel,
        out_shape=(
            jax.ShapeDtypeStruct((heads, length, dim), jnp.bfloat16),
            jax.ShapeDtypeStruct((heads, length, dim), f32),
            jax.ShapeDtypeStruct((heads, length, dim), f32),
            jax.ShapeDtypeStruct((heads, length, dim), f32),
        ),
        grid_spec=pltpu.PrefetchScalarGridSpec(
            num_scalar_prefetch=1,
            grid=(blocks, heads),
            in_specs=[
                row_block, whole_head, whole_head, row_block,
                pl.BlockSpec((rows, 1), lambda b, h, s: (b, 0)),
                pl.BlockSpec((1, length), lambda b, h, s: (0, 0)),
            ],
            out_specs=[row_block, row_block, resident, resident],
            scratch_shapes=[pltpu.VMEM((rows, length), f32)],
        ),
        compiler_params=pltpu.CompilerParams(dimension_semantics=("arbitrary", "arbitrary")),
        cost_estimate=pl.CostEstimate(
            flops=12 * heads * length * length * dim,
            transcendentals=heads * length * length,
            bytes_accessed=heads * length * dim * (4 * 2 + 3 * 4 + 2),
        ),
    )(span.reshape(1).astype(jnp.int32), queries, keys, values, grad_mixture, qpos, kpos)


def local(
    tokens,
    norm_gain,
    norm_shift,
    triple_weight,
    mixer_weight,
    inner_weight,
    inner_bias,
    outer_weight,
    outer_bias,
    prefix_length,
    pad_mask,
    cotangent,
):
    nc = lax.axis_size("ctx")
    nf = lax.axis_size("fsdp")
    me = lax.axis_index("ctx")
    _, own_rows, width = tokens.shape
    length = own_rows * nc
    shard_rows = triple_weight.shape[0]
    heads_here = HEADS // nc
    head_cols = heads_here * HEAD_DIM
    ff_here = inner_weight.shape[1] // nc
    ff_rows = outer_weight.shape[0]
    f32, bf16 = jnp.float32, jnp.bfloat16

    triple_cols = (
        triple_weight.reshape(shard_rows, 3, nc, head_cols)
        .transpose(2, 0, 1, 3)
        .reshape(nc, shard_rows, 3 * head_cols)
    )
    inner_cols = inner_weight.reshape(shard_rows, nc, ff_here).transpose(1, 0, 2)
    small = jnp.stack([norm_gain, norm_shift, outer_bias], -1)
    small = jnp.pad(small, ((0, 0), (0, 128 - small.shape[-1])))
    small = jnp.broadcast_to(small[None], (nc,) + small.shape)
    column_payload = jnp.concatenate([triple_cols, inner_cols, small], -1)
    column_payload = ring_all_to_all(column_payload, "ctx")
    column_block = lax.all_gather(column_payload, "fsdp", axis=0, tiled=False)
    column_block = column_block.swapaxes(0, 1).reshape(nc * nf * shard_rows, -1)
    triple_here = column_block[:, : 3 * head_cols]
    inner_here = column_block[:, 3 * head_cols : 3 * head_cols + ff_here]
    gain = column_block[:, 3 * head_cols + ff_here].astype(f32)
    shift = column_block[:, 3 * head_cols + ff_here + 1].astype(f32)
    obias = column_block[:, 3 * head_cols + ff_here + 2].astype(f32)

    bias_rows = jnp.pad(inner_bias[None], ((0, 15), (0, width - inner_bias.shape[0])))
    row_payload = jnp.concatenate([mixer_weight, outer_weight, bias_rows], 0)
    row_block = lax.all_gather(row_payload, "fsdp", axis=0, tiled=False)
    mixer_here = row_block[:, :shard_rows].reshape(nf * shard_rows, width)
    outer_here = row_block[:, shard_rows : shard_rows + ff_rows].reshape(nf * ff_rows, width)
    ibias_here = row_block[:, shard_rows + ff_rows, : inner_bias.shape[0]].reshape(-1).astype(f32)

    visible = (pad_mask[0] != 0).astype(f32)
    own_upstream = cotangent[0].astype(f32) * visible
    both = jnp.concatenate([tokens[0], own_upstream.astype(bf16)], -1)
    both = ring_gather(both, "ctx").reshape(length, 2 * width)
    all_tokens = both[:, :width]
    all_upstream = both[:, width:]

    input_rows = all_tokens.astype(f32)
    center = input_rows - jnp.mean(input_rows, -1, keepdims=True)
    scaling = lax.rsqrt(jnp.mean(center * center, -1, keepdims=True) + eps)
    whitened = center * scaling
    normed = (whitened * gain + shift).astype(bf16)

    owners = (me + jnp.arange(nc)) % nc
    positions = (owners[:, None] * own_rows + jnp.arange(own_rows)[None, :]).reshape(length)
    cos_table, sin_table = angles(positions)
    query_key_value = jnp.dot(normed, triple_here, preferred_element_type=f32)
    heads_shape = (length, heads_here, HEAD_DIM)
    queries = (
        rotate(query_key_value[:, :head_cols].reshape(heads_shape), cos_table, sin_table)
        * HEAD_DIM ** (-0.5)
    ).astype(bf16)
    key_rows = rotate(
        query_key_value[:, head_cols : 2 * head_cols].reshape(heads_shape), cos_table, sin_table
    ).astype(bf16)
    value_rows = query_key_value[:, 2 * head_cols :].reshape(heads_shape).astype(bf16)
    span = prefix_length[0]
    grad_mixture = jnp.dot(all_upstream, mixer_here.T, preferred_element_type=f32).astype(bf16)
    by_head = lambda values: values.reshape(heads_shape).swapaxes(0, 1)
    mixture, grad_queries, grad_keys, grad_values = fused_attention(
        span, by_head(queries), by_head(key_rows), by_head(value_rows), by_head(grad_mixture), positions
    )
    grad_queries, grad_keys, grad_values = (
        values.swapaxes(0, 1) for values in (grad_queries, grad_keys, grad_values)
    )
    mixture = mixture.swapaxes(0, 1).reshape(length, head_cols)
    attention = jnp.dot(mixture, mixer_here, preferred_element_type=f32)
    preact = jnp.dot(normed, inner_here, preferred_element_type=f32) + ibias_here
    gelu_result = jax.nn.gelu(preact, approximate=True).astype(bf16)
    feedforward = jnp.dot(gelu_result, outer_here, preferred_element_type=f32)
    block_sum = ring_scatter((attention + feedforward).reshape(nc, own_rows, width), "ctx")
    layer_output = (tokens[0].astype(f32) + block_sum + obias).astype(bf16)

    ones_block = jnp.ones((length, 16), bf16)
    row_lhs = jnp.concatenate([mixture, gelu_result, ones_block], -1)
    row_product = jnp.dot(row_lhs.T, all_upstream, preferred_element_type=f32).astype(bf16)
    grad_activated = jnp.dot(all_upstream, outer_here.T, preferred_element_type=f32)
    unused_value, gelu_pull = jax.vjp(partial(jax.nn.gelu, approximate=True), preact)
    grad_before_gelu = gelu_pull(grad_activated)[0].astype(bf16)
    grad_inner_weight = jnp.dot(normed.T, grad_before_gelu, preferred_element_type=f32)
    grad_inner_bias = jnp.sum(grad_before_gelu.astype(f32), 0)
    flat_shape = (length, head_cols)
    grad_query_key_value = jnp.concatenate(
        [
            rotate(grad_queries * HEAD_DIM ** (-0.5), cos_table, -sin_table).reshape(flat_shape),
            rotate(grad_keys, cos_table, -sin_table).reshape(flat_shape),
            grad_values.reshape(flat_shape),
        ],
        -1,
    ).astype(bf16)
    grad_triple_weight = jnp.dot(normed.T, grad_query_key_value, preferred_element_type=f32)
    grad_normed = jnp.dot(grad_query_key_value, triple_here.T, preferred_element_type=f32)
    grad_normed = grad_normed + jnp.dot(grad_before_gelu, inner_here.T, preferred_element_type=f32)
    grad_norm_gain = jnp.sum(grad_normed * whitened, 0)
    grad_norm_shift = jnp.sum(grad_normed, 0)
    grad_normed = ring_scatter(grad_normed.reshape(nc, own_rows, width), "ctx")

    own_whitened = whitened[:own_rows]
    own_scaling = scaling[:own_rows]
    grad_white = grad_normed * gain
    grad_inputs = own_scaling * (
        grad_white
        - jnp.mean(grad_white, -1, keepdims=True)
        - own_whitened * jnp.mean(grad_white * own_whitened, -1, keepdims=True)
    )
    input_grad = (own_upstream + grad_inputs).astype(bf16)

    small_grads = jnp.stack([grad_norm_gain, grad_norm_shift], -1)
    small_grads = jnp.pad(small_grads, ((0, 0), (0, 128 - small_grads.shape[-1])))
    column_grads = jnp.concatenate(
        [grad_triple_weight, grad_inner_weight, small_grads], -1
    ).astype(bf16)
    column_grads = column_grads.reshape(nc, nf, shard_rows, -1).swapaxes(0, 1).reshape(width, -1)
    column_grads = lax.psum_scatter(column_grads, "fsdp", scatter_dimension=0, tiled=True)
    column_grads = replica_sum(column_grads, "rep").astype(bf16)
    column_grads = column_grads.reshape(nc, shard_rows, -1)
    column_grads = ring_all_to_all(column_grads, "ctx").astype(f32)
    grad_triple_out = (
        column_grads[:, :, : 3 * head_cols]
        .reshape(nc, shard_rows, 3, head_cols)
        .transpose(1, 2, 0, 3)
        .reshape(shard_rows, 3 * nc * head_cols)
    )
    grad_inner_out = (
        column_grads[:, :, 3 * head_cols : 3 * head_cols + ff_here]
        .transpose(1, 0, 2)
        .reshape(shard_rows, nc * ff_here)
    )
    grad_gain_out = jnp.sum(column_grads[:, :, 3 * head_cols + ff_here], 0)
    grad_shift_out = jnp.sum(column_grads[:, :, 3 * head_cols + ff_here + 1], 0)

    mixer_part = row_product[:head_cols].reshape(nf, shard_rows, width)
    outer_part = row_product[head_cols : head_cols + ff_here].reshape(nf, ff_rows, width)
    sums_part = jnp.broadcast_to(row_product[head_cols + ff_here :][None], (nf, 16, width))
    row_grads = jnp.concatenate([mixer_part, outer_part, sums_part], 1)
    row_grads = row_grads.at[:, ff_rows + shard_rows + 1, :ff_rows].set(
        grad_inner_bias.reshape(nf, ff_rows).astype(bf16)
    )
    row_grads = lax.psum_scatter(row_grads, "fsdp", scatter_dimension=0, tiled=True)
    row_grads = replica_sum(row_grads, "rep")[0]
    grad_mixer_out = row_grads[:shard_rows]
    grad_outer_out = row_grads[shard_rows : shard_rows + ff_rows]
    grad_ibias_out = row_grads[shard_rows + ff_rows + 1, :ff_rows]
    fsdp_me = lax.axis_index("fsdp")
    grad_obias_out = lax.dynamic_slice_in_dim(
        row_grads[shard_rows + ff_rows], (me * nf + fsdp_me) * shard_rows, shard_rows
    )

    return (
        layer_output[None],
        input_grad[None],
        grad_gain_out,
        grad_shift_out,
        grad_triple_out,
        grad_mixer_out,
        grad_inner_out,
        grad_ibias_out,
        grad_outer_out,
        grad_obias_out,
    )


def solution(mesh):
    placed = (
        P(("rep", "fsdp"), "ctx", None),
        P(("ctx", "fsdp")),
        P(("ctx", "fsdp")),
        P(("ctx", "fsdp"), None),
        P(("ctx", "fsdp"), None),
        P(("ctx", "fsdp"), None),
        P(("ctx", "fsdp")),
        P(("ctx", "fsdp"), None),
        P(("ctx", "fsdp")),
        P(("rep", "fsdp")),
        P(("rep", "fsdp")),
        P(("rep", "fsdp"), "ctx", None),
    )
    return jax.shard_map(
        local,
        mesh=mesh,
        in_specs=placed,
        out_specs=(
            P(("rep", "fsdp"), "ctx", None),
            P(("rep", "fsdp"), "ctx", None),
            P(("ctx", "fsdp")),
            P(("ctx", "fsdp")),
            P(("ctx", "fsdp"), None),
            P(("ctx", "fsdp"), None),
            P(("ctx", "fsdp"), None),
            P(("ctx", "fsdp")),
            P(("ctx", "fsdp"), None),
            P(("ctx", "fsdp")),
        ),
        check_vma=False,
    )
```

```python
from functools import partial

import jax
import jax.numpy as jnp
from jax import lax
from jax.experimental import pallas as pl
from jax.experimental.pallas import tpu as pltpu
from jax.sharding import PartitionSpec as P

HEADS = 16
HEAD_DIM = 64
ROT = 32


eps = 1e-05


def angles(positions):
    frequency = 10000.0 ** (-(jnp.arange(ROT // 2, dtype=jnp.float32) * 2.0) / ROT)
    phases = positions.astype(jnp.float32)[:, None] * frequency[None, :]
    return (jnp.cos(phases), jnp.sin(phases))


def rotate(field, cos_table, sin_table):
    leading = field.shape[:-1]
    paired = field[..., :ROT].reshape(leading + (ROT // 2, 2))
    even_part = paired[..., 0]
    odd_part = paired[..., 1]
    cos_wide = cos_table[:, None, :]
    sin_wide = sin_table[:, None, :]
    turned = jnp.stack(
        [even_part * cos_wide - odd_part * sin_wide, odd_part * cos_wide + even_part * sin_wide], -1
    )
    return jnp.concatenate([turned.reshape(leading + (ROT,)), field[..., ROT:]], -1)


def ring_pairs(n, step):
    return [(i, (i + step) % n) for i in range(n)]


def ring_gather(block, axis):
    n = lax.axis_size(axis)
    half = block.shape[0] // 2
    from_left = lax.ppermute(block, axis, ring_pairs(n, 1))
    from_right = lax.ppermute(block, axis, ring_pairs(n, -1))
    far_first = lax.ppermute(from_left[:half], axis, ring_pairs(n, 1))
    far_second = lax.ppermute(from_right[half:], axis, ring_pairs(n, -1))
    far = jnp.concatenate([far_first, far_second], 0)
    return jnp.stack([block, from_right, far, from_left])


def ring_scatter(parts, axis):
    n = lax.axis_size(axis)
    half = parts.shape[1] // 2
    wire = jnp.bfloat16
    got_left = lax.ppermute(parts[2, :half].astype(wire), axis, ring_pairs(n, 1))
    got_right = lax.ppermute(parts[2, half:].astype(wire), axis, ring_pairs(n, -1))
    to_right = jnp.concatenate([parts[1, :half] + got_left.astype(jnp.float32), parts[1, half:]], 0)
    to_left = jnp.concatenate([parts[3, :half], parts[3, half:] + got_right.astype(jnp.float32)], 0)
    from_left = lax.ppermute(to_right.astype(wire), axis, ring_pairs(n, 1))
    from_right = lax.ppermute(to_left.astype(wire), axis, ring_pairs(n, -1))
    return parts[0] + from_left.astype(jnp.float32) + from_right.astype(jnp.float32)


def ring_all_to_all(payload, axis):
    n = lax.axis_size(axis)
    me = lax.axis_index(axis)
    pick = lambda d: lax.dynamic_index_in_dim(payload, d % n, 0, keepdims=False)
    got = [pick(me)] + [
        lax.ppermute(pick(me + s), axis, ring_pairs(n, s)) for s in range(1, n)
    ]
    mirrored = jnp.stack([got[(-k) % n] for k in range(n)])
    doubled = jnp.concatenate([mirrored, mirrored], 0)
    return lax.dynamic_slice_in_dim(doubled, n - me, n, 0)


def replica_sum(values, axis):
    n = lax.axis_size(axis)
    f32, wire = jnp.float32, jnp.bfloat16
    values = values.astype(wire)
    if n != 4:
        return lax.psum(values, axis).astype(f32)
    pair = values.astype(f32) + lax.ppermute(values, axis, [(i, i ^ 1) for i in range(n)]).astype(f32)
    pair = pair.astype(wire)
    return pair.astype(f32) + lax.ppermute(pair, axis, [(i, i ^ 2) for i in range(n)]).astype(f32)


def attention_kernel(span_ref, q_ref, k_ref, v_ref, gm_ref, qpos_ref, kpos_ref,
                     mix_ref, gq_ref, gk_ref, gv_ref, bias_ref):
    f32, bf16 = jnp.float32, jnp.bfloat16
    block = pl.program_id(0)
    head = pl.program_id(1)

    @pl.when(head == 0)
    def _():
        allowed = (kpos_ref[...] <= qpos_ref[...]) | (kpos_ref[...] < span_ref[0])
        bias_ref[...] = jnp.where(allowed, 0.0, -1e30).astype(f32)

    q = q_ref[...]
    k = k_ref[...]
    v = v_ref[...]
    gm = gm_ref[...]
    scores = lax.dot_general(q, k, (((1,), (1,)), ((), ())), preferred_element_type=f32)
    scores = scores + bias_ref[...]
    peak = jnp.max(scores, axis=1, keepdims=True)
    exps = jnp.exp(scores - peak)
    total = jnp.sum(exps, axis=1, keepdims=True)
    probs = exps * (1.0 / total)
    low_probs = probs.astype(bf16)
    mix_ref[...] = jnp.dot(low_probs, v, preferred_element_type=f32).astype(mix_ref.dtype)
    grad_probs = lax.dot_general(gm, v, (((1,), (1,)), ((), ())), preferred_element_type=f32)
    inner = jnp.sum(probs * grad_probs, axis=1, keepdims=True)
    grad_scores = (probs * (grad_probs - inner)).astype(bf16)
    gq_ref[...] = jnp.dot(grad_scores, k, preferred_element_type=f32)
    gk_part = lax.dot_general(grad_scores, q, (((0,), (0,)), ((), ())), preferred_element_type=f32)
    gv_part = lax.dot_general(low_probs, gm, (((0,), (0,)), ((), ())), preferred_element_type=f32)

    @pl.when(block == 0)
    def _():
        gk_ref[head] = gk_part
        gv_ref[head] = gv_part

    @pl.when(block != 0)
    def _():
        gk_ref[head] += gk_part
        gv_ref[head] += gv_part


def fused_attention(span, queries, keys, values, grad_mixture, positions, rows=256):
    heads, length, dim = queries.shape
    blocks = length // rows
    qpos = positions.reshape(length, 1).astype(jnp.int32)
    kpos = positions.reshape(1, length).astype(jnp.int32)
    row_block = pl.BlockSpec((None, rows, dim), lambda b, h, s: (h, b, 0))
    whole_head = pl.BlockSpec((None, length, dim), lambda b, h, s: (h, 0, 0))
    resident = pl.BlockSpec((heads, length, dim), lambda b, h, s: (0, 0, 0))
    f32 = jnp.float32
    return pl.pallas_call(
        attention_kernel,
        out_shape=(
            jax.ShapeDtypeStruct((heads, length, dim), jnp.bfloat16),
            jax.ShapeDtypeStruct((heads, length, dim), f32),
            jax.ShapeDtypeStruct((heads, length, dim), f32),
            jax.ShapeDtypeStruct((heads, length, dim), f32),
        ),
        grid_spec=pltpu.PrefetchScalarGridSpec(
            num_scalar_prefetch=1,
            grid=(blocks, heads),
            in_specs=[
                row_block, whole_head, whole_head, row_block,
                pl.BlockSpec((rows, 1), lambda b, h, s: (b, 0)),
                pl.BlockSpec((1, length), lambda b, h, s: (0, 0)),
            ],
            out_specs=[row_block, row_block, resident, resident],
            scratch_shapes=[pltpu.VMEM((rows, length), f32)],
        ),
        compiler_params=pltpu.CompilerParams(dimension_semantics=("arbitrary", "arbitrary")),
        cost_estimate=pl.CostEstimate(
            flops=12 * heads * length * length * dim,
            transcendentals=heads * length * length,
            bytes_accessed=heads * length * dim * (4 * 2 + 3 * 4 + 2),
        ),
    )(span.reshape(1).astype(jnp.int32), queries, keys, values, grad_mixture, qpos, kpos)


def local(
    tokens,
    norm_gain,
    norm_shift,
    triple_weight,
    mixer_weight,
    inner_weight,
    inner_bias,
    outer_weight,
    outer_bias,
    prefix_length,
    pad_mask,
    cotangent,
):
    nc = lax.axis_size("ctx")
    nf = lax.axis_size("fsdp")
    me = lax.axis_index("ctx")
    _, own_rows, width = tokens.shape
    length = own_rows * nc
    shard_rows = triple_weight.shape[0]
    heads_here = HEADS // nc
    head_cols = heads_here * HEAD_DIM
    ff_here = inner_weight.shape[1] // nc
    ff_rows = outer_weight.shape[0]
    f32, bf16 = jnp.float32, jnp.bfloat16

    triple_cols = (
        triple_weight.reshape(shard_rows, 3, nc, head_cols)
        .transpose(2, 0, 1, 3)
        .reshape(nc, shard_rows, 3 * head_cols)
    )
    inner_cols = inner_weight.reshape(shard_rows, nc, ff_here).transpose(1, 0, 2)
    small = jnp.stack([norm_gain, norm_shift, outer_bias], -1)
    small = jnp.pad(small, ((0, 0), (0, 128 - small.shape[-1])))
    small = jnp.broadcast_to(small[None], (nc,) + small.shape)
    column_payload = jnp.concatenate([triple_cols, inner_cols, small], -1)
    column_payload = ring_all_to_all(column_payload, "ctx")
    column_block = lax.all_gather(column_payload, "fsdp", axis=0, tiled=False)
    column_block = column_block.swapaxes(0, 1).reshape(nc * nf * shard_rows, -1)
    triple_here = column_block[:, : 3 * head_cols]
    inner_here = column_block[:, 3 * head_cols : 3 * head_cols + ff_here]
    gain = column_block[:, 3 * head_cols + ff_here].astype(f32)
    shift = column_block[:, 3 * head_cols + ff_here + 1].astype(f32)
    obias = column_block[:, 3 * head_cols + ff_here + 2].astype(f32)

    bias_rows = jnp.pad(inner_bias[None], ((0, 15), (0, width - inner_bias.shape[0])))
    row_payload = jnp.concatenate([mixer_weight, outer_weight, bias_rows], 0)
    row_block = lax.all_gather(row_payload, "fsdp", axis=0, tiled=False)
    mixer_here = row_block[:, :shard_rows].reshape(nf * shard_rows, width)
    outer_here = row_block[:, shard_rows : shard_rows + ff_rows].reshape(nf * ff_rows, width)
    ibias_here = row_block[:, shard_rows + ff_rows, : inner_bias.shape[0]].reshape(-1).astype(f32)

    visible = (pad_mask[0] != 0).astype(f32)
    own_upstream = cotangent[0].astype(f32) * visible
    both = jnp.concatenate([tokens[0], own_upstream.astype(bf16)], -1)
    both = ring_gather(both, "ctx").reshape(length, 2 * width)
    all_tokens = both[:, :width]
    all_upstream = both[:, width:]

    input_rows = all_tokens.astype(f32)
    center = input_rows - jnp.mean(input_rows, -1, keepdims=True)
    scaling = lax.rsqrt(jnp.mean(center * center, -1, keepdims=True) + eps)
    whitened = center * scaling
    normed = (whitened * gain + shift).astype(bf16)

    owners = (me + jnp.arange(nc)) % nc
    positions = (owners[:, None] * own_rows + jnp.arange(own_rows)[None, :]).reshape(length)
    cos_table, sin_table = angles(positions)
    query_key_value = jnp.dot(normed, triple_here, preferred_element_type=f32)
    heads_shape = (length, heads_here, HEAD_DIM)
    queries = (
        rotate(query_key_value[:, :head_cols].reshape(heads_shape), cos_table, sin_table)
        * HEAD_DIM ** (-0.5)
    ).astype(bf16)
    key_rows = rotate(
        query_key_value[:, head_cols : 2 * head_cols].reshape(heads_shape), cos_table, sin_table
    ).astype(bf16)
    value_rows = query_key_value[:, 2 * head_cols :].reshape(heads_shape).astype(bf16)
    span = prefix_length[0]
    grad_mixture = jnp.dot(all_upstream, mixer_here.T, preferred_element_type=f32).astype(bf16)
    by_head = lambda values: values.reshape(heads_shape).swapaxes(0, 1)
    mixture, grad_queries, grad_keys, grad_values = fused_attention(
        span, by_head(queries), by_head(key_rows), by_head(value_rows), by_head(grad_mixture), positions
    )
    grad_queries, grad_keys, grad_values = (
        values.swapaxes(0, 1) for values in (grad_queries, grad_keys, grad_values)
    )
    mixture = mixture.swapaxes(0, 1).reshape(length, head_cols)
    attention = jnp.dot(mixture, mixer_here, preferred_element_type=f32)
    preact = jnp.dot(normed, inner_here, preferred_element_type=f32) + ibias_here
    gelu_result = jax.nn.gelu(preact, approximate=True).astype(bf16)
    feedforward = jnp.dot(gelu_result, outer_here, preferred_element_type=f32)
    block_sum = ring_scatter((attention + feedforward).reshape(nc, own_rows, width), "ctx")
    layer_output = (tokens[0].astype(f32) + block_sum + obias).astype(bf16)

    ones_block = jnp.ones((length, 16), bf16)
    row_lhs = jnp.concatenate([mixture, gelu_result, ones_block], -1)
    row_product = jnp.dot(row_lhs.T, all_upstream, preferred_element_type=f32).astype(bf16)
    grad_activated = jnp.dot(all_upstream, outer_here.T, preferred_element_type=f32)
    unused_value, gelu_pull = jax.vjp(partial(jax.nn.gelu, approximate=True), preact)
    grad_before_gelu = gelu_pull(grad_activated)[0].astype(bf16)
    grad_inner_weight = jnp.dot(normed.T, grad_before_gelu, preferred_element_type=f32)
    grad_inner_bias = jnp.sum(grad_before_gelu.astype(f32), 0)
    flat_shape = (length, head_cols)
    grad_query_key_value = jnp.concatenate(
        [
            rotate(grad_queries * HEAD_DIM ** (-0.5), cos_table, -sin_table).reshape(flat_shape),
            rotate(grad_keys, cos_table, -sin_table).reshape(flat_shape),
            grad_values.reshape(flat_shape),
        ],
        -1,
    ).astype(bf16)
    grad_triple_weight = jnp.dot(normed.T, grad_query_key_value, preferred_element_type=f32)
    grad_normed = jnp.dot(grad_query_key_value, triple_here.T, preferred_element_type=f32)
    grad_normed = grad_normed + jnp.dot(grad_before_gelu, inner_here.T, preferred_element_type=f32)
    grad_norm_gain = jnp.sum(grad_normed * whitened, 0)
    grad_norm_shift = jnp.sum(grad_normed, 0)
    grad_normed = ring_scatter(grad_normed.reshape(nc, own_rows, width), "ctx")

    mixer_part = row_product[:head_cols].reshape(nf, shard_rows, width)
    outer_part = row_product[head_cols : head_cols + ff_here].reshape(nf, ff_rows, width)
    sums_part = jnp.broadcast_to(row_product[head_cols + ff_here :][None], (nf, 16, width))
    row_grads = jnp.concatenate([mixer_part, outer_part, sums_part], 1)
    row_grads = row_grads.at[:, ff_rows + shard_rows + 1, :ff_rows].set(
        grad_inner_bias.reshape(nf, ff_rows).astype(bf16)
    )
    row_grads = lax.psum_scatter(row_grads, "fsdp", scatter_dimension=0, tiled=True)
    row_grads = replica_sum(row_grads, "rep")[0]
    row_grads, grad_normed = lax.optimization_barrier((row_grads, grad_normed))
    own_whitened = whitened[:own_rows]
    own_scaling = scaling[:own_rows]
    grad_white = grad_normed * gain
    grad_inputs = own_scaling * (
        grad_white
        - jnp.mean(grad_white, -1, keepdims=True)
        - own_whitened * jnp.mean(grad_white * own_whitened, -1, keepdims=True)
    )
    input_grad = (own_upstream + grad_inputs).astype(bf16)

    small_grads = jnp.stack([grad_norm_gain, grad_norm_shift], -1)
    small_grads = jnp.pad(small_grads, ((0, 0), (0, 128 - small_grads.shape[-1])))
    column_grads = jnp.concatenate(
        [grad_triple_weight, grad_inner_weight, small_grads], -1
    ).astype(bf16)
    column_grads = column_grads.reshape(nc, nf, shard_rows, -1).swapaxes(0, 1).reshape(width, -1)
    column_grads = lax.psum_scatter(column_grads, "fsdp", scatter_dimension=0, tiled=True)
    column_grads = replica_sum(column_grads, "rep").astype(bf16)
    column_grads = column_grads.reshape(nc, shard_rows, -1)
    column_grads = ring_all_to_all(column_grads, "ctx").astype(f32)
    grad_triple_out = (
        column_grads[:, :, : 3 * head_cols]
        .reshape(nc, shard_rows, 3, head_cols)
        .transpose(1, 2, 0, 3)
        .reshape(shard_rows, 3 * nc * head_cols)
    )
    grad_inner_out = (
        column_grads[:, :, 3 * head_cols : 3 * head_cols + ff_here]
        .transpose(1, 0, 2)
        .reshape(shard_rows, nc * ff_here)
    )
    grad_gain_out = jnp.sum(column_grads[:, :, 3 * head_cols + ff_here], 0)
    grad_shift_out = jnp.sum(column_grads[:, :, 3 * head_cols + ff_here + 1], 0)

    grad_mixer_out = row_grads[:shard_rows]
    grad_outer_out = row_grads[shard_rows : shard_rows + ff_rows]
    grad_ibias_out = row_grads[shard_rows + ff_rows + 1, :ff_rows]
    fsdp_me = lax.axis_index("fsdp")
    grad_obias_out = lax.dynamic_slice_in_dim(
        row_grads[shard_rows + ff_rows], (me * nf + fsdp_me) * shard_rows, shard_rows
    )

    return (
        layer_output[None],
        input_grad[None],
        grad_gain_out,
        grad_shift_out,
        grad_triple_out,
        grad_mixer_out,
        grad_inner_out,
        grad_ibias_out,
        grad_outer_out,
        grad_obias_out,
    )


def solution(mesh):
    placed = (
        P(("rep", "fsdp"), "ctx", None),
        P(("ctx", "fsdp")),
        P(("ctx", "fsdp")),
        P(("ctx", "fsdp"), None),
        P(("ctx", "fsdp"), None),
        P(("ctx", "fsdp"), None),
        P(("ctx", "fsdp")),
        P(("ctx", "fsdp"), None),
        P(("ctx", "fsdp")),
        P(("rep", "fsdp")),
        P(("rep", "fsdp")),
        P(("rep", "fsdp"), "ctx", None),
    )
    return jax.shard_map(
        local,
        mesh=mesh,
        in_specs=placed,
        out_specs=(
            P(("rep", "fsdp"), "ctx", None),
            P(("rep", "fsdp"), "ctx", None),
            P(("ctx", "fsdp")),
            P(("ctx", "fsdp")),
            P(("ctx", "fsdp"), None),
            P(("ctx", "fsdp"), None),
            P(("ctx", "fsdp"), None),
            P(("ctx", "fsdp")),
            P(("ctx", "fsdp"), None),
            P(("ctx", "fsdp")),
        ),
        check_vma=False,
    )
```

```python
from functools import partial

import jax
import jax.numpy as jnp
from jax import lax
from jax.experimental import pallas as pl
from jax.experimental.pallas import tpu as pltpu
from jax.sharding import PartitionSpec as P

HEADS = 16
HEAD_DIM = 64
ROT = 32


eps = 1e-05


def angles(positions):
    frequency = 10000.0 ** (-(jnp.arange(ROT // 2, dtype=jnp.float32) * 2.0) / ROT)
    phases = positions.astype(jnp.float32)[:, None] * frequency[None, :]
    return (jnp.cos(phases), jnp.sin(phases))


def rotate(field, cos_table, sin_table):
    leading = field.shape[:-1]
    paired = field[..., :ROT].reshape(leading + (ROT // 2, 2))
    even_part = paired[..., 0]
    odd_part = paired[..., 1]
    cos_wide = cos_table[:, None, :]
    sin_wide = sin_table[:, None, :]
    turned = jnp.stack(
        [even_part * cos_wide - odd_part * sin_wide, odd_part * cos_wide + even_part * sin_wide], -1
    )
    return jnp.concatenate([turned.reshape(leading + (ROT,)), field[..., ROT:]], -1)


def ring_pairs(n, step):
    return [(i, (i + step) % n) for i in range(n)]


def ring_gather(block, axis):
    n = lax.axis_size(axis)
    half = block.shape[0] // 2
    from_left = lax.ppermute(block, axis, ring_pairs(n, 1))
    from_right = lax.ppermute(block, axis, ring_pairs(n, -1))
    far_first = lax.ppermute(from_left[:half], axis, ring_pairs(n, 1))
    far_second = lax.ppermute(from_right[half:], axis, ring_pairs(n, -1))
    far = jnp.concatenate([far_first, far_second], 0)
    return jnp.stack([block, from_right, far, from_left])


def ring_scatter(parts, axis):
    n = lax.axis_size(axis)
    half = parts.shape[1] // 2
    wire = jnp.bfloat16
    got_left = lax.ppermute(parts[2, :half].astype(wire), axis, ring_pairs(n, 1))
    got_right = lax.ppermute(parts[2, half:].astype(wire), axis, ring_pairs(n, -1))
    to_right = jnp.concatenate([parts[1, :half] + got_left.astype(jnp.float32), parts[1, half:]], 0)
    to_left = jnp.concatenate([parts[3, :half], parts[3, half:] + got_right.astype(jnp.float32)], 0)
    from_left = lax.ppermute(to_right.astype(wire), axis, ring_pairs(n, 1))
    from_right = lax.ppermute(to_left.astype(wire), axis, ring_pairs(n, -1))
    return parts[0] + from_left.astype(jnp.float32) + from_right.astype(jnp.float32)


def ring_all_to_all(payload, axis):
    n = lax.axis_size(axis)
    me = lax.axis_index(axis)
    pick = lambda d: lax.dynamic_index_in_dim(payload, d % n, 0, keepdims=False)
    got = [pick(me)] + [
        lax.ppermute(pick(me + s), axis, ring_pairs(n, s)) for s in range(1, n)
    ]
    mirrored = jnp.stack([got[(-k) % n] for k in range(n)])
    doubled = jnp.concatenate([mirrored, mirrored], 0)
    return lax.dynamic_slice_in_dim(doubled, n - me, n, 0)


def replica_sum(values, axis):
    n = lax.axis_size(axis)
    f32, wire = jnp.float32, jnp.bfloat16
    values = values.astype(wire)
    if n != 4:
        return lax.psum(values, axis).astype(f32)
    pair = values.astype(f32) + lax.ppermute(values, axis, [(i, i ^ 1) for i in range(n)]).astype(f32)
    pair = pair.astype(wire)
    return pair.astype(f32) + lax.ppermute(pair, axis, [(i, i ^ 2) for i in range(n)]).astype(f32)


def attention_kernel(span_ref, q_ref, k_ref, v_ref, gm_ref, qpos_ref, kpos_ref,
                     mix_ref, gq_ref, gk_ref, gv_ref, bias_ref):
    f32, bf16 = jnp.float32, jnp.bfloat16
    block = pl.program_id(0)
    head = pl.program_id(1)

    @pl.when(head == 0)
    def _():
        allowed = (kpos_ref[...] <= qpos_ref[...]) | (kpos_ref[...] < span_ref[0])
        bias_ref[...] = jnp.where(allowed, 0.0, -1e30).astype(f32)

    q = q_ref[...]
    k = k_ref[...]
    v = v_ref[...]
    gm = gm_ref[...]
    scores = lax.dot_general(q, k, (((1,), (1,)), ((), ())), preferred_element_type=f32)
    scores = scores + bias_ref[...]
    peak = jnp.max(scores, axis=1, keepdims=True)
    exps = jnp.exp(scores - peak)
    total = jnp.sum(exps, axis=1, keepdims=True)
    probs = exps * (1.0 / total)
    low_probs = probs.astype(bf16)
    mix_ref[...] = jnp.dot(low_probs, v, preferred_element_type=f32).astype(mix_ref.dtype)
    grad_probs = lax.dot_general(gm, v, (((1,), (1,)), ((), ())), preferred_element_type=f32)
    inner = jnp.sum(probs * grad_probs, axis=1, keepdims=True)
    grad_scores = (probs * (grad_probs - inner)).astype(bf16)
    gq_ref[...] = jnp.dot(grad_scores, k, preferred_element_type=f32)
    gk_part = lax.dot_general(grad_scores, q, (((0,), (0,)), ((), ())), preferred_element_type=f32)
    gv_part = lax.dot_general(low_probs, gm, (((0,), (0,)), ((), ())), preferred_element_type=f32)

    @pl.when(block == 0)
    def _():
        gk_ref[head] = gk_part
        gv_ref[head] = gv_part

    @pl.when(block != 0)
    def _():
        gk_ref[head] += gk_part
        gv_ref[head] += gv_part


def fused_attention(span, queries, keys, values, grad_mixture, positions, rows=256):
    heads, length, dim = queries.shape
    blocks = length // rows
    qpos = positions.reshape(length, 1).astype(jnp.int32)
    kpos = positions.reshape(1, length).astype(jnp.int32)
    row_block = pl.BlockSpec((None, rows, dim), lambda b, h, s: (h, b, 0))
    whole_head = pl.BlockSpec((None, length, dim), lambda b, h, s: (h, 0, 0))
    resident = pl.BlockSpec((heads, length, dim), lambda b, h, s: (0, 0, 0))
    f32 = jnp.float32
    return pl.pallas_call(
        attention_kernel,
        out_shape=(
            jax.ShapeDtypeStruct((heads, length, dim), jnp.bfloat16),
            jax.ShapeDtypeStruct((heads, length, dim), f32),
            jax.ShapeDtypeStruct((heads, length, dim), f32),
            jax.ShapeDtypeStruct((heads, length, dim), f32),
        ),
        grid_spec=pltpu.PrefetchScalarGridSpec(
            num_scalar_prefetch=1,
            grid=(blocks, heads),
            in_specs=[
                row_block, whole_head, whole_head, row_block,
                pl.BlockSpec((rows, 1), lambda b, h, s: (b, 0)),
                pl.BlockSpec((1, length), lambda b, h, s: (0, 0)),
            ],
            out_specs=[row_block, row_block, resident, resident],
            scratch_shapes=[pltpu.VMEM((rows, length), f32)],
        ),
        compiler_params=pltpu.CompilerParams(dimension_semantics=("arbitrary", "arbitrary")),
        cost_estimate=pl.CostEstimate(
            flops=12 * heads * length * length * dim,
            transcendentals=heads * length * length,
            bytes_accessed=heads * length * dim * (4 * 2 + 3 * 4 + 2),
        ),
    )(span.reshape(1).astype(jnp.int32), queries, keys, values, grad_mixture, qpos, kpos)


def local(
    tokens,
    norm_gain,
    norm_shift,
    triple_weight,
    mixer_weight,
    inner_weight,
    inner_bias,
    outer_weight,
    outer_bias,
    prefix_length,
    pad_mask,
    cotangent,
):
    nc = lax.axis_size("ctx")
    nf = lax.axis_size("fsdp")
    me = lax.axis_index("ctx")
    _, own_rows, width = tokens.shape
    length = own_rows * nc
    shard_rows = triple_weight.shape[0]
    heads_here = HEADS // nc
    head_cols = heads_here * HEAD_DIM
    ff_here = inner_weight.shape[1] // nc
    ff_rows = outer_weight.shape[0]
    f32, bf16 = jnp.float32, jnp.bfloat16

    triple_cols = (
        triple_weight.reshape(shard_rows, 3, nc, head_cols)
        .transpose(2, 0, 1, 3)
        .reshape(nc, shard_rows, 3 * head_cols)
    )
    inner_cols = inner_weight.reshape(shard_rows, nc, ff_here).transpose(1, 0, 2)
    small = jnp.stack([norm_gain, norm_shift, outer_bias], -1)
    small = jnp.pad(small, ((0, 0), (0, 128 - small.shape[-1])))
    small = jnp.broadcast_to(small[None], (nc,) + small.shape)
    column_payload = jnp.concatenate([triple_cols, inner_cols, small], -1)
    column_payload = ring_all_to_all(column_payload, "ctx")
    column_block = lax.all_gather(column_payload, "fsdp", axis=0, tiled=False)
    column_block = column_block.swapaxes(0, 1).reshape(nc * nf * shard_rows, -1)
    triple_here = column_block[:, : 3 * head_cols]
    inner_here = column_block[:, 3 * head_cols : 3 * head_cols + ff_here]
    gain = column_block[:, 3 * head_cols + ff_here].astype(f32)
    shift = column_block[:, 3 * head_cols + ff_here + 1].astype(f32)
    obias = column_block[:, 3 * head_cols + ff_here + 2].astype(f32)

    bias_rows = jnp.pad(inner_bias[None], ((0, 15), (0, width - inner_bias.shape[0])))
    row_payload = jnp.concatenate([mixer_weight, outer_weight, bias_rows], 0)
    row_block = lax.all_gather(row_payload, "fsdp", axis=0, tiled=False)
    mixer_here = row_block[:, :shard_rows].reshape(nf * shard_rows, width)
    outer_here = row_block[:, shard_rows : shard_rows + ff_rows].reshape(nf * ff_rows, width)
    ibias_here = row_block[:, shard_rows + ff_rows, : inner_bias.shape[0]].reshape(-1).astype(f32)

    visible = (pad_mask[0] != 0).astype(f32)
    own_upstream = cotangent[0].astype(f32) * visible
    both = jnp.concatenate([tokens[0], own_upstream.astype(bf16)], -1)
    both = ring_gather(both, "ctx").reshape(length, 2 * width)
    all_tokens = both[:, :width]
    all_upstream = both[:, width:]

    input_rows = all_tokens.astype(f32)
    center = input_rows - jnp.mean(input_rows, -1, keepdims=True)
    scaling = lax.rsqrt(jnp.mean(center * center, -1, keepdims=True) + eps)
    whitened = center * scaling
    normed = (whitened * gain + shift).astype(bf16)

    owners = (me + jnp.arange(nc)) % nc
    positions = (owners[:, None] * own_rows + jnp.arange(own_rows)[None, :]).reshape(length)
    cos_table, sin_table = angles(positions)
    query_key_value = jnp.dot(normed, triple_here, preferred_element_type=f32)
    heads_shape = (length, heads_here, HEAD_DIM)
    queries = (
        rotate(query_key_value[:, :head_cols].reshape(heads_shape), cos_table, sin_table)
        * HEAD_DIM ** (-0.5)
    ).astype(bf16)
    key_rows = rotate(
        query_key_value[:, head_cols : 2 * head_cols].reshape(heads_shape), cos_table, sin_table
    ).astype(bf16)
    value_rows = query_key_value[:, 2 * head_cols :].reshape(heads_shape).astype(bf16)
    span = prefix_length[0]
    grad_mixture = jnp.dot(all_upstream, mixer_here.T, preferred_element_type=f32).astype(bf16)
    by_head = lambda values: values.reshape(heads_shape).swapaxes(0, 1)
    mixture, grad_queries, grad_keys, grad_values = fused_attention(
        span, by_head(queries), by_head(key_rows), by_head(value_rows), by_head(grad_mixture), positions
    )
    grad_queries, grad_keys, grad_values = (
        values.swapaxes(0, 1) for values in (grad_queries, grad_keys, grad_values)
    )
    mixture = mixture.swapaxes(0, 1).reshape(length, head_cols)
    preact = jnp.dot(normed, inner_here, preferred_element_type=f32) + ibias_here
    gelu_result = jax.nn.gelu(preact, approximate=True).astype(bf16)
    feedforward = jnp.dot(gelu_result, outer_here, preferred_element_type=f32)
    ones_block = jnp.ones((length, 16), bf16)
    row_lhs = jnp.concatenate([mixture, gelu_result, ones_block], -1)
    row_product = jnp.dot(row_lhs.T, all_upstream, preferred_element_type=f32).astype(bf16)
    grad_activated = jnp.dot(all_upstream, outer_here.T, preferred_element_type=f32)
    unused_value, gelu_pull = jax.vjp(partial(jax.nn.gelu, approximate=True), preact)
    grad_before_gelu = gelu_pull(grad_activated)[0].astype(bf16)
    grad_inner_weight = jnp.dot(normed.T, grad_before_gelu, preferred_element_type=f32)
    grad_inner_bias = jnp.sum(grad_before_gelu.astype(f32), 0)
    flat_shape = (length, head_cols)
    grad_query_key_value = jnp.concatenate(
        [
            rotate(grad_queries * HEAD_DIM ** (-0.5), cos_table, -sin_table).reshape(flat_shape),
            rotate(grad_keys, cos_table, -sin_table).reshape(flat_shape),
            grad_values.reshape(flat_shape),
        ],
        -1,
    ).astype(bf16)
    grad_triple_weight = jnp.dot(normed.T, grad_query_key_value, preferred_element_type=f32)
    grad_normed = jnp.dot(grad_query_key_value, triple_here.T, preferred_element_type=f32)
    grad_normed = grad_normed + jnp.dot(grad_before_gelu, inner_here.T, preferred_element_type=f32)
    grad_norm_gain = jnp.sum(grad_normed * whitened, 0)
    grad_norm_shift = jnp.sum(grad_normed, 0)
    grad_normed = ring_scatter(grad_normed.reshape(nc, own_rows, width), "ctx")

    own_whitened = whitened[:own_rows]
    own_scaling = scaling[:own_rows]
    grad_white = grad_normed * gain
    grad_inputs = own_scaling * (
        grad_white
        - jnp.mean(grad_white, -1, keepdims=True)
        - own_whitened * jnp.mean(grad_white * own_whitened, -1, keepdims=True)
    )
    input_grad = (own_upstream + grad_inputs).astype(bf16)

    small_grads = jnp.stack([grad_norm_gain, grad_norm_shift], -1)
    small_grads = jnp.pad(small_grads, ((0, 0), (0, 128 - small_grads.shape[-1])))
    column_grads = jnp.concatenate(
        [grad_triple_weight, grad_inner_weight, small_grads], -1
    ).astype(bf16)
    column_grads = column_grads.reshape(nc, nf, shard_rows, -1).swapaxes(0, 1).reshape(width, -1)
    column_grads, mixture_late = lax.optimization_barrier((column_grads, mixture))
    attention = jnp.dot(mixture_late, mixer_here, preferred_element_type=f32)
    block_sum = ring_scatter((attention + feedforward).reshape(nc, own_rows, width), "ctx")
    layer_output = (tokens[0].astype(f32) + block_sum + obias).astype(bf16)

    column_grads = lax.psum_scatter(column_grads, "fsdp", scatter_dimension=0, tiled=True)
    column_grads = replica_sum(column_grads, "rep").astype(bf16)
    column_grads = column_grads.reshape(nc, shard_rows, -1)
    column_grads = ring_all_to_all(column_grads, "ctx").astype(f32)
    grad_triple_out = (
        column_grads[:, :, : 3 * head_cols]
        .reshape(nc, shard_rows, 3, head_cols)
        .transpose(1, 2, 0, 3)
        .reshape(shard_rows, 3 * nc * head_cols)
    )
    grad_inner_out = (
        column_grads[:, :, 3 * head_cols : 3 * head_cols + ff_here]
        .transpose(1, 0, 2)
        .reshape(shard_rows, nc * ff_here)
    )
    grad_gain_out = jnp.sum(column_grads[:, :, 3 * head_cols + ff_here], 0)
    grad_shift_out = jnp.sum(column_grads[:, :, 3 * head_cols + ff_here + 1], 0)

    mixer_part = row_product[:head_cols].reshape(nf, shard_rows, width)
    outer_part = row_product[head_cols : head_cols + ff_here].reshape(nf, ff_rows, width)
    sums_part = jnp.broadcast_to(row_product[head_cols + ff_here :][None], (nf, 16, width))
    row_grads = jnp.concatenate([mixer_part, outer_part, sums_part], 1)
    row_grads = row_grads.at[:, ff_rows + shard_rows + 1, :ff_rows].set(
        grad_inner_bias.reshape(nf, ff_rows).astype(bf16)
    )
    row_grads = lax.psum_scatter(row_grads, "fsdp", scatter_dimension=0, tiled=True)
    row_grads = replica_sum(row_grads, "rep")[0]
    grad_mixer_out = row_grads[:shard_rows]
    grad_outer_out = row_grads[shard_rows : shard_rows + ff_rows]
    grad_ibias_out = row_grads[shard_rows + ff_rows + 1, :ff_rows]
    fsdp_me = lax.axis_index("fsdp")
    grad_obias_out = lax.dynamic_slice_in_dim(
        row_grads[shard_rows + ff_rows], (me * nf + fsdp_me) * shard_rows, shard_rows
    )

    return (
        layer_output[None],
        input_grad[None],
        grad_gain_out,
        grad_shift_out,
        grad_triple_out,
        grad_mixer_out,
        grad_inner_out,
        grad_ibias_out,
        grad_outer_out,
        grad_obias_out,
    )


def solution(mesh):
    placed = (
        P(("rep", "fsdp"), "ctx", None),
        P(("ctx", "fsdp")),
        P(("ctx", "fsdp")),
        P(("ctx", "fsdp"), None),
        P(("ctx", "fsdp"), None),
        P(("ctx", "fsdp"), None),
        P(("ctx", "fsdp")),
        P(("ctx", "fsdp"), None),
        P(("ctx", "fsdp")),
        P(("rep", "fsdp")),
        P(("rep", "fsdp")),
        P(("rep", "fsdp"), "ctx", None),
    )
    return jax.shard_map(
        local,
        mesh=mesh,
        in_specs=placed,
        out_specs=(
            P(("rep", "fsdp"), "ctx", None),
            P(("rep", "fsdp"), "ctx", None),
            P(("ctx", "fsdp")),
            P(("ctx", "fsdp")),
            P(("ctx", "fsdp"), None),
            P(("ctx", "fsdp"), None),
            P(("ctx", "fsdp"), None),
            P(("ctx", "fsdp")),
            P(("ctx", "fsdp"), None),
            P(("ctx", "fsdp")),
        ),
        check_vma=False,
    )
```

```python
from functools import partial

import jax
import jax.numpy as jnp
from jax import lax
from jax.experimental import pallas as pl
from jax.experimental.pallas import tpu as pltpu
from jax.sharding import PartitionSpec as P

HEADS = 16
HEAD_DIM = 64
ROT = 32


eps = 1e-05


def angles(positions):
    frequency = 10000.0 ** (-(jnp.arange(ROT // 2, dtype=jnp.float32) * 2.0) / ROT)
    phases = positions.astype(jnp.float32)[:, None] * frequency[None, :]
    return (jnp.cos(phases), jnp.sin(phases))


def rotate(field, cos_table, sin_table):
    leading = field.shape[:-1]
    paired = field[..., :ROT].reshape(leading + (ROT // 2, 2))
    even_part = paired[..., 0]
    odd_part = paired[..., 1]
    cos_wide = cos_table[:, None, :]
    sin_wide = sin_table[:, None, :]
    turned = jnp.stack(
        [even_part * cos_wide - odd_part * sin_wide, odd_part * cos_wide + even_part * sin_wide], -1
    )
    return jnp.concatenate([turned.reshape(leading + (ROT,)), field[..., ROT:]], -1)


def pair_tables(positions, width):
    f32 = jnp.float32
    highest = lax.Precision.HIGHEST
    cos_table, sin_table = angles(positions)
    feature = jnp.arange(width) % HEAD_DIM
    pick = (feature[None, :] // 2 == jnp.arange(ROT // 2)[:, None]) & (feature[None, :] < ROT)
    pick = pick.astype(f32)
    sign = jnp.where(feature % 2 == 0, -1.0, 1.0).astype(f32)
    cos_full = jnp.dot(cos_table, pick, precision=highest) + (feature >= ROT).astype(f32)
    sin_full = jnp.dot(sin_table, pick, precision=highest) * sign
    return cos_full, sin_full


def swap_pairs(values):
    width = values.shape[-1]
    index = jnp.arange(width)
    swap = (index[:, None] == (index[None, :] ^ 1)).astype(jnp.float32)
    return jnp.dot(values, swap, precision=lax.Precision.HIGHEST)


def ring_pairs(n, step):
    return [(i, (i + step) % n) for i in range(n)]


def ring_gather(block, axis):
    n = lax.axis_size(axis)
    half = block.shape[0] // 2
    from_left = lax.ppermute(block, axis, ring_pairs(n, 1))
    from_right = lax.ppermute(block, axis, ring_pairs(n, -1))
    far_first = lax.ppermute(from_left[:half], axis, ring_pairs(n, 1))
    far_second = lax.ppermute(from_right[half:], axis, ring_pairs(n, -1))
    far = jnp.concatenate([far_first, far_second], 0)
    return jnp.stack([block, from_right, far, from_left])


def ring_scatter(parts, axis):
    n = lax.axis_size(axis)
    half = parts.shape[1] // 2
    wire = jnp.bfloat16
    got_left = lax.ppermute(parts[2, :half].astype(wire), axis, ring_pairs(n, 1))
    got_right = lax.ppermute(parts[2, half:].astype(wire), axis, ring_pairs(n, -1))
    to_right = jnp.concatenate([parts[1, :half] + got_left.astype(jnp.float32), parts[1, half:]], 0)
    to_left = jnp.concatenate([parts[3, :half], parts[3, half:] + got_right.astype(jnp.float32)], 0)
    from_left = lax.ppermute(to_right.astype(wire), axis, ring_pairs(n, 1))
    from_right = lax.ppermute(to_left.astype(wire), axis, ring_pairs(n, -1))
    return parts[0] + from_left.astype(jnp.float32) + from_right.astype(jnp.float32)


def ring_all_to_all(payload, axis):
    n = lax.axis_size(axis)
    me = lax.axis_index(axis)
    pick = lambda d: lax.dynamic_index_in_dim(payload, d % n, 0, keepdims=False)
    got = [pick(me)] + [
        lax.ppermute(pick(me + s), axis, ring_pairs(n, s)) for s in range(1, n)
    ]
    mirrored = jnp.stack([got[(-k) % n] for k in range(n)])
    doubled = jnp.concatenate([mirrored, mirrored], 0)
    return lax.dynamic_slice_in_dim(doubled, n - me, n, 0)


def replica_sum(values, axis):
    n = lax.axis_size(axis)
    f32, wire = jnp.float32, jnp.bfloat16
    values = values.astype(wire)
    if n != 4:
        return lax.psum(values, axis).astype(f32)
    pair = values.astype(f32) + lax.ppermute(values, axis, [(i, i ^ 1) for i in range(n)]).astype(f32)
    pair = pair.astype(wire)
    return pair.astype(f32) + lax.ppermute(pair, axis, [(i, i ^ 2) for i in range(n)]).astype(f32)


def attention_kernel(span_ref, q_ref, k_ref, v_ref, gm_ref, qpos_ref, kpos_ref,
                     mix_ref, gq_ref, gk_ref, gv_ref, bias_ref):
    f32, bf16 = jnp.float32, jnp.bfloat16
    block = pl.program_id(0)
    head = pl.program_id(1)

    @pl.when(head == 0)
    def _():
        allowed = (kpos_ref[...] <= qpos_ref[...]) | (kpos_ref[...] < span_ref[0])
        bias_ref[...] = jnp.where(allowed, 0.0, -1e30).astype(f32)

    q = q_ref[...]
    k = k_ref[...]
    v = v_ref[...]
    gm = gm_ref[...]
    scores = lax.dot_general(q, k, (((1,), (1,)), ((), ())), preferred_element_type=f32)
    scores = scores + bias_ref[...]
    peak = jnp.max(scores, axis=1, keepdims=True)
    exps = jnp.exp(scores - peak)
    total = jnp.sum(exps, axis=1, keepdims=True)
    probs = exps * (1.0 / total)
    low_probs = probs.astype(bf16)
    mix_ref[...] = jnp.dot(low_probs, v, preferred_element_type=f32).astype(mix_ref.dtype)
    grad_probs = lax.dot_general(gm, v, (((1,), (1,)), ((), ())), preferred_element_type=f32)
    inner = jnp.sum(probs * grad_probs, axis=1, keepdims=True)
    grad_scores = (probs * (grad_probs - inner)).astype(bf16)
    gq_ref[...] = jnp.dot(grad_scores, k, preferred_element_type=f32)
    gk_part = lax.dot_general(grad_scores, q, (((0,), (0,)), ((), ())), preferred_element_type=f32)
    gv_part = lax.dot_general(low_probs, gm, (((0,), (0,)), ((), ())), preferred_element_type=f32)

    @pl.when(block == 0)
    def _():
        gk_ref[head] = gk_part
        gv_ref[head] = gv_part

    @pl.when(block != 0)
    def _():
        gk_ref[head] += gk_part
        gv_ref[head] += gv_part


def fused_attention(span, queries, keys, values, grad_mixture, positions, rows=256):
    heads, length, dim = queries.shape
    blocks = length // rows
    qpos = positions.reshape(length, 1).astype(jnp.int32)
    kpos = positions.reshape(1, length).astype(jnp.int32)
    row_block = pl.BlockSpec((None, rows, dim), lambda b, h, s: (h, b, 0))
    whole_head = pl.BlockSpec((None, length, dim), lambda b, h, s: (h, 0, 0))
    resident = pl.BlockSpec((heads, length, dim), lambda b, h, s: (0, 0, 0))
    f32 = jnp.float32
    return pl.pallas_call(
        attention_kernel,
        out_shape=(
            jax.ShapeDtypeStruct((heads, length, dim), jnp.bfloat16),
            jax.ShapeDtypeStruct((heads, length, dim), f32),
            jax.ShapeDtypeStruct((heads, length, dim), f32),
            jax.ShapeDtypeStruct((heads, length, dim), f32),
        ),
        grid_spec=pltpu.PrefetchScalarGridSpec(
            num_scalar_prefetch=1,
            grid=(blocks, heads),
            in_specs=[
                row_block, whole_head, whole_head, row_block,
                pl.BlockSpec((rows, 1), lambda b, h, s: (b, 0)),
                pl.BlockSpec((1, length), lambda b, h, s: (0, 0)),
            ],
            out_specs=[row_block, row_block, resident, resident],
            scratch_shapes=[pltpu.VMEM((rows, length), f32)],
        ),
        compiler_params=pltpu.CompilerParams(dimension_semantics=("arbitrary", "arbitrary")),
        cost_estimate=pl.CostEstimate(
            flops=12 * heads * length * length * dim,
            transcendentals=heads * length * length,
            bytes_accessed=heads * length * dim * (4 * 2 + 3 * 4 + 2),
        ),
    )(span.reshape(1).astype(jnp.int32), queries, keys, values, grad_mixture, qpos, kpos)


def local(
    tokens,
    norm_gain,
    norm_shift,
    triple_weight,
    mixer_weight,
    inner_weight,
    inner_bias,
    outer_weight,
    outer_bias,
    prefix_length,
    pad_mask,
    cotangent,
):
    nc = lax.axis_size("ctx")
    nf = lax.axis_size("fsdp")
    me = lax.axis_index("ctx")
    _, own_rows, width = tokens.shape
    length = own_rows * nc
    shard_rows = triple_weight.shape[0]
    heads_here = HEADS // nc
    head_cols = heads_here * HEAD_DIM
    ff_here = inner_weight.shape[1] // nc
    ff_rows = outer_weight.shape[0]
    f32, bf16 = jnp.float32, jnp.bfloat16

    triple_cols = (
        triple_weight.reshape(shard_rows, 3, nc, head_cols)
        .transpose(2, 0, 1, 3)
        .reshape(nc, shard_rows, 3 * head_cols)
    )
    inner_cols = inner_weight.reshape(shard_rows, nc, ff_here).transpose(1, 0, 2)
    small = jnp.stack([norm_gain, norm_shift, outer_bias], -1)
    small = jnp.pad(small, ((0, 0), (0, 128 - small.shape[-1])))
    small = jnp.broadcast_to(small[None], (nc,) + small.shape)
    column_payload = jnp.concatenate([triple_cols, inner_cols, small], -1)
    column_payload = ring_all_to_all(column_payload, "ctx")
    column_block = lax.all_gather(column_payload, "fsdp", axis=0, tiled=False)
    column_block = column_block.swapaxes(0, 1).reshape(nc * nf * shard_rows, -1)
    triple_here = column_block[:, : 3 * head_cols]
    inner_here = column_block[:, 3 * head_cols : 3 * head_cols + ff_here]
    gain = column_block[:, 3 * head_cols + ff_here].astype(f32)
    shift = column_block[:, 3 * head_cols + ff_here + 1].astype(f32)
    obias = column_block[:, 3 * head_cols + ff_here + 2].astype(f32)

    bias_rows = jnp.pad(inner_bias[None], ((0, 15), (0, width - inner_bias.shape[0])))
    row_payload = jnp.concatenate([mixer_weight, outer_weight, bias_rows], 0)
    row_block = lax.all_gather(row_payload, "fsdp", axis=0, tiled=False)
    mixer_here = row_block[:, :shard_rows].reshape(nf * shard_rows, width)
    outer_here = row_block[:, shard_rows : shard_rows + ff_rows].reshape(nf * ff_rows, width)
    ibias_here = row_block[:, shard_rows + ff_rows, : inner_bias.shape[0]].reshape(-1).astype(f32)

    visible = (pad_mask[0] != 0).astype(f32)
    own_upstream = cotangent[0].astype(f32) * visible
    both = jnp.concatenate([tokens[0], own_upstream.astype(bf16)], -1)
    both = ring_gather(both, "ctx").reshape(length, 2 * width)
    all_tokens = both[:, :width]
    all_upstream = both[:, width:]

    input_rows = all_tokens.astype(f32)
    center = input_rows - jnp.mean(input_rows, -1, keepdims=True)
    scaling = lax.rsqrt(jnp.mean(center * center, -1, keepdims=True) + eps)
    whitened = center * scaling
    normed = (whitened * gain + shift).astype(bf16)

    owners = (me + jnp.arange(nc)) % nc
    positions = (owners[:, None] * own_rows + jnp.arange(own_rows)[None, :]).reshape(length)
    cos_table, sin_table = angles(positions)
    query_key_value = jnp.dot(normed, triple_here, preferred_element_type=f32)
    heads_shape = (length, heads_here, HEAD_DIM)
    queries = (
        rotate(query_key_value[:, :head_cols].reshape(heads_shape), cos_table, sin_table)
        * HEAD_DIM ** (-0.5)
    ).astype(bf16)
    key_rows = rotate(
        query_key_value[:, head_cols : 2 * head_cols].reshape(heads_shape), cos_table, sin_table
    ).astype(bf16)
    value_rows = query_key_value[:, 2 * head_cols :].reshape(heads_shape).astype(bf16)
    span = prefix_length[0]
    grad_mixture = jnp.dot(all_upstream, mixer_here.T, preferred_element_type=f32).astype(bf16)
    by_head = lambda values: values.reshape(heads_shape).swapaxes(0, 1)
    mixture, grad_queries, grad_keys, grad_values = fused_attention(
        span, by_head(queries), by_head(key_rows), by_head(value_rows), by_head(grad_mixture), positions
    )
    grad_queries, grad_keys, grad_values = (
        values.swapaxes(0, 1) for values in (grad_queries, grad_keys, grad_values)
    )
    mixture = mixture.swapaxes(0, 1).reshape(length, head_cols)
    attention = jnp.dot(mixture, mixer_here, preferred_element_type=f32)
    preact = jnp.dot(normed, inner_here, preferred_element_type=f32) + ibias_here
    gelu_result = jax.nn.gelu(preact, approximate=True).astype(bf16)
    feedforward = jnp.dot(gelu_result, outer_here, preferred_element_type=f32)
    block_sum = ring_scatter((attention + feedforward).reshape(nc, own_rows, width), "ctx")
    layer_output = (tokens[0].astype(f32) + block_sum + obias).astype(bf16)

    ones_block = jnp.ones((length, 16), bf16)
    row_lhs = jnp.concatenate([mixture, gelu_result, ones_block], -1)
    row_product = jnp.dot(row_lhs.T, all_upstream, preferred_element_type=f32).astype(bf16)
    grad_activated = jnp.dot(all_upstream, outer_here.T, preferred_element_type=f32)
    unused_value, gelu_pull = jax.vjp(partial(jax.nn.gelu, approximate=True), preact)
    grad_before_gelu = gelu_pull(grad_activated)[0].astype(bf16)
    grad_inner_weight = jnp.dot(normed.T, grad_before_gelu, preferred_element_type=f32)
    grad_inner_bias = jnp.sum(grad_before_gelu.astype(f32), 0)
    flat_shape = (length, head_cols)
    cos_full, sin_full = pair_tables(positions, 2 * head_cols)
    grad_turned = jnp.concatenate(
        [(grad_queries * HEAD_DIM ** (-0.5)).reshape(flat_shape), grad_keys.reshape(flat_shape)], -1
    )
    grad_turned = grad_turned * cos_full - swap_pairs(grad_turned) * sin_full
    grad_query_key_value = jnp.concatenate(
        [grad_turned, grad_values.reshape(flat_shape)], -1
    ).astype(bf16)
    grad_triple_weight = jnp.dot(normed.T, grad_query_key_value, preferred_element_type=f32)
    grad_normed = jnp.dot(grad_query_key_value, triple_here.T, preferred_element_type=f32)
    grad_normed = grad_normed + jnp.dot(grad_before_gelu, inner_here.T, preferred_element_type=f32)
    grad_norm_gain = jnp.sum(grad_normed * whitened, 0)
    grad_norm_shift = jnp.sum(grad_normed, 0)
    grad_normed = ring_scatter(grad_normed.reshape(nc, own_rows, width), "ctx")

    own_whitened = whitened[:own_rows]
    own_scaling = scaling[:own_rows]
    grad_white = grad_normed * gain
    grad_inputs = own_scaling * (
        grad_white
        - jnp.mean(grad_white, -1, keepdims=True)
        - own_whitened * jnp.mean(grad_white * own_whitened, -1, keepdims=True)
    )
    input_grad = (own_upstream + grad_inputs).astype(bf16)

    small_grads = jnp.stack([grad_norm_gain, grad_norm_shift], -1)
    small_grads = jnp.pad(small_grads, ((0, 0), (0, 128 - small_grads.shape[-1])))
    column_grads = jnp.concatenate(
        [grad_triple_weight, grad_inner_weight, small_grads], -1
    ).astype(bf16)
    column_grads = column_grads.reshape(nc, nf, shard_rows, -1).swapaxes(0, 1).reshape(width, -1)
    column_grads = lax.psum_scatter(column_grads, "fsdp", scatter_dimension=0, tiled=True)
    column_grads = replica_sum(column_grads, "rep").astype(bf16)
    column_grads = column_grads.reshape(nc, shard_rows, -1)
    column_grads = ring_all_to_all(column_grads, "ctx").astype(f32)
    grad_triple_out = (
        column_grads[:, :, : 3 * head_cols]
        .reshape(nc, shard_rows, 3, head_cols)
        .transpose(1, 2, 0, 3)
        .reshape(shard_rows, 3 * nc * head_cols)
    )
    grad_inner_out = (
        column_grads[:, :, 3 * head_cols : 3 * head_cols + ff_here]
        .transpose(1, 0, 2)
        .reshape(shard_rows, nc * ff_here)
    )
    grad_gain_out = jnp.sum(column_grads[:, :, 3 * head_cols + ff_here], 0)
    grad_shift_out = jnp.sum(column_grads[:, :, 3 * head_cols + ff_here + 1], 0)

    mixer_part = row_product[:head_cols].reshape(nf, shard_rows, width)
    outer_part = row_product[head_cols : head_cols + ff_here].reshape(nf, ff_rows, width)
    sums_part = jnp.broadcast_to(row_product[head_cols + ff_here :][None], (nf, 16, width))
    row_grads = jnp.concatenate([mixer_part, outer_part, sums_part], 1)
    row_grads = row_grads.at[:, ff_rows + shard_rows + 1, :ff_rows].set(
        grad_inner_bias.reshape(nf, ff_rows).astype(bf16)
    )
    row_grads = lax.psum_scatter(row_grads, "fsdp", scatter_dimension=0, tiled=True)
    row_grads = replica_sum(row_grads, "rep")[0]
    grad_mixer_out = row_grads[:shard_rows]
    grad_outer_out = row_grads[shard_rows : shard_rows + ff_rows]
    grad_ibias_out = row_grads[shard_rows + ff_rows + 1, :ff_rows]
    fsdp_me = lax.axis_index("fsdp")
    grad_obias_out = lax.dynamic_slice_in_dim(
        row_grads[shard_rows + ff_rows], (me * nf + fsdp_me) * shard_rows, shard_rows
    )

    return (
        layer_output[None],
        input_grad[None],
        grad_gain_out,
        grad_shift_out,
        grad_triple_out,
        grad_mixer_out,
        grad_inner_out,
        grad_ibias_out,
        grad_outer_out,
        grad_obias_out,
    )


def solution(mesh):
    placed = (
        P(("rep", "fsdp"), "ctx", None),
        P(("ctx", "fsdp")),
        P(("ctx", "fsdp")),
        P(("ctx", "fsdp"), None),
        P(("ctx", "fsdp"), None),
        P(("ctx", "fsdp"), None),
        P(("ctx", "fsdp")),
        P(("ctx", "fsdp"), None),
        P(("ctx", "fsdp")),
        P(("rep", "fsdp")),
        P(("rep", "fsdp")),
        P(("rep", "fsdp"), "ctx", None),
    )
    return jax.shard_map(
        local,
        mesh=mesh,
        in_specs=placed,
        out_specs=(
            P(("rep", "fsdp"), "ctx", None),
            P(("rep", "fsdp"), "ctx", None),
            P(("ctx", "fsdp")),
            P(("ctx", "fsdp")),
            P(("ctx", "fsdp"), None),
            P(("ctx", "fsdp"), None),
            P(("ctx", "fsdp"), None),
            P(("ctx", "fsdp")),
            P(("ctx", "fsdp"), None),
            P(("ctx", "fsdp")),
        ),
        check_vma=False,
    )
```

```python
from functools import partial

import jax
import jax.numpy as jnp
from jax import lax
from jax.experimental import pallas as pl
from jax.experimental.pallas import tpu as pltpu
from jax.sharding import PartitionSpec as P

HEADS = 16
HEAD_DIM = 64
ROT = 32


eps = 1e-05


def angles(positions):
    frequency = 10000.0 ** (-(jnp.arange(ROT // 2, dtype=jnp.float32) * 2.0) / ROT)
    phases = positions.astype(jnp.float32)[:, None] * frequency[None, :]
    return (jnp.cos(phases), jnp.sin(phases))


def rotate(field, cos_table, sin_table):
    leading = field.shape[:-1]
    paired = field[..., :ROT].reshape(leading + (ROT // 2, 2))
    even_part = paired[..., 0]
    odd_part = paired[..., 1]
    cos_wide = cos_table[:, None, :]
    sin_wide = sin_table[:, None, :]
    turned = jnp.stack(
        [even_part * cos_wide - odd_part * sin_wide, odd_part * cos_wide + even_part * sin_wide], -1
    )
    return jnp.concatenate([turned.reshape(leading + (ROT,)), field[..., ROT:]], -1)


def pair_tables(positions, width):
    f32 = jnp.float32
    highest = lax.Precision.HIGHEST
    cos_table, sin_table = angles(positions)
    feature = jnp.arange(width) % HEAD_DIM
    pick = (feature[None, :] // 2 == jnp.arange(ROT // 2)[:, None]) & (feature[None, :] < ROT)
    pick = pick.astype(f32)
    sign = jnp.where(feature % 2 == 0, -1.0, 1.0).astype(f32)
    cos_full = jnp.dot(cos_table, pick, precision=highest) + (feature >= ROT).astype(f32)
    sin_full = jnp.dot(sin_table, pick, precision=highest) * sign
    return cos_full, sin_full


def swap_pairs(values):
    width = values.shape[-1]
    index = jnp.arange(width)
    swap = (index[:, None] == (index[None, :] ^ 1)).astype(jnp.float32)
    return jnp.dot(values, swap, precision=lax.Precision.HIGHEST)


def ring_pairs(n, step):
    return [(i, (i + step) % n) for i in range(n)]


def ring_gather(block, axis):
    n = lax.axis_size(axis)
    half = block.shape[0] // 2
    from_left = lax.ppermute(block, axis, ring_pairs(n, 1))
    from_right = lax.ppermute(block, axis, ring_pairs(n, -1))
    far_first = lax.ppermute(from_left[:half], axis, ring_pairs(n, 1))
    far_second = lax.ppermute(from_right[half:], axis, ring_pairs(n, -1))
    far = jnp.concatenate([far_first, far_second], 0)
    return jnp.stack([block, from_right, far, from_left])


def ring_scatter(parts, axis):
    n = lax.axis_size(axis)
    half = parts.shape[1] // 2
    wire = jnp.bfloat16
    got_left = lax.ppermute(parts[2, :half].astype(wire), axis, ring_pairs(n, 1))
    got_right = lax.ppermute(parts[2, half:].astype(wire), axis, ring_pairs(n, -1))
    to_right = jnp.concatenate([parts[1, :half] + got_left.astype(jnp.float32), parts[1, half:]], 0)
    to_left = jnp.concatenate([parts[3, :half], parts[3, half:] + got_right.astype(jnp.float32)], 0)
    from_left = lax.ppermute(to_right.astype(wire), axis, ring_pairs(n, 1))
    from_right = lax.ppermute(to_left.astype(wire), axis, ring_pairs(n, -1))
    return parts[0] + from_left.astype(jnp.float32) + from_right.astype(jnp.float32)


def ring_all_to_all(payload, axis):
    n = lax.axis_size(axis)
    me = lax.axis_index(axis)
    pick = lambda d: lax.dynamic_index_in_dim(payload, d % n, 0, keepdims=False)
    got = [pick(me)] + [
        lax.ppermute(pick(me + s), axis, ring_pairs(n, s)) for s in range(1, n)
    ]
    mirrored = jnp.stack([got[(-k) % n] for k in range(n)])
    doubled = jnp.concatenate([mirrored, mirrored], 0)
    return lax.dynamic_slice_in_dim(doubled, n - me, n, 0)


def replica_sum(values, axis):
    n = lax.axis_size(axis)
    f32, wire = jnp.float32, jnp.bfloat16
    values = values.astype(wire)
    if n != 4:
        return lax.psum(values, axis).astype(f32)
    pair = values.astype(f32) + lax.ppermute(values, axis, [(i, i ^ 1) for i in range(n)]).astype(f32)
    pair = pair.astype(wire)
    return pair.astype(f32) + lax.ppermute(pair, axis, [(i, i ^ 2) for i in range(n)]).astype(f32)


def attention_kernel(span_ref, q_ref, k_ref, v_ref, gm_ref, qpos_ref, kpos_ref,
                     mix_ref, gq_ref, gk_ref, gv_ref, bias_ref):
    f32, bf16 = jnp.float32, jnp.bfloat16
    block = pl.program_id(0)
    head = pl.program_id(1)

    @pl.when(head == 0)
    def _():
        allowed = (kpos_ref[...] <= qpos_ref[...]) | (kpos_ref[...] < span_ref[0])
        bias_ref[...] = jnp.where(allowed, 0.0, -1e30).astype(f32)

    q = q_ref[...]
    k = k_ref[...]
    v = v_ref[...]
    gm = gm_ref[...]
    scores = lax.dot_general(q, k, (((1,), (1,)), ((), ())), preferred_element_type=f32)
    scores = scores + bias_ref[...]
    peak = jnp.max(scores, axis=1, keepdims=True)
    exps = jnp.exp(scores - peak)
    total = jnp.sum(exps, axis=1, keepdims=True)
    probs = exps * (1.0 / total)
    low_probs = probs.astype(bf16)
    mix_ref[...] = jnp.dot(low_probs, v, preferred_element_type=f32).astype(mix_ref.dtype)
    grad_probs = lax.dot_general(gm, v, (((1,), (1,)), ((), ())), preferred_element_type=f32)
    inner = jnp.sum(probs * grad_probs, axis=1, keepdims=True)
    grad_scores = (probs * (grad_probs - inner)).astype(bf16)
    gq_ref[...] = jnp.dot(grad_scores, k, preferred_element_type=f32)
    gk_part = lax.dot_general(grad_scores, q, (((0,), (0,)), ((), ())), preferred_element_type=f32)
    gv_part = lax.dot_general(low_probs, gm, (((0,), (0,)), ((), ())), preferred_element_type=f32)

    @pl.when(block == 0)
    def _():
        gk_ref[head] = gk_part
        gv_ref[head] = gv_part

    @pl.when(block != 0)
    def _():
        gk_ref[head] += gk_part
        gv_ref[head] += gv_part


def fused_attention(span, queries, keys, values, grad_mixture, positions, rows=256):
    heads, length, dim = queries.shape
    blocks = length // rows
    qpos = positions.reshape(length, 1).astype(jnp.int32)
    kpos = positions.reshape(1, length).astype(jnp.int32)
    row_block = pl.BlockSpec((None, rows, dim), lambda b, h, s: (h, b, 0))
    whole_head = pl.BlockSpec((None, length, dim), lambda b, h, s: (h, 0, 0))
    resident = pl.BlockSpec((heads, length, dim), lambda b, h, s: (0, 0, 0))
    f32 = jnp.float32
    return pl.pallas_call(
        attention_kernel,
        out_shape=(
            jax.ShapeDtypeStruct((heads, length, dim), jnp.bfloat16),
            jax.ShapeDtypeStruct((heads, length, dim), f32),
            jax.ShapeDtypeStruct((heads, length, dim), f32),
            jax.ShapeDtypeStruct((heads, length, dim), f32),
        ),
        grid_spec=pltpu.PrefetchScalarGridSpec(
            num_scalar_prefetch=1,
            grid=(blocks, heads),
            in_specs=[
                row_block, whole_head, whole_head, row_block,
                pl.BlockSpec((rows, 1), lambda b, h, s: (b, 0)),
                pl.BlockSpec((1, length), lambda b, h, s: (0, 0)),
            ],
            out_specs=[row_block, row_block, resident, resident],
            scratch_shapes=[pltpu.VMEM((rows, length), f32)],
        ),
        compiler_params=pltpu.CompilerParams(dimension_semantics=("arbitrary", "arbitrary")),
        cost_estimate=pl.CostEstimate(
            flops=12 * heads * length * length * dim,
            transcendentals=heads * length * length,
            bytes_accessed=heads * length * dim * (4 * 2 + 3 * 4 + 2),
        ),
    )(span.reshape(1).astype(jnp.int32), queries, keys, values, grad_mixture, qpos, kpos)


def local(
    tokens,
    norm_gain,
    norm_shift,
    triple_weight,
    mixer_weight,
    inner_weight,
    inner_bias,
    outer_weight,
    outer_bias,
    prefix_length,
    pad_mask,
    cotangent,
):
    nc = lax.axis_size("ctx")
    nf = lax.axis_size("fsdp")
    me = lax.axis_index("ctx")
    _, own_rows, width = tokens.shape
    length = own_rows * nc
    shard_rows = triple_weight.shape[0]
    heads_here = HEADS // nc
    head_cols = heads_here * HEAD_DIM
    ff_here = inner_weight.shape[1] // nc
    ff_rows = outer_weight.shape[0]
    f32, bf16 = jnp.float32, jnp.bfloat16

    triple_cols = (
        triple_weight.reshape(shard_rows, 3, nc, head_cols)
        .transpose(2, 0, 1, 3)
        .reshape(nc, shard_rows, 3 * head_cols)
    )
    inner_cols = inner_weight.reshape(shard_rows, nc, ff_here).transpose(1, 0, 2)
    small = jnp.stack([norm_gain, norm_shift, outer_bias], -1)
    small = jnp.pad(small, ((0, 0), (0, 128 - small.shape[-1])))
    small = jnp.broadcast_to(small[None], (nc,) + small.shape)
    column_payload = jnp.concatenate([triple_cols, inner_cols, small], -1)
    column_payload = ring_all_to_all(column_payload, "ctx")
    column_block = lax.all_gather(column_payload, "fsdp", axis=0, tiled=False)
    column_block = column_block.swapaxes(0, 1).reshape(nc * nf * shard_rows, -1)
    triple_here = column_block[:, : 3 * head_cols]
    inner_here = column_block[:, 3 * head_cols : 3 * head_cols + ff_here]
    gain = column_block[:, 3 * head_cols + ff_here].astype(f32)
    shift = column_block[:, 3 * head_cols + ff_here + 1].astype(f32)
    obias = column_block[:, 3 * head_cols + ff_here + 2].astype(f32)

    bias_rows = jnp.pad(inner_bias[None], ((0, 15), (0, width - inner_bias.shape[0])))
    row_payload = jnp.concatenate([mixer_weight, outer_weight, bias_rows], 0)
    row_block = lax.all_gather(row_payload, "fsdp", axis=0, tiled=False)
    mixer_here = row_block[:, :shard_rows].reshape(nf * shard_rows, width)
    outer_here = row_block[:, shard_rows : shard_rows + ff_rows].reshape(nf * ff_rows, width)
    ibias_here = row_block[:, shard_rows + ff_rows, : inner_bias.shape[0]].reshape(-1).astype(f32)

    visible = (pad_mask[0] != 0).astype(f32)
    own_upstream = cotangent[0].astype(f32) * visible
    both = jnp.concatenate([tokens[0], own_upstream.astype(bf16)], -1)
    both = ring_gather(both, "ctx").reshape(length, 2 * width)
    all_tokens = both[:, :width]
    all_upstream = both[:, width:]

    input_rows = all_tokens.astype(f32)
    center = input_rows - jnp.mean(input_rows, -1, keepdims=True)
    scaling = lax.rsqrt(jnp.mean(center * center, -1, keepdims=True) + eps)
    whitened = center * scaling
    normed = (whitened * gain + shift).astype(bf16)

    owners = (me + jnp.arange(nc)) % nc
    positions = (owners[:, None] * own_rows + jnp.arange(own_rows)[None, :]).reshape(length)
    cos_table, sin_table = angles(positions)
    query_key_value = jnp.dot(normed, triple_here, preferred_element_type=f32)
    heads_shape = (length, heads_here, HEAD_DIM)
    queries = (
        rotate(query_key_value[:, :head_cols].reshape(heads_shape), cos_table, sin_table)
        * HEAD_DIM ** (-0.5)
    ).astype(bf16)
    key_rows = rotate(
        query_key_value[:, head_cols : 2 * head_cols].reshape(heads_shape), cos_table, sin_table
    ).astype(bf16)
    value_rows = query_key_value[:, 2 * head_cols :].reshape(heads_shape).astype(bf16)
    span = prefix_length[0]
    grad_mixture = jnp.dot(all_upstream, mixer_here.T, preferred_element_type=f32).astype(bf16)
    by_head = lambda values: values.reshape(heads_shape).swapaxes(0, 1)
    mixture, grad_queries, grad_keys, grad_values = fused_attention(
        span, by_head(queries), by_head(key_rows), by_head(value_rows), by_head(grad_mixture), positions
    )
    grad_queries, grad_keys, grad_values = (
        values.swapaxes(0, 1) for values in (grad_queries, grad_keys, grad_values)
    )
    mixture = mixture.swapaxes(0, 1).reshape(length, head_cols)
    attention = jnp.dot(mixture, mixer_here, preferred_element_type=f32)
    preact = jnp.dot(normed, inner_here, preferred_element_type=f32) + ibias_here
    gelu_result = jax.nn.gelu(preact, approximate=True).astype(bf16)
    feedforward = jnp.dot(gelu_result, outer_here, preferred_element_type=f32)
    block_sum = ring_scatter((attention + feedforward).reshape(nc, own_rows, width), "ctx")
    layer_output = (tokens[0].astype(f32) + block_sum + obias).astype(bf16)

    ones_block = jnp.ones((length, 16), bf16)
    row_lhs = jnp.concatenate([mixture, gelu_result, ones_block], -1)
    row_product = jnp.dot(row_lhs.T, all_upstream, preferred_element_type=f32).astype(bf16)
    grad_activated = jnp.dot(all_upstream, outer_here.T, preferred_element_type=f32)
    unused_value, gelu_pull = jax.vjp(partial(jax.nn.gelu, approximate=True), preact)
    grad_before_gelu = gelu_pull(grad_activated)[0].astype(bf16)
    grad_inner_weight = jnp.dot(normed.T, grad_before_gelu, preferred_element_type=f32)
    grad_inner_bias = jnp.sum(grad_before_gelu.astype(f32), 0)
    flat_shape = (length, head_cols)
    cos_full, sin_full = pair_tables(positions, 2 * head_cols)
    grad_turned = jnp.concatenate(
        [(grad_queries * HEAD_DIM ** (-0.5)).reshape(flat_shape), grad_keys.reshape(flat_shape)], -1
    )
    grad_turned = grad_turned * cos_full - swap_pairs(grad_turned) * sin_full
    grad_query_key_value = jnp.concatenate(
        [grad_turned, grad_values.reshape(flat_shape)], -1
    ).astype(bf16)
    grad_triple_weight = jnp.dot(normed.T, grad_query_key_value, preferred_element_type=f32)
    grad_normed = jnp.dot(grad_query_key_value, triple_here.T, preferred_element_type=f32)
    grad_normed = grad_normed + jnp.dot(grad_before_gelu, inner_here.T, preferred_element_type=f32)
    grad_norm_gain = jnp.sum(grad_normed * whitened, 0)
    grad_norm_shift = jnp.sum(grad_normed, 0)
    grad_normed = ring_scatter(grad_normed.reshape(nc, own_rows, width), "ctx")

    own_whitened = whitened[:own_rows]
    own_scaling = scaling[:own_rows]
    grad_white = grad_normed * gain
    grad_inputs = own_scaling * (
        grad_white
        - jnp.mean(grad_white, -1, keepdims=True)
        - own_whitened * jnp.mean(grad_white * own_whitened, -1, keepdims=True)
    )
    input_grad = (own_upstream + grad_inputs).astype(bf16)

    small_grads = jnp.stack([grad_norm_gain, grad_norm_shift], -1)
    small_grads = jnp.pad(small_grads, ((0, 0), (0, 128 - small_grads.shape[-1])))
    column_grads = jnp.concatenate(
        [grad_triple_weight, grad_inner_weight, small_grads], -1
    ).astype(bf16)
    grad_cols = column_grads.shape[-1]
    column_grads = ring_all_to_all(column_grads.reshape(nc, nf * shard_rows, grad_cols), "ctx")
    column_grads = column_grads.swapaxes(0, 1).reshape(nf * shard_rows, nc * grad_cols)
    column_grads = lax.psum_scatter(column_grads, "fsdp", scatter_dimension=0, tiled=True)
    column_grads = replica_sum(column_grads, "rep").astype(bf16).astype(f32)
    column_grads = column_grads.reshape(shard_rows, nc, grad_cols).swapaxes(0, 1)
    grad_triple_out = (
        column_grads[:, :, : 3 * head_cols]
        .reshape(nc, shard_rows, 3, head_cols)
        .transpose(1, 2, 0, 3)
        .reshape(shard_rows, 3 * nc * head_cols)
    )
    grad_inner_out = (
        column_grads[:, :, 3 * head_cols : 3 * head_cols + ff_here]
        .transpose(1, 0, 2)
        .reshape(shard_rows, nc * ff_here)
    )
    grad_gain_out = jnp.sum(column_grads[:, :, 3 * head_cols + ff_here], 0)
    grad_shift_out = jnp.sum(column_grads[:, :, 3 * head_cols + ff_here + 1], 0)

    mixer_part = row_product[:head_cols].reshape(nf, shard_rows, width)
    outer_part = row_product[head_cols : head_cols + ff_here].reshape(nf, ff_rows, width)
    sums_part = jnp.broadcast_to(row_product[head_cols + ff_here :][None], (nf, 16, width))
    row_grads = jnp.concatenate([mixer_part, outer_part, sums_part], 1)
    row_grads = row_grads.at[:, ff_rows + shard_rows + 1, :ff_rows].set(
        grad_inner_bias.reshape(nf, ff_rows).astype(bf16)
    )
    row_grads = lax.psum_scatter(row_grads, "fsdp", scatter_dimension=0, tiled=True)
    row_grads = replica_sum(row_grads, "rep")[0]
    grad_mixer_out = row_grads[:shard_rows]
    grad_outer_out = row_grads[shard_rows : shard_rows + ff_rows]
    grad_ibias_out = row_grads[shard_rows + ff_rows + 1, :ff_rows]
    fsdp_me = lax.axis_index("fsdp")
    grad_obias_out = lax.dynamic_slice_in_dim(
        row_grads[shard_rows + ff_rows], (me * nf + fsdp_me) * shard_rows, shard_rows
    )

    return (
        layer_output[None],
        input_grad[None],
        grad_gain_out,
        grad_shift_out,
        grad_triple_out,
        grad_mixer_out,
        grad_inner_out,
        grad_ibias_out,
        grad_outer_out,
        grad_obias_out,
    )


def solution(mesh):
    placed = (
        P(("rep", "fsdp"), "ctx", None),
        P(("ctx", "fsdp")),
        P(("ctx", "fsdp")),
        P(("ctx", "fsdp"), None),
        P(("ctx", "fsdp"), None),
        P(("ctx", "fsdp"), None),
        P(("ctx", "fsdp")),
        P(("ctx", "fsdp"), None),
        P(("ctx", "fsdp")),
        P(("rep", "fsdp")),
        P(("rep", "fsdp")),
        P(("rep", "fsdp"), "ctx", None),
    )
    return jax.shard_map(
        local,
        mesh=mesh,
        in_specs=placed,
        out_specs=(
            P(("rep", "fsdp"), "ctx", None),
            P(("rep", "fsdp"), "ctx", None),
            P(("ctx", "fsdp")),
            P(("ctx", "fsdp")),
            P(("ctx", "fsdp"), None),
            P(("ctx", "fsdp"), None),
            P(("ctx", "fsdp"), None),
            P(("ctx", "fsdp")),
            P(("ctx", "fsdp"), None),
            P(("ctx", "fsdp")),
        ),
        check_vma=False,
    )
```

```python
from functools import partial

import jax
import jax.numpy as jnp
from jax import lax
from jax.experimental import pallas as pl
from jax.experimental.pallas import tpu as pltpu
from jax.sharding import PartitionSpec as P

HEADS = 16
HEAD_DIM = 64
ROT = 32


eps = 1e-05


def angles(positions):
    frequency = 10000.0 ** (-(jnp.arange(ROT // 2, dtype=jnp.float32) * 2.0) / ROT)
    phases = positions.astype(jnp.float32)[:, None] * frequency[None, :]
    return (jnp.cos(phases), jnp.sin(phases))


def rotate(field, cos_table, sin_table):
    leading = field.shape[:-1]
    paired = field[..., :ROT].reshape(leading + (ROT // 2, 2))
    even_part = paired[..., 0]
    odd_part = paired[..., 1]
    cos_wide = cos_table[:, None, :]
    sin_wide = sin_table[:, None, :]
    turned = jnp.stack(
        [even_part * cos_wide - odd_part * sin_wide, odd_part * cos_wide + even_part * sin_wide], -1
    )
    return jnp.concatenate([turned.reshape(leading + (ROT,)), field[..., ROT:]], -1)


def pair_tables(positions, width):
    f32 = jnp.float32
    highest = lax.Precision.HIGHEST
    cos_table, sin_table = angles(positions)
    feature = jnp.arange(width) % HEAD_DIM
    pick = (feature[None, :] // 2 == jnp.arange(ROT // 2)[:, None]) & (feature[None, :] < ROT)
    pick = pick.astype(f32)
    sign = jnp.where(feature % 2 == 0, -1.0, 1.0).astype(f32)
    cos_full = jnp.dot(cos_table, pick, precision=highest) + (feature >= ROT).astype(f32)
    sin_full = jnp.dot(sin_table, pick, precision=highest) * sign
    return cos_full, sin_full


def swap_pairs(values):
    width = values.shape[-1]
    index = jnp.arange(width)
    swap = (index[:, None] == (index[None, :] ^ 1)).astype(jnp.float32)
    return jnp.dot(values, swap, precision=lax.Precision.HIGHEST)


def ring_pairs(n, step):
    return [(i, (i + step) % n) for i in range(n)]


def ring_gather(block, axis):
    n = lax.axis_size(axis)
    half = block.shape[0] // 2
    from_left = lax.ppermute(block, axis, ring_pairs(n, 1))
    from_right = lax.ppermute(block, axis, ring_pairs(n, -1))
    far_first = lax.ppermute(from_left[:half], axis, ring_pairs(n, 1))
    far_second = lax.ppermute(from_right[half:], axis, ring_pairs(n, -1))
    far = jnp.concatenate([far_first, far_second], 0)
    return jnp.stack([block, from_right, far, from_left])


def ring_scatter(parts, axis):
    n = lax.axis_size(axis)
    half = parts.shape[1] // 2
    wire = jnp.bfloat16
    got_left = lax.ppermute(parts[2, :half].astype(wire), axis, ring_pairs(n, 1))
    got_right = lax.ppermute(parts[2, half:].astype(wire), axis, ring_pairs(n, -1))
    to_right = jnp.concatenate([parts[1, :half] + got_left.astype(jnp.float32), parts[1, half:]], 0)
    to_left = jnp.concatenate([parts[3, :half], parts[3, half:] + got_right.astype(jnp.float32)], 0)
    from_left = lax.ppermute(to_right.astype(wire), axis, ring_pairs(n, 1))
    from_right = lax.ppermute(to_left.astype(wire), axis, ring_pairs(n, -1))
    return parts[0] + from_left.astype(jnp.float32) + from_right.astype(jnp.float32)


def ring_all_to_all(payload, axis):
    n = lax.axis_size(axis)
    me = lax.axis_index(axis)
    pick = lambda d: lax.dynamic_index_in_dim(payload, d % n, 0, keepdims=False)
    got = [pick(me)] + [
        lax.ppermute(pick(me + s), axis, ring_pairs(n, s)) for s in range(1, n)
    ]
    mirrored = jnp.stack([got[(-k) % n] for k in range(n)])
    doubled = jnp.concatenate([mirrored, mirrored], 0)
    return lax.dynamic_slice_in_dim(doubled, n - me, n, 0)


def replica_sum(values, axis):
    n = lax.axis_size(axis)
    f32, wire = jnp.float32, jnp.bfloat16
    values = values.astype(wire)
    if n != 4:
        return lax.psum(values, axis).astype(f32)
    pair = values.astype(f32) + lax.ppermute(values, axis, [(i, i ^ 1) for i in range(n)]).astype(f32)
    pair = pair.astype(wire)
    return pair.astype(f32) + lax.ppermute(pair, axis, [(i, i ^ 2) for i in range(n)]).astype(f32)


def attention_kernel(span_ref, q_ref, k_ref, v_ref, gm_ref, qpos_ref, kpos_ref,
                     mix_ref, gq_ref, gk_ref, gv_ref, bias_ref):
    f32, bf16 = jnp.float32, jnp.bfloat16
    block = pl.program_id(0)
    head = pl.program_id(1)

    @pl.when(head == 0)
    def _():
        allowed = (kpos_ref[...] <= qpos_ref[...]) | (kpos_ref[...] < span_ref[0])
        bias_ref[...] = jnp.where(allowed, 0.0, -1e30).astype(f32)

    q = q_ref[...]
    k = k_ref[...]
    v = v_ref[...]
    gm = gm_ref[...]
    scores = lax.dot_general(q, k, (((1,), (1,)), ((), ())), preferred_element_type=f32)
    scores = scores + bias_ref[...]
    peak = jnp.max(scores, axis=1, keepdims=True)
    exps = jnp.exp(scores - peak)
    total = jnp.sum(exps, axis=1, keepdims=True)
    probs = exps * (1.0 / total)
    low_probs = probs.astype(bf16)
    mix_ref[...] = jnp.dot(low_probs, v, preferred_element_type=f32).astype(mix_ref.dtype)
    grad_probs = lax.dot_general(gm, v, (((1,), (1,)), ((), ())), preferred_element_type=f32)
    inner = jnp.sum(probs * grad_probs, axis=1, keepdims=True)
    grad_scores = (probs * (grad_probs - inner)).astype(bf16)
    gq_ref[...] = jnp.dot(grad_scores, k, preferred_element_type=f32)
    gk_part = lax.dot_general(grad_scores, q, (((0,), (0,)), ((), ())), preferred_element_type=f32)
    gv_part = lax.dot_general(low_probs, gm, (((0,), (0,)), ((), ())), preferred_element_type=f32)

    @pl.when(block == 0)
    def _():
        gk_ref[head] = gk_part
        gv_ref[head] = gv_part

    @pl.when(block != 0)
    def _():
        gk_ref[head] += gk_part
        gv_ref[head] += gv_part


def fused_attention(span, queries, keys, values, grad_mixture, positions, rows=256):
    heads, length, dim = queries.shape
    blocks = length // rows
    qpos = positions.reshape(length, 1).astype(jnp.int32)
    kpos = positions.reshape(1, length).astype(jnp.int32)
    row_block = pl.BlockSpec((None, rows, dim), lambda b, h, s: (h, b, 0))
    whole_head = pl.BlockSpec((None, length, dim), lambda b, h, s: (h, 0, 0))
    resident = pl.BlockSpec((heads, length, dim), lambda b, h, s: (0, 0, 0))
    f32 = jnp.float32
    return pl.pallas_call(
        attention_kernel,
        out_shape=(
            jax.ShapeDtypeStruct((heads, length, dim), jnp.bfloat16),
            jax.ShapeDtypeStruct((heads, length, dim), f32),
            jax.ShapeDtypeStruct((heads, length, dim), f32),
            jax.ShapeDtypeStruct((heads, length, dim), f32),
        ),
        grid_spec=pltpu.PrefetchScalarGridSpec(
            num_scalar_prefetch=1,
            grid=(blocks, heads),
            in_specs=[
                row_block, whole_head, whole_head, row_block,
                pl.BlockSpec((rows, 1), lambda b, h, s: (b, 0)),
                pl.BlockSpec((1, length), lambda b, h, s: (0, 0)),
            ],
            out_specs=[row_block, row_block, resident, resident],
            scratch_shapes=[pltpu.VMEM((rows, length), f32)],
        ),
        compiler_params=pltpu.CompilerParams(dimension_semantics=("arbitrary", "arbitrary")),
        cost_estimate=pl.CostEstimate(
            flops=12 * heads * length * length * dim,
            transcendentals=heads * length * length,
            bytes_accessed=heads * length * dim * (4 * 2 + 3 * 4 + 2),
        ),
    )(span.reshape(1).astype(jnp.int32), queries, keys, values, grad_mixture, qpos, kpos)


def local(
    tokens,
    norm_gain,
    norm_shift,
    triple_weight,
    mixer_weight,
    inner_weight,
    inner_bias,
    outer_weight,
    outer_bias,
    prefix_length,
    pad_mask,
    cotangent,
):
    nc = lax.axis_size("ctx")
    nf = lax.axis_size("fsdp")
    me = lax.axis_index("ctx")
    _, own_rows, width = tokens.shape
    length = own_rows * nc
    shard_rows = triple_weight.shape[0]
    heads_here = HEADS // nc
    head_cols = heads_here * HEAD_DIM
    ff_here = inner_weight.shape[1] // nc
    ff_rows = outer_weight.shape[0]
    f32, bf16 = jnp.float32, jnp.bfloat16

    triple_cols = (
        triple_weight.reshape(shard_rows, 3, nc, head_cols)
        .transpose(2, 0, 1, 3)
        .reshape(nc, shard_rows, 3 * head_cols)
    )
    inner_cols = inner_weight.reshape(shard_rows, nc, ff_here).transpose(1, 0, 2)
    small = jnp.stack([norm_gain, norm_shift, outer_bias], -1)
    small = jnp.pad(small, ((0, 0), (0, 128 - small.shape[-1])))
    small = jnp.broadcast_to(small[None], (nc,) + small.shape)
    column_payload = jnp.concatenate([triple_cols, inner_cols, small], -1)
    column_payload = ring_all_to_all(column_payload, "ctx")
    split = 3 * head_cols

    bias_rows = jnp.pad(inner_bias[None], ((0, 15), (0, width - inner_bias.shape[0])))
    triple_payload = jnp.concatenate([column_payload[..., :split], column_payload[..., split + ff_here :]], -1)
    pieces = (triple_payload, mixer_weight, bias_rows)
    first_payload = jnp.concatenate([piece.reshape(-1) for piece in pieces]).reshape(-1, width)
    first_block = lax.all_gather(first_payload, "fsdp", axis=0, tiled=False).reshape(nf, -1)
    sizes = [piece.size for piece in pieces]
    triple_block = first_block[:, : sizes[0]].reshape((nf,) + triple_payload.shape)
    triple_block = triple_block.swapaxes(0, 1).reshape(nc * nf * shard_rows, -1)
    mixer_here = first_block[:, sizes[0] : sizes[0] + sizes[1]].reshape(nf * shard_rows, width)
    ibias_here = (
        first_block[:, sizes[0] + sizes[1] : sizes[0] + sizes[1] + inner_bias.shape[0]].reshape(-1).astype(f32)
    )

    ff_payload = jnp.concatenate(
        [column_payload[..., split : split + ff_here].reshape(nc * shard_rows, ff_here), outer_weight], 0
    )
    ff_payload, triple_block = lax.optimization_barrier((ff_payload, triple_block))
    ff_block = lax.all_gather(ff_payload, "fsdp", axis=0, tiled=False)
    inner_here = (
        ff_block[:, : nc * shard_rows]
        .reshape(nf, nc, shard_rows, ff_here)
        .swapaxes(0, 1)
        .reshape(nc * nf * shard_rows, ff_here)
    )
    outer_here = ff_block[:, nc * shard_rows :].reshape(nf * ff_rows, width)

    triple_here = triple_block[:, :split]
    gain = triple_block[:, split].astype(f32)
    shift = triple_block[:, split + 1].astype(f32)
    obias = triple_block[:, split + 2].astype(f32)

    visible = (pad_mask[0] != 0).astype(f32)
    own_upstream = cotangent[0].astype(f32) * visible
    both = jnp.concatenate([tokens[0], own_upstream.astype(bf16)], -1)
    both = ring_gather(both, "ctx").reshape(length, 2 * width)
    all_tokens = both[:, :width]
    all_upstream = both[:, width:]

    input_rows = all_tokens.astype(f32)
    center = input_rows - jnp.mean(input_rows, -1, keepdims=True)
    scaling = lax.rsqrt(jnp.mean(center * center, -1, keepdims=True) + eps)
    whitened = center * scaling
    normed = (whitened * gain + shift).astype(bf16)

    owners = (me + jnp.arange(nc)) % nc
    positions = (owners[:, None] * own_rows + jnp.arange(own_rows)[None, :]).reshape(length)
    cos_table, sin_table = angles(positions)
    query_key_value = jnp.dot(normed, triple_here, preferred_element_type=f32)
    heads_shape = (length, heads_here, HEAD_DIM)
    queries = (
        rotate(query_key_value[:, :head_cols].reshape(heads_shape), cos_table, sin_table)
        * HEAD_DIM ** (-0.5)
    ).astype(bf16)
    key_rows = rotate(
        query_key_value[:, head_cols : 2 * head_cols].reshape(heads_shape), cos_table, sin_table
    ).astype(bf16)
    value_rows = query_key_value[:, 2 * head_cols :].reshape(heads_shape).astype(bf16)
    span = prefix_length[0]
    grad_mixture = jnp.dot(all_upstream, mixer_here.T, preferred_element_type=f32).astype(bf16)
    by_head = lambda values: values.reshape(heads_shape).swapaxes(0, 1)
    mixture, grad_queries, grad_keys, grad_values = fused_attention(
        span, by_head(queries), by_head(key_rows), by_head(value_rows), by_head(grad_mixture), positions
    )
    grad_queries, grad_keys, grad_values = (
        values.swapaxes(0, 1) for values in (grad_queries, grad_keys, grad_values)
    )
    mixture = mixture.swapaxes(0, 1).reshape(length, head_cols)
    attention = jnp.dot(mixture, mixer_here, preferred_element_type=f32)
    preact = jnp.dot(normed, inner_here, preferred_element_type=f32) + ibias_here
    gelu_result = jax.nn.gelu(preact, approximate=True).astype(bf16)
    feedforward = jnp.dot(gelu_result, outer_here, preferred_element_type=f32)
    block_sum = ring_scatter((attention + feedforward).reshape(nc, own_rows, width), "ctx")
    layer_output = (tokens[0].astype(f32) + block_sum + obias).astype(bf16)

    ones_block = jnp.ones((length, 16), bf16)
    row_lhs = jnp.concatenate([mixture, gelu_result, ones_block], -1)
    row_product = jnp.dot(row_lhs.T, all_upstream, preferred_element_type=f32).astype(bf16)
    grad_activated = jnp.dot(all_upstream, outer_here.T, preferred_element_type=f32)
    unused_value, gelu_pull = jax.vjp(partial(jax.nn.gelu, approximate=True), preact)
    grad_before_gelu = gelu_pull(grad_activated)[0].astype(bf16)
    grad_inner_weight = jnp.dot(normed.T, grad_before_gelu, preferred_element_type=f32)
    grad_inner_bias = jnp.sum(grad_before_gelu.astype(f32), 0)
    flat_shape = (length, head_cols)
    cos_full, sin_full = pair_tables(positions, 2 * head_cols)
    grad_turned = jnp.concatenate(
        [(grad_queries * HEAD_DIM ** (-0.5)).reshape(flat_shape), grad_keys.reshape(flat_shape)], -1
    )
    grad_turned = grad_turned * cos_full - swap_pairs(grad_turned) * sin_full
    grad_query_key_value = jnp.concatenate(
        [grad_turned, grad_values.reshape(flat_shape)], -1
    ).astype(bf16)
    grad_triple_weight = jnp.dot(normed.T, grad_query_key_value, preferred_element_type=f32)
    grad_normed = jnp.dot(grad_query_key_value, triple_here.T, preferred_element_type=f32)
    grad_normed = grad_normed + jnp.dot(grad_before_gelu, inner_here.T, preferred_element_type=f32)
    grad_norm_gain = jnp.sum(grad_normed * whitened, 0)
    grad_norm_shift = jnp.sum(grad_normed, 0)
    grad_normed = ring_scatter(grad_normed.reshape(nc, own_rows, width), "ctx")

    own_whitened = whitened[:own_rows]
    own_scaling = scaling[:own_rows]
    grad_white = grad_normed * gain
    grad_inputs = own_scaling * (
        grad_white
        - jnp.mean(grad_white, -1, keepdims=True)
        - own_whitened * jnp.mean(grad_white * own_whitened, -1, keepdims=True)
    )
    input_grad = (own_upstream + grad_inputs).astype(bf16)

    small_grads = jnp.stack([grad_norm_gain, grad_norm_shift], -1)
    small_grads = jnp.pad(small_grads, ((0, 0), (0, 128 - small_grads.shape[-1])))
    column_grads = jnp.concatenate(
        [grad_triple_weight, grad_inner_weight, small_grads], -1
    ).astype(bf16)
    column_grads = column_grads.reshape(nc, nf, shard_rows, -1).swapaxes(0, 1).reshape(width, -1)
    column_grads = lax.psum_scatter(column_grads, "fsdp", scatter_dimension=0, tiled=True)
    column_grads = replica_sum(column_grads, "rep").astype(bf16)
    column_grads = column_grads.reshape(nc, shard_rows, -1)
    column_grads = ring_all_to_all(column_grads, "ctx").astype(f32)
    grad_triple_out = (
        column_grads[:, :, : 3 * head_cols]
        .reshape(nc, shard_rows, 3, head_cols)
        .transpose(1, 2, 0, 3)
        .reshape(shard_rows, 3 * nc * head_cols)
    )
    grad_inner_out = (
        column_grads[:, :, 3 * head_cols : 3 * head_cols + ff_here]
        .transpose(1, 0, 2)
        .reshape(shard_rows, nc * ff_here)
    )
    grad_gain_out = jnp.sum(column_grads[:, :, 3 * head_cols + ff_here], 0)
    grad_shift_out = jnp.sum(column_grads[:, :, 3 * head_cols + ff_here + 1], 0)

    mixer_part = row_product[:head_cols].reshape(nf, shard_rows, width)
    outer_part = row_product[head_cols : head_cols + ff_here].reshape(nf, ff_rows, width)
    sums_part = jnp.broadcast_to(row_product[head_cols + ff_here :][None], (nf, 16, width))
    row_grads = jnp.concatenate([mixer_part, outer_part, sums_part], 1)
    row_grads = row_grads.at[:, ff_rows + shard_rows + 1, :ff_rows].set(
        grad_inner_bias.reshape(nf, ff_rows).astype(bf16)
    )
    row_grads = lax.psum_scatter(row_grads, "fsdp", scatter_dimension=0, tiled=True)
    row_grads = replica_sum(row_grads, "rep")[0]
    grad_mixer_out = row_grads[:shard_rows]
    grad_outer_out = row_grads[shard_rows : shard_rows + ff_rows]
    grad_ibias_out = row_grads[shard_rows + ff_rows + 1, :ff_rows]
    fsdp_me = lax.axis_index("fsdp")
    grad_obias_out = lax.dynamic_slice_in_dim(
        row_grads[shard_rows + ff_rows], (me * nf + fsdp_me) * shard_rows, shard_rows
    )

    return (
        layer_output[None],
        input_grad[None],
        grad_gain_out,
        grad_shift_out,
        grad_triple_out,
        grad_mixer_out,
        grad_inner_out,
        grad_ibias_out,
        grad_outer_out,
        grad_obias_out,
    )


def solution(mesh):
    placed = (
        P(("rep", "fsdp"), "ctx", None),
        P(("ctx", "fsdp")),
        P(("ctx", "fsdp")),
        P(("ctx", "fsdp"), None),
        P(("ctx", "fsdp"), None),
        P(("ctx", "fsdp"), None),
        P(("ctx", "fsdp")),
        P(("ctx", "fsdp"), None),
        P(("ctx", "fsdp")),
        P(("rep", "fsdp")),
        P(("rep", "fsdp")),
        P(("rep", "fsdp"), "ctx", None),
    )
    return jax.shard_map(
        local,
        mesh=mesh,
        in_specs=placed,
        out_specs=(
            P(("rep", "fsdp"), "ctx", None),
            P(("rep", "fsdp"), "ctx", None),
            P(("ctx", "fsdp")),
            P(("ctx", "fsdp")),
            P(("ctx", "fsdp"), None),
            P(("ctx", "fsdp"), None),
            P(("ctx", "fsdp"), None),
            P(("ctx", "fsdp")),
            P(("ctx", "fsdp"), None),
            P(("ctx", "fsdp")),
        ),
        check_vma=False,
    )
```

```python
from functools import partial

import jax
import jax.numpy as jnp
from jax import lax
from jax.experimental import pallas as pl
from jax.experimental.pallas import tpu as pltpu
from jax.sharding import PartitionSpec as P

HEADS = 16
HEAD_DIM = 64
ROT = 32


eps = 1e-05


def angles(positions):
    frequency = 10000.0 ** (-(jnp.arange(ROT // 2, dtype=jnp.float32) * 2.0) / ROT)
    phases = positions.astype(jnp.float32)[:, None] * frequency[None, :]
    return (jnp.cos(phases), jnp.sin(phases))


def rotate(field, cos_table, sin_table):
    leading = field.shape[:-1]
    paired = field[..., :ROT].reshape(leading + (ROT // 2, 2))
    even_part = paired[..., 0]
    odd_part = paired[..., 1]
    cos_wide = cos_table[:, None, :]
    sin_wide = sin_table[:, None, :]
    turned = jnp.stack(
        [even_part * cos_wide - odd_part * sin_wide, odd_part * cos_wide + even_part * sin_wide], -1
    )
    return jnp.concatenate([turned.reshape(leading + (ROT,)), field[..., ROT:]], -1)


def pair_tables(positions, width):
    f32 = jnp.float32
    highest = lax.Precision.HIGHEST
    cos_table, sin_table = angles(positions)
    feature = jnp.arange(width) % HEAD_DIM
    pick = (feature[None, :] // 2 == jnp.arange(ROT // 2)[:, None]) & (feature[None, :] < ROT)
    pick = pick.astype(f32)
    sign = jnp.where(feature % 2 == 0, -1.0, 1.0).astype(f32)
    cos_full = jnp.dot(cos_table, pick, precision=highest) + (feature >= ROT).astype(f32)
    sin_full = jnp.dot(sin_table, pick, precision=highest) * sign
    return cos_full, sin_full


def swap_pairs(values):
    width = values.shape[-1]
    index = jnp.arange(width)
    swap = (index[:, None] == (index[None, :] ^ 1)).astype(jnp.float32)
    return jnp.dot(values, swap, precision=lax.Precision.HIGHEST)


def ring_pairs(n, step):
    return [(i, (i + step) % n) for i in range(n)]


def ring_gather(block, axis):
    n = lax.axis_size(axis)
    half = block.shape[0] // 2
    from_left = lax.ppermute(block, axis, ring_pairs(n, 1))
    from_right = lax.ppermute(block, axis, ring_pairs(n, -1))
    far_first = lax.ppermute(from_left[:half], axis, ring_pairs(n, 1))
    far_second = lax.ppermute(from_right[half:], axis, ring_pairs(n, -1))
    far = jnp.concatenate([far_first, far_second], 0)
    return jnp.stack([block, from_right, far, from_left])


def ring_scatter(parts, axis):
    n = lax.axis_size(axis)
    half = parts.shape[1] // 2
    wire = jnp.bfloat16
    got_left = lax.ppermute(parts[2, :half].astype(wire), axis, ring_pairs(n, 1))
    got_right = lax.ppermute(parts[2, half:].astype(wire), axis, ring_pairs(n, -1))
    to_right = jnp.concatenate([parts[1, :half] + got_left.astype(jnp.float32), parts[1, half:]], 0)
    to_left = jnp.concatenate([parts[3, :half], parts[3, half:] + got_right.astype(jnp.float32)], 0)
    from_left = lax.ppermute(to_right.astype(wire), axis, ring_pairs(n, 1))
    from_right = lax.ppermute(to_left.astype(wire), axis, ring_pairs(n, -1))
    return parts[0] + from_left.astype(jnp.float32) + from_right.astype(jnp.float32)


def ring_all_to_all(payload, axis):
    n = lax.axis_size(axis)
    me = lax.axis_index(axis)
    pick = lambda d: lax.dynamic_index_in_dim(payload, d % n, 0, keepdims=False)
    got = [pick(me)] + [
        lax.ppermute(pick(me + s), axis, ring_pairs(n, s)) for s in range(1, n)
    ]
    mirrored = jnp.stack([got[(-k) % n] for k in range(n)])
    doubled = jnp.concatenate([mirrored, mirrored], 0)
    return lax.dynamic_slice_in_dim(doubled, n - me, n, 0)


def replica_sum(values, axis):
    n = lax.axis_size(axis)
    f32, wire = jnp.float32, jnp.bfloat16
    values = values.astype(wire)
    if n != 4:
        return lax.psum(values, axis).astype(f32)
    pair = values.astype(f32) + lax.ppermute(values, axis, [(i, i ^ 1) for i in range(n)]).astype(f32)
    pair = pair.astype(wire)
    return pair.astype(f32) + lax.ppermute(pair, axis, [(i, i ^ 2) for i in range(n)]).astype(f32)


def attention_kernel(span_ref, q_ref, k_ref, v_ref, gm_ref, qpos_ref, kpos_ref,
                     mix_ref, gq_ref, gk_ref, gv_ref, bias_ref):
    f32, bf16 = jnp.float32, jnp.bfloat16
    block = pl.program_id(0)
    head = pl.program_id(1)

    @pl.when(head == 0)
    def _():
        allowed = (kpos_ref[...] <= qpos_ref[...]) | (kpos_ref[...] < span_ref[0])
        bias_ref[...] = jnp.where(allowed, 0.0, -1e30).astype(f32)

    q = q_ref[...]
    k = k_ref[...]
    v = v_ref[...]
    gm = gm_ref[...]
    scores = lax.dot_general(q, k, (((1,), (1,)), ((), ())), preferred_element_type=f32)
    scores = scores + bias_ref[...]
    peak = jnp.max(scores, axis=1, keepdims=True)
    exps = jnp.exp(scores - peak)
    total = jnp.sum(exps, axis=1, keepdims=True)
    probs = exps * (1.0 / total)
    low_probs = probs.astype(bf16)
    mix_ref[...] = jnp.dot(low_probs, v, preferred_element_type=f32).astype(mix_ref.dtype)
    grad_probs = lax.dot_general(gm, v, (((1,), (1,)), ((), ())), preferred_element_type=f32)
    inner = jnp.sum(probs * grad_probs, axis=1, keepdims=True)
    grad_scores = (probs * (grad_probs - inner)).astype(bf16)
    gq_ref[...] = jnp.dot(grad_scores, k, preferred_element_type=f32)
    gk_part = lax.dot_general(grad_scores, q, (((0,), (0,)), ((), ())), preferred_element_type=f32)
    gv_part = lax.dot_general(low_probs, gm, (((0,), (0,)), ((), ())), preferred_element_type=f32)

    @pl.when(block == 0)
    def _():
        gk_ref[head] = gk_part
        gv_ref[head] = gv_part

    @pl.when(block != 0)
    def _():
        gk_ref[head] += gk_part
        gv_ref[head] += gv_part


def fused_attention(span, queries, keys, values, grad_mixture, positions, rows=256):
    heads, length, dim = queries.shape
    blocks = length // rows
    qpos = positions.reshape(length, 1).astype(jnp.int32)
    kpos = positions.reshape(1, length).astype(jnp.int32)
    row_block = pl.BlockSpec((None, rows, dim), lambda b, h, s: (h, b, 0))
    whole_head = pl.BlockSpec((None, length, dim), lambda b, h, s: (h, 0, 0))
    resident = pl.BlockSpec((heads, length, dim), lambda b, h, s: (0, 0, 0))
    f32 = jnp.float32
    return pl.pallas_call(
        attention_kernel,
        out_shape=(
            jax.ShapeDtypeStruct((heads, length, dim), jnp.bfloat16),
            jax.ShapeDtypeStruct((heads, length, dim), f32),
            jax.ShapeDtypeStruct((heads, length, dim), f32),
            jax.ShapeDtypeStruct((heads, length, dim), f32),
        ),
        grid_spec=pltpu.PrefetchScalarGridSpec(
            num_scalar_prefetch=1,
            grid=(blocks, heads),
            in_specs=[
                row_block, whole_head, whole_head, row_block,
                pl.BlockSpec((rows, 1), lambda b, h, s: (b, 0)),
                pl.BlockSpec((1, length), lambda b, h, s: (0, 0)),
            ],
            out_specs=[row_block, row_block, resident, resident],
            scratch_shapes=[pltpu.VMEM((rows, length), f32)],
        ),
        compiler_params=pltpu.CompilerParams(dimension_semantics=("arbitrary", "arbitrary")),
        cost_estimate=pl.CostEstimate(
            flops=12 * heads * length * length * dim,
            transcendentals=heads * length * length,
            bytes_accessed=heads * length * dim * (4 * 2 + 3 * 4 + 2),
        ),
    )(span.reshape(1).astype(jnp.int32), queries, keys, values, grad_mixture, qpos, kpos)


def local(
    tokens,
    norm_gain,
    norm_shift,
    triple_weight,
    mixer_weight,
    inner_weight,
    inner_bias,
    outer_weight,
    outer_bias,
    prefix_length,
    pad_mask,
    cotangent,
):
    nc = lax.axis_size("ctx")
    nf = lax.axis_size("fsdp")
    me = lax.axis_index("ctx")
    _, own_rows, width = tokens.shape
    length = own_rows * nc
    shard_rows = triple_weight.shape[0]
    heads_here = HEADS // nc
    head_cols = heads_here * HEAD_DIM
    ff_here = inner_weight.shape[1] // nc
    ff_rows = outer_weight.shape[0]
    f32, bf16 = jnp.float32, jnp.bfloat16

    triple_cols = (
        triple_weight.reshape(shard_rows, 3, nc, head_cols)
        .transpose(2, 0, 1, 3)
        .reshape(nc, shard_rows, 3 * head_cols)
    )
    inner_cols = inner_weight.reshape(shard_rows, nc, ff_here).transpose(1, 0, 2)
    small = jnp.stack([norm_gain, norm_shift, outer_bias], -1)
    small = jnp.pad(small, ((0, 0), (0, 128 - small.shape[-1])))
    small = jnp.broadcast_to(small[None], (nc,) + small.shape)
    column_payload = jnp.concatenate([triple_cols, inner_cols, small], -1)
    column_payload = ring_all_to_all(column_payload, "ctx")
    split = 3 * head_cols

    bias_rows = jnp.pad(inner_bias[None], ((0, 15), (0, width - inner_bias.shape[0])))
    triple_payload = jnp.concatenate([column_payload[..., :split], column_payload[..., split + ff_here :]], -1)
    pieces = (triple_payload, mixer_weight, bias_rows)
    first_payload = jnp.concatenate([piece.reshape(-1) for piece in pieces]).reshape(-1, width)
    first_block = lax.all_gather(first_payload, "fsdp", axis=0, tiled=False).reshape(nf, -1)
    sizes = [piece.size for piece in pieces]
    triple_block = first_block[:, : sizes[0]].reshape((nf,) + triple_payload.shape)
    triple_block = triple_block.swapaxes(0, 1).reshape(nc * nf * shard_rows, -1)
    mixer_here = first_block[:, sizes[0] : sizes[0] + sizes[1]].reshape(nf * shard_rows, width)
    ibias_here = (
        first_block[:, sizes[0] + sizes[1] : sizes[0] + sizes[1] + inner_bias.shape[0]].reshape(-1).astype(f32)
    )

    ff_payload = jnp.concatenate(
        [column_payload[..., split : split + ff_here].reshape(nc * shard_rows, ff_here), outer_weight], 0
    )
    visible = (pad_mask[0] != 0).astype(f32)
    own_upstream = cotangent[0].astype(f32) * visible
    both = jnp.concatenate([tokens[0], own_upstream.astype(bf16)], -1)
    both = ring_gather(both, "ctx").reshape(length, 2 * width)
    ff_payload, triple_block, both = lax.optimization_barrier((ff_payload, triple_block, both))
    ff_block = lax.all_gather(ff_payload, "fsdp", axis=0, tiled=False)
    triple_here = triple_block[:, :split]
    gain = triple_block[:, split].astype(f32)
    shift = triple_block[:, split + 1].astype(f32)
    obias = triple_block[:, split + 2].astype(f32)

    all_tokens = both[:, :width]
    all_upstream = both[:, width:]

    input_rows = all_tokens.astype(f32)
    center = input_rows - jnp.mean(input_rows, -1, keepdims=True)
    scaling = lax.rsqrt(jnp.mean(center * center, -1, keepdims=True) + eps)
    whitened = center * scaling
    normed = (whitened * gain + shift).astype(bf16)

    owners = (me + jnp.arange(nc)) % nc
    positions = (owners[:, None] * own_rows + jnp.arange(own_rows)[None, :]).reshape(length)
    cos_table, sin_table = angles(positions)
    query_key_value = jnp.dot(normed, triple_here, preferred_element_type=f32)
    heads_shape = (length, heads_here, HEAD_DIM)
    queries = (
        rotate(query_key_value[:, :head_cols].reshape(heads_shape), cos_table, sin_table)
        * HEAD_DIM ** (-0.5)
    ).astype(bf16)
    key_rows = rotate(
        query_key_value[:, head_cols : 2 * head_cols].reshape(heads_shape), cos_table, sin_table
    ).astype(bf16)
    value_rows = query_key_value[:, 2 * head_cols :].reshape(heads_shape).astype(bf16)
    span = prefix_length[0]
    grad_mixture = jnp.dot(all_upstream, mixer_here.T, preferred_element_type=f32).astype(bf16)
    by_head = lambda values: values.reshape(heads_shape).swapaxes(0, 1)
    mixture, grad_queries, grad_keys, grad_values = fused_attention(
        span, by_head(queries), by_head(key_rows), by_head(value_rows), by_head(grad_mixture), positions
    )
    grad_queries, grad_keys, grad_values = (
        values.swapaxes(0, 1) for values in (grad_queries, grad_keys, grad_values)
    )
    mixture = mixture.swapaxes(0, 1).reshape(length, head_cols)
    ff_block, mixture = lax.optimization_barrier((ff_block, mixture))
    inner_here = (
        ff_block[:, : nc * shard_rows]
        .reshape(nf, nc, shard_rows, ff_here)
        .swapaxes(0, 1)
        .reshape(nc * nf * shard_rows, ff_here)
    )
    outer_here = ff_block[:, nc * shard_rows :].reshape(nf * ff_rows, width)

    attention = jnp.dot(mixture, mixer_here, preferred_element_type=f32)
    preact = jnp.dot(normed, inner_here, preferred_element_type=f32) + ibias_here
    gelu_result = jax.nn.gelu(preact, approximate=True).astype(bf16)
    feedforward = jnp.dot(gelu_result, outer_here, preferred_element_type=f32)
    block_sum = ring_scatter((attention + feedforward).reshape(nc, own_rows, width), "ctx")
    layer_output = (tokens[0].astype(f32) + block_sum + obias).astype(bf16)

    ones_block = jnp.ones((length, 16), bf16)
    row_lhs = jnp.concatenate([mixture, gelu_result, ones_block], -1)
    row_product = jnp.dot(row_lhs.T, all_upstream, preferred_element_type=f32).astype(bf16)
    grad_activated = jnp.dot(all_upstream, outer_here.T, preferred_element_type=f32)
    unused_value, gelu_pull = jax.vjp(partial(jax.nn.gelu, approximate=True), preact)
    grad_before_gelu = gelu_pull(grad_activated)[0].astype(bf16)
    grad_inner_weight = jnp.dot(normed.T, grad_before_gelu, preferred_element_type=f32)
    grad_inner_bias = jnp.sum(grad_before_gelu.astype(f32), 0)
    flat_shape = (length, head_cols)
    cos_full, sin_full = pair_tables(positions, 2 * head_cols)
    grad_turned = jnp.concatenate(
        [(grad_queries * HEAD_DIM ** (-0.5)).reshape(flat_shape), grad_keys.reshape(flat_shape)], -1
    )
    grad_turned = grad_turned * cos_full - swap_pairs(grad_turned) * sin_full
    grad_query_key_value = jnp.concatenate(
        [grad_turned, grad_values.reshape(flat_shape)], -1
    ).astype(bf16)
    grad_triple_weight = jnp.dot(normed.T, grad_query_key_value, preferred_element_type=f32)
    grad_normed = jnp.dot(grad_query_key_value, triple_here.T, preferred_element_type=f32)
    grad_normed = grad_normed + jnp.dot(grad_before_gelu, inner_here.T, preferred_element_type=f32)
    grad_norm_gain = jnp.sum(grad_normed * whitened, 0)
    grad_norm_shift = jnp.sum(grad_normed, 0)
    grad_normed = ring_scatter(grad_normed.reshape(nc, own_rows, width), "ctx")

    own_whitened = whitened[:own_rows]
    own_scaling = scaling[:own_rows]
    grad_white = grad_normed * gain
    grad_inputs = own_scaling * (
        grad_white
        - jnp.mean(grad_white, -1, keepdims=True)
        - own_whitened * jnp.mean(grad_white * own_whitened, -1, keepdims=True)
    )
    input_grad = (own_upstream + grad_inputs).astype(bf16)

    small_grads = jnp.stack([grad_norm_gain, grad_norm_shift], -1)
    small_grads = jnp.pad(small_grads, ((0, 0), (0, 128 - small_grads.shape[-1])))
    column_grads = jnp.concatenate(
        [grad_triple_weight, grad_inner_weight, small_grads], -1
    ).astype(bf16)
    column_grads = column_grads.reshape(nc, nf, shard_rows, -1).swapaxes(0, 1).reshape(width, -1)
    column_grads = lax.psum_scatter(column_grads, "fsdp", scatter_dimension=0, tiled=True)
    column_grads = replica_sum(column_grads, "rep").astype(bf16)
    column_grads = column_grads.reshape(nc, shard_rows, -1)
    column_grads = ring_all_to_all(column_grads, "ctx").astype(f32)
    grad_triple_out = (
        column_grads[:, :, : 3 * head_cols]
        .reshape(nc, shard_rows, 3, head_cols)
        .transpose(1, 2, 0, 3)
        .reshape(shard_rows, 3 * nc * head_cols)
    )
    grad_inner_out = (
        column_grads[:, :, 3 * head_cols : 3 * head_cols + ff_here]
        .transpose(1, 0, 2)
        .reshape(shard_rows, nc * ff_here)
    )
    grad_gain_out = jnp.sum(column_grads[:, :, 3 * head_cols + ff_here], 0)
    grad_shift_out = jnp.sum(column_grads[:, :, 3 * head_cols + ff_here + 1], 0)

    mixer_part = row_product[:head_cols].reshape(nf, shard_rows, width)
    outer_part = row_product[head_cols : head_cols + ff_here].reshape(nf, ff_rows, width)
    sums_part = jnp.broadcast_to(row_product[head_cols + ff_here :][None], (nf, 16, width))
    row_grads = jnp.concatenate([mixer_part, outer_part, sums_part], 1)
    row_grads = row_grads.at[:, ff_rows + shard_rows + 1, :ff_rows].set(
        grad_inner_bias.reshape(nf, ff_rows).astype(bf16)
    )
    row_grads = lax.psum_scatter(row_grads, "fsdp", scatter_dimension=0, tiled=True)
    row_grads = replica_sum(row_grads, "rep")[0]
    grad_mixer_out = row_grads[:shard_rows]
    grad_outer_out = row_grads[shard_rows : shard_rows + ff_rows]
    grad_ibias_out = row_grads[shard_rows + ff_rows + 1, :ff_rows]
    fsdp_me = lax.axis_index("fsdp")
    grad_obias_out = lax.dynamic_slice_in_dim(
        row_grads[shard_rows + ff_rows], (me * nf + fsdp_me) * shard_rows, shard_rows
    )

    return (
        layer_output[None],
        input_grad[None],
        grad_gain_out,
        grad_shift_out,
        grad_triple_out,
        grad_mixer_out,
        grad_inner_out,
        grad_ibias_out,
        grad_outer_out,
        grad_obias_out,
    )


def solution(mesh):
    placed = (
        P(("rep", "fsdp"), "ctx", None),
        P(("ctx", "fsdp")),
        P(("ctx", "fsdp")),
        P(("ctx", "fsdp"), None),
        P(("ctx", "fsdp"), None),
        P(("ctx", "fsdp"), None),
        P(("ctx", "fsdp")),
        P(("ctx", "fsdp"), None),
        P(("ctx", "fsdp")),
        P(("rep", "fsdp")),
        P(("rep", "fsdp")),
        P(("rep", "fsdp"), "ctx", None),
    )
    return jax.shard_map(
        local,
        mesh=mesh,
        in_specs=placed,
        out_specs=(
            P(("rep", "fsdp"), "ctx", None),
            P(("rep", "fsdp"), "ctx", None),
            P(("ctx", "fsdp")),
            P(("ctx", "fsdp")),
            P(("ctx", "fsdp"), None),
            P(("ctx", "fsdp"), None),
            P(("ctx", "fsdp"), None),
            P(("ctx", "fsdp")),
            P(("ctx", "fsdp"), None),
            P(("ctx", "fsdp")),
        ),
        check_vma=False,
    )
```

```python
from functools import partial

import jax
import jax.numpy as jnp
from jax import lax
from jax.experimental import pallas as pl
from jax.experimental.pallas import tpu as pltpu
from jax.sharding import PartitionSpec as P

HEADS = 16
HEAD_DIM = 64
ROT = 32


eps = 1e-05


def angles(positions):
    frequency = 10000.0 ** (-(jnp.arange(ROT // 2, dtype=jnp.float32) * 2.0) / ROT)
    phases = positions.astype(jnp.float32)[:, None] * frequency[None, :]
    return (jnp.cos(phases), jnp.sin(phases))


def rotate(field, cos_table, sin_table):
    leading = field.shape[:-1]
    paired = field[..., :ROT].reshape(leading + (ROT // 2, 2))
    even_part = paired[..., 0]
    odd_part = paired[..., 1]
    cos_wide = cos_table[:, None, :]
    sin_wide = sin_table[:, None, :]
    turned = jnp.stack(
        [even_part * cos_wide - odd_part * sin_wide, odd_part * cos_wide + even_part * sin_wide], -1
    )
    return jnp.concatenate([turned.reshape(leading + (ROT,)), field[..., ROT:]], -1)


def pair_tables(positions, width):
    f32 = jnp.float32
    highest = lax.Precision.HIGHEST
    cos_table, sin_table = angles(positions)
    feature = jnp.arange(width) % HEAD_DIM
    pick = (feature[None, :] // 2 == jnp.arange(ROT // 2)[:, None]) & (feature[None, :] < ROT)
    pick = pick.astype(f32)
    sign = jnp.where(feature % 2 == 0, -1.0, 1.0).astype(f32)
    cos_full = jnp.dot(cos_table, pick, precision=highest) + (feature >= ROT).astype(f32)
    sin_full = jnp.dot(sin_table, pick, precision=highest) * sign
    return cos_full, sin_full


def swap_pairs(values):
    width = values.shape[-1]
    index = jnp.arange(width)
    swap = (index[:, None] == (index[None, :] ^ 1)).astype(jnp.float32)
    return jnp.dot(values, swap, precision=lax.Precision.HIGHEST)


def ring_pairs(n, step):
    return [(i, (i + step) % n) for i in range(n)]


def ring_gather(block, axis):
    n = lax.axis_size(axis)
    half = block.shape[0] // 2
    from_left = lax.ppermute(block, axis, ring_pairs(n, 1))
    from_right = lax.ppermute(block, axis, ring_pairs(n, -1))
    far_first = lax.ppermute(from_left[:half], axis, ring_pairs(n, 1))
    far_second = lax.ppermute(from_right[half:], axis, ring_pairs(n, -1))
    far = jnp.concatenate([far_first, far_second], 0)
    return jnp.stack([block, from_right, far, from_left])


def ring_scatter(parts, axis):
    n = lax.axis_size(axis)
    half = parts.shape[1] // 2
    wire = jnp.bfloat16
    got_left = lax.ppermute(parts[2, :half].astype(wire), axis, ring_pairs(n, 1))
    got_right = lax.ppermute(parts[2, half:].astype(wire), axis, ring_pairs(n, -1))
    to_right = jnp.concatenate([parts[1, :half] + got_left.astype(jnp.float32), parts[1, half:]], 0)
    to_left = jnp.concatenate([parts[3, :half], parts[3, half:] + got_right.astype(jnp.float32)], 0)
    from_left = lax.ppermute(to_right.astype(wire), axis, ring_pairs(n, 1))
    from_right = lax.ppermute(to_left.astype(wire), axis, ring_pairs(n, -1))
    return parts[0] + from_left.astype(jnp.float32) + from_right.astype(jnp.float32)


def ring_all_to_all(payload, axis):
    n = lax.axis_size(axis)
    me = lax.axis_index(axis)
    pick = lambda d: lax.dynamic_index_in_dim(payload, d % n, 0, keepdims=False)
    got = [pick(me)] + [
        lax.ppermute(pick(me + s), axis, ring_pairs(n, s)) for s in range(1, n)
    ]
    mirrored = jnp.stack([got[(-k) % n] for k in range(n)])
    doubled = jnp.concatenate([mirrored, mirrored], 0)
    return lax.dynamic_slice_in_dim(doubled, n - me, n, 0)


def replica_sum(values, axis):
    n = lax.axis_size(axis)
    f32, wire = jnp.float32, jnp.bfloat16
    values = values.astype(wire)
    if n != 4:
        return lax.psum(values, axis).astype(f32)
    pair = values.astype(f32) + lax.ppermute(values, axis, [(i, i ^ 1) for i in range(n)]).astype(f32)
    pair = pair.astype(wire)
    return pair.astype(f32) + lax.ppermute(pair, axis, [(i, i ^ 2) for i in range(n)]).astype(f32)


def attention_kernel(span_ref, q_ref, k_ref, v_ref, gm_ref, qpos_ref, kpos_ref,
                     mix_ref, gq_ref, gk_ref, gv_ref, bias_ref):
    f32, bf16 = jnp.float32, jnp.bfloat16
    block = pl.program_id(0)
    head = pl.program_id(1)

    @pl.when(head == 0)
    def _():
        allowed = (kpos_ref[...] <= qpos_ref[...]) | (kpos_ref[...] < span_ref[0])
        bias_ref[...] = jnp.where(allowed, 0.0, -1e30).astype(f32)

    q = q_ref[...]
    k = k_ref[...]
    v = v_ref[...]
    gm = gm_ref[...]
    scores = lax.dot_general(q, k, (((1,), (1,)), ((), ())), preferred_element_type=f32)
    scores = scores + bias_ref[...]
    peak = jnp.max(scores, axis=1, keepdims=True)
    exps = jnp.exp(scores - peak)
    total = jnp.sum(exps, axis=1, keepdims=True)
    probs = exps * (1.0 / total)
    low_probs = probs.astype(bf16)
    mix_ref[...] = jnp.dot(low_probs, v, preferred_element_type=f32).astype(mix_ref.dtype)
    grad_probs = lax.dot_general(gm, v, (((1,), (1,)), ((), ())), preferred_element_type=f32)
    inner = jnp.sum(probs * grad_probs, axis=1, keepdims=True)
    grad_scores = (probs * (grad_probs - inner)).astype(bf16)
    gq_ref[...] = jnp.dot(grad_scores, k, preferred_element_type=f32)
    gk_part = lax.dot_general(grad_scores, q, (((0,), (0,)), ((), ())), preferred_element_type=f32)
    gv_part = lax.dot_general(low_probs, gm, (((0,), (0,)), ((), ())), preferred_element_type=f32)

    @pl.when(block == 0)
    def _():
        gk_ref[head] = gk_part
        gv_ref[head] = gv_part

    @pl.when(block != 0)
    def _():
        gk_ref[head] += gk_part
        gv_ref[head] += gv_part


def fused_attention(span, queries, keys, values, grad_mixture, positions, rows=256):
    heads, length, dim = queries.shape
    blocks = length // rows
    qpos = positions.reshape(length, 1).astype(jnp.int32)
    kpos = positions.reshape(1, length).astype(jnp.int32)
    row_block = pl.BlockSpec((None, rows, dim), lambda b, h, s: (h, b, 0))
    whole_head = pl.BlockSpec((None, length, dim), lambda b, h, s: (h, 0, 0))
    resident = pl.BlockSpec((heads, length, dim), lambda b, h, s: (0, 0, 0))
    f32 = jnp.float32
    return pl.pallas_call(
        attention_kernel,
        out_shape=(
            jax.ShapeDtypeStruct((heads, length, dim), jnp.bfloat16),
            jax.ShapeDtypeStruct((heads, length, dim), f32),
            jax.ShapeDtypeStruct((heads, length, dim), f32),
            jax.ShapeDtypeStruct((heads, length, dim), f32),
        ),
        grid_spec=pltpu.PrefetchScalarGridSpec(
            num_scalar_prefetch=1,
            grid=(blocks, heads),
            in_specs=[
                row_block, whole_head, whole_head, row_block,
                pl.BlockSpec((rows, 1), lambda b, h, s: (b, 0)),
                pl.BlockSpec((1, length), lambda b, h, s: (0, 0)),
            ],
            out_specs=[row_block, row_block, resident, resident],
            scratch_shapes=[pltpu.VMEM((rows, length), f32)],
        ),
        compiler_params=pltpu.CompilerParams(dimension_semantics=("arbitrary", "arbitrary")),
        cost_estimate=pl.CostEstimate(
            flops=12 * heads * length * length * dim,
            transcendentals=heads * length * length,
            bytes_accessed=heads * length * dim * (4 * 2 + 3 * 4 + 2),
        ),
    )(span.reshape(1).astype(jnp.int32), queries, keys, values, grad_mixture, qpos, kpos)


def local(
    tokens,
    norm_gain,
    norm_shift,
    triple_weight,
    mixer_weight,
    inner_weight,
    inner_bias,
    outer_weight,
    outer_bias,
    prefix_length,
    pad_mask,
    cotangent,
):
    nc = lax.axis_size("ctx")
    nf = lax.axis_size("fsdp")
    me = lax.axis_index("ctx")
    _, own_rows, width = tokens.shape
    length = own_rows * nc
    shard_rows = triple_weight.shape[0]
    heads_here = HEADS // nc
    head_cols = heads_here * HEAD_DIM
    ff_here = inner_weight.shape[1] // nc
    ff_rows = outer_weight.shape[0]
    f32, bf16 = jnp.float32, jnp.bfloat16

    triple_cols = (
        triple_weight.reshape(shard_rows, 3, nc, head_cols)
        .transpose(2, 0, 1, 3)
        .reshape(nc, shard_rows, 3 * head_cols)
    )
    inner_cols = inner_weight.reshape(shard_rows, nc, ff_here).transpose(1, 0, 2)
    small = jnp.stack([norm_gain, norm_shift, outer_bias], -1)
    small = jnp.pad(small, ((0, 0), (0, 128 - small.shape[-1])))
    small = jnp.broadcast_to(small[None], (nc,) + small.shape)
    column_payload = jnp.concatenate([triple_cols, inner_cols, small], -1)
    column_payload = ring_all_to_all(column_payload, "ctx")
    split = 3 * head_cols

    bias_rows = jnp.pad(inner_bias[None], ((0, 15), (0, width - inner_bias.shape[0])))
    triple_payload = jnp.concatenate([column_payload[..., :split], column_payload[..., split + ff_here :]], -1)
    pieces = (triple_payload, mixer_weight, bias_rows)
    first_payload = jnp.concatenate([piece.reshape(-1) for piece in pieces]).reshape(-1, width)
    first_block = lax.all_gather(first_payload, "fsdp", axis=0, tiled=False).reshape(nf, -1)
    sizes = [piece.size for piece in pieces]
    triple_block = first_block[:, : sizes[0]].reshape((nf,) + triple_payload.shape)
    triple_block = triple_block.swapaxes(0, 1).reshape(nc * nf * shard_rows, -1)
    mixer_here = first_block[:, sizes[0] : sizes[0] + sizes[1]].reshape(nf * shard_rows, width)
    ibias_here = (
        first_block[:, sizes[0] + sizes[1] : sizes[0] + sizes[1] + inner_bias.shape[0]].reshape(-1).astype(f32)
    )

    ff_payload = jnp.concatenate(
        [column_payload[..., split : split + ff_here].reshape(nc * shard_rows, ff_here), outer_weight], 0
    )
    visible = (pad_mask[0] != 0).astype(f32)
    own_upstream = cotangent[0].astype(f32) * visible
    both = jnp.concatenate([tokens[0], own_upstream.astype(bf16)], -1)
    both = ring_gather(both, "ctx").reshape(length, 2 * width)
    ff_payload, triple_block, both = lax.optimization_barrier((ff_payload, triple_block, both))
    ff_block = lax.all_gather(ff_payload, "fsdp", axis=0, tiled=False)
    triple_here = triple_block[:, :split]
    gain = triple_block[:, split].astype(f32)
    shift = triple_block[:, split + 1].astype(f32)
    obias = triple_block[:, split + 2].astype(f32)

    all_tokens = both[:, :width]
    all_upstream = both[:, width:]

    input_rows = all_tokens.astype(f32)
    center = input_rows - jnp.mean(input_rows, -1, keepdims=True)
    scaling = lax.rsqrt(jnp.mean(center * center, -1, keepdims=True) + eps)
    whitened = center * scaling
    normed = (whitened * gain + shift).astype(bf16)

    owners = (me + jnp.arange(nc)) % nc
    positions = (owners[:, None] * own_rows + jnp.arange(own_rows)[None, :]).reshape(length)
    cos_full, sin_full = pair_tables(positions, 2 * head_cols)
    query_key_value = jnp.dot(normed, triple_here, preferred_element_type=f32)
    heads_shape = (length, heads_here, HEAD_DIM)
    turned = query_key_value[:, : 2 * head_cols]
    turned = turned * cos_full + swap_pairs(turned) * sin_full
    queries = (turned[:, :head_cols] * HEAD_DIM ** (-0.5)).astype(bf16).reshape(heads_shape)
    key_rows = turned[:, head_cols:].astype(bf16).reshape(heads_shape)
    value_rows = query_key_value[:, 2 * head_cols :].reshape(heads_shape).astype(bf16)
    span = prefix_length[0]
    grad_mixture = jnp.dot(all_upstream, mixer_here.T, preferred_element_type=f32).astype(bf16)
    by_head = lambda values: values.reshape(heads_shape).swapaxes(0, 1)
    mixture, grad_queries, grad_keys, grad_values = fused_attention(
        span, by_head(queries), by_head(key_rows), by_head(value_rows), by_head(grad_mixture), positions
    )
    grad_queries, grad_keys, grad_values = (
        values.swapaxes(0, 1) for values in (grad_queries, grad_keys, grad_values)
    )
    mixture = mixture.swapaxes(0, 1).reshape(length, head_cols)
    ff_block, mixture = lax.optimization_barrier((ff_block, mixture))
    inner_here = (
        ff_block[:, : nc * shard_rows]
        .reshape(nf, nc, shard_rows, ff_here)
        .swapaxes(0, 1)
        .reshape(nc * nf * shard_rows, ff_here)
    )
    outer_here = ff_block[:, nc * shard_rows :].reshape(nf * ff_rows, width)

    attention = jnp.dot(mixture, mixer_here, preferred_element_type=f32)
    preact = jnp.dot(normed, inner_here, preferred_element_type=f32) + ibias_here
    gelu_result = jax.nn.gelu(preact, approximate=True).astype(bf16)
    feedforward = jnp.dot(gelu_result, outer_here, preferred_element_type=f32)
    block_sum = ring_scatter((attention + feedforward).reshape(nc, own_rows, width), "ctx")
    layer_output = (tokens[0].astype(f32) + block_sum + obias).astype(bf16)

    ones_block = jnp.ones((length, 16), bf16)
    row_lhs = jnp.concatenate([mixture, gelu_result, ones_block], -1)
    row_product = jnp.dot(row_lhs.T, all_upstream, preferred_element_type=f32).astype(bf16)
    grad_activated = jnp.dot(all_upstream, outer_here.T, preferred_element_type=f32)
    unused_value, gelu_pull = jax.vjp(partial(jax.nn.gelu, approximate=True), preact)
    grad_before_gelu = gelu_pull(grad_activated)[0].astype(bf16)
    grad_inner_weight = jnp.dot(normed.T, grad_before_gelu, preferred_element_type=f32)
    grad_inner_bias = jnp.sum(grad_before_gelu.astype(f32), 0)
    flat_shape = (length, head_cols)
    grad_turned = jnp.concatenate(
        [(grad_queries * HEAD_DIM ** (-0.5)).reshape(flat_shape), grad_keys.reshape(flat_shape)], -1
    )
    grad_turned = grad_turned * cos_full - swap_pairs(grad_turned) * sin_full
    grad_query_key_value = jnp.concatenate(
        [grad_turned, grad_values.reshape(flat_shape)], -1
    ).astype(bf16)
    grad_triple_weight = jnp.dot(normed.T, grad_query_key_value, preferred_element_type=f32)
    grad_normed = jnp.dot(grad_query_key_value, triple_here.T, preferred_element_type=f32)
    grad_normed = grad_normed + jnp.dot(grad_before_gelu, inner_here.T, preferred_element_type=f32)
    grad_norm_gain = jnp.sum(grad_normed * whitened, 0)
    grad_norm_shift = jnp.sum(grad_normed, 0)
    grad_normed = ring_scatter(grad_normed.reshape(nc, own_rows, width), "ctx")

    own_whitened = whitened[:own_rows]
    own_scaling = scaling[:own_rows]
    grad_white = grad_normed * gain
    grad_inputs = own_scaling * (
        grad_white
        - jnp.mean(grad_white, -1, keepdims=True)
        - own_whitened * jnp.mean(grad_white * own_whitened, -1, keepdims=True)
    )
    input_grad = (own_upstream + grad_inputs).astype(bf16)

    small_grads = jnp.stack([grad_norm_gain, grad_norm_shift], -1)
    small_grads = jnp.pad(small_grads, ((0, 0), (0, 128 - small_grads.shape[-1])))
    column_grads = jnp.concatenate(
        [grad_triple_weight, grad_inner_weight, small_grads], -1
    ).astype(bf16)
    column_grads = column_grads.reshape(nc, nf, shard_rows, -1).swapaxes(0, 1).reshape(width, -1)
    column_grads = lax.psum_scatter(column_grads, "fsdp", scatter_dimension=0, tiled=True)
    column_grads = replica_sum(column_grads, "rep").astype(bf16)
    column_grads = column_grads.reshape(nc, shard_rows, -1)
    column_grads = ring_all_to_all(column_grads, "ctx").astype(f32)
    grad_triple_out = (
        column_grads[:, :, : 3 * head_cols]
        .reshape(nc, shard_rows, 3, head_cols)
        .transpose(1, 2, 0, 3)
        .reshape(shard_rows, 3 * nc * head_cols)
    )
    grad_inner_out = (
        column_grads[:, :, 3 * head_cols : 3 * head_cols + ff_here]
        .transpose(1, 0, 2)
        .reshape(shard_rows, nc * ff_here)
    )
    grad_gain_out = jnp.sum(column_grads[:, :, 3 * head_cols + ff_here], 0)
    grad_shift_out = jnp.sum(column_grads[:, :, 3 * head_cols + ff_here + 1], 0)

    mixer_part = row_product[:head_cols].reshape(nf, shard_rows, width)
    outer_part = row_product[head_cols : head_cols + ff_here].reshape(nf, ff_rows, width)
    sums_part = jnp.broadcast_to(row_product[head_cols + ff_here :][None], (nf, 16, width))
    row_grads = jnp.concatenate([mixer_part, outer_part, sums_part], 1)
    row_grads = row_grads.at[:, ff_rows + shard_rows + 1, :ff_rows].set(
        grad_inner_bias.reshape(nf, ff_rows).astype(bf16)
    )
    row_grads = lax.psum_scatter(row_grads, "fsdp", scatter_dimension=0, tiled=True)
    row_grads = replica_sum(row_grads, "rep")[0]
    grad_mixer_out = row_grads[:shard_rows]
    grad_outer_out = row_grads[shard_rows : shard_rows + ff_rows]
    grad_ibias_out = row_grads[shard_rows + ff_rows + 1, :ff_rows]
    fsdp_me = lax.axis_index("fsdp")
    grad_obias_out = lax.dynamic_slice_in_dim(
        row_grads[shard_rows + ff_rows], (me * nf + fsdp_me) * shard_rows, shard_rows
    )

    return (
        layer_output[None],
        input_grad[None],
        grad_gain_out,
        grad_shift_out,
        grad_triple_out,
        grad_mixer_out,
        grad_inner_out,
        grad_ibias_out,
        grad_outer_out,
        grad_obias_out,
    )


def solution(mesh):
    placed = (
        P(("rep", "fsdp"), "ctx", None),
        P(("ctx", "fsdp")),
        P(("ctx", "fsdp")),
        P(("ctx", "fsdp"), None),
        P(("ctx", "fsdp"), None),
        P(("ctx", "fsdp"), None),
        P(("ctx", "fsdp")),
        P(("ctx", "fsdp"), None),
        P(("ctx", "fsdp")),
        P(("rep", "fsdp")),
        P(("rep", "fsdp")),
        P(("rep", "fsdp"), "ctx", None),
    )
    return jax.shard_map(
        local,
        mesh=mesh,
        in_specs=placed,
        out_specs=(
            P(("rep", "fsdp"), "ctx", None),
            P(("rep", "fsdp"), "ctx", None),
            P(("ctx", "fsdp")),
            P(("ctx", "fsdp")),
            P(("ctx", "fsdp"), None),
            P(("ctx", "fsdp"), None),
            P(("ctx", "fsdp"), None),
            P(("ctx", "fsdp")),
            P(("ctx", "fsdp"), None),
            P(("ctx", "fsdp")),
        ),
        check_vma=False,
    )
```

```python
from functools import partial

import jax
import jax.numpy as jnp
from jax import lax
from jax.experimental import pallas as pl
from jax.experimental.pallas import tpu as pltpu
from jax.sharding import PartitionSpec as P

HEADS = 16
HEAD_DIM = 64
ROT = 32


eps = 1e-05


def angles(positions):
    frequency = 10000.0 ** (-(jnp.arange(ROT // 2, dtype=jnp.float32) * 2.0) / ROT)
    phases = positions.astype(jnp.float32)[:, None] * frequency[None, :]
    return (jnp.cos(phases), jnp.sin(phases))


def rotate(field, cos_table, sin_table):
    leading = field.shape[:-1]
    paired = field[..., :ROT].reshape(leading + (ROT // 2, 2))
    even_part = paired[..., 0]
    odd_part = paired[..., 1]
    cos_wide = cos_table[:, None, :]
    sin_wide = sin_table[:, None, :]
    turned = jnp.stack(
        [even_part * cos_wide - odd_part * sin_wide, odd_part * cos_wide + even_part * sin_wide], -1
    )
    return jnp.concatenate([turned.reshape(leading + (ROT,)), field[..., ROT:]], -1)


def pair_tables(positions, width):
    f32 = jnp.float32
    highest = lax.Precision.HIGHEST
    cos_table, sin_table = angles(positions)
    feature = jnp.arange(width) % HEAD_DIM
    pick = (feature[None, :] // 2 == jnp.arange(ROT // 2)[:, None]) & (feature[None, :] < ROT)
    pick = pick.astype(f32)
    sign = jnp.where(feature % 2 == 0, -1.0, 1.0).astype(f32)
    cos_full = jnp.dot(cos_table, pick, precision=highest) + (feature >= ROT).astype(f32)
    sin_full = jnp.dot(sin_table, pick, precision=highest) * sign
    return cos_full, sin_full


def swap_pairs(values):
    width = values.shape[-1]
    index = jnp.arange(width)
    swap = (index[:, None] == (index[None, :] ^ 1)).astype(jnp.float32)
    return jnp.dot(values, swap, precision=lax.Precision.HIGHEST)


def ring_pairs(n, step):
    return [(i, (i + step) % n) for i in range(n)]


def ring_gather(block, axis):
    n = lax.axis_size(axis)
    half = block.shape[0] // 2
    from_left = lax.ppermute(block, axis, ring_pairs(n, 1))
    from_right = lax.ppermute(block, axis, ring_pairs(n, -1))
    far_first = lax.ppermute(from_left[:half], axis, ring_pairs(n, 1))
    far_second = lax.ppermute(from_right[half:], axis, ring_pairs(n, -1))
    far = jnp.concatenate([far_first, far_second], 0)
    return jnp.stack([block, from_right, far, from_left])


def ring_scatter(parts, axis):
    n = lax.axis_size(axis)
    half = parts.shape[1] // 2
    wire = jnp.bfloat16
    got_left = lax.ppermute(parts[2, :half].astype(wire), axis, ring_pairs(n, 1))
    got_right = lax.ppermute(parts[2, half:].astype(wire), axis, ring_pairs(n, -1))
    to_right = jnp.concatenate([parts[1, :half] + got_left.astype(jnp.float32), parts[1, half:]], 0)
    to_left = jnp.concatenate([parts[3, :half], parts[3, half:] + got_right.astype(jnp.float32)], 0)
    from_left = lax.ppermute(to_right.astype(wire), axis, ring_pairs(n, 1))
    from_right = lax.ppermute(to_left.astype(wire), axis, ring_pairs(n, -1))
    return parts[0] + from_left.astype(jnp.float32) + from_right.astype(jnp.float32)


def ring_all_to_all(payload, axis):
    n = lax.axis_size(axis)
    me = lax.axis_index(axis)
    pick = lambda d: lax.dynamic_index_in_dim(payload, d % n, 0, keepdims=False)
    got = [pick(me)] + [
        lax.ppermute(pick(me + s), axis, ring_pairs(n, s)) for s in range(1, n)
    ]
    mirrored = jnp.stack([got[(-k) % n] for k in range(n)])
    doubled = jnp.concatenate([mirrored, mirrored], 0)
    return lax.dynamic_slice_in_dim(doubled, n - me, n, 0)


def replica_sum(values, axis):
    n = lax.axis_size(axis)
    f32, wire = jnp.float32, jnp.bfloat16
    values = values.astype(wire)
    if n != 4:
        return lax.psum(values, axis).astype(f32)
    pair = values.astype(f32) + lax.ppermute(values, axis, [(i, i ^ 1) for i in range(n)]).astype(f32)
    pair = pair.astype(wire)
    return pair.astype(f32) + lax.ppermute(pair, axis, [(i, i ^ 2) for i in range(n)]).astype(f32)


def attention_kernel(span_ref, q_ref, k_ref, v_ref, gm_ref, qpos_ref, kpos_ref,
                     mix_ref, gq_ref, gk_ref, gv_ref, bias_ref):
    f32, bf16 = jnp.float32, jnp.bfloat16
    block = pl.program_id(0)
    head = pl.program_id(1)

    @pl.when(head == 0)
    def _():
        allowed = (kpos_ref[...] <= qpos_ref[...]) | (kpos_ref[...] < span_ref[0])
        bias_ref[...] = jnp.where(allowed, 0.0, -1e30).astype(f32)

    q = q_ref[...]
    k = k_ref[...]
    v = v_ref[...]
    gm = gm_ref[...]
    scores = lax.dot_general(q, k, (((1,), (1,)), ((), ())), preferred_element_type=f32)
    scores = scores + bias_ref[...]
    peak = jnp.max(scores, axis=1, keepdims=True)
    exps = jnp.exp(scores - peak)
    total = jnp.sum(exps, axis=1, keepdims=True)
    probs = exps * (1.0 / total)
    low_probs = probs.astype(bf16)
    mix_ref[...] = jnp.dot(low_probs, v, preferred_element_type=f32).astype(mix_ref.dtype)
    grad_probs = lax.dot_general(gm, v, (((1,), (1,)), ((), ())), preferred_element_type=f32)
    inner = jnp.sum(probs * grad_probs, axis=1, keepdims=True)
    grad_scores = (probs * (grad_probs - inner)).astype(bf16)
    gq_ref[...] = jnp.dot(grad_scores, k, preferred_element_type=f32)
    gk_part = lax.dot_general(grad_scores, q, (((0,), (0,)), ((), ())), preferred_element_type=f32)
    gv_part = lax.dot_general(low_probs, gm, (((0,), (0,)), ((), ())), preferred_element_type=f32)

    @pl.when(block == 0)
    def _():
        gk_ref[head] = gk_part
        gv_ref[head] = gv_part

    @pl.when(block != 0)
    def _():
        gk_ref[head] += gk_part
        gv_ref[head] += gv_part


def fused_attention(span, queries, keys, values, grad_mixture, positions, rows=256):
    heads, length, dim = queries.shape
    blocks = length // rows
    qpos = positions.reshape(length, 1).astype(jnp.int32)
    kpos = positions.reshape(1, length).astype(jnp.int32)
    row_block = pl.BlockSpec((None, rows, dim), lambda b, h, s: (h, b, 0))
    whole_head = pl.BlockSpec((None, length, dim), lambda b, h, s: (h, 0, 0))
    resident = pl.BlockSpec((heads, length, dim), lambda b, h, s: (0, 0, 0))
    f32 = jnp.float32
    return pl.pallas_call(
        attention_kernel,
        out_shape=(
            jax.ShapeDtypeStruct((heads, length, dim), jnp.bfloat16),
            jax.ShapeDtypeStruct((heads, length, dim), f32),
            jax.ShapeDtypeStruct((heads, length, dim), f32),
            jax.ShapeDtypeStruct((heads, length, dim), f32),
        ),
        grid_spec=pltpu.PrefetchScalarGridSpec(
            num_scalar_prefetch=1,
            grid=(blocks, heads),
            in_specs=[
                row_block, whole_head, whole_head, row_block,
                pl.BlockSpec((rows, 1), lambda b, h, s: (b, 0)),
                pl.BlockSpec((1, length), lambda b, h, s: (0, 0)),
            ],
            out_specs=[row_block, row_block, resident, resident],
            scratch_shapes=[pltpu.VMEM((rows, length), f32)],
        ),
        compiler_params=pltpu.CompilerParams(dimension_semantics=("arbitrary", "arbitrary")),
        cost_estimate=pl.CostEstimate(
            flops=12 * heads * length * length * dim,
            transcendentals=heads * length * length,
            bytes_accessed=heads * length * dim * (4 * 2 + 3 * 4 + 2),
        ),
    )(span.reshape(1).astype(jnp.int32), queries, keys, values, grad_mixture, qpos, kpos)


def local(
    tokens,
    norm_gain,
    norm_shift,
    triple_weight,
    mixer_weight,
    inner_weight,
    inner_bias,
    outer_weight,
    outer_bias,
    prefix_length,
    pad_mask,
    cotangent,
):
    nc = lax.axis_size("ctx")
    nf = lax.axis_size("fsdp")
    me = lax.axis_index("ctx")
    _, own_rows, width = tokens.shape
    length = own_rows * nc
    shard_rows = triple_weight.shape[0]
    heads_here = HEADS // nc
    head_cols = heads_here * HEAD_DIM
    ff_here = inner_weight.shape[1] // nc
    ff_rows = outer_weight.shape[0]
    f32, bf16 = jnp.float32, jnp.bfloat16

    triple_cols = (
        triple_weight.reshape(shard_rows, 3, nc, head_cols)
        .transpose(2, 0, 1, 3)
        .reshape(nc, shard_rows, 3 * head_cols)
    )
    inner_cols = inner_weight.reshape(shard_rows, nc, ff_here).transpose(1, 0, 2)
    small = jnp.stack([norm_gain, norm_shift, outer_bias], -1)
    small = jnp.pad(small, ((0, 0), (0, 128 - small.shape[-1])))
    small = jnp.broadcast_to(small[None], (nc,) + small.shape)
    column_payload = jnp.concatenate([triple_cols, inner_cols, small], -1)
    column_payload = ring_all_to_all(column_payload, "ctx")
    split = 3 * head_cols

    bias_rows = jnp.pad(inner_bias[None], ((0, 15), (0, width - inner_bias.shape[0])))
    triple_payload = jnp.concatenate([column_payload[..., :split], column_payload[..., split + ff_here :]], -1)
    pieces = (triple_payload, mixer_weight, bias_rows)
    first_payload = jnp.concatenate([piece.reshape(-1) for piece in pieces]).reshape(-1, width)
    first_block = lax.all_gather(first_payload, "fsdp", axis=0, tiled=False).reshape(nf, -1)
    sizes = [piece.size for piece in pieces]
    triple_block = first_block[:, : sizes[0]].reshape((nf,) + triple_payload.shape)
    triple_block = triple_block.swapaxes(0, 1).reshape(nc * nf * shard_rows, -1)
    mixer_here = first_block[:, sizes[0] : sizes[0] + sizes[1]].reshape(nf * shard_rows, width)
    ibias_here = (
        first_block[:, sizes[0] + sizes[1] : sizes[0] + sizes[1] + inner_bias.shape[0]].reshape(-1).astype(f32)
    )

    ff_payload = jnp.concatenate(
        [column_payload[..., split : split + ff_here].reshape(nc * shard_rows, ff_here), outer_weight], 0
    )
    visible = (pad_mask[0] != 0).astype(f32)
    own_upstream = cotangent[0].astype(f32) * visible
    both = jnp.concatenate([tokens[0], own_upstream.astype(bf16)], -1)
    both = ring_gather(both, "ctx").reshape(length, 2 * width)
    ff_payload, triple_block, both = lax.optimization_barrier((ff_payload, triple_block, both))
    ff_block = lax.all_gather(ff_payload, "fsdp", axis=0, tiled=False)
    triple_here = triple_block[:, :split]
    gain = triple_block[:, split].astype(f32)
    shift = triple_block[:, split + 1].astype(f32)
    obias = triple_block[:, split + 2].astype(f32)

    all_tokens = both[:, :width]
    all_upstream = both[:, width:]

    input_rows = all_tokens.astype(f32)
    center = input_rows - jnp.mean(input_rows, -1, keepdims=True)
    scaling = lax.rsqrt(jnp.mean(center * center, -1, keepdims=True) + eps)
    whitened = center * scaling
    normed = (whitened * gain + shift).astype(bf16)

    owners = (me + jnp.arange(nc)) % nc
    positions = (owners[:, None] * own_rows + jnp.arange(own_rows)[None, :]).reshape(length)
    cos_full, sin_full = pair_tables(positions, 2 * head_cols)
    query_key_value = jnp.dot(normed, triple_here, preferred_element_type=f32)
    heads_shape = (length, heads_here, HEAD_DIM)
    turned = query_key_value[:, : 2 * head_cols]
    turned = turned * cos_full + swap_pairs(turned) * sin_full
    queries = (turned[:, :head_cols] * HEAD_DIM ** (-0.5)).astype(bf16).reshape(heads_shape)
    key_rows = turned[:, head_cols:].astype(bf16).reshape(heads_shape)
    value_rows = query_key_value[:, 2 * head_cols :].reshape(heads_shape).astype(bf16)
    span = prefix_length[0]
    grad_mixture = jnp.dot(all_upstream, mixer_here.T, preferred_element_type=f32).astype(bf16)
    by_head = lambda values: values.reshape(heads_shape).swapaxes(0, 1)
    mixture, grad_queries, grad_keys, grad_values = fused_attention(
        span, by_head(queries), by_head(key_rows), by_head(value_rows), by_head(grad_mixture), positions
    )
    grad_queries, grad_keys, grad_values = (
        values.swapaxes(0, 1) for values in (grad_queries, grad_keys, grad_values)
    )
    mixture = mixture.swapaxes(0, 1).reshape(length, head_cols)
    ff_block, mixture = lax.optimization_barrier((ff_block, mixture))
    inner_here = (
        ff_block[:, : nc * shard_rows]
        .reshape(nf, nc, shard_rows, ff_here)
        .swapaxes(0, 1)
        .reshape(nc * nf * shard_rows, ff_here)
    )
    outer_here = ff_block[:, nc * shard_rows :].reshape(nf * ff_rows, width)

    attention = jnp.dot(mixture, mixer_here, preferred_element_type=f32)
    preact = jnp.dot(normed, inner_here, preferred_element_type=f32) + ibias_here
    gelu_result = jax.nn.gelu(preact, approximate=True).astype(bf16)
    feedforward = jnp.dot(gelu_result, outer_here, preferred_element_type=f32)
    block_sum = ring_scatter((attention + feedforward).reshape(nc, own_rows, width), "ctx")
    layer_output = (tokens[0].astype(f32) + block_sum + obias).astype(bf16)

    ones_block = jnp.ones((length, 16), bf16)
    row_lhs = jnp.concatenate([mixture, gelu_result, ones_block], -1)
    row_product = jnp.dot(row_lhs.T, all_upstream, preferred_element_type=f32).astype(bf16)
    grad_activated = jnp.dot(all_upstream, outer_here.T, preferred_element_type=f32)
    unused_value, gelu_pull = jax.vjp(partial(jax.nn.gelu, approximate=True), preact)
    grad_before_gelu = gelu_pull(grad_activated)[0].astype(bf16)
    grad_inner_weight = jnp.dot(normed.T, grad_before_gelu, preferred_element_type=f32)
    grad_inner_bias = jnp.sum(grad_before_gelu.astype(f32), 0)
    flat_shape = (length, head_cols)
    grad_turned = jnp.concatenate(
        [(grad_queries * HEAD_DIM ** (-0.5)).reshape(flat_shape), grad_keys.reshape(flat_shape)], -1
    )
    grad_turned = grad_turned * cos_full - swap_pairs(grad_turned) * sin_full
    grad_query_key_value = jnp.concatenate(
        [grad_turned, grad_values.reshape(flat_shape)], -1
    ).astype(bf16)
    grad_triple_weight = jnp.dot(normed.T, grad_query_key_value, preferred_element_type=f32)
    grad_normed = jnp.dot(grad_query_key_value, triple_here.T, preferred_element_type=f32)
    grad_normed = grad_normed + jnp.dot(grad_before_gelu, inner_here.T, preferred_element_type=f32)
    grad_norm_gain = jnp.sum(grad_normed * whitened, 0)
    grad_norm_shift = jnp.sum(grad_normed, 0)
    grad_normed = ring_scatter(grad_normed.reshape(nc, own_rows, width), "ctx")

    own_whitened = whitened[:own_rows]
    own_scaling = scaling[:own_rows]
    grad_white = grad_normed * gain
    grad_inputs = own_scaling * (
        grad_white
        - jnp.mean(grad_white, -1, keepdims=True)
        - own_whitened * jnp.mean(grad_white * own_whitened, -1, keepdims=True)
    )
    input_grad = (own_upstream + grad_inputs).astype(bf16)

    small_grads = jnp.stack([grad_norm_gain, grad_norm_shift], -1)
    small_grads = jnp.pad(small_grads, ((0, 0), (0, 128 - small_grads.shape[-1])))
    column_grads = jnp.concatenate(
        [grad_triple_weight, grad_inner_weight, small_grads], -1
    ).astype(bf16)
    column_grads = column_grads.reshape(nc, nf, shard_rows, -1).swapaxes(0, 1).reshape(width, -1)
    column_grads = lax.psum_scatter(column_grads, "fsdp", scatter_dimension=0, tiled=True)

    mixer_part = row_product[:head_cols].reshape(nf, shard_rows, width)
    outer_part = row_product[head_cols : head_cols + ff_here].reshape(nf, ff_rows, width)
    sums_part = jnp.broadcast_to(row_product[head_cols + ff_here :][None], (nf, 16, width))
    row_grads = jnp.concatenate([mixer_part, outer_part, sums_part], 1)
    row_grads = row_grads.at[:, ff_rows + shard_rows + 1, :ff_rows].set(
        grad_inner_bias.reshape(nf, ff_rows).astype(bf16)
    )
    row_grads = lax.psum_scatter(row_grads, "fsdp", scatter_dimension=0, tiled=True)
    column_size = column_grads.size
    both_grads = jnp.concatenate([column_grads.reshape(-1), row_grads.reshape(-1)])
    both_grads = replica_sum(both_grads, "rep")
    row_grads = both_grads[column_size:].reshape(row_grads.shape[1:])
    column_grads = both_grads[:column_size].astype(bf16).reshape(nc, shard_rows, -1)
    column_grads = ring_all_to_all(column_grads, "ctx").astype(f32)
    grad_triple_out = (
        column_grads[:, :, : 3 * head_cols]
        .reshape(nc, shard_rows, 3, head_cols)
        .transpose(1, 2, 0, 3)
        .reshape(shard_rows, 3 * nc * head_cols)
    )
    grad_inner_out = (
        column_grads[:, :, 3 * head_cols : 3 * head_cols + ff_here]
        .transpose(1, 0, 2)
        .reshape(shard_rows, nc * ff_here)
    )
    grad_gain_out = jnp.sum(column_grads[:, :, 3 * head_cols + ff_here], 0)
    grad_shift_out = jnp.sum(column_grads[:, :, 3 * head_cols + ff_here + 1], 0)
    grad_mixer_out = row_grads[:shard_rows]
    grad_outer_out = row_grads[shard_rows : shard_rows + ff_rows]
    grad_ibias_out = row_grads[shard_rows + ff_rows + 1, :ff_rows]
    fsdp_me = lax.axis_index("fsdp")
    grad_obias_out = lax.dynamic_slice_in_dim(
        row_grads[shard_rows + ff_rows], (me * nf + fsdp_me) * shard_rows, shard_rows
    )

    return (
        layer_output[None],
        input_grad[None],
        grad_gain_out,
        grad_shift_out,
        grad_triple_out,
        grad_mixer_out,
        grad_inner_out,
        grad_ibias_out,
        grad_outer_out,
        grad_obias_out,
    )


def solution(mesh):
    placed = (
        P(("rep", "fsdp"), "ctx", None),
        P(("ctx", "fsdp")),
        P(("ctx", "fsdp")),
        P(("ctx", "fsdp"), None),
        P(("ctx", "fsdp"), None),
        P(("ctx", "fsdp"), None),
        P(("ctx", "fsdp")),
        P(("ctx", "fsdp"), None),
        P(("ctx", "fsdp")),
        P(("rep", "fsdp")),
        P(("rep", "fsdp")),
        P(("rep", "fsdp"), "ctx", None),
    )
    return jax.shard_map(
        local,
        mesh=mesh,
        in_specs=placed,
        out_specs=(
            P(("rep", "fsdp"), "ctx", None),
            P(("rep", "fsdp"), "ctx", None),
            P(("ctx", "fsdp")),
            P(("ctx", "fsdp")),
            P(("ctx", "fsdp"), None),
            P(("ctx", "fsdp"), None),
            P(("ctx", "fsdp"), None),
            P(("ctx", "fsdp")),
            P(("ctx", "fsdp"), None),
            P(("ctx", "fsdp")),
        ),
        check_vma=False,
    )
```

```python
from functools import partial

import jax
import jax.numpy as jnp
from jax import lax
from jax.experimental import pallas as pl
from jax.experimental.pallas import tpu as pltpu
from jax.sharding import PartitionSpec as P

HEADS = 16
HEAD_DIM = 64
ROT = 32


eps = 1e-05


def angles(positions):
    frequency = 10000.0 ** (-(jnp.arange(ROT // 2, dtype=jnp.float32) * 2.0) / ROT)
    phases = positions.astype(jnp.float32)[:, None] * frequency[None, :]
    return (jnp.cos(phases), jnp.sin(phases))


def rotate(field, cos_table, sin_table):
    leading = field.shape[:-1]
    paired = field[..., :ROT].reshape(leading + (ROT // 2, 2))
    even_part = paired[..., 0]
    odd_part = paired[..., 1]
    cos_wide = cos_table[:, None, :]
    sin_wide = sin_table[:, None, :]
    turned = jnp.stack(
        [even_part * cos_wide - odd_part * sin_wide, odd_part * cos_wide + even_part * sin_wide], -1
    )
    return jnp.concatenate([turned.reshape(leading + (ROT,)), field[..., ROT:]], -1)


def pair_tables(positions, width):
    f32 = jnp.float32
    highest = lax.Precision.HIGHEST
    cos_table, sin_table = angles(positions)
    feature = jnp.arange(width) % HEAD_DIM
    pick = (feature[None, :] // 2 == jnp.arange(ROT // 2)[:, None]) & (feature[None, :] < ROT)
    pick = pick.astype(f32)
    sign = jnp.where(feature % 2 == 0, -1.0, 1.0).astype(f32)
    cos_full = jnp.dot(cos_table, pick, precision=highest) + (feature >= ROT).astype(f32)
    sin_full = jnp.dot(sin_table, pick, precision=highest) * sign
    return cos_full, sin_full


def swap_pairs(values):
    width = values.shape[-1]
    index = jnp.arange(width)
    swap = (index[:, None] == (index[None, :] ^ 1)).astype(jnp.float32)
    return jnp.dot(values, swap, precision=lax.Precision.HIGHEST)


def ring_pairs(n, step):
    return [(i, (i + step) % n) for i in range(n)]


def ring_gather(block, axis):
    n = lax.axis_size(axis)
    half = block.shape[0] // 2
    from_left = lax.ppermute(block, axis, ring_pairs(n, 1))
    from_right = lax.ppermute(block, axis, ring_pairs(n, -1))
    far_first = lax.ppermute(from_left[:half], axis, ring_pairs(n, 1))
    far_second = lax.ppermute(from_right[half:], axis, ring_pairs(n, -1))
    far = jnp.concatenate([far_first, far_second], 0)
    return jnp.stack([block, from_right, far, from_left])


def ring_scatter(parts, axis):
    n = lax.axis_size(axis)
    half = parts.shape[1] // 2
    wire = jnp.bfloat16
    got_left = lax.ppermute(parts[2, :half].astype(wire), axis, ring_pairs(n, 1))
    got_right = lax.ppermute(parts[2, half:].astype(wire), axis, ring_pairs(n, -1))
    to_right = jnp.concatenate([parts[1, :half] + got_left.astype(jnp.float32), parts[1, half:]], 0)
    to_left = jnp.concatenate([parts[3, :half], parts[3, half:] + got_right.astype(jnp.float32)], 0)
    from_left = lax.ppermute(to_right.astype(wire), axis, ring_pairs(n, 1))
    from_right = lax.ppermute(to_left.astype(wire), axis, ring_pairs(n, -1))
    return parts[0] + from_left.astype(jnp.float32) + from_right.astype(jnp.float32)


def ring_all_to_all(payload, axis):
    n = lax.axis_size(axis)
    me = lax.axis_index(axis)
    pick = lambda d: lax.dynamic_index_in_dim(payload, d % n, 0, keepdims=False)
    got = [pick(me)] + [
        lax.ppermute(pick(me + s), axis, ring_pairs(n, s)) for s in range(1, n)
    ]
    mirrored = jnp.stack([got[(-k) % n] for k in range(n)])
    doubled = jnp.concatenate([mirrored, mirrored], 0)
    return lax.dynamic_slice_in_dim(doubled, n - me, n, 0)


def replica_sum(values, axis):
    n = lax.axis_size(axis)
    f32, wire = jnp.float32, jnp.bfloat16
    values = values.astype(wire)
    if n != 4:
        return lax.psum(values, axis).astype(f32)
    pair = values.astype(f32) + lax.ppermute(values, axis, [(i, i ^ 1) for i in range(n)]).astype(f32)
    pair = pair.astype(wire)
    return pair.astype(f32) + lax.ppermute(pair, axis, [(i, i ^ 2) for i in range(n)]).astype(f32)


def attention_kernel(span_ref, q_ref, k_ref, v_ref, gm_ref, qpos_ref, kpos_ref,
                     mix_ref, gq_ref, gk_ref, gv_ref, bias_ref):
    f32, bf16 = jnp.float32, jnp.bfloat16
    block = pl.program_id(0)
    head = pl.program_id(1)

    @pl.when(head == 0)
    def _():
        allowed = (kpos_ref[...] <= qpos_ref[...]) | (kpos_ref[...] < span_ref[0])
        bias_ref[...] = jnp.where(allowed, 0.0, -1e30).astype(f32)

    q = q_ref[...]
    k = k_ref[...]
    v = v_ref[...]
    gm = gm_ref[...]
    scores = lax.dot_general(q, k, (((1,), (1,)), ((), ())), preferred_element_type=f32)
    scores = scores + bias_ref[...]
    peak = jnp.max(scores, axis=1, keepdims=True)
    exps = jnp.exp(scores - peak)
    total = jnp.sum(exps, axis=1, keepdims=True)
    probs = exps * (1.0 / total)
    low_probs = probs.astype(bf16)
    mix_ref[...] = jnp.dot(low_probs, v, preferred_element_type=f32).astype(mix_ref.dtype)
    grad_probs = lax.dot_general(gm, v, (((1,), (1,)), ((), ())), preferred_element_type=f32)
    inner = jnp.sum(probs * grad_probs, axis=1, keepdims=True)
    grad_scores = (probs * (grad_probs - inner)).astype(bf16)
    gq_ref[...] = jnp.dot(grad_scores, k, preferred_element_type=f32)
    gk_part = lax.dot_general(grad_scores, q, (((0,), (0,)), ((), ())), preferred_element_type=f32)
    gv_part = lax.dot_general(low_probs, gm, (((0,), (0,)), ((), ())), preferred_element_type=f32)

    @pl.when(block == 0)
    def _():
        gk_ref[head] = gk_part
        gv_ref[head] = gv_part

    @pl.when(block != 0)
    def _():
        gk_ref[head] += gk_part
        gv_ref[head] += gv_part


def fused_attention(span, queries, keys, values, grad_mixture, positions, rows=256):
    heads, length, dim = queries.shape
    blocks = length // rows
    qpos = positions.reshape(length, 1).astype(jnp.int32)
    kpos = positions.reshape(1, length).astype(jnp.int32)
    row_block = pl.BlockSpec((None, rows, dim), lambda b, h, s: (h, b, 0))
    whole_head = pl.BlockSpec((None, length, dim), lambda b, h, s: (h, 0, 0))
    resident = pl.BlockSpec((heads, length, dim), lambda b, h, s: (0, 0, 0))
    f32 = jnp.float32
    return pl.pallas_call(
        attention_kernel,
        out_shape=(
            jax.ShapeDtypeStruct((heads, length, dim), jnp.bfloat16),
            jax.ShapeDtypeStruct((heads, length, dim), f32),
            jax.ShapeDtypeStruct((heads, length, dim), f32),
            jax.ShapeDtypeStruct((heads, length, dim), f32),
        ),
        grid_spec=pltpu.PrefetchScalarGridSpec(
            num_scalar_prefetch=1,
            grid=(blocks, heads),
            in_specs=[
                row_block, whole_head, whole_head, row_block,
                pl.BlockSpec((rows, 1), lambda b, h, s: (b, 0)),
                pl.BlockSpec((1, length), lambda b, h, s: (0, 0)),
            ],
            out_specs=[row_block, row_block, resident, resident],
            scratch_shapes=[pltpu.VMEM((rows, length), f32)],
        ),
        compiler_params=pltpu.CompilerParams(dimension_semantics=("arbitrary", "arbitrary")),
        cost_estimate=pl.CostEstimate(
            flops=12 * heads * length * length * dim,
            transcendentals=heads * length * length,
            bytes_accessed=heads * length * dim * (4 * 2 + 3 * 4 + 2),
        ),
    )(span.reshape(1).astype(jnp.int32), queries, keys, values, grad_mixture, qpos, kpos)


def local(
    tokens,
    norm_gain,
    norm_shift,
    triple_weight,
    mixer_weight,
    inner_weight,
    inner_bias,
    outer_weight,
    outer_bias,
    prefix_length,
    pad_mask,
    cotangent,
):
    nc = lax.axis_size("ctx")
    nf = lax.axis_size("fsdp")
    me = lax.axis_index("ctx")
    _, own_rows, width = tokens.shape
    length = own_rows * nc
    shard_rows = triple_weight.shape[0]
    heads_here = HEADS // nc
    head_cols = heads_here * HEAD_DIM
    ff_here = inner_weight.shape[1] // nc
    ff_rows = outer_weight.shape[0]
    f32, bf16 = jnp.float32, jnp.bfloat16

    triple_cols = (
        triple_weight.reshape(shard_rows, 3, nc, head_cols)
        .transpose(2, 0, 1, 3)
        .reshape(nc, shard_rows, 3 * head_cols)
    )
    inner_cols = inner_weight.reshape(shard_rows, nc, ff_here).transpose(1, 0, 2)
    small = jnp.stack([norm_gain, norm_shift, outer_bias], -1)
    small = jnp.pad(small, ((0, 0), (0, 128 - small.shape[-1])))
    small = jnp.broadcast_to(small[None], (nc,) + small.shape)
    column_payload = jnp.concatenate([triple_cols, inner_cols, small], -1)
    column_payload = ring_all_to_all(column_payload, "ctx")
    split = 3 * head_cols

    bias_rows = jnp.pad(inner_bias[None], ((0, 15), (0, width - inner_bias.shape[0])))
    triple_payload = jnp.concatenate([column_payload[..., :split], column_payload[..., split + ff_here :]], -1)
    pieces = (triple_payload, mixer_weight, bias_rows)
    first_payload = jnp.concatenate([piece.reshape(-1) for piece in pieces]).reshape(-1, width)
    first_block = lax.all_gather(first_payload, "fsdp", axis=0, tiled=False).reshape(nf, -1)
    sizes = [piece.size for piece in pieces]
    triple_block = first_block[:, : sizes[0]].reshape((nf,) + triple_payload.shape)
    triple_block = triple_block.swapaxes(0, 1).reshape(nc * nf * shard_rows, -1)
    mixer_here = first_block[:, sizes[0] : sizes[0] + sizes[1]].reshape(nf * shard_rows, width)
    ibias_here = (
        first_block[:, sizes[0] + sizes[1] : sizes[0] + sizes[1] + inner_bias.shape[0]].reshape(-1).astype(f32)
    )

    ff_payload = jnp.concatenate(
        [column_payload[..., split : split + ff_here].reshape(nc * shard_rows, ff_here), outer_weight], 0
    )
    visible = (pad_mask[0] != 0).astype(f32)
    own_upstream = cotangent[0].astype(f32) * visible
    both = jnp.concatenate([tokens[0], own_upstream.astype(bf16)], -1)
    both = ring_gather(both, "ctx").reshape(length, 2 * width)
    ff_payload, triple_block, both = lax.optimization_barrier((ff_payload, triple_block, both))
    ff_block = lax.all_gather(ff_payload, "fsdp", axis=0, tiled=False)
    triple_here = triple_block[:, :split]
    gain = triple_block[:, split].astype(f32)
    shift = triple_block[:, split + 1].astype(f32)
    obias = triple_block[:, split + 2].astype(f32)

    all_tokens = both[:, :width]
    all_upstream = both[:, width:]

    input_rows = all_tokens.astype(f32)
    center = input_rows - jnp.mean(input_rows, -1, keepdims=True)
    scaling = lax.rsqrt(jnp.mean(center * center, -1, keepdims=True) + eps)
    whitened = center * scaling
    normed = (whitened * gain + shift).astype(bf16)

    owners = (me + jnp.arange(nc)) % nc
    positions = (owners[:, None] * own_rows + jnp.arange(own_rows)[None, :]).reshape(length)
    cos_full, sin_full = pair_tables(positions, 2 * head_cols)
    query_key_value = jnp.dot(normed, triple_here, preferred_element_type=f32)
    heads_shape = (length, heads_here, HEAD_DIM)
    turned = query_key_value[:, : 2 * head_cols]
    turned = turned * cos_full + swap_pairs(turned) * sin_full
    queries = (turned[:, :head_cols] * HEAD_DIM ** (-0.5)).astype(bf16).reshape(heads_shape)
    key_rows = turned[:, head_cols:].astype(bf16).reshape(heads_shape)
    value_rows = query_key_value[:, 2 * head_cols :].reshape(heads_shape).astype(bf16)
    span = prefix_length[0]
    grad_mixture = jnp.dot(all_upstream, mixer_here.T, preferred_element_type=f32).astype(bf16)
    by_head = lambda values: values.reshape(heads_shape).swapaxes(0, 1)
    mixture, grad_queries, grad_keys, grad_values = fused_attention(
        span, by_head(queries), by_head(key_rows), by_head(value_rows), by_head(grad_mixture), positions
    )
    grad_queries, grad_keys, grad_values = (
        values.swapaxes(0, 1) for values in (grad_queries, grad_keys, grad_values)
    )
    mixture = mixture.swapaxes(0, 1).reshape(length, head_cols)
    ff_block, mixture = lax.optimization_barrier((ff_block, mixture))
    inner_here = (
        ff_block[:, : nc * shard_rows]
        .reshape(nf, nc, shard_rows, ff_here)
        .swapaxes(0, 1)
        .reshape(nc * nf * shard_rows, ff_here)
    )
    outer_here = ff_block[:, nc * shard_rows :].reshape(nf * ff_rows, width)

    attention = jnp.dot(mixture, mixer_here, preferred_element_type=f32)
    preact = jnp.dot(normed, inner_here, preferred_element_type=f32) + ibias_here
    gelu_result = jax.nn.gelu(preact, approximate=True).astype(bf16)
    feedforward = jnp.dot(gelu_result, outer_here, preferred_element_type=f32)
    block_sum = ring_scatter((attention + feedforward).reshape(nc, own_rows, width), "ctx")
    layer_output = (tokens[0].astype(f32) + block_sum + obias).astype(bf16)

    grad_activated = jnp.dot(all_upstream, outer_here.T, preferred_element_type=f32)
    unused_value, gelu_pull = jax.vjp(partial(jax.nn.gelu, approximate=True), preact)
    grad_before_gelu = gelu_pull(grad_activated)[0].astype(bf16)
    grad_inner_weight = jnp.dot(normed.T, grad_before_gelu, preferred_element_type=f32)
    grad_inner_bias = jnp.sum(grad_before_gelu.astype(f32), 0)
    flat_shape = (length, head_cols)
    grad_turned = jnp.concatenate(
        [(grad_queries * HEAD_DIM ** (-0.5)).reshape(flat_shape), grad_keys.reshape(flat_shape)], -1
    )
    grad_turned = grad_turned * cos_full - swap_pairs(grad_turned) * sin_full
    grad_query_key_value = jnp.concatenate(
        [grad_turned, grad_values.reshape(flat_shape)], -1
    ).astype(bf16)
    grad_triple_weight = jnp.dot(normed.T, grad_query_key_value, preferred_element_type=f32)
    grad_normed = jnp.dot(grad_query_key_value, triple_here.T, preferred_element_type=f32)
    grad_normed = grad_normed + jnp.dot(grad_before_gelu, inner_here.T, preferred_element_type=f32)
    grad_norm_gain = jnp.sum(grad_normed * whitened, 0)
    grad_norm_shift = jnp.sum(grad_normed, 0)
    grad_normed = ring_scatter(grad_normed.reshape(nc, own_rows, width), "ctx")

    own_whitened = whitened[:own_rows]
    own_scaling = scaling[:own_rows]
    grad_white = grad_normed * gain
    grad_inputs = own_scaling * (
        grad_white
        - jnp.mean(grad_white, -1, keepdims=True)
        - own_whitened * jnp.mean(grad_white * own_whitened, -1, keepdims=True)
    )
    input_grad = (own_upstream + grad_inputs).astype(bf16)

    small_grads = jnp.stack([grad_norm_gain, grad_norm_shift], -1)
    small_grads = jnp.pad(small_grads, ((0, 0), (0, 128 - small_grads.shape[-1])))
    column_grads = jnp.concatenate(
        [grad_triple_weight, grad_inner_weight, small_grads], -1
    ).astype(bf16)
    column_grads = column_grads.reshape(nc, nf, shard_rows, -1).swapaxes(0, 1).reshape(width, -1)
    column_grads, mixture_late = lax.optimization_barrier((column_grads, mixture))
    ones_block = jnp.ones((length, 16), bf16)
    row_lhs = jnp.concatenate([mixture_late, gelu_result, ones_block], -1)
    row_product = jnp.dot(row_lhs.T, all_upstream, preferred_element_type=f32).astype(bf16)
    column_grads = lax.psum_scatter(column_grads, "fsdp", scatter_dimension=0, tiled=True)
    column_scattered = column_grads
    column_grads = replica_sum(column_grads, "rep").astype(bf16)
    column_grads = column_grads.reshape(nc, shard_rows, -1)
    column_grads = ring_all_to_all(column_grads, "ctx").astype(f32)
    grad_triple_out = (
        column_grads[:, :, : 3 * head_cols]
        .reshape(nc, shard_rows, 3, head_cols)
        .transpose(1, 2, 0, 3)
        .reshape(shard_rows, 3 * nc * head_cols)
    )
    grad_inner_out = (
        column_grads[:, :, 3 * head_cols : 3 * head_cols + ff_here]
        .transpose(1, 0, 2)
        .reshape(shard_rows, nc * ff_here)
    )
    grad_gain_out = jnp.sum(column_grads[:, :, 3 * head_cols + ff_here], 0)
    grad_shift_out = jnp.sum(column_grads[:, :, 3 * head_cols + ff_here + 1], 0)

    mixer_part = row_product[:head_cols].reshape(nf, shard_rows, width)
    outer_part = row_product[head_cols : head_cols + ff_here].reshape(nf, ff_rows, width)
    sums_part = jnp.broadcast_to(row_product[head_cols + ff_here :][None], (nf, 16, width))
    row_grads = jnp.concatenate([mixer_part, outer_part, sums_part], 1)
    row_grads = row_grads.at[:, ff_rows + shard_rows + 1, :ff_rows].set(
        grad_inner_bias.reshape(nf, ff_rows).astype(bf16)
    )
    row_grads, column_scattered = lax.optimization_barrier((row_grads, column_scattered))
    row_grads = lax.psum_scatter(row_grads, "fsdp", scatter_dimension=0, tiled=True)
    row_grads = replica_sum(row_grads, "rep")[0]
    grad_mixer_out = row_grads[:shard_rows]
    grad_outer_out = row_grads[shard_rows : shard_rows + ff_rows]
    grad_ibias_out = row_grads[shard_rows + ff_rows + 1, :ff_rows]
    fsdp_me = lax.axis_index("fsdp")
    grad_obias_out = lax.dynamic_slice_in_dim(
        row_grads[shard_rows + ff_rows], (me * nf + fsdp_me) * shard_rows, shard_rows
    )

    return (
        layer_output[None],
        input_grad[None],
        grad_gain_out,
        grad_shift_out,
        grad_triple_out,
        grad_mixer_out,
        grad_inner_out,
        grad_ibias_out,
        grad_outer_out,
        grad_obias_out,
    )


def solution(mesh):
    placed = (
        P(("rep", "fsdp"), "ctx", None),
        P(("ctx", "fsdp")),
        P(("ctx", "fsdp")),
        P(("ctx", "fsdp"), None),
        P(("ctx", "fsdp"), None),
        P(("ctx", "fsdp"), None),
        P(("ctx", "fsdp")),
        P(("ctx", "fsdp"), None),
        P(("ctx", "fsdp")),
        P(("rep", "fsdp")),
        P(("rep", "fsdp")),
        P(("rep", "fsdp"), "ctx", None),
    )
    return jax.shard_map(
        local,
        mesh=mesh,
        in_specs=placed,
        out_specs=(
            P(("rep", "fsdp"), "ctx", None),
            P(("rep", "fsdp"), "ctx", None),
            P(("ctx", "fsdp")),
            P(("ctx", "fsdp")),
            P(("ctx", "fsdp"), None),
            P(("ctx", "fsdp"), None),
            P(("ctx", "fsdp"), None),
            P(("ctx", "fsdp")),
            P(("ctx", "fsdp"), None),
            P(("ctx", "fsdp")),
        ),
        check_vma=False,
    )
```

```python
from functools import partial

import jax
import jax.numpy as jnp
from jax import lax
from jax.experimental import pallas as pl
from jax.experimental.pallas import tpu as pltpu
from jax.sharding import PartitionSpec as P

HEADS = 16
HEAD_DIM = 64
ROT = 32


eps = 1e-05


def angles(positions):
    frequency = 10000.0 ** (-(jnp.arange(ROT // 2, dtype=jnp.float32) * 2.0) / ROT)
    phases = positions.astype(jnp.float32)[:, None] * frequency[None, :]
    return (jnp.cos(phases), jnp.sin(phases))


def rotate(field, cos_table, sin_table):
    leading = field.shape[:-1]
    paired = field[..., :ROT].reshape(leading + (ROT // 2, 2))
    even_part = paired[..., 0]
    odd_part = paired[..., 1]
    cos_wide = cos_table[:, None, :]
    sin_wide = sin_table[:, None, :]
    turned = jnp.stack(
        [even_part * cos_wide - odd_part * sin_wide, odd_part * cos_wide + even_part * sin_wide], -1
    )
    return jnp.concatenate([turned.reshape(leading + (ROT,)), field[..., ROT:]], -1)


def pair_tables(positions, width):
    f32 = jnp.float32
    highest = lax.Precision.HIGHEST
    cos_table, sin_table = angles(positions)
    feature = jnp.arange(width) % HEAD_DIM
    pick = (feature[None, :] // 2 == jnp.arange(ROT // 2)[:, None]) & (feature[None, :] < ROT)
    pick = pick.astype(f32)
    sign = jnp.where(feature % 2 == 0, -1.0, 1.0).astype(f32)
    cos_full = jnp.dot(cos_table, pick, precision=highest) + (feature >= ROT).astype(f32)
    sin_full = jnp.dot(sin_table, pick, precision=highest) * sign
    return cos_full, sin_full


def swap_pairs(values):
    width = values.shape[-1]
    index = jnp.arange(width)
    swap = (index[:, None] == (index[None, :] ^ 1)).astype(jnp.float32)
    return jnp.dot(values, swap, precision=lax.Precision.HIGHEST)


def ring_pairs(n, step):
    return [(i, (i + step) % n) for i in range(n)]


def ring_gather(block, axis):
    n = lax.axis_size(axis)
    half = block.shape[0] // 2
    from_left = lax.ppermute(block, axis, ring_pairs(n, 1))
    from_right = lax.ppermute(block, axis, ring_pairs(n, -1))
    far_first = lax.ppermute(from_left[:half], axis, ring_pairs(n, 1))
    far_second = lax.ppermute(from_right[half:], axis, ring_pairs(n, -1))
    far = jnp.concatenate([far_first, far_second], 0)
    return jnp.stack([block, from_right, far, from_left])


def ring_scatter(parts, axis):
    n = lax.axis_size(axis)
    half = parts.shape[1] // 2
    wire = jnp.bfloat16
    got_left = lax.ppermute(parts[2, :half].astype(wire), axis, ring_pairs(n, 1))
    got_right = lax.ppermute(parts[2, half:].astype(wire), axis, ring_pairs(n, -1))
    to_right = jnp.concatenate([parts[1, :half] + got_left.astype(jnp.float32), parts[1, half:]], 0)
    to_left = jnp.concatenate([parts[3, :half], parts[3, half:] + got_right.astype(jnp.float32)], 0)
    from_left = lax.ppermute(to_right.astype(wire), axis, ring_pairs(n, 1))
    from_right = lax.ppermute(to_left.astype(wire), axis, ring_pairs(n, -1))
    return parts[0] + from_left.astype(jnp.float32) + from_right.astype(jnp.float32)


def ring_all_to_all(payload, axis):
    n = lax.axis_size(axis)
    me = lax.axis_index(axis)
    pick = lambda d: lax.dynamic_index_in_dim(payload, d % n, 0, keepdims=False)
    got = [pick(me)] + [
        lax.ppermute(pick(me + s), axis, ring_pairs(n, s)) for s in range(1, n)
    ]
    mirrored = jnp.stack([got[(-k) % n] for k in range(n)])
    doubled = jnp.concatenate([mirrored, mirrored], 0)
    return lax.dynamic_slice_in_dim(doubled, n - me, n, 0)


def replica_sum(values, axis):
    n = lax.axis_size(axis)
    f32, wire = jnp.float32, jnp.bfloat16
    values = values.astype(wire)
    if n != 4:
        return lax.psum(values, axis).astype(f32)
    pair = values.astype(f32) + lax.ppermute(values, axis, [(i, i ^ 1) for i in range(n)]).astype(f32)
    pair = pair.astype(wire)
    return pair.astype(f32) + lax.ppermute(pair, axis, [(i, i ^ 2) for i in range(n)]).astype(f32)


def attention_kernel(span_ref, q_ref, k_ref, v_ref, gm_ref, qpos_ref, kpos_ref,
                     mix_ref, gq_ref, gk_ref, gv_ref, bias_ref):
    f32, bf16 = jnp.float32, jnp.bfloat16
    block = pl.program_id(0)
    head = pl.program_id(1)

    @pl.when(head == 0)
    def _():
        allowed = (kpos_ref[...] <= qpos_ref[...]) | (kpos_ref[...] < span_ref[0])
        bias_ref[...] = jnp.where(allowed, 0.0, -1e30).astype(f32)

    q = q_ref[...]
    k = k_ref[...]
    v = v_ref[...]
    gm = gm_ref[...]
    scores = lax.dot_general(q, k, (((1,), (1,)), ((), ())), preferred_element_type=f32)
    scores = scores + bias_ref[...]
    peak = jnp.max(scores, axis=1, keepdims=True)
    exps = jnp.exp(scores - peak)
    total = jnp.sum(exps, axis=1, keepdims=True)
    probs = exps * (1.0 / total)
    low_probs = probs.astype(bf16)
    mix_ref[...] = jnp.dot(low_probs, v, preferred_element_type=f32).astype(mix_ref.dtype)
    grad_probs = lax.dot_general(gm, v, (((1,), (1,)), ((), ())), preferred_element_type=f32)
    inner = jnp.sum(probs * grad_probs, axis=1, keepdims=True)
    grad_scores = (probs * (grad_probs - inner)).astype(bf16)
    gq_ref[...] = jnp.dot(grad_scores, k, preferred_element_type=f32)
    gk_part = lax.dot_general(grad_scores, q, (((0,), (0,)), ((), ())), preferred_element_type=f32)
    gv_part = lax.dot_general(low_probs, gm, (((0,), (0,)), ((), ())), preferred_element_type=f32)

    @pl.when(block == 0)
    def _():
        gk_ref[head] = gk_part
        gv_ref[head] = gv_part

    @pl.when(block != 0)
    def _():
        gk_ref[head] += gk_part
        gv_ref[head] += gv_part


def fused_attention(span, queries, keys, values, grad_mixture, positions, rows=512):
    heads, length, dim = queries.shape
    blocks = length // rows
    qpos = positions.reshape(length, 1).astype(jnp.int32)
    kpos = positions.reshape(1, length).astype(jnp.int32)
    row_block = pl.BlockSpec((None, rows, dim), lambda b, h, s: (h, b, 0))
    whole_head = pl.BlockSpec((None, length, dim), lambda b, h, s: (h, 0, 0))
    resident = pl.BlockSpec((heads, length, dim), lambda b, h, s: (0, 0, 0))
    f32 = jnp.float32
    return pl.pallas_call(
        attention_kernel,
        out_shape=(
            jax.ShapeDtypeStruct((heads, length, dim), jnp.bfloat16),
            jax.ShapeDtypeStruct((heads, length, dim), f32),
            jax.ShapeDtypeStruct((heads, length, dim), f32),
            jax.ShapeDtypeStruct((heads, length, dim), f32),
        ),
        grid_spec=pltpu.PrefetchScalarGridSpec(
            num_scalar_prefetch=1,
            grid=(blocks, heads),
            in_specs=[
                row_block, whole_head, whole_head, row_block,
                pl.BlockSpec((rows, 1), lambda b, h, s: (b, 0)),
                pl.BlockSpec((1, length), lambda b, h, s: (0, 0)),
            ],
            out_specs=[row_block, row_block, resident, resident],
            scratch_shapes=[pltpu.VMEM((rows, length), f32)],
        ),
        compiler_params=pltpu.CompilerParams(dimension_semantics=("arbitrary", "arbitrary")),
        cost_estimate=pl.CostEstimate(
            flops=12 * heads * length * length * dim,
            transcendentals=heads * length * length,
            bytes_accessed=heads * length * dim * (4 * 2 + 3 * 4 + 2),
        ),
    )(span.reshape(1).astype(jnp.int32), queries, keys, values, grad_mixture, qpos, kpos)


def local(
    tokens,
    norm_gain,
    norm_shift,
    triple_weight,
    mixer_weight,
    inner_weight,
    inner_bias,
    outer_weight,
    outer_bias,
    prefix_length,
    pad_mask,
    cotangent,
):
    nc = lax.axis_size("ctx")
    nf = lax.axis_size("fsdp")
    me = lax.axis_index("ctx")
    _, own_rows, width = tokens.shape
    length = own_rows * nc
    shard_rows = triple_weight.shape[0]
    heads_here = HEADS // nc
    head_cols = heads_here * HEAD_DIM
    ff_here = inner_weight.shape[1] // nc
    ff_rows = outer_weight.shape[0]
    f32, bf16 = jnp.float32, jnp.bfloat16

    triple_cols = (
        triple_weight.reshape(shard_rows, 3, nc, head_cols)
        .transpose(2, 0, 1, 3)
        .reshape(nc, shard_rows, 3 * head_cols)
    )
    inner_cols = inner_weight.reshape(shard_rows, nc, ff_here).transpose(1, 0, 2)
    small = jnp.stack([norm_gain, norm_shift, outer_bias], -1)
    small = jnp.pad(small, ((0, 0), (0, 128 - small.shape[-1])))
    small = jnp.broadcast_to(small[None], (nc,) + small.shape)
    column_payload = jnp.concatenate([triple_cols, inner_cols, small], -1)
    column_payload = ring_all_to_all(column_payload, "ctx")
    split = 3 * head_cols

    bias_rows = jnp.pad(inner_bias[None], ((0, 15), (0, width - inner_bias.shape[0])))
    triple_payload = jnp.concatenate([column_payload[..., :split], column_payload[..., split + ff_here :]], -1)
    pieces = (triple_payload, mixer_weight, bias_rows)
    first_payload = jnp.concatenate([piece.reshape(-1) for piece in pieces]).reshape(-1, width)
    first_block = lax.all_gather(first_payload, "fsdp", axis=0, tiled=False).reshape(nf, -1)
    sizes = [piece.size for piece in pieces]
    triple_block = first_block[:, : sizes[0]].reshape((nf,) + triple_payload.shape)
    triple_block = triple_block.swapaxes(0, 1).reshape(nc * nf * shard_rows, -1)
    mixer_here = first_block[:, sizes[0] : sizes[0] + sizes[1]].reshape(nf * shard_rows, width)
    ibias_here = (
        first_block[:, sizes[0] + sizes[1] : sizes[0] + sizes[1] + inner_bias.shape[0]].reshape(-1).astype(f32)
    )

    ff_payload = jnp.concatenate(
        [column_payload[..., split : split + ff_here].reshape(nc * shard_rows, ff_here), outer_weight], 0
    )
    visible = (pad_mask[0] != 0).astype(f32)
    own_upstream = cotangent[0].astype(f32) * visible
    both = jnp.concatenate([tokens[0], own_upstream.astype(bf16)], -1)
    both = ring_gather(both, "ctx").reshape(length, 2 * width)
    ff_payload, triple_block, both = lax.optimization_barrier((ff_payload, triple_block, both))
    ff_block = lax.all_gather(ff_payload, "fsdp", axis=0, tiled=False)
    triple_here = triple_block[:, :split]
    gain = triple_block[:, split].astype(f32)
    shift = triple_block[:, split + 1].astype(f32)
    obias = triple_block[:, split + 2].astype(f32)

    all_tokens = both[:, :width]
    all_upstream = both[:, width:]

    input_rows = all_tokens.astype(f32)
    center = input_rows - jnp.mean(input_rows, -1, keepdims=True)
    scaling = lax.rsqrt(jnp.mean(center * center, -1, keepdims=True) + eps)
    whitened = center * scaling
    normed = (whitened * gain + shift).astype(bf16)

    owners = (me + jnp.arange(nc)) % nc
    positions = (owners[:, None] * own_rows + jnp.arange(own_rows)[None, :]).reshape(length)
    cos_full, sin_full = pair_tables(positions, 2 * head_cols)
    query_key_value = jnp.dot(normed, triple_here, preferred_element_type=f32)
    heads_shape = (length, heads_here, HEAD_DIM)
    turned = query_key_value[:, : 2 * head_cols]
    turned = turned * cos_full + swap_pairs(turned) * sin_full
    queries = (turned[:, :head_cols] * HEAD_DIM ** (-0.5)).astype(bf16).reshape(heads_shape)
    key_rows = turned[:, head_cols:].astype(bf16).reshape(heads_shape)
    value_rows = query_key_value[:, 2 * head_cols :].reshape(heads_shape).astype(bf16)
    span = prefix_length[0]
    grad_mixture = jnp.dot(all_upstream, mixer_here.T, preferred_element_type=f32).astype(bf16)
    by_head = lambda values: values.reshape(heads_shape).swapaxes(0, 1)
    mixture, grad_queries, grad_keys, grad_values = fused_attention(
        span, by_head(queries), by_head(key_rows), by_head(value_rows), by_head(grad_mixture), positions
    )
    grad_queries, grad_keys, grad_values = (
        values.swapaxes(0, 1) for values in (grad_queries, grad_keys, grad_values)
    )
    mixture = mixture.swapaxes(0, 1).reshape(length, head_cols)
    ff_block, mixture = lax.optimization_barrier((ff_block, mixture))
    inner_here = (
        ff_block[:, : nc * shard_rows]
        .reshape(nf, nc, shard_rows, ff_here)
        .swapaxes(0, 1)
        .reshape(nc * nf * shard_rows, ff_here)
    )
    outer_here = ff_block[:, nc * shard_rows :].reshape(nf * ff_rows, width)

    attention = jnp.dot(mixture, mixer_here, preferred_element_type=f32)
    preact = jnp.dot(normed, inner_here, preferred_element_type=f32) + ibias_here
    gelu_result = jax.nn.gelu(preact, approximate=True).astype(bf16)
    feedforward = jnp.dot(gelu_result, outer_here, preferred_element_type=f32)
    block_sum = ring_scatter((attention + feedforward).reshape(nc, own_rows, width), "ctx")
    layer_output = (tokens[0].astype(f32) + block_sum + obias).astype(bf16)

    ones_block = jnp.ones((length, 16), bf16)
    row_lhs = jnp.concatenate([mixture, gelu_result, ones_block], -1)
    row_product = jnp.dot(row_lhs.T, all_upstream, preferred_element_type=f32).astype(bf16)
    grad_activated = jnp.dot(all_upstream, outer_here.T, preferred_element_type=f32)
    unused_value, gelu_pull = jax.vjp(partial(jax.nn.gelu, approximate=True), preact)
    grad_before_gelu = gelu_pull(grad_activated)[0].astype(bf16)
    grad_inner_weight = jnp.dot(normed.T, grad_before_gelu, preferred_element_type=f32)
    grad_inner_bias = jnp.sum(grad_before_gelu.astype(f32), 0)
    flat_shape = (length, head_cols)
    grad_turned = jnp.concatenate(
        [(grad_queries * HEAD_DIM ** (-0.5)).reshape(flat_shape), grad_keys.reshape(flat_shape)], -1
    )
    grad_turned = grad_turned * cos_full - swap_pairs(grad_turned) * sin_full
    grad_query_key_value = jnp.concatenate(
        [grad_turned, grad_values.reshape(flat_shape)], -1
    ).astype(bf16)
    grad_triple_weight = jnp.dot(normed.T, grad_query_key_value, preferred_element_type=f32)
    grad_normed = jnp.dot(grad_query_key_value, triple_here.T, preferred_element_type=f32)
    grad_normed = grad_normed + jnp.dot(grad_before_gelu, inner_here.T, preferred_element_type=f32)
    grad_norm_gain = jnp.sum(grad_normed * whitened, 0)
    grad_norm_shift = jnp.sum(grad_normed, 0)
    grad_normed = ring_scatter(grad_normed.reshape(nc, own_rows, width), "ctx")

    own_whitened = whitened[:own_rows]
    own_scaling = scaling[:own_rows]
    grad_white = grad_normed * gain
    grad_inputs = own_scaling * (
        grad_white
        - jnp.mean(grad_white, -1, keepdims=True)
        - own_whitened * jnp.mean(grad_white * own_whitened, -1, keepdims=True)
    )
    input_grad = (own_upstream + grad_inputs).astype(bf16)

    small_grads = jnp.stack([grad_norm_gain, grad_norm_shift], -1)
    small_grads = jnp.pad(small_grads, ((0, 0), (0, 128 - small_grads.shape[-1])))
    column_grads = jnp.concatenate(
        [grad_triple_weight, grad_inner_weight, small_grads], -1
    ).astype(bf16)
    column_grads = column_grads.reshape(nc, nf, shard_rows, -1).swapaxes(0, 1).reshape(width, -1)
    column_grads = lax.psum_scatter(column_grads, "fsdp", scatter_dimension=0, tiled=True)
    column_grads = replica_sum(column_grads, "rep").astype(bf16)
    column_grads = column_grads.reshape(nc, shard_rows, -1)
    column_grads = ring_all_to_all(column_grads, "ctx").astype(f32)
    grad_triple_out = (
        column_grads[:, :, : 3 * head_cols]
        .reshape(nc, shard_rows, 3, head_cols)
        .transpose(1, 2, 0, 3)
        .reshape(shard_rows, 3 * nc * head_cols)
    )
    grad_inner_out = (
        column_grads[:, :, 3 * head_cols : 3 * head_cols + ff_here]
        .transpose(1, 0, 2)
        .reshape(shard_rows, nc * ff_here)
    )
    grad_gain_out = jnp.sum(column_grads[:, :, 3 * head_cols + ff_here], 0)
    grad_shift_out = jnp.sum(column_grads[:, :, 3 * head_cols + ff_here + 1], 0)

    mixer_part = row_product[:head_cols].reshape(nf, shard_rows, width)
    outer_part = row_product[head_cols : head_cols + ff_here].reshape(nf, ff_rows, width)
    sums_part = jnp.broadcast_to(row_product[head_cols + ff_here :][None], (nf, 16, width))
    row_grads = jnp.concatenate([mixer_part, outer_part, sums_part], 1)
    row_grads = row_grads.at[:, ff_rows + shard_rows + 1, :ff_rows].set(
        grad_inner_bias.reshape(nf, ff_rows).astype(bf16)
    )
    row_grads = lax.psum_scatter(row_grads, "fsdp", scatter_dimension=0, tiled=True)
    row_grads = replica_sum(row_grads, "rep")[0]
    grad_mixer_out = row_grads[:shard_rows]
    grad_outer_out = row_grads[shard_rows : shard_rows + ff_rows]
    grad_ibias_out = row_grads[shard_rows + ff_rows + 1, :ff_rows]
    fsdp_me = lax.axis_index("fsdp")
    grad_obias_out = lax.dynamic_slice_in_dim(
        row_grads[shard_rows + ff_rows], (me * nf + fsdp_me) * shard_rows, shard_rows
    )

    return (
        layer_output[None],
        input_grad[None],
        grad_gain_out,
        grad_shift_out,
        grad_triple_out,
        grad_mixer_out,
        grad_inner_out,
        grad_ibias_out,
        grad_outer_out,
        grad_obias_out,
    )


def solution(mesh):
    placed = (
        P(("rep", "fsdp"), "ctx", None),
        P(("ctx", "fsdp")),
        P(("ctx", "fsdp")),
        P(("ctx", "fsdp"), None),
        P(("ctx", "fsdp"), None),
        P(("ctx", "fsdp"), None),
        P(("ctx", "fsdp")),
        P(("ctx", "fsdp"), None),
        P(("ctx", "fsdp")),
        P(("rep", "fsdp")),
        P(("rep", "fsdp")),
        P(("rep", "fsdp"), "ctx", None),
    )
    return jax.shard_map(
        local,
        mesh=mesh,
        in_specs=placed,
        out_specs=(
            P(("rep", "fsdp"), "ctx", None),
            P(("rep", "fsdp"), "ctx", None),
            P(("ctx", "fsdp")),
            P(("ctx", "fsdp")),
            P(("ctx", "fsdp"), None),
            P(("ctx", "fsdp"), None),
            P(("ctx", "fsdp"), None),
            P(("ctx", "fsdp")),
            P(("ctx", "fsdp"), None),
            P(("ctx", "fsdp")),
        ),
        check_vma=False,
    )
```

```python
from functools import partial

import jax
import jax.numpy as jnp
from jax import lax
from jax.experimental import pallas as pl
from jax.experimental.pallas import tpu as pltpu
from jax.sharding import PartitionSpec as P

HEADS = 16
HEAD_DIM = 64
ROT = 32


eps = 1e-05


def angles(positions):
    frequency = 10000.0 ** (-(jnp.arange(ROT // 2, dtype=jnp.float32) * 2.0) / ROT)
    phases = positions.astype(jnp.float32)[:, None] * frequency[None, :]
    return (jnp.cos(phases), jnp.sin(phases))


def rotate(field, cos_table, sin_table):
    leading = field.shape[:-1]
    paired = field[..., :ROT].reshape(leading + (ROT // 2, 2))
    even_part = paired[..., 0]
    odd_part = paired[..., 1]
    cos_wide = cos_table[:, None, :]
    sin_wide = sin_table[:, None, :]
    turned = jnp.stack(
        [even_part * cos_wide - odd_part * sin_wide, odd_part * cos_wide + even_part * sin_wide], -1
    )
    return jnp.concatenate([turned.reshape(leading + (ROT,)), field[..., ROT:]], -1)


def pair_tables(positions, width):
    f32 = jnp.float32
    highest = lax.Precision.HIGHEST
    cos_table, sin_table = angles(positions)
    feature = jnp.arange(width) % HEAD_DIM
    pick = (feature[None, :] // 2 == jnp.arange(ROT // 2)[:, None]) & (feature[None, :] < ROT)
    pick = pick.astype(f32)
    sign = jnp.where(feature % 2 == 0, -1.0, 1.0).astype(f32)
    cos_full = jnp.dot(cos_table, pick, precision=highest) + (feature >= ROT).astype(f32)
    sin_full = jnp.dot(sin_table, pick, precision=highest) * sign
    return cos_full, sin_full


def swap_pairs(values):
    width = values.shape[-1]
    index = jnp.arange(width)
    swap = (index[:, None] == (index[None, :] ^ 1)).astype(jnp.float32)
    return jnp.dot(values, swap, precision=lax.Precision.HIGHEST)


def ring_pairs(n, step):
    return [(i, (i + step) % n) for i in range(n)]


def ring_gather(block, axis):
    n = lax.axis_size(axis)
    half = block.shape[0] // 2
    from_left = lax.ppermute(block, axis, ring_pairs(n, 1))
    from_right = lax.ppermute(block, axis, ring_pairs(n, -1))
    far_first = lax.ppermute(from_left[:half], axis, ring_pairs(n, 1))
    far_second = lax.ppermute(from_right[half:], axis, ring_pairs(n, -1))
    far = jnp.concatenate([far_first, far_second], 0)
    return jnp.stack([block, from_right, far, from_left])


def ring_scatter(parts, axis):
    n = lax.axis_size(axis)
    half = parts.shape[1] // 2
    wire = jnp.bfloat16
    got_left = lax.ppermute(parts[2, :half].astype(wire), axis, ring_pairs(n, 1))
    got_right = lax.ppermute(parts[2, half:].astype(wire), axis, ring_pairs(n, -1))
    to_right = jnp.concatenate([parts[1, :half] + got_left.astype(jnp.float32), parts[1, half:]], 0)
    to_left = jnp.concatenate([parts[3, :half], parts[3, half:] + got_right.astype(jnp.float32)], 0)
    from_left = lax.ppermute(to_right.astype(wire), axis, ring_pairs(n, 1))
    from_right = lax.ppermute(to_left.astype(wire), axis, ring_pairs(n, -1))
    return parts[0] + from_left.astype(jnp.float32) + from_right.astype(jnp.float32)


def ring_all_to_all(payload, axis):
    n = lax.axis_size(axis)
    me = lax.axis_index(axis)
    pick = lambda d: lax.dynamic_index_in_dim(payload, d % n, 0, keepdims=False)
    got = [pick(me)] + [
        lax.ppermute(pick(me + s), axis, ring_pairs(n, s)) for s in range(1, n)
    ]
    mirrored = jnp.stack([got[(-k) % n] for k in range(n)])
    doubled = jnp.concatenate([mirrored, mirrored], 0)
    return lax.dynamic_slice_in_dim(doubled, n - me, n, 0)


def replica_sum(values, axis):
    n = lax.axis_size(axis)
    f32, wire = jnp.float32, jnp.bfloat16
    values = values.astype(wire)
    if n != 4:
        return lax.psum(values, axis).astype(f32)
    pair = values.astype(f32) + lax.ppermute(values, axis, [(i, i ^ 1) for i in range(n)]).astype(f32)
    pair = pair.astype(wire)
    return pair.astype(f32) + lax.ppermute(pair, axis, [(i, i ^ 2) for i in range(n)]).astype(f32)


def attention_kernel(span_ref, q_ref, k_ref, v_ref, gm_ref, qpos_ref, kpos_ref,
                     mix_ref, gq_ref, gk_ref, gv_ref, bias_ref):
    f32, bf16 = jnp.float32, jnp.bfloat16
    block = pl.program_id(0)
    head = pl.program_id(1)

    @pl.when(head == 0)
    def _():
        allowed = (kpos_ref[...] <= qpos_ref[...]) | (kpos_ref[...] < span_ref[0])
        bias_ref[...] = jnp.where(allowed, 0.0, -1e30).astype(f32)

    q = q_ref[...]
    k = k_ref[...]
    v = v_ref[...]
    gm = gm_ref[...]
    scores = lax.dot_general(q, k, (((1,), (1,)), ((), ())), preferred_element_type=f32)
    scores = scores + bias_ref[...]
    peak = jnp.max(scores, axis=1, keepdims=True)
    exps = jnp.exp(scores - peak)
    total = jnp.sum(exps, axis=1, keepdims=True)
    probs = exps * (1.0 / total)
    low_probs = probs.astype(bf16)
    mix_ref[...] = jnp.dot(low_probs, v, preferred_element_type=f32).astype(mix_ref.dtype)
    grad_probs = lax.dot_general(gm, v, (((1,), (1,)), ((), ())), preferred_element_type=f32)
    inner = jnp.sum(probs * grad_probs, axis=1, keepdims=True)
    grad_scores = (probs * (grad_probs - inner)).astype(bf16)
    gq_ref[...] = jnp.dot(grad_scores, k, preferred_element_type=f32)
    gk_part = lax.dot_general(grad_scores, q, (((0,), (0,)), ((), ())), preferred_element_type=f32)
    gv_part = lax.dot_general(low_probs, gm, (((0,), (0,)), ((), ())), preferred_element_type=f32)

    @pl.when(block == 0)
    def _():
        gk_ref[head] = gk_part
        gv_ref[head] = gv_part

    @pl.when(block != 0)
    def _():
        gk_ref[head] += gk_part
        gv_ref[head] += gv_part


def fused_attention(span, queries, keys, values, grad_mixture, positions, rows=1024):
    heads, length, dim = queries.shape
    blocks = length // rows
    qpos = positions.reshape(length, 1).astype(jnp.int32)
    kpos = positions.reshape(1, length).astype(jnp.int32)
    row_block = pl.BlockSpec((None, rows, dim), lambda b, h, s: (h, b, 0))
    whole_head = pl.BlockSpec((None, length, dim), lambda b, h, s: (h, 0, 0))
    resident = pl.BlockSpec((heads, length, dim), lambda b, h, s: (0, 0, 0))
    f32 = jnp.float32
    return pl.pallas_call(
        attention_kernel,
        out_shape=(
            jax.ShapeDtypeStruct((heads, length, dim), jnp.bfloat16),
            jax.ShapeDtypeStruct((heads, length, dim), f32),
            jax.ShapeDtypeStruct((heads, length, dim), f32),
            jax.ShapeDtypeStruct((heads, length, dim), f32),
        ),
        grid_spec=pltpu.PrefetchScalarGridSpec(
            num_scalar_prefetch=1,
            grid=(blocks, heads),
            in_specs=[
                row_block, whole_head, whole_head, row_block,
                pl.BlockSpec((rows, 1), lambda b, h, s: (b, 0)),
                pl.BlockSpec((1, length), lambda b, h, s: (0, 0)),
            ],
            out_specs=[row_block, row_block, resident, resident],
            scratch_shapes=[pltpu.VMEM((rows, length), f32)],
        ),
        compiler_params=pltpu.CompilerParams(dimension_semantics=("arbitrary", "arbitrary")),
        cost_estimate=pl.CostEstimate(
            flops=12 * heads * length * length * dim,
            transcendentals=heads * length * length,
            bytes_accessed=heads * length * dim * (4 * 2 + 3 * 4 + 2),
        ),
    )(span.reshape(1).astype(jnp.int32), queries, keys, values, grad_mixture, qpos, kpos)


def local(
    tokens,
    norm_gain,
    norm_shift,
    triple_weight,
    mixer_weight,
    inner_weight,
    inner_bias,
    outer_weight,
    outer_bias,
    prefix_length,
    pad_mask,
    cotangent,
):
    nc = lax.axis_size("ctx")
    nf = lax.axis_size("fsdp")
    me = lax.axis_index("ctx")
    _, own_rows, width = tokens.shape
    length = own_rows * nc
    shard_rows = triple_weight.shape[0]
    heads_here = HEADS // nc
    head_cols = heads_here * HEAD_DIM
    ff_here = inner_weight.shape[1] // nc
    ff_rows = outer_weight.shape[0]
    f32, bf16 = jnp.float32, jnp.bfloat16

    triple_cols = (
        triple_weight.reshape(shard_rows, 3, nc, head_cols)
        .transpose(2, 0, 1, 3)
        .reshape(nc, shard_rows, 3 * head_cols)
    )
    inner_cols = inner_weight.reshape(shard_rows, nc, ff_here).transpose(1, 0, 2)
    small = jnp.stack([norm_gain, norm_shift, outer_bias], -1)
    small = jnp.pad(small, ((0, 0), (0, 128 - small.shape[-1])))
    small = jnp.broadcast_to(small[None], (nc,) + small.shape)
    column_payload = jnp.concatenate([triple_cols, inner_cols, small], -1)
    column_payload = ring_all_to_all(column_payload, "ctx")
    split = 3 * head_cols

    bias_rows = jnp.pad(inner_bias[None], ((0, 15), (0, width - inner_bias.shape[0])))
    triple_payload = jnp.concatenate([column_payload[..., :split], column_payload[..., split + ff_here :]], -1)
    pieces = (triple_payload, mixer_weight, bias_rows)
    first_payload = jnp.concatenate([piece.reshape(-1) for piece in pieces]).reshape(-1, width)
    first_block = lax.all_gather(first_payload, "fsdp", axis=0, tiled=False).reshape(nf, -1)
    sizes = [piece.size for piece in pieces]
    triple_block = first_block[:, : sizes[0]].reshape((nf,) + triple_payload.shape)
    triple_block = triple_block.swapaxes(0, 1).reshape(nc * nf * shard_rows, -1)
    mixer_here = first_block[:, sizes[0] : sizes[0] + sizes[1]].reshape(nf * shard_rows, width)
    ibias_here = (
        first_block[:, sizes[0] + sizes[1] : sizes[0] + sizes[1] + inner_bias.shape[0]].reshape(-1).astype(f32)
    )

    ff_payload = jnp.concatenate(
        [column_payload[..., split : split + ff_here].reshape(nc * shard_rows, ff_here), outer_weight], 0
    )
    visible = (pad_mask[0] != 0).astype(f32)
    own_upstream = cotangent[0].astype(f32) * visible
    both = jnp.concatenate([tokens[0], own_upstream.astype(bf16)], -1)
    both = ring_gather(both, "ctx").reshape(length, 2 * width)
    ff_payload, triple_block, both = lax.optimization_barrier((ff_payload, triple_block, both))
    ff_block = lax.all_gather(ff_payload, "fsdp", axis=0, tiled=False)
    triple_here = triple_block[:, :split]
    gain = triple_block[:, split].astype(f32)
    shift = triple_block[:, split + 1].astype(f32)
    obias = triple_block[:, split + 2].astype(f32)

    all_tokens = both[:, :width]
    all_upstream = both[:, width:]

    input_rows = all_tokens.astype(f32)
    center = input_rows - jnp.mean(input_rows, -1, keepdims=True)
    scaling = lax.rsqrt(jnp.mean(center * center, -1, keepdims=True) + eps)
    whitened = center * scaling
    normed = (whitened * gain + shift).astype(bf16)

    owners = (me + jnp.arange(nc)) % nc
    positions = (owners[:, None] * own_rows + jnp.arange(own_rows)[None, :]).reshape(length)
    cos_full, sin_full = pair_tables(positions, 2 * head_cols)
    query_key_value = jnp.dot(normed, triple_here, preferred_element_type=f32)
    heads_shape = (length, heads_here, HEAD_DIM)
    turned = query_key_value[:, : 2 * head_cols]
    turned = turned * cos_full + swap_pairs(turned) * sin_full
    queries = (turned[:, :head_cols] * HEAD_DIM ** (-0.5)).astype(bf16).reshape(heads_shape)
    key_rows = turned[:, head_cols:].astype(bf16).reshape(heads_shape)
    value_rows = query_key_value[:, 2 * head_cols :].reshape(heads_shape).astype(bf16)
    span = prefix_length[0]
    grad_mixture = jnp.dot(all_upstream, mixer_here.T, preferred_element_type=f32).astype(bf16)
    by_head = lambda values: values.reshape(heads_shape).swapaxes(0, 1)
    mixture, grad_queries, grad_keys, grad_values = fused_attention(
        span, by_head(queries), by_head(key_rows), by_head(value_rows), by_head(grad_mixture), positions
    )
    grad_queries, grad_keys, grad_values = (
        values.swapaxes(0, 1) for values in (grad_queries, grad_keys, grad_values)
    )
    mixture = mixture.swapaxes(0, 1).reshape(length, head_cols)
    ff_block, mixture = lax.optimization_barrier((ff_block, mixture))
    inner_here = (
        ff_block[:, : nc * shard_rows]
        .reshape(nf, nc, shard_rows, ff_here)
        .swapaxes(0, 1)
        .reshape(nc * nf * shard_rows, ff_here)
    )
    outer_here = ff_block[:, nc * shard_rows :].reshape(nf * ff_rows, width)

    attention = jnp.dot(mixture, mixer_here, preferred_element_type=f32)
    preact = jnp.dot(normed, inner_here, preferred_element_type=f32) + ibias_here
    gelu_result = jax.nn.gelu(preact, approximate=True).astype(bf16)
    feedforward = jnp.dot(gelu_result, outer_here, preferred_element_type=f32)
    block_sum = ring_scatter((attention + feedforward).reshape(nc, own_rows, width), "ctx")
    layer_output = (tokens[0].astype(f32) + block_sum + obias).astype(bf16)

    ones_block = jnp.ones((length, 16), bf16)
    row_lhs = jnp.concatenate([mixture, gelu_result, ones_block], -1)
    row_product = jnp.dot(row_lhs.T, all_upstream, preferred_element_type=f32).astype(bf16)
    grad_activated = jnp.dot(all_upstream, outer_here.T, preferred_element_type=f32)
    unused_value, gelu_pull = jax.vjp(partial(jax.nn.gelu, approximate=True), preact)
    grad_before_gelu = gelu_pull(grad_activated)[0].astype(bf16)
    grad_inner_weight = jnp.dot(normed.T, grad_before_gelu, preferred_element_type=f32)
    grad_inner_bias = jnp.sum(grad_before_gelu.astype(f32), 0)
    flat_shape = (length, head_cols)
    grad_turned = jnp.concatenate(
        [(grad_queries * HEAD_DIM ** (-0.5)).reshape(flat_shape), grad_keys.reshape(flat_shape)], -1
    )
    grad_turned = grad_turned * cos_full - swap_pairs(grad_turned) * sin_full
    grad_query_key_value = jnp.concatenate(
        [grad_turned, grad_values.reshape(flat_shape)], -1
    ).astype(bf16)
    grad_triple_weight = jnp.dot(normed.T, grad_query_key_value, preferred_element_type=f32)
    grad_normed = jnp.dot(grad_query_key_value, triple_here.T, preferred_element_type=f32)
    grad_normed = grad_normed + jnp.dot(grad_before_gelu, inner_here.T, preferred_element_type=f32)
    grad_norm_gain = jnp.sum(grad_normed * whitened, 0)
    grad_norm_shift = jnp.sum(grad_normed, 0)
    grad_normed = ring_scatter(grad_normed.reshape(nc, own_rows, width), "ctx")

    own_whitened = whitened[:own_rows]
    own_scaling = scaling[:own_rows]
    grad_white = grad_normed * gain
    grad_inputs = own_scaling * (
        grad_white
        - jnp.mean(grad_white, -1, keepdims=True)
        - own_whitened * jnp.mean(grad_white * own_whitened, -1, keepdims=True)
    )
    input_grad = (own_upstream + grad_inputs).astype(bf16)

    small_grads = jnp.stack([grad_norm_gain, grad_norm_shift], -1)
    small_grads = jnp.pad(small_grads, ((0, 0), (0, 128 - small_grads.shape[-1])))
    column_grads = jnp.concatenate(
        [grad_triple_weight, grad_inner_weight, small_grads], -1
    ).astype(bf16)
    column_grads = column_grads.reshape(nc, nf, shard_rows, -1).swapaxes(0, 1).reshape(width, -1)
    column_grads = lax.psum_scatter(column_grads, "fsdp", scatter_dimension=0, tiled=True)
    column_grads = replica_sum(column_grads, "rep").astype(bf16)
    column_grads = column_grads.reshape(nc, shard_rows, -1)
    column_grads = ring_all_to_all(column_grads, "ctx").astype(f32)
    grad_triple_out = (
        column_grads[:, :, : 3 * head_cols]
        .reshape(nc, shard_rows, 3, head_cols)
        .transpose(1, 2, 0, 3)
        .reshape(shard_rows, 3 * nc * head_cols)
    )
    grad_inner_out = (
        column_grads[:, :, 3 * head_cols : 3 * head_cols + ff_here]
        .transpose(1, 0, 2)
        .reshape(shard_rows, nc * ff_here)
    )
    grad_gain_out = jnp.sum(column_grads[:, :, 3 * head_cols + ff_here], 0)
    grad_shift_out = jnp.sum(column_grads[:, :, 3 * head_cols + ff_here + 1], 0)

    mixer_part = row_product[:head_cols].reshape(nf, shard_rows, width)
    outer_part = row_product[head_cols : head_cols + ff_here].reshape(nf, ff_rows, width)
    sums_part = jnp.broadcast_to(row_product[head_cols + ff_here :][None], (nf, 16, width))
    row_grads = jnp.concatenate([mixer_part, outer_part, sums_part], 1)
    row_grads = row_grads.at[:, ff_rows + shard_rows + 1, :ff_rows].set(
        grad_inner_bias.reshape(nf, ff_rows).astype(bf16)
    )
    row_grads = lax.psum_scatter(row_grads, "fsdp", scatter_dimension=0, tiled=True)
    row_grads = replica_sum(row_grads, "rep")[0]
    grad_mixer_out = row_grads[:shard_rows]
    grad_outer_out = row_grads[shard_rows : shard_rows + ff_rows]
    grad_ibias_out = row_grads[shard_rows + ff_rows + 1, :ff_rows]
    fsdp_me = lax.axis_index("fsdp")
    grad_obias_out = lax.dynamic_slice_in_dim(
        row_grads[shard_rows + ff_rows], (me * nf + fsdp_me) * shard_rows, shard_rows
    )

    return (
        layer_output[None],
        input_grad[None],
        grad_gain_out,
        grad_shift_out,
        grad_triple_out,
        grad_mixer_out,
        grad_inner_out,
        grad_ibias_out,
        grad_outer_out,
        grad_obias_out,
    )


def solution(mesh):
    placed = (
        P(("rep", "fsdp"), "ctx", None),
        P(("ctx", "fsdp")),
        P(("ctx", "fsdp")),
        P(("ctx", "fsdp"), None),
        P(("ctx", "fsdp"), None),
        P(("ctx", "fsdp"), None),
        P(("ctx", "fsdp")),
        P(("ctx", "fsdp"), None),
        P(("ctx", "fsdp")),
        P(("rep", "fsdp")),
        P(("rep", "fsdp")),
        P(("rep", "fsdp"), "ctx", None),
    )
    return jax.shard_map(
        local,
        mesh=mesh,
        in_specs=placed,
        out_specs=(
            P(("rep", "fsdp"), "ctx", None),
            P(("rep", "fsdp"), "ctx", None),
            P(("ctx", "fsdp")),
            P(("ctx", "fsdp")),
            P(("ctx", "fsdp"), None),
            P(("ctx", "fsdp"), None),
            P(("ctx", "fsdp"), None),
            P(("ctx", "fsdp")),
            P(("ctx", "fsdp"), None),
            P(("ctx", "fsdp")),
        ),
        check_vma=False,
    )
```

```python
from functools import partial

import jax
import jax.numpy as jnp
from jax import lax
from jax.experimental import pallas as pl
from jax.experimental.pallas import tpu as pltpu
from jax.sharding import PartitionSpec as P

HEADS = 16
HEAD_DIM = 64
ROT = 32


eps = 1e-05


def angles(positions):
    frequency = 10000.0 ** (-(jnp.arange(ROT // 2, dtype=jnp.float32) * 2.0) / ROT)
    phases = positions.astype(jnp.float32)[:, None] * frequency[None, :]
    return (jnp.cos(phases), jnp.sin(phases))


def rotate(field, cos_table, sin_table):
    leading = field.shape[:-1]
    paired = field[..., :ROT].reshape(leading + (ROT // 2, 2))
    even_part = paired[..., 0]
    odd_part = paired[..., 1]
    cos_wide = cos_table[:, None, :]
    sin_wide = sin_table[:, None, :]
    turned = jnp.stack(
        [even_part * cos_wide - odd_part * sin_wide, odd_part * cos_wide + even_part * sin_wide], -1
    )
    return jnp.concatenate([turned.reshape(leading + (ROT,)), field[..., ROT:]], -1)


def pair_tables(positions, width):
    f32 = jnp.float32
    highest = lax.Precision.HIGHEST
    cos_table, sin_table = angles(positions)
    feature = jnp.arange(width) % HEAD_DIM
    pick = (feature[None, :] // 2 == jnp.arange(ROT // 2)[:, None]) & (feature[None, :] < ROT)
    pick = pick.astype(f32)
    sign = jnp.where(feature % 2 == 0, -1.0, 1.0).astype(f32)
    cos_full = jnp.dot(cos_table, pick, precision=highest) + (feature >= ROT).astype(f32)
    sin_full = jnp.dot(sin_table, pick, precision=highest) * sign
    return cos_full, sin_full


def swap_pairs(values):
    width = values.shape[-1]
    index = jnp.arange(width)
    swap = (index[:, None] == (index[None, :] ^ 1)).astype(jnp.float32)
    return jnp.dot(values, swap, precision=lax.Precision.HIGHEST)


def ring_pairs(n, step):
    return [(i, (i + step) % n) for i in range(n)]


def ring_gather(block, axis):
    n = lax.axis_size(axis)
    half = block.shape[0] // 2
    from_left = lax.ppermute(block, axis, ring_pairs(n, 1))
    from_right = lax.ppermute(block, axis, ring_pairs(n, -1))
    far_first = lax.ppermute(from_left[:half], axis, ring_pairs(n, 1))
    far_second = lax.ppermute(from_right[half:], axis, ring_pairs(n, -1))
    far = jnp.concatenate([far_first, far_second], 0)
    return jnp.stack([block, from_right, far, from_left])


def ring_scatter(parts, axis):
    n = lax.axis_size(axis)
    half = parts.shape[1] // 2
    wire = jnp.bfloat16
    got_left = lax.ppermute(parts[2, :half].astype(wire), axis, ring_pairs(n, 1))
    got_right = lax.ppermute(parts[2, half:].astype(wire), axis, ring_pairs(n, -1))
    to_right = jnp.concatenate([parts[1, :half] + got_left.astype(jnp.float32), parts[1, half:]], 0)
    to_left = jnp.concatenate([parts[3, :half], parts[3, half:] + got_right.astype(jnp.float32)], 0)
    from_left = lax.ppermute(to_right.astype(wire), axis, ring_pairs(n, 1))
    from_right = lax.ppermute(to_left.astype(wire), axis, ring_pairs(n, -1))
    return parts[0] + from_left.astype(jnp.float32) + from_right.astype(jnp.float32)


def ring_all_to_all(payload, axis):
    n = lax.axis_size(axis)
    me = lax.axis_index(axis)
    pick = lambda d: lax.dynamic_index_in_dim(payload, d % n, 0, keepdims=False)
    got = [pick(me)] + [
        lax.ppermute(pick(me + s), axis, ring_pairs(n, s)) for s in range(1, n)
    ]
    mirrored = jnp.stack([got[(-k) % n] for k in range(n)])
    doubled = jnp.concatenate([mirrored, mirrored], 0)
    return lax.dynamic_slice_in_dim(doubled, n - me, n, 0)


def replica_sum(values, axis):
    n = lax.axis_size(axis)
    f32, wire = jnp.float32, jnp.bfloat16
    values = values.astype(wire)
    if n != 4:
        return lax.psum(values, axis).astype(f32)
    pair = values.astype(f32) + lax.ppermute(values, axis, [(i, i ^ 1) for i in range(n)]).astype(f32)
    pair = pair.astype(wire)
    return pair.astype(f32) + lax.ppermute(pair, axis, [(i, i ^ 2) for i in range(n)]).astype(f32)


def attention_kernel(span_ref, q_ref, k_ref, v_ref, gm_ref, qpos_ref, kpos_ref,
                     mix_ref, gq_ref, gk_ref, gv_ref, bias_ref):
    f32, bf16 = jnp.float32, jnp.bfloat16
    block = pl.program_id(0)
    head = pl.program_id(1)

    @pl.when(head == 0)
    def _():
        allowed = (kpos_ref[...] <= qpos_ref[...]) | (kpos_ref[...] < span_ref[0])
        bias_ref[...] = jnp.where(allowed, 0.0, -1e30).astype(f32)

    q = q_ref[...]
    k = k_ref[...]
    v = v_ref[...]
    gm = gm_ref[...]
    scores = lax.dot_general(q, k, (((1,), (1,)), ((), ())), preferred_element_type=f32)
    scores = scores + bias_ref[...]
    peak = jnp.max(scores, axis=1, keepdims=True)
    exps = jnp.exp(scores - peak)
    total = jnp.sum(exps, axis=1, keepdims=True)
    probs = exps * (1.0 / total)
    low_probs = probs.astype(bf16)
    mix_ref[...] = jnp.dot(low_probs, v, preferred_element_type=f32).astype(mix_ref.dtype)
    grad_probs = lax.dot_general(gm, v, (((1,), (1,)), ((), ())), preferred_element_type=f32)
    inner = jnp.sum(probs * grad_probs, axis=1, keepdims=True)
    grad_scores = (probs * (grad_probs - inner)).astype(bf16)
    gq_ref[...] = jnp.dot(grad_scores, k, preferred_element_type=f32)
    gk_part = lax.dot_general(q, grad_scores, (((0,), (0,)), ((), ())), preferred_element_type=f32)
    gv_part = lax.dot_general(gm, low_probs, (((0,), (0,)), ((), ())), preferred_element_type=f32)

    @pl.when(block == 0)
    def _():
        gk_ref[head] = gk_part
        gv_ref[head] = gv_part

    @pl.when(block != 0)
    def _():
        gk_ref[head] += gk_part
        gv_ref[head] += gv_part


def fused_attention(span, queries, keys, values, grad_mixture, positions, rows=512):
    heads, length, dim = queries.shape
    blocks = length // rows
    qpos = positions.reshape(length, 1).astype(jnp.int32)
    kpos = positions.reshape(1, length).astype(jnp.int32)
    row_block = pl.BlockSpec((None, rows, dim), lambda b, h, s: (h, b, 0))
    whole_head = pl.BlockSpec((None, length, dim), lambda b, h, s: (h, 0, 0))
    resident = pl.BlockSpec((heads, dim, length), lambda b, h, s: (0, 0, 0))
    f32 = jnp.float32
    return pl.pallas_call(
        attention_kernel,
        out_shape=(
            jax.ShapeDtypeStruct((heads, length, dim), jnp.bfloat16),
            jax.ShapeDtypeStruct((heads, length, dim), f32),
            jax.ShapeDtypeStruct((heads, dim, length), f32),
            jax.ShapeDtypeStruct((heads, dim, length), f32),
        ),
        grid_spec=pltpu.PrefetchScalarGridSpec(
            num_scalar_prefetch=1,
            grid=(blocks, heads),
            in_specs=[
                row_block, whole_head, whole_head, row_block,
                pl.BlockSpec((rows, 1), lambda b, h, s: (b, 0)),
                pl.BlockSpec((1, length), lambda b, h, s: (0, 0)),
            ],
            out_specs=[row_block, row_block, resident, resident],
            scratch_shapes=[pltpu.VMEM((rows, length), f32)],
        ),
        compiler_params=pltpu.CompilerParams(dimension_semantics=("arbitrary", "arbitrary")),
        cost_estimate=pl.CostEstimate(
            flops=12 * heads * length * length * dim,
            transcendentals=heads * length * length,
            bytes_accessed=heads * length * dim * (4 * 2 + 3 * 4 + 2),
        ),
    )(span.reshape(1).astype(jnp.int32), queries, keys, values, grad_mixture, qpos, kpos)


def local(
    tokens,
    norm_gain,
    norm_shift,
    triple_weight,
    mixer_weight,
    inner_weight,
    inner_bias,
    outer_weight,
    outer_bias,
    prefix_length,
    pad_mask,
    cotangent,
):
    nc = lax.axis_size("ctx")
    nf = lax.axis_size("fsdp")
    me = lax.axis_index("ctx")
    _, own_rows, width = tokens.shape
    length = own_rows * nc
    shard_rows = triple_weight.shape[0]
    heads_here = HEADS // nc
    head_cols = heads_here * HEAD_DIM
    ff_here = inner_weight.shape[1] // nc
    ff_rows = outer_weight.shape[0]
    f32, bf16 = jnp.float32, jnp.bfloat16

    triple_cols = (
        triple_weight.reshape(shard_rows, 3, nc, head_cols)
        .transpose(2, 0, 1, 3)
        .reshape(nc, shard_rows, 3 * head_cols)
    )
    inner_cols = inner_weight.reshape(shard_rows, nc, ff_here).transpose(1, 0, 2)
    small = jnp.stack([norm_gain, norm_shift, outer_bias], -1)
    small = jnp.pad(small, ((0, 0), (0, 128 - small.shape[-1])))
    small = jnp.broadcast_to(small[None], (nc,) + small.shape)
    column_payload = jnp.concatenate([triple_cols, inner_cols, small], -1)
    column_payload = ring_all_to_all(column_payload, "ctx")
    split = 3 * head_cols

    bias_rows = jnp.pad(inner_bias[None], ((0, 15), (0, width - inner_bias.shape[0])))
    triple_payload = jnp.concatenate([column_payload[..., :split], column_payload[..., split + ff_here :]], -1)
    pieces = (triple_payload, mixer_weight, bias_rows)
    first_payload = jnp.concatenate([piece.reshape(-1) for piece in pieces]).reshape(-1, width)
    first_block = lax.all_gather(first_payload, "fsdp", axis=0, tiled=False).reshape(nf, -1)
    sizes = [piece.size for piece in pieces]
    triple_block = first_block[:, : sizes[0]].reshape((nf,) + triple_payload.shape)
    triple_block = triple_block.swapaxes(0, 1).reshape(nc * nf * shard_rows, -1)
    mixer_here = first_block[:, sizes[0] : sizes[0] + sizes[1]].reshape(nf * shard_rows, width)
    ibias_here = (
        first_block[:, sizes[0] + sizes[1] : sizes[0] + sizes[1] + inner_bias.shape[0]].reshape(-1).astype(f32)
    )

    ff_payload = jnp.concatenate(
        [column_payload[..., split : split + ff_here].reshape(nc * shard_rows, ff_here), outer_weight], 0
    )
    visible = (pad_mask[0] != 0).astype(f32)
    own_upstream = cotangent[0].astype(f32) * visible
    both = jnp.concatenate([tokens[0], own_upstream.astype(bf16)], -1)
    both = ring_gather(both, "ctx").reshape(length, 2 * width)
    ff_payload, triple_block, both = lax.optimization_barrier((ff_payload, triple_block, both))
    ff_block = lax.all_gather(ff_payload, "fsdp", axis=0, tiled=False)
    triple_here = triple_block[:, :split]
    gain = triple_block[:, split].astype(f32)
    shift = triple_block[:, split + 1].astype(f32)
    obias = triple_block[:, split + 2].astype(f32)

    all_tokens = both[:, :width]
    all_upstream = both[:, width:]

    input_rows = all_tokens.astype(f32)
    center = input_rows - jnp.mean(input_rows, -1, keepdims=True)
    scaling = lax.rsqrt(jnp.mean(center * center, -1, keepdims=True) + eps)
    whitened = center * scaling
    normed = (whitened * gain + shift).astype(bf16)

    owners = (me + jnp.arange(nc)) % nc
    positions = (owners[:, None] * own_rows + jnp.arange(own_rows)[None, :]).reshape(length)
    cos_full, sin_full = pair_tables(positions, 2 * head_cols)
    query_key_value = jnp.dot(normed, triple_here, preferred_element_type=f32)
    heads_shape = (length, heads_here, HEAD_DIM)
    turned = query_key_value[:, : 2 * head_cols]
    turned = turned * cos_full + swap_pairs(turned) * sin_full
    queries = (turned[:, :head_cols] * HEAD_DIM ** (-0.5)).astype(bf16).reshape(heads_shape)
    key_rows = turned[:, head_cols:].astype(bf16).reshape(heads_shape)
    value_rows = query_key_value[:, 2 * head_cols :].reshape(heads_shape).astype(bf16)
    span = prefix_length[0]
    grad_mixture = jnp.dot(all_upstream, mixer_here.T, preferred_element_type=f32).astype(bf16)
    by_head = lambda values: values.reshape(heads_shape).swapaxes(0, 1)
    mixture, grad_queries, grad_keys, grad_values = fused_attention(
        span, by_head(queries), by_head(key_rows), by_head(value_rows), by_head(grad_mixture), positions
    )
    grad_queries = grad_queries.swapaxes(0, 1)
    grad_keys, grad_values = (values.transpose(2, 0, 1) for values in (grad_keys, grad_values))
    mixture = mixture.swapaxes(0, 1).reshape(length, head_cols)
    ff_block, mixture = lax.optimization_barrier((ff_block, mixture))
    inner_here = (
        ff_block[:, : nc * shard_rows]
        .reshape(nf, nc, shard_rows, ff_here)
        .swapaxes(0, 1)
        .reshape(nc * nf * shard_rows, ff_here)
    )
    outer_here = ff_block[:, nc * shard_rows :].reshape(nf * ff_rows, width)

    attention = jnp.dot(mixture, mixer_here, preferred_element_type=f32)
    preact = jnp.dot(normed, inner_here, preferred_element_type=f32) + ibias_here
    gelu_result = jax.nn.gelu(preact, approximate=True).astype(bf16)
    feedforward = jnp.dot(gelu_result, outer_here, preferred_element_type=f32)
    block_sum = ring_scatter((attention + feedforward).reshape(nc, own_rows, width), "ctx")
    layer_output = (tokens[0].astype(f32) + block_sum + obias).astype(bf16)

    ones_block = jnp.ones((length, 16), bf16)
    row_lhs = jnp.concatenate([mixture, gelu_result, ones_block], -1)
    row_product = jnp.dot(row_lhs.T, all_upstream, preferred_element_type=f32).astype(bf16)
    grad_activated = jnp.dot(all_upstream, outer_here.T, preferred_element_type=f32)
    unused_value, gelu_pull = jax.vjp(partial(jax.nn.gelu, approximate=True), preact)
    grad_before_gelu = gelu_pull(grad_activated)[0].astype(bf16)
    grad_inner_weight = jnp.dot(normed.T, grad_before_gelu, preferred_element_type=f32)
    grad_inner_bias = jnp.sum(grad_before_gelu.astype(f32), 0)
    flat_shape = (length, head_cols)
    grad_turned = jnp.concatenate(
        [(grad_queries * HEAD_DIM ** (-0.5)).reshape(flat_shape), grad_keys.reshape(flat_shape)], -1
    )
    grad_turned = grad_turned * cos_full - swap_pairs(grad_turned) * sin_full
    grad_query_key_value = jnp.concatenate(
        [grad_turned, grad_values.reshape(flat_shape)], -1
    ).astype(bf16)
    grad_triple_weight = jnp.dot(normed.T, grad_query_key_value, preferred_element_type=f32)
    grad_normed = jnp.dot(grad_query_key_value, triple_here.T, preferred_element_type=f32)
    grad_normed = grad_normed + jnp.dot(grad_before_gelu, inner_here.T, preferred_element_type=f32)
    grad_norm_gain = jnp.sum(grad_normed * whitened, 0)
    grad_norm_shift = jnp.sum(grad_normed, 0)
    grad_normed = ring_scatter(grad_normed.reshape(nc, own_rows, width), "ctx")

    own_whitened = whitened[:own_rows]
    own_scaling = scaling[:own_rows]
    grad_white = grad_normed * gain
    grad_inputs = own_scaling * (
        grad_white
        - jnp.mean(grad_white, -1, keepdims=True)
        - own_whitened * jnp.mean(grad_white * own_whitened, -1, keepdims=True)
    )
    input_grad = (own_upstream + grad_inputs).astype(bf16)

    small_grads = jnp.stack([grad_norm_gain, grad_norm_shift], -1)
    small_grads = jnp.pad(small_grads, ((0, 0), (0, 128 - small_grads.shape[-1])))
    column_grads = jnp.concatenate(
        [grad_triple_weight, grad_inner_weight, small_grads], -1
    ).astype(bf16)
    column_grads = column_grads.reshape(nc, nf, shard_rows, -1).swapaxes(0, 1).reshape(width, -1)
    column_grads = lax.psum_scatter(column_grads, "fsdp", scatter_dimension=0, tiled=True)
    column_grads = replica_sum(column_grads, "rep").astype(bf16)
    column_grads = column_grads.reshape(nc, shard_rows, -1)
    column_grads = ring_all_to_all(column_grads, "ctx").astype(f32)
    grad_triple_out = (
        column_grads[:, :, : 3 * head_cols]
        .reshape(nc, shard_rows, 3, head_cols)
        .transpose(1, 2, 0, 3)
        .reshape(shard_rows, 3 * nc * head_cols)
    )
    grad_inner_out = (
        column_grads[:, :, 3 * head_cols : 3 * head_cols + ff_here]
        .transpose(1, 0, 2)
        .reshape(shard_rows, nc * ff_here)
    )
    grad_gain_out = jnp.sum(column_grads[:, :, 3 * head_cols + ff_here], 0)
    grad_shift_out = jnp.sum(column_grads[:, :, 3 * head_cols + ff_here + 1], 0)

    mixer_part = row_product[:head_cols].reshape(nf, shard_rows, width)
    outer_part = row_product[head_cols : head_cols + ff_here].reshape(nf, ff_rows, width)
    sums_part = jnp.broadcast_to(row_product[head_cols + ff_here :][None], (nf, 16, width))
    row_grads = jnp.concatenate([mixer_part, outer_part, sums_part], 1)
    row_grads = row_grads.at[:, ff_rows + shard_rows + 1, :ff_rows].set(
        grad_inner_bias.reshape(nf, ff_rows).astype(bf16)
    )
    row_grads = lax.psum_scatter(row_grads, "fsdp", scatter_dimension=0, tiled=True)
    row_grads = replica_sum(row_grads, "rep")[0]
    grad_mixer_out = row_grads[:shard_rows]
    grad_outer_out = row_grads[shard_rows : shard_rows + ff_rows]
    grad_ibias_out = row_grads[shard_rows + ff_rows + 1, :ff_rows]
    fsdp_me = lax.axis_index("fsdp")
    grad_obias_out = lax.dynamic_slice_in_dim(
        row_grads[shard_rows + ff_rows], (me * nf + fsdp_me) * shard_rows, shard_rows
    )

    return (
        layer_output[None],
        input_grad[None],
        grad_gain_out,
        grad_shift_out,
        grad_triple_out,
        grad_mixer_out,
        grad_inner_out,
        grad_ibias_out,
        grad_outer_out,
        grad_obias_out,
    )


def solution(mesh):
    placed = (
        P(("rep", "fsdp"), "ctx", None),
        P(("ctx", "fsdp")),
        P(("ctx", "fsdp")),
        P(("ctx", "fsdp"), None),
        P(("ctx", "fsdp"), None),
        P(("ctx", "fsdp"), None),
        P(("ctx", "fsdp")),
        P(("ctx", "fsdp"), None),
        P(("ctx", "fsdp")),
        P(("rep", "fsdp")),
        P(("rep", "fsdp")),
        P(("rep", "fsdp"), "ctx", None),
    )
    return jax.shard_map(
        local,
        mesh=mesh,
        in_specs=placed,
        out_specs=(
            P(("rep", "fsdp"), "ctx", None),
            P(("rep", "fsdp"), "ctx", None),
            P(("ctx", "fsdp")),
            P(("ctx", "fsdp")),
            P(("ctx", "fsdp"), None),
            P(("ctx", "fsdp"), None),
            P(("ctx", "fsdp"), None),
            P(("ctx", "fsdp")),
            P(("ctx", "fsdp"), None),
            P(("ctx", "fsdp")),
        ),
        check_vma=False,
    )
```

```python
from functools import partial

import jax
import jax.numpy as jnp
from jax import lax
from jax.experimental import pallas as pl
from jax.experimental.pallas import tpu as pltpu
from jax.sharding import PartitionSpec as P

HEADS = 16
HEAD_DIM = 64
ROT = 32


eps = 1e-05


def angles(positions):
    frequency = 10000.0 ** (-(jnp.arange(ROT // 2, dtype=jnp.float32) * 2.0) / ROT)
    phases = positions.astype(jnp.float32)[:, None] * frequency[None, :]
    return (jnp.cos(phases), jnp.sin(phases))


def rotate(field, cos_table, sin_table):
    leading = field.shape[:-1]
    paired = field[..., :ROT].reshape(leading + (ROT // 2, 2))
    even_part = paired[..., 0]
    odd_part = paired[..., 1]
    cos_wide = cos_table[:, None, :]
    sin_wide = sin_table[:, None, :]
    turned = jnp.stack(
        [even_part * cos_wide - odd_part * sin_wide, odd_part * cos_wide + even_part * sin_wide], -1
    )
    return jnp.concatenate([turned.reshape(leading + (ROT,)), field[..., ROT:]], -1)


def pair_tables(positions, width):
    f32 = jnp.float32
    highest = lax.Precision.HIGHEST
    cos_table, sin_table = angles(positions)
    feature = jnp.arange(width) % HEAD_DIM
    pick = (feature[None, :] // 2 == jnp.arange(ROT // 2)[:, None]) & (feature[None, :] < ROT)
    pick = pick.astype(f32)
    sign = jnp.where(feature % 2 == 0, -1.0, 1.0).astype(f32)
    cos_full = jnp.dot(cos_table, pick, precision=highest) + (feature >= ROT).astype(f32)
    sin_full = jnp.dot(sin_table, pick, precision=highest) * sign
    return cos_full, sin_full


def swap_pairs(values):
    width = values.shape[-1]
    index = jnp.arange(width)
    swap = (index[:, None] == (index[None, :] ^ 1)).astype(jnp.float32)
    return jnp.dot(values, swap, precision=lax.Precision.HIGHEST)


def ring_pairs(n, step):
    return [(i, (i + step) % n) for i in range(n)]


def ring_gather(block, axis):
    n = lax.axis_size(axis)
    half = block.shape[0] // 2
    from_left = lax.ppermute(block, axis, ring_pairs(n, 1))
    from_right = lax.ppermute(block, axis, ring_pairs(n, -1))
    far_first = lax.ppermute(from_left[:half], axis, ring_pairs(n, 1))
    far_second = lax.ppermute(from_right[half:], axis, ring_pairs(n, -1))
    far = jnp.concatenate([far_first, far_second], 0)
    return jnp.stack([block, from_right, far, from_left])


def ring_scatter(parts, axis):
    n = lax.axis_size(axis)
    half = parts.shape[1] // 2
    wire = jnp.bfloat16
    got_left = lax.ppermute(parts[2, :half].astype(wire), axis, ring_pairs(n, 1))
    got_right = lax.ppermute(parts[2, half:].astype(wire), axis, ring_pairs(n, -1))
    to_right = jnp.concatenate([parts[1, :half] + got_left.astype(jnp.float32), parts[1, half:]], 0)
    to_left = jnp.concatenate([parts[3, :half], parts[3, half:] + got_right.astype(jnp.float32)], 0)
    from_left = lax.ppermute(to_right.astype(wire), axis, ring_pairs(n, 1))
    from_right = lax.ppermute(to_left.astype(wire), axis, ring_pairs(n, -1))
    return parts[0] + from_left.astype(jnp.float32) + from_right.astype(jnp.float32)


def ring_all_to_all(payload, axis):
    n = lax.axis_size(axis)
    me = lax.axis_index(axis)
    pick = lambda d: lax.dynamic_index_in_dim(payload, d % n, 0, keepdims=False)
    got = [pick(me)] + [
        lax.ppermute(pick(me + s), axis, ring_pairs(n, s)) for s in range(1, n)
    ]
    mirrored = jnp.stack([got[(-k) % n] for k in range(n)])
    doubled = jnp.concatenate([mirrored, mirrored], 0)
    return lax.dynamic_slice_in_dim(doubled, n - me, n, 0)


def replica_sum(values, axis):
    n = lax.axis_size(axis)
    f32, wire = jnp.float32, jnp.bfloat16
    values = values.astype(wire)
    if n != 4:
        return lax.psum(values, axis).astype(f32)
    pair = values.astype(f32) + lax.ppermute(values, axis, [(i, i ^ 1) for i in range(n)]).astype(f32)
    pair = pair.astype(wire)
    return pair.astype(f32) + lax.ppermute(pair, axis, [(i, i ^ 2) for i in range(n)]).astype(f32)


def attention_kernel(span_ref, q_ref, k_ref, v_ref, gm_ref, qpos_ref, kpos_ref,
                     mix_ref, gq_ref, gk_ref, gv_ref, bias_ref):
    f32, bf16 = jnp.float32, jnp.bfloat16
    block = pl.program_id(0)
    head = pl.program_id(1)

    @pl.when(head == 0)
    def _():
        allowed = (kpos_ref[...] <= qpos_ref[...]) | (kpos_ref[...] < span_ref[0])
        bias_ref[...] = jnp.where(allowed, 0.0, -1e30).astype(f32)

    q = q_ref[...]
    k = k_ref[...]
    v = v_ref[...]
    gm = gm_ref[...]
    scores = lax.dot_general(q, k, (((1,), (1,)), ((), ())), preferred_element_type=f32)
    scores = scores + bias_ref[...]
    peak = jnp.max(scores, axis=1, keepdims=True)
    exps = jnp.exp(scores - peak)
    total = jnp.sum(exps, axis=1, keepdims=True)
    probs = exps * (1.0 / total)
    low_probs = probs.astype(bf16)
    mix_ref[...] = jnp.dot(low_probs, v, preferred_element_type=f32).astype(mix_ref.dtype)
    grad_probs = lax.dot_general(gm, v, (((1,), (1,)), ((), ())), preferred_element_type=f32)
    inner = jnp.sum(probs * grad_probs, axis=1, keepdims=True)
    grad_scores = (probs * (grad_probs - inner)).astype(bf16)
    gq_ref[...] = jnp.dot(grad_scores, k, preferred_element_type=f32)
    gk_part = lax.dot_general(q, grad_scores, (((0,), (0,)), ((), ())), preferred_element_type=f32)
    gv_part = lax.dot_general(gm, low_probs, (((0,), (0,)), ((), ())), preferred_element_type=f32)

    @pl.when(block == 0)
    def _():
        gk_ref[head] = gk_part
        gv_ref[head] = gv_part

    @pl.when(block != 0)
    def _():
        gk_ref[head] += gk_part
        gv_ref[head] += gv_part


def fused_attention(span, queries, keys, values, grad_mixture, positions, rows=1024):
    heads, length, dim = queries.shape
    blocks = length // rows
    qpos = positions.reshape(length, 1).astype(jnp.int32)
    kpos = positions.reshape(1, length).astype(jnp.int32)
    row_block = pl.BlockSpec((None, rows, dim), lambda b, h, s: (h, b, 0))
    whole_head = pl.BlockSpec((None, length, dim), lambda b, h, s: (h, 0, 0))
    resident = pl.BlockSpec((heads, dim, length), lambda b, h, s: (0, 0, 0))
    f32 = jnp.float32
    return pl.pallas_call(
        attention_kernel,
        out_shape=(
            jax.ShapeDtypeStruct((heads, length, dim), jnp.bfloat16),
            jax.ShapeDtypeStruct((heads, length, dim), f32),
            jax.ShapeDtypeStruct((heads, dim, length), f32),
            jax.ShapeDtypeStruct((heads, dim, length), f32),
        ),
        grid_spec=pltpu.PrefetchScalarGridSpec(
            num_scalar_prefetch=1,
            grid=(blocks, heads),
            in_specs=[
                row_block, whole_head, whole_head, row_block,
                pl.BlockSpec((rows, 1), lambda b, h, s: (b, 0)),
                pl.BlockSpec((1, length), lambda b, h, s: (0, 0)),
            ],
            out_specs=[row_block, row_block, resident, resident],
            scratch_shapes=[pltpu.VMEM((rows, length), f32)],
        ),
        compiler_params=pltpu.CompilerParams(dimension_semantics=("arbitrary", "arbitrary")),
        cost_estimate=pl.CostEstimate(
            flops=12 * heads * length * length * dim,
            transcendentals=heads * length * length,
            bytes_accessed=heads * length * dim * (4 * 2 + 3 * 4 + 2),
        ),
    )(span.reshape(1).astype(jnp.int32), queries, keys, values, grad_mixture, qpos, kpos)


def local(
    tokens,
    norm_gain,
    norm_shift,
    triple_weight,
    mixer_weight,
    inner_weight,
    inner_bias,
    outer_weight,
    outer_bias,
    prefix_length,
    pad_mask,
    cotangent,
):
    nc = lax.axis_size("ctx")
    nf = lax.axis_size("fsdp")
    me = lax.axis_index("ctx")
    _, own_rows, width = tokens.shape
    length = own_rows * nc
    shard_rows = triple_weight.shape[0]
    heads_here = HEADS // nc
    head_cols = heads_here * HEAD_DIM
    ff_here = inner_weight.shape[1] // nc
    ff_rows = outer_weight.shape[0]
    f32, bf16 = jnp.float32, jnp.bfloat16

    triple_cols = (
        triple_weight.reshape(shard_rows, 3, nc, head_cols)
        .transpose(2, 0, 1, 3)
        .reshape(nc, shard_rows, 3 * head_cols)
    )
    inner_cols = inner_weight.reshape(shard_rows, nc, ff_here).transpose(1, 0, 2)
    small = jnp.stack([norm_gain, norm_shift, outer_bias], -1)
    small = jnp.pad(small, ((0, 0), (0, 128 - small.shape[-1])))
    small = jnp.broadcast_to(small[None], (nc,) + small.shape)
    column_payload = jnp.concatenate([triple_cols, inner_cols, small], -1)
    column_payload = ring_all_to_all(column_payload, "ctx")
    split = 3 * head_cols

    bias_rows = jnp.pad(inner_bias[None], ((0, 15), (0, width - inner_bias.shape[0])))
    triple_payload = jnp.concatenate([column_payload[..., :split], column_payload[..., split + ff_here :]], -1)
    pieces = (triple_payload, mixer_weight, bias_rows)
    first_payload = jnp.concatenate([piece.reshape(-1) for piece in pieces]).reshape(-1, width)
    first_block = lax.all_gather(first_payload, "fsdp", axis=0, tiled=False).reshape(nf, -1)
    sizes = [piece.size for piece in pieces]
    triple_block = first_block[:, : sizes[0]].reshape((nf,) + triple_payload.shape)
    triple_block = triple_block.swapaxes(0, 1).reshape(nc * nf * shard_rows, -1)
    mixer_here = first_block[:, sizes[0] : sizes[0] + sizes[1]].reshape(nf * shard_rows, width)
    ibias_here = (
        first_block[:, sizes[0] + sizes[1] : sizes[0] + sizes[1] + inner_bias.shape[0]].reshape(-1).astype(f32)
    )

    ff_payload = jnp.concatenate(
        [column_payload[..., split : split + ff_here].reshape(nc * shard_rows, ff_here), outer_weight], 0
    )
    visible = (pad_mask[0] != 0).astype(f32)
    own_upstream = cotangent[0].astype(f32) * visible
    both = jnp.concatenate([tokens[0], own_upstream.astype(bf16)], -1)
    both = ring_gather(both, "ctx").reshape(length, 2 * width)
    ff_payload, triple_block, both = lax.optimization_barrier((ff_payload, triple_block, both))
    ff_block = lax.all_gather(ff_payload, "fsdp", axis=0, tiled=False)
    triple_here = triple_block[:, :split]
    gain = triple_block[:, split].astype(f32)
    shift = triple_block[:, split + 1].astype(f32)
    obias = triple_block[:, split + 2].astype(f32)

    all_tokens = both[:, :width]
    all_upstream = both[:, width:]

    input_rows = all_tokens.astype(f32)
    center = input_rows - jnp.mean(input_rows, -1, keepdims=True)
    scaling = lax.rsqrt(jnp.mean(center * center, -1, keepdims=True) + eps)
    whitened = center * scaling
    normed = (whitened * gain + shift).astype(bf16)

    owners = (me + jnp.arange(nc)) % nc
    positions = (owners[:, None] * own_rows + jnp.arange(own_rows)[None, :]).reshape(length)
    cos_full, sin_full = pair_tables(positions, 2 * head_cols)
    query_key_value = jnp.dot(normed, triple_here, preferred_element_type=f32)
    heads_shape = (length, heads_here, HEAD_DIM)
    turned = query_key_value[:, : 2 * head_cols]
    turned = turned * cos_full + swap_pairs(turned) * sin_full
    queries = (turned[:, :head_cols] * HEAD_DIM ** (-0.5)).astype(bf16).reshape(heads_shape)
    key_rows = turned[:, head_cols:].astype(bf16).reshape(heads_shape)
    value_rows = query_key_value[:, 2 * head_cols :].reshape(heads_shape).astype(bf16)
    span = prefix_length[0]
    grad_mixture = jnp.dot(all_upstream, mixer_here.T, preferred_element_type=f32).astype(bf16)
    by_head = lambda values: values.reshape(heads_shape).swapaxes(0, 1)
    mixture, grad_queries, grad_keys, grad_values = fused_attention(
        span, by_head(queries), by_head(key_rows), by_head(value_rows), by_head(grad_mixture), positions
    )
    grad_queries = grad_queries.swapaxes(0, 1)
    grad_keys, grad_values = (values.transpose(2, 0, 1) for values in (grad_keys, grad_values))
    mixture = mixture.swapaxes(0, 1).reshape(length, head_cols)
    ff_block, mixture = lax.optimization_barrier((ff_block, mixture))
    inner_here = (
        ff_block[:, : nc * shard_rows]
        .reshape(nf, nc, shard_rows, ff_here)
        .swapaxes(0, 1)
        .reshape(nc * nf * shard_rows, ff_here)
    )
    outer_here = ff_block[:, nc * shard_rows :].reshape(nf * ff_rows, width)

    attention = jnp.dot(mixture, mixer_here, preferred_element_type=f32)
    preact = jnp.dot(normed, inner_here, preferred_element_type=f32) + ibias_here
    gelu_result = jax.nn.gelu(preact, approximate=True).astype(bf16)
    feedforward = jnp.dot(gelu_result, outer_here, preferred_element_type=f32)
    block_sum = ring_scatter((attention + feedforward).reshape(nc, own_rows, width), "ctx")
    layer_output = (tokens[0].astype(f32) + block_sum + obias).astype(bf16)

    ones_block = jnp.ones((length, 16), bf16)
    row_lhs = jnp.concatenate([mixture, gelu_result, ones_block], -1)
    row_product = jnp.dot(row_lhs.T, all_upstream, preferred_element_type=f32).astype(bf16)
    grad_activated = jnp.dot(all_upstream, outer_here.T, preferred_element_type=f32)
    unused_value, gelu_pull = jax.vjp(partial(jax.nn.gelu, approximate=True), preact)
    grad_before_gelu = gelu_pull(grad_activated)[0].astype(bf16)
    grad_inner_weight = jnp.dot(normed.T, grad_before_gelu, preferred_element_type=f32)
    grad_inner_bias = jnp.sum(grad_before_gelu.astype(f32), 0)
    flat_shape = (length, head_cols)
    grad_turned = jnp.concatenate(
        [(grad_queries * HEAD_DIM ** (-0.5)).reshape(flat_shape), grad_keys.reshape(flat_shape)], -1
    )
    grad_turned = grad_turned * cos_full - swap_pairs(grad_turned) * sin_full
    grad_query_key_value = jnp.concatenate(
        [grad_turned, grad_values.reshape(flat_shape)], -1
    ).astype(bf16)
    grad_triple_weight = jnp.dot(normed.T, grad_query_key_value, preferred_element_type=f32)
    grad_normed = jnp.dot(grad_query_key_value, triple_here.T, preferred_element_type=f32)
    grad_normed = grad_normed + jnp.dot(grad_before_gelu, inner_here.T, preferred_element_type=f32)
    grad_norm_gain = jnp.sum(grad_normed * whitened, 0)
    grad_norm_shift = jnp.sum(grad_normed, 0)
    grad_normed = ring_scatter(grad_normed.reshape(nc, own_rows, width), "ctx")

    own_whitened = whitened[:own_rows]
    own_scaling = scaling[:own_rows]
    grad_white = grad_normed * gain
    grad_inputs = own_scaling * (
        grad_white
        - jnp.mean(grad_white, -1, keepdims=True)
        - own_whitened * jnp.mean(grad_white * own_whitened, -1, keepdims=True)
    )
    input_grad = (own_upstream + grad_inputs).astype(bf16)

    small_grads = jnp.stack([grad_norm_gain, grad_norm_shift], -1)
    small_grads = jnp.pad(small_grads, ((0, 0), (0, 128 - small_grads.shape[-1])))
    column_grads = jnp.concatenate(
        [grad_triple_weight, grad_inner_weight, small_grads], -1
    ).astype(bf16)
    column_grads = column_grads.reshape(nc, nf, shard_rows, -1).swapaxes(0, 1).reshape(width, -1)
    column_grads = lax.psum_scatter(column_grads, "fsdp", scatter_dimension=0, tiled=True)
    column_grads = replica_sum(column_grads, "rep").astype(bf16)
    column_grads = column_grads.reshape(nc, shard_rows, -1)
    column_grads = ring_all_to_all(column_grads, "ctx").astype(f32)
    grad_triple_out = (
        column_grads[:, :, : 3 * head_cols]
        .reshape(nc, shard_rows, 3, head_cols)
        .transpose(1, 2, 0, 3)
        .reshape(shard_rows, 3 * nc * head_cols)
    )
    grad_inner_out = (
        column_grads[:, :, 3 * head_cols : 3 * head_cols + ff_here]
        .transpose(1, 0, 2)
        .reshape(shard_rows, nc * ff_here)
    )
    grad_gain_out = jnp.sum(column_grads[:, :, 3 * head_cols + ff_here], 0)
    grad_shift_out = jnp.sum(column_grads[:, :, 3 * head_cols + ff_here + 1], 0)

    mixer_part = row_product[:head_cols].reshape(nf, shard_rows, width)
    outer_part = row_product[head_cols : head_cols + ff_here].reshape(nf, ff_rows, width)
    sums_part = jnp.broadcast_to(row_product[head_cols + ff_here :][None], (nf, 16, width))
    row_grads = jnp.concatenate([mixer_part, outer_part, sums_part], 1)
    row_grads = row_grads.at[:, ff_rows + shard_rows + 1, :ff_rows].set(
        grad_inner_bias.reshape(nf, ff_rows).astype(bf16)
    )
    row_grads = lax.psum_scatter(row_grads, "fsdp", scatter_dimension=0, tiled=True)
    row_grads = replica_sum(row_grads, "rep")[0]
    grad_mixer_out = row_grads[:shard_rows]
    grad_outer_out = row_grads[shard_rows : shard_rows + ff_rows]
    grad_ibias_out = row_grads[shard_rows + ff_rows + 1, :ff_rows]
    fsdp_me = lax.axis_index("fsdp")
    grad_obias_out = lax.dynamic_slice_in_dim(
        row_grads[shard_rows + ff_rows], (me * nf + fsdp_me) * shard_rows, shard_rows
    )

    return (
        layer_output[None],
        input_grad[None],
        grad_gain_out,
        grad_shift_out,
        grad_triple_out,
        grad_mixer_out,
        grad_inner_out,
        grad_ibias_out,
        grad_outer_out,
        grad_obias_out,
    )


def solution(mesh):
    placed = (
        P(("rep", "fsdp"), "ctx", None),
        P(("ctx", "fsdp")),
        P(("ctx", "fsdp")),
        P(("ctx", "fsdp"), None),
        P(("ctx", "fsdp"), None),
        P(("ctx", "fsdp"), None),
        P(("ctx", "fsdp")),
        P(("ctx", "fsdp"), None),
        P(("ctx", "fsdp")),
        P(("rep", "fsdp")),
        P(("rep", "fsdp")),
        P(("rep", "fsdp"), "ctx", None),
    )
    return jax.shard_map(
        local,
        mesh=mesh,
        in_specs=placed,
        out_specs=(
            P(("rep", "fsdp"), "ctx", None),
            P(("rep", "fsdp"), "ctx", None),
            P(("ctx", "fsdp")),
            P(("ctx", "fsdp")),
            P(("ctx", "fsdp"), None),
            P(("ctx", "fsdp"), None),
            P(("ctx", "fsdp"), None),
            P(("ctx", "fsdp")),
            P(("ctx", "fsdp"), None),
            P(("ctx", "fsdp")),
        ),
        check_vma=False,
    )
```

```python
from functools import partial

import jax
import jax.numpy as jnp
from jax import lax
from jax.experimental import pallas as pl
from jax.experimental.pallas import tpu as pltpu
from jax.sharding import PartitionSpec as P

HEADS = 16
HEAD_DIM = 64
ROT = 32


eps = 1e-05


def angles(positions):
    frequency = 10000.0 ** (-(jnp.arange(ROT // 2, dtype=jnp.float32) * 2.0) / ROT)
    phases = positions.astype(jnp.float32)[:, None] * frequency[None, :]
    return (jnp.cos(phases), jnp.sin(phases))


def rotate(field, cos_table, sin_table):
    leading = field.shape[:-1]
    paired = field[..., :ROT].reshape(leading + (ROT // 2, 2))
    even_part = paired[..., 0]
    odd_part = paired[..., 1]
    cos_wide = cos_table[:, None, :]
    sin_wide = sin_table[:, None, :]
    turned = jnp.stack(
        [even_part * cos_wide - odd_part * sin_wide, odd_part * cos_wide + even_part * sin_wide], -1
    )
    return jnp.concatenate([turned.reshape(leading + (ROT,)), field[..., ROT:]], -1)


def pair_tables(positions, width):
    f32 = jnp.float32
    highest = lax.Precision.HIGHEST
    cos_table, sin_table = angles(positions)
    feature = jnp.arange(width) % HEAD_DIM
    pick = (feature[None, :] // 2 == jnp.arange(ROT // 2)[:, None]) & (feature[None, :] < ROT)
    pick = pick.astype(f32)
    sign = jnp.where(feature % 2 == 0, -1.0, 1.0).astype(f32)
    cos_full = jnp.dot(cos_table, pick, precision=highest) + (feature >= ROT).astype(f32)
    sin_full = jnp.dot(sin_table, pick, precision=highest) * sign
    return cos_full, sin_full


def swap_pairs(values):
    width = values.shape[-1]
    index = jnp.arange(width)
    swap = (index[:, None] == (index[None, :] ^ 1)).astype(jnp.float32)
    return jnp.dot(values, swap, precision=lax.Precision.HIGHEST)


def ring_pairs(n, step):
    return [(i, (i + step) % n) for i in range(n)]


def ring_gather(block, axis):
    n = lax.axis_size(axis)
    half = block.shape[0] // 2
    from_left = lax.ppermute(block, axis, ring_pairs(n, 1))
    from_right = lax.ppermute(block, axis, ring_pairs(n, -1))
    far_first = lax.ppermute(from_left[:half], axis, ring_pairs(n, 1))
    far_second = lax.ppermute(from_right[half:], axis, ring_pairs(n, -1))
    far = jnp.concatenate([far_first, far_second], 0)
    return jnp.stack([block, from_right, far, from_left])


def ring_scatter(parts, axis):
    n = lax.axis_size(axis)
    half = parts.shape[1] // 2
    wire = jnp.bfloat16
    got_left = lax.ppermute(parts[2, :half].astype(wire), axis, ring_pairs(n, 1))
    got_right = lax.ppermute(parts[2, half:].astype(wire), axis, ring_pairs(n, -1))
    to_right = jnp.concatenate([parts[1, :half] + got_left.astype(jnp.float32), parts[1, half:]], 0)
    to_left = jnp.concatenate([parts[3, :half], parts[3, half:] + got_right.astype(jnp.float32)], 0)
    from_left = lax.ppermute(to_right.astype(wire), axis, ring_pairs(n, 1))
    from_right = lax.ppermute(to_left.astype(wire), axis, ring_pairs(n, -1))
    return parts[0] + from_left.astype(jnp.float32) + from_right.astype(jnp.float32)


def ring_all_to_all(payload, axis):
    n = lax.axis_size(axis)
    me = lax.axis_index(axis)
    pick = lambda d: lax.dynamic_index_in_dim(payload, d % n, 0, keepdims=False)
    got = [pick(me)] + [
        lax.ppermute(pick(me + s), axis, ring_pairs(n, s)) for s in range(1, n)
    ]
    mirrored = jnp.stack([got[(-k) % n] for k in range(n)])
    doubled = jnp.concatenate([mirrored, mirrored], 0)
    return lax.dynamic_slice_in_dim(doubled, n - me, n, 0)


def replica_sum(values, axis):
    n = lax.axis_size(axis)
    f32, wire = jnp.float32, jnp.bfloat16
    values = values.astype(wire)
    if n != 4:
        return lax.psum(values, axis).astype(f32)
    pair = values.astype(f32) + lax.ppermute(values, axis, [(i, i ^ 1) for i in range(n)]).astype(f32)
    pair = pair.astype(wire)
    return pair.astype(f32) + lax.ppermute(pair, axis, [(i, i ^ 2) for i in range(n)]).astype(f32)


def attention_kernel(span_ref, q_ref, k_ref, v_ref, gm_ref, qpos_ref, kpos_ref,
                     mix_ref, gq_ref, gk_ref, gv_ref, bias_ref):
    f32, bf16 = jnp.float32, jnp.bfloat16
    block = pl.program_id(0)
    head = pl.program_id(1)

    @pl.when(head == 0)
    def _():
        allowed = (kpos_ref[...] <= qpos_ref[...]) | (kpos_ref[...] < span_ref[0])
        bias_ref[...] = jnp.where(allowed, 0.0, -1e30).astype(f32)

    q = q_ref[...]
    k = k_ref[...]
    v = v_ref[...]
    gm = gm_ref[...]
    scores = lax.dot_general(q, k, (((1,), (1,)), ((), ())), preferred_element_type=f32)
    scores = scores + bias_ref[...]
    peak = jnp.max(scores, axis=1, keepdims=True)
    exps = jnp.exp(scores - peak)
    total = jnp.sum(exps, axis=1, keepdims=True)
    probs = exps * (1.0 / total)
    low_probs = probs.astype(bf16)
    mix_ref[...] = jnp.dot(low_probs, v, preferred_element_type=f32).astype(mix_ref.dtype)
    grad_probs = lax.dot_general(gm, v, (((1,), (1,)), ((), ())), preferred_element_type=f32)
    weighted_values = jnp.dot(
        probs, v.astype(f32), precision=lax.Precision.HIGHEST, preferred_element_type=f32
    )
    inner = jnp.sum(gm.astype(f32) * weighted_values, axis=1, keepdims=True)
    grad_scores = (probs * (grad_probs - inner)).astype(bf16)
    gq_ref[...] = jnp.dot(grad_scores, k, preferred_element_type=f32)
    gk_part = lax.dot_general(q, grad_scores, (((0,), (0,)), ((), ())), preferred_element_type=f32)
    gv_part = lax.dot_general(gm, low_probs, (((0,), (0,)), ((), ())), preferred_element_type=f32)

    @pl.when(block == 0)
    def _():
        gk_ref[head] = gk_part
        gv_ref[head] = gv_part

    @pl.when(block != 0)
    def _():
        gk_ref[head] += gk_part
        gv_ref[head] += gv_part


def fused_attention(span, queries, keys, values, grad_mixture, positions, rows=1024):
    heads, length, dim = queries.shape
    blocks = length // rows
    qpos = positions.reshape(length, 1).astype(jnp.int32)
    kpos = positions.reshape(1, length).astype(jnp.int32)
    row_block = pl.BlockSpec((None, rows, dim), lambda b, h, s: (h, b, 0))
    whole_head = pl.BlockSpec((None, length, dim), lambda b, h, s: (h, 0, 0))
    resident = pl.BlockSpec((heads, dim, length), lambda b, h, s: (0, 0, 0))
    f32 = jnp.float32
    return pl.pallas_call(
        attention_kernel,
        out_shape=(
            jax.ShapeDtypeStruct((heads, length, dim), jnp.bfloat16),
            jax.ShapeDtypeStruct((heads, length, dim), f32),
            jax.ShapeDtypeStruct((heads, dim, length), f32),
            jax.ShapeDtypeStruct((heads, dim, length), f32),
        ),
        grid_spec=pltpu.PrefetchScalarGridSpec(
            num_scalar_prefetch=1,
            grid=(blocks, heads),
            in_specs=[
                row_block, whole_head, whole_head, row_block,
                pl.BlockSpec((rows, 1), lambda b, h, s: (b, 0)),
                pl.BlockSpec((1, length), lambda b, h, s: (0, 0)),
            ],
            out_specs=[row_block, row_block, resident, resident],
            scratch_shapes=[pltpu.VMEM((rows, length), f32)],
        ),
        compiler_params=pltpu.CompilerParams(dimension_semantics=("arbitrary", "arbitrary")),
        cost_estimate=pl.CostEstimate(
            flops=12 * heads * length * length * dim,
            transcendentals=heads * length * length,
            bytes_accessed=heads * length * dim * (4 * 2 + 3 * 4 + 2),
        ),
    )(span.reshape(1).astype(jnp.int32), queries, keys, values, grad_mixture, qpos, kpos)


def local(
    tokens,
    norm_gain,
    norm_shift,
    triple_weight,
    mixer_weight,
    inner_weight,
    inner_bias,
    outer_weight,
    outer_bias,
    prefix_length,
    pad_mask,
    cotangent,
):
    nc = lax.axis_size("ctx")
    nf = lax.axis_size("fsdp")
    me = lax.axis_index("ctx")
    _, own_rows, width = tokens.shape
    length = own_rows * nc
    shard_rows = triple_weight.shape[0]
    heads_here = HEADS // nc
    head_cols = heads_here * HEAD_DIM
    ff_here = inner_weight.shape[1] // nc
    ff_rows = outer_weight.shape[0]
    f32, bf16 = jnp.float32, jnp.bfloat16

    triple_cols = (
        triple_weight.reshape(shard_rows, 3, nc, head_cols)
        .transpose(2, 0, 1, 3)
        .reshape(nc, shard_rows, 3 * head_cols)
    )
    inner_cols = inner_weight.reshape(shard_rows, nc, ff_here).transpose(1, 0, 2)
    small = jnp.stack([norm_gain, norm_shift, outer_bias], -1)
    small = jnp.pad(small, ((0, 0), (0, 128 - small.shape[-1])))
    small = jnp.broadcast_to(small[None], (nc,) + small.shape)
    column_payload = jnp.concatenate([triple_cols, inner_cols, small], -1)
    column_payload = ring_all_to_all(column_payload, "ctx")
    split = 3 * head_cols

    bias_rows = jnp.pad(inner_bias[None], ((0, 15), (0, width - inner_bias.shape[0])))
    triple_payload = jnp.concatenate([column_payload[..., :split], column_payload[..., split + ff_here :]], -1)
    pieces = (triple_payload, mixer_weight, bias_rows)
    first_payload = jnp.concatenate([piece.reshape(-1) for piece in pieces]).reshape(-1, width)
    first_block = lax.all_gather(first_payload, "fsdp", axis=0, tiled=False).reshape(nf, -1)
    sizes = [piece.size for piece in pieces]
    triple_block = first_block[:, : sizes[0]].reshape((nf,) + triple_payload.shape)
    triple_block = triple_block.swapaxes(0, 1).reshape(nc * nf * shard_rows, -1)
    mixer_here = first_block[:, sizes[0] : sizes[0] + sizes[1]].reshape(nf * shard_rows, width)
    ibias_here = (
        first_block[:, sizes[0] + sizes[1] : sizes[0] + sizes[1] + inner_bias.shape[0]].reshape(-1).astype(f32)
    )

    ff_payload = jnp.concatenate(
        [column_payload[..., split : split + ff_here].reshape(nc * shard_rows, ff_here), outer_weight], 0
    )
    visible = (pad_mask[0] != 0).astype(f32)
    own_upstream = cotangent[0].astype(f32) * visible
    both = jnp.concatenate([tokens[0], own_upstream.astype(bf16)], -1)
    both = ring_gather(both, "ctx").reshape(length, 2 * width)
    ff_payload, triple_block, both = lax.optimization_barrier((ff_payload, triple_block, both))
    ff_block = lax.all_gather(ff_payload, "fsdp", axis=0, tiled=False)
    triple_here = triple_block[:, :split]
    gain = triple_block[:, split].astype(f32)
    shift = triple_block[:, split + 1].astype(f32)
    obias = triple_block[:, split + 2].astype(f32)

    all_tokens = both[:, :width]
    all_upstream = both[:, width:]

    input_rows = all_tokens.astype(f32)
    center = input_rows - jnp.mean(input_rows, -1, keepdims=True)
    scaling = lax.rsqrt(jnp.mean(center * center, -1, keepdims=True) + eps)
    whitened = center * scaling
    normed = (whitened * gain + shift).astype(bf16)

    owners = (me + jnp.arange(nc)) % nc
    positions = (owners[:, None] * own_rows + jnp.arange(own_rows)[None, :]).reshape(length)
    cos_full, sin_full = pair_tables(positions, 2 * head_cols)
    query_key_value = jnp.dot(normed, triple_here, preferred_element_type=f32)
    heads_shape = (length, heads_here, HEAD_DIM)
    turned = query_key_value[:, : 2 * head_cols]
    turned = turned * cos_full + swap_pairs(turned) * sin_full
    queries = (turned[:, :head_cols] * HEAD_DIM ** (-0.5)).astype(bf16).reshape(heads_shape)
    key_rows = turned[:, head_cols:].astype(bf16).reshape(heads_shape)
    value_rows = query_key_value[:, 2 * head_cols :].reshape(heads_shape).astype(bf16)
    span = prefix_length[0]
    grad_mixture = jnp.dot(all_upstream, mixer_here.T, preferred_element_type=f32).astype(bf16)
    by_head = lambda values: values.reshape(heads_shape).swapaxes(0, 1)
    mixture, grad_queries, grad_keys, grad_values = fused_attention(
        span, by_head(queries), by_head(key_rows), by_head(value_rows), by_head(grad_mixture), positions
    )
    grad_queries = grad_queries.swapaxes(0, 1)
    grad_keys, grad_values = (values.transpose(2, 0, 1) for values in (grad_keys, grad_values))
    mixture = mixture.swapaxes(0, 1).reshape(length, head_cols)
    ff_block, mixture = lax.optimization_barrier((ff_block, mixture))
    inner_here = (
        ff_block[:, : nc * shard_rows]
        .reshape(nf, nc, shard_rows, ff_here)
        .swapaxes(0, 1)
        .reshape(nc * nf * shard_rows, ff_here)
    )
    outer_here = ff_block[:, nc * shard_rows :].reshape(nf * ff_rows, width)

    attention = jnp.dot(mixture, mixer_here, preferred_element_type=f32)
    preact = jnp.dot(normed, inner_here, preferred_element_type=f32) + ibias_here
    gelu_result = jax.nn.gelu(preact, approximate=True).astype(bf16)
    feedforward = jnp.dot(gelu_result, outer_here, preferred_element_type=f32)
    block_sum = ring_scatter((attention + feedforward).reshape(nc, own_rows, width), "ctx")
    layer_output = (tokens[0].astype(f32) + block_sum + obias).astype(bf16)

    ones_block = jnp.ones((length, 16), bf16)
    row_lhs = jnp.concatenate([mixture, gelu_result, ones_block], -1)
    row_product = jnp.dot(row_lhs.T, all_upstream, preferred_element_type=f32).astype(bf16)
    grad_activated = jnp.dot(all_upstream, outer_here.T, preferred_element_type=f32)
    unused_value, gelu_pull = jax.vjp(partial(jax.nn.gelu, approximate=True), preact)
    grad_before_gelu = gelu_pull(grad_activated)[0].astype(bf16)
    grad_inner_weight = jnp.dot(normed.T, grad_before_gelu, preferred_element_type=f32)
    grad_inner_bias = jnp.sum(grad_before_gelu.astype(f32), 0)
    flat_shape = (length, head_cols)
    grad_turned = jnp.concatenate(
        [(grad_queries * HEAD_DIM ** (-0.5)).reshape(flat_shape), grad_keys.reshape(flat_shape)], -1
    )
    grad_turned = grad_turned * cos_full - swap_pairs(grad_turned) * sin_full
    grad_query_key_value = jnp.concatenate(
        [grad_turned, grad_values.reshape(flat_shape)], -1
    ).astype(bf16)
    grad_triple_weight = jnp.dot(normed.T, grad_query_key_value, preferred_element_type=f32)
    grad_normed = jnp.dot(grad_query_key_value, triple_here.T, preferred_element_type=f32)
    grad_normed = grad_normed + jnp.dot(grad_before_gelu, inner_here.T, preferred_element_type=f32)
    grad_norm_gain = jnp.sum(grad_normed * whitened, 0)
    grad_norm_shift = jnp.sum(grad_normed, 0)
    grad_normed = ring_scatter(grad_normed.reshape(nc, own_rows, width), "ctx")

    own_whitened = whitened[:own_rows]
    own_scaling = scaling[:own_rows]
    grad_white = grad_normed * gain
    grad_inputs = own_scaling * (
        grad_white
        - jnp.mean(grad_white, -1, keepdims=True)
        - own_whitened * jnp.mean(grad_white * own_whitened, -1, keepdims=True)
    )
    input_grad = (own_upstream + grad_inputs).astype(bf16)

    small_grads = jnp.stack([grad_norm_gain, grad_norm_shift], -1)
    small_grads = jnp.pad(small_grads, ((0, 0), (0, 128 - small_grads.shape[-1])))
    column_grads = jnp.concatenate(
        [grad_triple_weight, grad_inner_weight, small_grads], -1
    ).astype(bf16)
    column_grads = column_grads.reshape(nc, nf, shard_rows, -1).swapaxes(0, 1).reshape(width, -1)
    column_grads = lax.psum_scatter(column_grads, "fsdp", scatter_dimension=0, tiled=True)
    column_grads = replica_sum(column_grads, "rep").astype(bf16)
    column_grads = column_grads.reshape(nc, shard_rows, -1)
    column_grads = ring_all_to_all(column_grads, "ctx").astype(f32)
    grad_triple_out = (
        column_grads[:, :, : 3 * head_cols]
        .reshape(nc, shard_rows, 3, head_cols)
        .transpose(1, 2, 0, 3)
        .reshape(shard_rows, 3 * nc * head_cols)
    )
    grad_inner_out = (
        column_grads[:, :, 3 * head_cols : 3 * head_cols + ff_here]
        .transpose(1, 0, 2)
        .reshape(shard_rows, nc * ff_here)
    )
    grad_gain_out = jnp.sum(column_grads[:, :, 3 * head_cols + ff_here], 0)
    grad_shift_out = jnp.sum(column_grads[:, :, 3 * head_cols + ff_here + 1], 0)

    mixer_part = row_product[:head_cols].reshape(nf, shard_rows, width)
    outer_part = row_product[head_cols : head_cols + ff_here].reshape(nf, ff_rows, width)
    sums_part = jnp.broadcast_to(row_product[head_cols + ff_here :][None], (nf, 16, width))
    row_grads = jnp.concatenate([mixer_part, outer_part, sums_part], 1)
    row_grads = row_grads.at[:, ff_rows + shard_rows + 1, :ff_rows].set(
        grad_inner_bias.reshape(nf, ff_rows).astype(bf16)
    )
    row_grads = lax.psum_scatter(row_grads, "fsdp", scatter_dimension=0, tiled=True)
    row_grads = replica_sum(row_grads, "rep")[0]
    grad_mixer_out = row_grads[:shard_rows]
    grad_outer_out = row_grads[shard_rows : shard_rows + ff_rows]
    grad_ibias_out = row_grads[shard_rows + ff_rows + 1, :ff_rows]
    fsdp_me = lax.axis_index("fsdp")
    grad_obias_out = lax.dynamic_slice_in_dim(
        row_grads[shard_rows + ff_rows], (me * nf + fsdp_me) * shard_rows, shard_rows
    )

    return (
        layer_output[None],
        input_grad[None],
        grad_gain_out,
        grad_shift_out,
        grad_triple_out,
        grad_mixer_out,
        grad_inner_out,
        grad_ibias_out,
        grad_outer_out,
        grad_obias_out,
    )


def solution(mesh):
    placed = (
        P(("rep", "fsdp"), "ctx", None),
        P(("ctx", "fsdp")),
        P(("ctx", "fsdp")),
        P(("ctx", "fsdp"), None),
        P(("ctx", "fsdp"), None),
        P(("ctx", "fsdp"), None),
        P(("ctx", "fsdp")),
        P(("ctx", "fsdp"), None),
        P(("ctx", "fsdp")),
        P(("rep", "fsdp")),
        P(("rep", "fsdp")),
        P(("rep", "fsdp"), "ctx", None),
    )
    return jax.shard_map(
        local,
        mesh=mesh,
        in_specs=placed,
        out_specs=(
            P(("rep", "fsdp"), "ctx", None),
            P(("rep", "fsdp"), "ctx", None),
            P(("ctx", "fsdp")),
            P(("ctx", "fsdp")),
            P(("ctx", "fsdp"), None),
            P(("ctx", "fsdp"), None),
            P(("ctx", "fsdp"), None),
            P(("ctx", "fsdp")),
            P(("ctx", "fsdp"), None),
            P(("ctx", "fsdp")),
        ),
        check_vma=False,
    )
```
